32 devices in a mesh: ctx: 16 (over z, x, core), fsdp: 2 (over y).
Axes of the slice: x: 2, y: 2, z: 4, core: 2. Of those that a mesh axis runs over, the one named last changes fastest.
Arguments:
- tokens: bfloat16 [2, 2048, 1536], P('fsdp', 'ctx'), may hold values from -6 to 6
- cotangent: bfloat16 [2, 2048, 1536], P('fsdp', 'ctx'), may hold values from -6 to 6
- norm_gain1: bfloat16 [1536], P(('ctx', 'fsdp')), may hold values from 0.5 to 1.5
- w_query: bfloat16 [1536, 1536], P(('ctx', 'fsdp')), may hold values from -0.15625 to 0.15625
- key_weight: bfloat16 [1536, 768], P(('ctx', 'fsdp')), may hold values from -0.15625 to 0.15625
- value_weight: bfloat16 [1536, 768], P(('ctx', 'fsdp')), may hold values from -0.15625 to 0.15625
- w_out: bfloat16 [1536, 1536], P(('ctx', 'fsdp')), may hold values from -1.5 to 1.5
- norm_gain2: bfloat16 [1536], P(('ctx', 'fsdp')), may hold values from 0.5 to 1.5
- w_gate: bfloat16 [1536, 4096], P(('ctx', 'fsdp')), may hold values from -0.15625 to 0.15625
- w_up: bfloat16 [1536, 4096], P(('ctx', 'fsdp')), may hold values from -0.15625 to 0.15625
- w_down: bfloat16 [4096, 1536], P(('ctx', 'fsdp')), may hold values from -0.09375 to 0.09375
Outputs:
- output: bfloat16 [2, 2048, 1536], P('fsdp', 'ctx')
- input_grad: float32 [2, 2048, 1536], P('fsdp', 'ctx')
- grad_gain1: float32 [1536], P(('ctx', 'fsdp'))
- grad_query: float32 [1536, 1536], P(('ctx', 'fsdp'))
- grad_key: float32 [1536, 768], P(('ctx', 'fsdp'))
- grad_value: float32 [1536, 768], P(('ctx', 'fsdp'))
- grad_out: float32 [1536, 1536], P(('ctx', 'fsdp'))
- grad_gain2: float32 [1536], P(('ctx', 'fsdp'))
- grad_gate: float32 [1536, 4096], P(('ctx', 'fsdp'))
- grad_up: float32 [1536, 4096], P(('ctx', 'fsdp'))
- grad_down: float32 [4096, 1536], P(('ctx', 'fsdp'))
The draws below stay inside these ranges and needn't reach their ends.
All inputs are finite; a program needn't handle non-finite values.
Results may differ from the reference program's by a relative error of at most 0.025.
Values may be sent and summed in bfloat16 or wider, within the bound.
No kernel may reach another device: no remote copies, remote signals or barrier semaphores. Data moves between devices by JAX's collectives and lax.ppermute only.
A program may use at most 384 MiB of HBM per device.

```python
import jax
import jax.numpy as jnp
from jax import lax

MODEL_WIDTH = 1536
QUERY_HEADS = 16
KEY_VALUE_HEADS = 8
HEAD_SIZE = 96
FF = 4096
SEQ = 2048
SEQS = 2


def level_of(own_key, shape, pieces, least, high):
    level = 1.0
    for position, parts in pieces:
        heights = jax.random.uniform(jax.random.fold_in(jax.random.fold_in(own_key, 6), position), (parts,), jnp.float32, least / len(pieces), high / len(pieces))
        level = level * jnp.repeat(jnp.exp(heights), shape[position] // parts).reshape((-1,) + (1,) * (len(shape) - 1 - position))
    return level


def scatter_about(key, shape, width, bound, pieces=(), kind=jnp.bfloat16):
    entries = jax.random.normal(key, shape, jnp.float32) * width
    if len(pieces) > 0:
        entries = level_of(key, shape, pieces, -0.22, 0.18) * entries
    return jnp.clip(entries, min=-bound, max=bound).astype(kind)


def setup_inputs(seed: int = 0) -> dict:
    seeds = jax.random.split(jax.random.key(seed), 12)
    tokens = scatter_about(seeds[0], (SEQS, SEQ, MODEL_WIDTH), 1.0, 6.0, ((0, 2), (1, 16)))
    cotangent = scatter_about(seeds[1], (SEQS, SEQ, MODEL_WIDTH), 1.0, 6.0, ((0, 2), (1, 16)))
    norm_gain1 = jnp.clip(1.0 + 0.1 * jax.random.normal(seeds[2], (MODEL_WIDTH,), jnp.float32), 0.5, 1.5).astype(jnp.bfloat16)
    w_query = scatter_about(seeds[3], (MODEL_WIDTH, QUERY_HEADS * HEAD_SIZE), MODEL_WIDTH ** -0.5, 0.15625, ((0, 32),))
    key_weight = scatter_about(seeds[4], (MODEL_WIDTH, KEY_VALUE_HEADS * HEAD_SIZE), MODEL_WIDTH ** -0.5, 0.15625, ((0, 32),))
    value_weight = scatter_about(seeds[5], (MODEL_WIDTH, KEY_VALUE_HEADS * HEAD_SIZE), MODEL_WIDTH ** -0.5, 0.15625, ((0, 32),))
    w_out = scatter_about(seeds[6], (QUERY_HEADS * HEAD_SIZE, MODEL_WIDTH), 16 ** -0.5, 1.5, ((0, 32),))
    norm_gain2 = jnp.clip(1.0 + 0.1 * jax.random.normal(seeds[7], (MODEL_WIDTH,), jnp.float32), 0.5, 1.5).astype(jnp.bfloat16)
    w_gate = scatter_about(seeds[8], (MODEL_WIDTH, FF), MODEL_WIDTH ** -0.5, 0.15625, ((0, 32),))
    w_up = scatter_about(seeds[9], (MODEL_WIDTH, FF), MODEL_WIDTH ** -0.5, 0.15625, ((0, 32),))
    w_down = scatter_about(seeds[10], (FF, MODEL_WIDTH), FF ** -0.5, 0.09375, ((0, 32),))
    return {"tokens": tokens, "cotangent": cotangent, "norm_gain1": norm_gain1, "w_query": w_query, "key_weight": key_weight, "value_weight": value_weight, "w_out": w_out, "norm_gain2": norm_gain2, "w_gate": w_gate, "w_up": w_up, "w_down": w_down}


rope_base = 100000.0
norm_eps = 1e-05
masked_value = -1e+30
highest = lax.Precision.HIGHEST

@jax.custom_vjp
def low(v):
    return lax.optimization_barrier(v.astype(jnp.bfloat16)).astype(jnp.float32)

@jax.custom_vjp
def low_back(v):
    return v

def low_keep(v):
    return (low(v), None)

def low_pass(kept, grad):
    return (grad,)

def back_keep(v):
    return (v, None)

def back_low(kept, grad):
    return (low(grad),)
low.defvjp(low_keep, low_pass)
low_back.defvjp(back_keep, back_low)

def rms_norm(value_rows, gain):
    return value_rows * lax.rsqrt(lax.optimization_barrier(jnp.mean(value_rows * value_rows, axis=-1, keepdims=True)) + norm_eps) * gain

def apply_rotary(value_rows, token_position):
    half = value_rows.shape[-1] // 2
    exponent = jnp.arange(half, dtype=jnp.float32) * (2.0 / value_rows.shape[-1])
    freq = rope_base ** (-exponent)
    angle = token_position[:, None] * freq[None, :]
    cosine = jnp.cos(angle)[:, None, :]
    sine = jnp.sin(angle)[:, None, :]
    first = value_rows[..., :half]
    second = value_rows[..., half:]
    return jnp.concatenate([first * cosine - second * sine, second * cosine + first * sine], axis=-1)

def product(left, right):
    return jnp.dot(left, right, precision=highest)

def attention_layer(query_rows, key_rows, value_rows):
    sequence_length = query_rows.shape[0]
    sequence_block = min(512, sequence_length)
    scale = HEAD_SIZE ** (-0.5)
    key_pos = jnp.arange(sequence_length, dtype=jnp.int32)
    sequence_blocks = query_rows.reshape(sequence_length // sequence_block, sequence_block, KEY_VALUE_HEADS, QUERY_HEADS // KEY_VALUE_HEADS, HEAD_SIZE)
    starts = jnp.arange(sequence_length // sequence_block, dtype=jnp.int32) * sequence_block

    def one_block(item):
        query_block, first = item
        scores = low_back(jnp.einsum('tkgd,skd->kgts', query_block, key_rows, precision=highest) * scale)
        query_pos = first + jnp.arange(sequence_block, dtype=jnp.int32)
        visible = key_pos[None, :] <= query_pos[:, None]
        scores = jnp.where(visible, scores, masked_value)
        shifted = jnp.exp(scores - lax.optimization_barrier(jnp.max(scores, axis=-1, keepdims=True)))
        prob = low(shifted / lax.optimization_barrier(jnp.sum(shifted, axis=-1, keepdims=True)))
        return jnp.einsum('kgts,skd->tkgd', prob, value_rows, precision=highest)
    mixed_heads = lax.map(jax.checkpoint(one_block), (sequence_blocks, starts))
    return mixed_heads.reshape(sequence_length, QUERY_HEADS * HEAD_SIZE)

def layer(inputs, gain1, w_query, key_weight, value_weight, w_out, gain2, w_gate, w_up, w_down):
    sequence_length = inputs.shape[0]
    token_position = jnp.arange(sequence_length, dtype=jnp.float32)
    normed1 = low(rms_norm(inputs, gain1))
    query_rows = low_back(product(normed1, w_query))
    key_rows = low_back(product(normed1, key_weight))
    value_rows = low(low_back(product(normed1, value_weight)))
    query_rows = low(apply_rotary(query_rows.reshape(sequence_length, QUERY_HEADS, HEAD_SIZE), token_position))
    key_rows = low(apply_rotary(key_rows.reshape(sequence_length, KEY_VALUE_HEADS, HEAD_SIZE), token_position))
    mixed_heads = attention_layer(query_rows.reshape(sequence_length, KEY_VALUE_HEADS, QUERY_HEADS // KEY_VALUE_HEADS, HEAD_SIZE), key_rows, value_rows.reshape(sequence_length, KEY_VALUE_HEADS, HEAD_SIZE))
    mixed_heads = low(low_back(mixed_heads))
    branch = low_back(product(mixed_heads, w_out))
    middle = inputs + branch
    normed2 = low(rms_norm(middle, gain2))
    gate = low_back(product(normed2, w_gate))
    upper = low_back(product(normed2, w_up))
    hidden = low(jax.nn.silu(gate) * upper)
    return middle + low_back(product(hidden, w_down))

def reference(tokens, cotangent, norm_gain1, w_query, key_weight, value_weight, w_out, norm_gain2, w_gate, w_up, w_down):
    params = tuple((item.astype(jnp.float32) for item in (norm_gain1, w_query, key_weight, value_weight, w_out, norm_gain2, w_gate, w_up, w_down)))

    def one_sequence(item):
        inputs, incoming = item
        result, backward = jax.vjp(layer, inputs, *params)
        return (result, backward(incoming))
    results, grads = lax.map(one_sequence, (tokens.astype(jnp.float32), cotangent.astype(jnp.float32)))
    summed = tuple((lax.optimization_barrier(jnp.sum(item, axis=0)) for item in grads[1:]))
    return (results.astype(jnp.bfloat16), grads[0], summed[0], summed[1], summed[2], summed[3], summed[4], summed[5], summed[6], summed[7], summed[8])
```

```python
import functools

import jax
import jax.numpy as jnp
import numpy as np
from jax import lax
from jax.experimental import pallas as pl
from jax.experimental.pallas import tpu as pltpu
from jax.sharding import Mesh
from jax.sharding import PartitionSpec as P

QUERY_HEADS = 16
KEY_VALUE_HEADS = 8
HEAD_SIZE = 96


rope_base = 100000.0
norm_eps = 1e-05
masked_value = -1e30
key_block = 512


def rms_norm(value_rows, gain):
    return (
        value_rows
        * lax.rsqrt(jnp.mean(value_rows * value_rows, axis=-1, keepdims=True) + norm_eps)
        * gain
    )


def apply_rotary(value_rows, token_position):
    half = value_rows.shape[-1] // 2
    exponent = jnp.arange(half, dtype=jnp.float32) * (2.0 / value_rows.shape[-1])
    freq = rope_base ** (-exponent)
    angle = token_position[:, None] * freq[None, :]
    cosine = jnp.cos(angle)[:, None, :]
    sine = jnp.sin(angle)[:, None, :]
    first = value_rows[..., :half]
    second = value_rows[..., half:]
    return jnp.concatenate(
        [first * cosine - second * sine, second * cosine + first * sine], axis=-1
    )


def matmul(left, right):
    return jnp.dot(left, right, preferred_element_type=jnp.float32)


def key_pieces(key_rows, value_rows, key_value_heads, head_dim):
    count = key_rows.shape[0]
    number = count // key_block
    key_sets = key_rows.reshape(number, key_block, key_value_heads, head_dim)
    value_sets = value_rows.reshape(number, key_block, key_value_heads, head_dim)
    starts = jnp.arange(number, dtype=jnp.int32) * key_block
    return (key_sets, value_sets, starts, key_block)


def fold_keys(carry, key_rows, value_rows, query_rows, query_pos):
    key_value_heads = query_rows.shape[1]
    head_dim = query_rows.shape[3]
    scale = head_dim ** (-0.5)
    key_sets, value_sets, starts, size = key_pieces(key_rows, value_rows, key_value_heads, head_dim)

    def fold_one_piece(state, item):
        key_set, value_set, begin = item

        def fold_live(state):
            top, total, summed = state
            scores = (
                jnp.einsum(
                    "tkgd,skd->kgts", query_rows, key_set, preferred_element_type=jnp.float32
                )
                * scale
            )
            visible = (begin + jnp.arange(size, dtype=jnp.int32))[None, :] <= query_pos[:, None]
            scores = jnp.where(visible, scores, masked_value)
            new_top = jnp.maximum(top, jnp.max(scores, axis=-1))
            weights = jnp.where(visible, jnp.exp(scores - new_top[..., None]), 0.0)
            factor = jnp.exp(top - new_top)
            total = total * factor + jnp.sum(weights, axis=-1)
            summed = summed * factor[..., None] + jnp.einsum(
                "kgts,skd->kgtd",
                weights.astype(jnp.bfloat16),
                value_set,
                preferred_element_type=jnp.float32,
            )
            return (new_top, total, summed)

        def fold_skipped(state):
            return state

        return (lax.cond(begin <= query_pos[-1], fold_live, fold_skipped, state), None)

    carry, _ = lax.scan(fold_one_piece, carry, (key_sets, value_sets, starts))
    return carry


def back_keys(key_rows, value_rows, query_rows, query_pos, d_heads, log_total, delta):
    rows, key_value_heads, groups, head_dim = query_rows.shape
    scale = head_dim ** (-0.5)
    key_sets, value_sets, starts, size = key_pieces(key_rows, value_rows, key_value_heads, head_dim)

    def back_one_piece(d_query, item):
        key_set, value_set, begin = item

        def back_live(d_query):
            scores = (
                jnp.einsum(
                    "tkgd,skd->kgts", query_rows, key_set, preferred_element_type=jnp.float32
                )
                * scale
            )
            visible = (begin + jnp.arange(size, dtype=jnp.int32))[None, :] <= query_pos[:, None]
            prob = jnp.where(visible, jnp.exp(scores - log_total[..., None]), 0.0)
            d_prob = jnp.einsum(
                "tkgd,skd->kgts", d_heads, value_set, preferred_element_type=jnp.float32
            )
            d_scores = (prob * (d_prob - delta[..., None])).astype(jnp.bfloat16)
            d_query = d_query + scale * jnp.einsum(
                "kgts,skd->tkgd", d_scores, key_set, preferred_element_type=jnp.float32
            )
            d_key = scale * jnp.einsum(
                "kgts,tkgd->skd", d_scores, query_rows, preferred_element_type=jnp.float32
            )
            d_value = jnp.einsum(
                "kgts,tkgd->skd",
                prob.astype(jnp.bfloat16),
                d_heads,
                preferred_element_type=jnp.float32,
            )
            return (
                d_query,
                (
                    d_key.reshape(size, key_value_heads * head_dim),
                    d_value.reshape(size, key_value_heads * head_dim),
                ),
            )

        def back_skipped(d_query):
            empty = jnp.zeros((size, key_value_heads * head_dim), jnp.float32)
            return (d_query, (empty, empty))

        return lax.cond(begin <= query_pos[-1], back_live, back_skipped, d_query)

    start_grad = jnp.zeros((rows, key_value_heads, groups, head_dim), jnp.float32)
    d_query, (d_keys, d_values) = lax.scan(
        back_one_piece, start_grad, (key_sets, value_sets, starts)
    )
    return (
        d_query,
        d_keys.reshape(key_rows.shape[0], key_value_heads * head_dim),
        d_values.reshape(key_rows.shape[0], key_value_heads * head_dim),
    )


def local(
    tokens,
    cotangent,
    norm_gain1,
    w_query,
    key_weight,
    value_weight,
    w_out,
    norm_gain2,
    w_gate,
    w_up,
    w_down,
):
    rows = tokens.shape[1]
    key_value_heads = KEY_VALUE_HEADS
    heads = QUERY_HEADS
    head_dim = HEAD_SIZE
    groups = heads // key_value_heads
    first_row = lax.axis_index("ctx") * rows
    query_pos = first_row + jnp.arange(rows, dtype=jnp.int32)
    token_position = query_pos.astype(jnp.float32)
    inputs = tokens[0].astype(jnp.float32)
    gathered = (
        lax.all_gather(norm_gain1, ("ctx", "fsdp"), axis=0, tiled=True),
        lax.all_gather(w_query, ("ctx", "fsdp"), axis=0, tiled=True),
        lax.all_gather(key_weight, ("ctx", "fsdp"), axis=0, tiled=True),
        lax.all_gather(value_weight, ("ctx", "fsdp"), axis=0, tiled=True),
        lax.all_gather(w_out, ("ctx", "fsdp"), axis=0, tiled=True),
        lax.all_gather(norm_gain2, ("ctx", "fsdp"), axis=0, tiled=True),
        lax.all_gather(w_gate, ("ctx", "fsdp"), axis=0, tiled=True),
        lax.all_gather(w_up, ("ctx", "fsdp"), axis=0, tiled=True),
        lax.all_gather(w_down, ("ctx", "fsdp"), axis=0, tiled=True),
    )
    gain_one = gathered[0].astype(jnp.float32)
    gain_two = gathered[5].astype(jnp.float32)
    normed1 = rms_norm(inputs, gain_one).astype(jnp.bfloat16)
    query_pre = matmul(normed1, gathered[1]).reshape(rows, heads, head_dim)
    key_pre = matmul(normed1, gathered[2]).reshape(rows, key_value_heads, head_dim)
    value = matmul(normed1, gathered[3]).astype(jnp.bfloat16)
    query_rows = (
        apply_rotary(query_pre, token_position)
        .astype(jnp.bfloat16)
        .reshape(rows, key_value_heads, groups, head_dim)
    )
    key_rows = (
        apply_rotary(key_pre, token_position)
        .reshape(rows, key_value_heads * head_dim)
        .astype(jnp.bfloat16)
    )
    start_state = (
        jnp.full((key_value_heads, groups, rows), masked_value, jnp.float32),
        jnp.zeros((key_value_heads, groups, rows), jnp.float32),
        jnp.zeros((key_value_heads, groups, rows, head_dim), jnp.float32),
    )
    top, total, summed = fold_keys(
        start_state,
        lax.all_gather(key_rows, "ctx", axis=0, tiled=True),
        lax.all_gather(value, "ctx", axis=0, tiled=True),
        query_rows,
        query_pos,
    )
    mixed_heads = jnp.transpose(summed / total[..., None], (2, 0, 1, 3))
    log_total = top + jnp.log(total)
    mixed_low = mixed_heads.reshape(rows, heads * head_dim).astype(jnp.bfloat16)
    middle = inputs + matmul(mixed_low, gathered[4])
    normed2 = rms_norm(middle, gain_two).astype(jnp.bfloat16)
    gate = matmul(normed2, gathered[6])
    upper = matmul(normed2, gathered[7])
    hidden = (jax.nn.silu(gate) * upper).astype(jnp.bfloat16)
    result = middle + matmul(hidden, gathered[8])
    gathered = (
        lax.all_gather(norm_gain1, ("ctx", "fsdp"), axis=0, tiled=True),
        lax.all_gather(w_query, ("ctx", "fsdp"), axis=0, tiled=True),
        lax.all_gather(key_weight, ("ctx", "fsdp"), axis=0, tiled=True),
        lax.all_gather(value_weight, ("ctx", "fsdp"), axis=0, tiled=True),
        lax.all_gather(w_out, ("ctx", "fsdp"), axis=0, tiled=True),
        lax.all_gather(norm_gain2, ("ctx", "fsdp"), axis=0, tiled=True),
        lax.all_gather(w_gate, ("ctx", "fsdp"), axis=0, tiled=True),
        lax.all_gather(w_up, ("ctx", "fsdp"), axis=0, tiled=True),
        lax.all_gather(w_down, ("ctx", "fsdp"), axis=0, tiled=True),
    )
    incoming = cotangent[0].astype(jnp.float32)
    incoming_low = incoming.astype(jnp.bfloat16)
    grad_down = matmul(hidden.T, incoming_low)
    d_hidden = matmul(incoming_low, gathered[8].T)
    _, swiglu_back = jax.vjp(lambda gate_in, upper_in: jax.nn.silu(gate_in) * upper_in, gate, upper)
    d_gate, d_upper = swiglu_back(d_hidden)
    d_gate = d_gate.astype(jnp.bfloat16)
    d_upper = d_upper.astype(jnp.bfloat16)
    grad_gate = matmul(normed2.T, d_gate)
    grad_up = matmul(normed2.T, d_upper)
    d_normed2 = matmul(d_gate, gathered[6].T) + matmul(d_upper, gathered[7].T)
    _, norm_back2 = jax.vjp(rms_norm, middle, gain_two)
    d_middle, grad_gain2 = norm_back2(d_normed2)
    d_middle = d_middle + incoming
    owned_gain2, owned_gate, owned_up, owned_down = (
        lax.psum_scatter(grad_gain2, ("ctx", "fsdp"), scatter_dimension=0, tiled=True),
        lax.psum_scatter(grad_gate, ("ctx", "fsdp"), scatter_dimension=0, tiled=True),
        lax.psum_scatter(grad_up, ("ctx", "fsdp"), scatter_dimension=0, tiled=True),
        lax.psum_scatter(grad_down, ("ctx", "fsdp"), scatter_dimension=0, tiled=True),
    )
    d_middle_low = d_middle.astype(jnp.bfloat16)
    grad_out = matmul(mixed_low.T, d_middle_low)
    d_mixed = matmul(d_middle_low, gathered[4].T).astype(jnp.bfloat16)
    d_heads = d_mixed.reshape(rows, key_value_heads, groups, head_dim)
    delta = jnp.transpose(jnp.sum(d_heads.astype(jnp.float32) * mixed_heads, axis=-1), (1, 2, 0))
    back_keys_all, back_values_all = (
        lax.all_gather(key_rows, "ctx", axis=0, tiled=True),
        lax.all_gather(value, "ctx", axis=0, tiled=True),
    )
    d_query_rot, d_keys_all, d_values_all = back_keys(
        back_keys_all, back_values_all, query_rows, query_pos, d_heads, log_total, delta
    )
    d_keys_rot, d_value = (
        lax.psum_scatter(d_keys_all, "ctx", scatter_dimension=0, tiled=True),
        lax.psum_scatter(d_values_all, "ctx", scatter_dimension=0, tiled=True),
    )
    _, rotate_back_query = jax.vjp(
        lambda values_in: apply_rotary(values_in, token_position), query_pre
    )
    _, rotate_back_key = jax.vjp(lambda values_in: apply_rotary(values_in, token_position), key_pre)
    d_query = (
        rotate_back_query(d_query_rot.reshape(rows, heads, head_dim))[0]
        .reshape(rows, heads * head_dim)
        .astype(jnp.bfloat16)
    )
    d_key = (
        rotate_back_key(d_keys_rot.reshape(rows, key_value_heads, head_dim))[0]
        .reshape(rows, key_value_heads * head_dim)
        .astype(jnp.bfloat16)
    )
    d_value = d_value.astype(jnp.bfloat16)
    grad_query = matmul(normed1.T, d_query)
    grad_key = matmul(normed1.T, d_key)
    grad_value = matmul(normed1.T, d_value)
    d_normed1 = (
        matmul(d_query, gathered[1].T)
        + matmul(d_key, gathered[2].T)
        + matmul(d_value, gathered[3].T)
    )
    _, norm_back1 = jax.vjp(rms_norm, inputs, gain_one)
    d_inputs, grad_gain1 = norm_back1(d_normed1)
    input_grad = d_inputs + d_middle
    owned_gain1, owned_query, owned_key, owned_value, owned_out = (
        lax.psum_scatter(grad_gain1, ("ctx", "fsdp"), scatter_dimension=0, tiled=True),
        lax.psum_scatter(grad_query, ("ctx", "fsdp"), scatter_dimension=0, tiled=True),
        lax.psum_scatter(grad_key, ("ctx", "fsdp"), scatter_dimension=0, tiled=True),
        lax.psum_scatter(grad_value, ("ctx", "fsdp"), scatter_dimension=0, tiled=True),
        lax.psum_scatter(grad_out, ("ctx", "fsdp"), scatter_dimension=0, tiled=True),
    )
    return (
        result.astype(jnp.bfloat16)[None],
        input_grad[None],
        owned_gain1,
        owned_query,
        owned_key,
        owned_value,
        owned_out,
        owned_gain2,
        owned_gate,
        owned_up,
        owned_down,
    )


bf16 = jnp.bfloat16
f32 = jnp.float32
score_scale = HEAD_SIZE ** (-0.5)
log2_e = 1.4426950408889634
ln_2 = 0.6931471805599453


def dot_at(left, right, left_dim, right_dim):
    return lax.dot_general(
        left, right, (((left_dim,), (right_dim,)), ((), ())), preferred_element_type=jnp.float32
    )


def heads_forward_kernel(step, q_ref, k_ref, v_ref, mixed_ref, prob_ref):
    tokens = q_ref.shape[1]
    offset = 0
    for begin in range(0, tokens, step):
        end = begin + step
        scores = dot_at(k_ref[:, 0:end], q_ref[:, begin:end], 0, 0)
        key = lax.broadcasted_iota(jnp.int32, (step, step), 0)
        query = lax.broadcasted_iota(jnp.int32, (step, step), 1)
        last = jnp.where(key <= query, scores[begin:end], masked_value)
        top = jnp.max(last, axis=0, keepdims=True)
        if begin:
            top = jnp.maximum(top, jnp.max(scores[:begin], axis=0, keepdims=True))
        last = jnp.exp2(last - top)
        total = jnp.sum(last, axis=0, keepdims=True)
        if begin:
            first = jnp.exp2(scores[:begin] - top)
            total = total + jnp.sum(first, axis=0, keepdims=True)
        inverse = 1.0 / total
        prob_ref[offset + begin : offset + end, :] = (last * inverse).astype(bf16)
        if begin:
            prob_ref[offset : offset + begin, :] = (first * inverse).astype(bf16)
        mixed_ref[:, begin:end] = dot_at(
            v_ref[:, 0:end], prob_ref[offset : offset + end, :], 1, 0
        )
        offset += end


def heads_backward_kernel(
    step, q_ref, k_ref, v_ref, prob_ref, mixed_ref, d_mixed_ref, d_q_ref, d_k_ref, d_v_ref
):
    tokens = q_ref.shape[1]
    offset = 0
    for begin in range(0, tokens, step):
        end = begin + step
        d_mixed = d_mixed_ref[:, begin:end]
        delta = jnp.sum(d_mixed.astype(f32) * mixed_ref[:, begin:end], axis=0, keepdims=True)
        prob = prob_ref[offset : offset + end, :]
        d_prob = dot_at(v_ref[:, 0:end], d_mixed, 0, 0)
        d_scores = (prob.astype(f32) * (d_prob - delta)).astype(bf16)
        d_q_ref[:, begin:end] = dot_at(k_ref[:, 0:end], d_scores, 1, 0) * score_scale
        d_v = dot_at(d_mixed, prob, 1, 1)
        d_k = dot_at(q_ref[:, begin:end], d_scores, 1, 1) * ln_2
        if begin:
            d_v_ref[:, 0:begin] += d_v[:, 0:begin]
            d_k_ref[:, 0:begin] += d_k[:, 0:begin]
        d_v_ref[:, begin:end] = d_v[:, begin:end]
        d_k_ref[:, begin:end] = d_k[:, begin:end]
        offset += end


def heads_forward(q, k, v, step):
    size, tokens = q.shape
    blocks = tokens // step
    pairs = step * blocks * (blocks + 1) // 2
    whole = pl.BlockSpec(memory_space=pltpu.VMEM)
    return pl.pallas_call(
        functools.partial(heads_forward_kernel, step),
        out_shape=(
            jax.ShapeDtypeStruct((size, tokens), f32),
            jax.ShapeDtypeStruct((pairs, step), bf16),
        ),
        in_specs=[whole] * 3,
        out_specs=(whole, whole),
        compiler_params=pltpu.CompilerParams(vmem_limit_bytes=40 * 2**20),
        cost_estimate=pl.CostEstimate(
            flops=4 * size * pairs * step, bytes_accessed=pairs * step * 2, transcendentals=pairs * step
        ),
        name="heads_forward",
    )(q, k, v)


def heads_backward(q, k, v, prob, mixed, d_mixed, step):
    size, tokens = q.shape
    whole = pl.BlockSpec(memory_space=pltpu.VMEM)
    return pl.pallas_call(
        functools.partial(heads_backward_kernel, step),
        out_shape=(jax.ShapeDtypeStruct((size, tokens), f32),) * 3,
        in_specs=[whole] * 6,
        out_specs=(whole,) * 3,
        compiler_params=pltpu.CompilerParams(vmem_limit_bytes=40 * 2**20),
        cost_estimate=pl.CostEstimate(
            flops=8 * size * prob.size, bytes_accessed=prob.size * 2, transcendentals=0
        ),
        name="heads_backward",
    )(q, k, v, prob, mixed, d_mixed)


def ring_of(count):
    order = list(range(0, count, 2)) + list(range(count - 1, 0, -2))
    forward = [(order[i], order[(i + 1) % count]) for i in range(count)]
    backward = [(there, here) for here, there in forward]
    return order, forward, backward


def ring_gather(shards, count):
    order, forward, backward = ring_of(count)
    order = jnp.array(order, jnp.int32)
    place = jnp.argsort(order)[lax.axis_index("d")]
    outs = []
    for shard in shards:
        out = jnp.zeros((count,) + shard.shape, shard.dtype)
        outs.append(lax.dynamic_update_slice_in_dim(out, shard[None], lax.axis_index("d"), 0))
    ahead = list(shards)
    behind = list(shards)
    for hop in range(1, count // 2 + 1):
        left = order[(place + count - hop) % count]
        right = order[(place + hop) % count]
        if hop < count // 2:
            ahead = [lax.ppermute(a, "d", forward) for a in ahead]
            behind = [lax.ppermute(b, "d", backward) for b in behind]
            ahead, behind = lax.optimization_barrier((ahead, behind))
            outs = [
                lax.dynamic_update_slice_in_dim(o, a[None], left, 0) for o, a in zip(outs, ahead)
            ]
            outs = [
                lax.dynamic_update_slice_in_dim(o, b[None], right, 0) for o, b in zip(outs, behind)
            ]
        else:
            half = [a.shape[0] // 2 for a in ahead]
            ahead = [lax.ppermute(a[:h], "d", forward) for a, h in zip(ahead, half)]
            behind = [lax.ppermute(b[h:], "d", backward) for b, h in zip(behind, half)]
            outs = [
                lax.dynamic_update_slice(o, a[None], (left,) + (0,) * a.ndim)
                for o, a in zip(outs, ahead)
            ]
            outs = [
                lax.dynamic_update_slice(o, b[None], (left, h) + (0,) * (b.ndim - 1))
                for o, b, h in zip(outs, behind, half)
            ]
    return outs


def ring_scatter(terms, count):
    order, forward, backward = ring_of(count)
    order = jnp.array(order, jnp.int32)
    place = jnp.argsort(order)[lax.axis_index("d")]

    def part(term, position, side):
        half = term.shape[1] // 2
        start = (order[position % count], side * half) + (0,) * (term.ndim - 2)
        return lax.dynamic_slice(term, start, (1, half) + term.shape[2:])[0]

    ahead = [part(t, place + count - 1, 0) for t in terms]
    behind = [part(t, place + 1, 1) for t in terms]
    for hop in range(1, count):
        ahead = [lax.ppermute(a, "d", forward) for a in ahead]
        behind = [lax.ppermute(b, "d", backward) for b in behind]
        ahead, behind = lax.optimization_barrier((ahead, behind))
        kind = f32 if hop == count - 1 else bf16
        ahead = [
            (a.astype(f32) + part(t, place + 2 * count - 1 - hop, 0).astype(f32)).astype(kind)
            for a, t in zip(ahead, terms)
        ]
        behind = [
            (b.astype(f32) + part(t, place + 1 + hop, 1).astype(f32)).astype(kind)
            for b, t in zip(behind, terms)
        ]
    return [jnp.concatenate([a, b], axis=0) for a, b in zip(ahead, behind)]


def swap(values, axis):
    return lax.ppermute(values, axis, [(0, 1), (1, 0)])


def rows_of_group(own):
    pair = lax.all_gather(own, "y", axis=0)
    return lax.all_gather(pair, "core", axis=1)


def own_rows_sum(terms):
    core = lax.axis_index("core")
    seq = lax.axis_index("y")
    away = lax.dynamic_index_in_dim(terms, 1 - core, 1, False).astype(bf16)
    kept = lax.dynamic_index_in_dim(terms, core, 1, False)
    pair = kept + swap(away, "core").astype(f32)
    away = lax.dynamic_index_in_dim(pair, 1 - seq, 0, False).astype(bf16)
    kept = lax.dynamic_index_in_dim(pair, seq, 0, False)
    return kept + swap(away, "y").astype(f32)


def all_to_all(values, axes):
    return lax.all_to_all(values, axes, 0, 0, tiled=True)


def inverse_rms(values):
    return lax.rsqrt(jnp.mean(values * values, axis=-1, keepdims=True) + norm_eps)


def head_layer(
    count,
    tokens,
    cotangent,
    norm_gain1,
    w_query,
    key_weight,
    value_weight,
    w_out,
    norm_gain2,
    w_gate,
    w_up,
    w_down,
):
    rows, width = tokens.shape[1:]
    own = w_query.shape[0]
    ff_own = w_down.shape[0]
    half = HEAD_SIZE // 2
    quarter = HEAD_SIZE // 4
    group = 4 * own
    seq_rows = 2 * rows
    length = count * seq_rows
    step = seq_rows

    gain1 = norm_gain1.astype(f32)[:, None]
    gain2 = norm_gain2.astype(f32)[:, None]

    with jax.named_scope("attention_weights"):
        query_cols = (gain1 * w_query.astype(f32)).astype(bf16)
        key_cols = (gain1 * key_weight.astype(f32)).astype(bf16)
        value_cols = (gain1 * value_weight.astype(f32)).astype(bf16)
        qkv_cols = jnp.concatenate(
            [
                query_cols.reshape(own, count, 4, half).transpose(2, 0, 1, 3),
                key_cols.reshape(own, count, 4, quarter).transpose(2, 0, 1, 3),
                value_cols.reshape(own, count, 4, quarter).transpose(2, 0, 1, 3),
            ],
            axis=-1,
        ).reshape(4, own, count * HEAD_SIZE)
        qkv_rows = all_to_all(qkv_cols, ("core", "y")).reshape(group, count * HEAD_SIZE)
        (qkv_weight,) = ring_gather([qkv_rows], count)
        qkv_weight = qkv_weight.reshape(width, count * HEAD_SIZE)
    with jax.named_scope("feed_forward_weights"):
        gate_cols = (gain2 * w_gate.astype(f32)).astype(bf16)
        up_cols = (gain2 * w_up.astype(f32)).astype(bf16)
        pair_cols = jnp.concatenate(
            [
                gate_cols.reshape(own, count, 4, ff_own).transpose(2, 0, 1, 3),
                up_cols.reshape(own, count, 4, ff_own).transpose(2, 0, 1, 3),
            ],
            axis=2,
        ).reshape(4, own, 2 * count * ff_own)
        pair_rows = all_to_all(pair_cols, ("core", "y")).reshape(group, 2 * count * ff_own)
        pair_rows, own_out, own_down, qkv_weight = lax.optimization_barrier(
            (pair_rows, w_out, w_down, qkv_weight)
        )
        pair_weight, out_weight, down_weight = ring_gather([pair_rows, own_out, own_down], count)
        pair_weight = pair_weight.reshape(width, 2 * count * ff_own)
        out_weight = out_weight.reshape(count * own, width)
        down_weight = down_weight.reshape(count * ff_own, width)

    inputs = tokens[0].astype(f32)
    r1 = inverse_rms(inputs)
    n1_own = (inputs * r1).astype(bf16)
    n1 = rows_of_group(n1_own).reshape(2 * seq_rows, width)
    d_out = rows_of_group(cotangent[0]).reshape(2 * seq_rows, width)
    qkv = dot_at(qkv_weight, n1, 0, 1).astype(bf16)
    qkv = qkv.reshape(count, HEAD_SIZE, 2, seq_rows).transpose(0, 2, 1, 3)
    qkv = all_to_all(qkv.reshape(2 * count, HEAD_SIZE, seq_rows), ("d", "y"))
    qkv = qkv.reshape(count, 2, HEAD_SIZE, seq_rows)
    q_parts = qkv[:, :, :half].transpose(1, 2, 0, 3).reshape(2, half, length)
    kv = lax.all_gather(qkv[:, :, half:], "core", axis=0)
    kv = kv.reshape(2, count, 2, 2, quarter, seq_rows).transpose(3, 0, 2, 4, 1, 5)
    k_parts, v_parts = kv.reshape(2, 2, half, length)
    position = jnp.arange(length, dtype=f32)
    exponent = jnp.arange(half, dtype=f32) * (2.0 / HEAD_SIZE)
    angle = (rope_base ** (-exponent))[:, None] * position[None, :]
    cosine = jnp.cos(angle)
    sine = jnp.sin(angle)

    def rotate(first, second):
        return jnp.concatenate(
            [first * cosine - second * sine, second * cosine + first * sine], axis=0
        )

    def rotate_back(turned):
        first = turned[:half]
        second = turned[half:]
        return jnp.stack(
            [first * cosine + second * sine, second * cosine - first * sine], axis=0
        )

    q_parts = q_parts.astype(f32)
    k_parts = k_parts.astype(f32)
    q = (rotate(q_parts[0], q_parts[1]) * (score_scale * log2_e)).astype(bf16)
    k = rotate(k_parts[0], k_parts[1]).astype(bf16)
    v = v_parts.reshape(HEAD_SIZE, length)
    mixed, prob = heads_forward(q, k, v, step)
    mixed_send = mixed.astype(bf16).reshape(2, half, count, seq_rows).transpose(2, 0, 1, 3)
    mixed_low = all_to_all(mixed_send.reshape(2 * count, half, seq_rows), ("d", "y"))
    mixed_low = mixed_low.reshape(count, 2, half, seq_rows).transpose(0, 2, 1, 3)
    mixed_low = mixed_low.reshape(count * half, 2 * seq_rows)
    branch = dot_at(mixed_low, out_weight, 0, 0).reshape(2, 2, rows, width)
    middle = inputs + own_rows_sum(branch)

    r2 = inverse_rms(middle)
    n2_own = middle * r2
    n2 = rows_of_group(n2_own.astype(bf16)).reshape(2 * seq_rows, width)
    both = dot_at(n2, pair_weight, 1, 0)
    gate = both[:, : count * ff_own]
    upper = both[:, count * ff_own :]
    sigma = jax.nn.sigmoid(gate)
    silu = gate * sigma
    hidden = (silu * upper).astype(bf16)
    d_hidden = dot_at(d_out, down_weight, 1, 1)
    d_gate = (d_hidden * upper * (sigma + silu * (1.0 - sigma))).astype(bf16)
    d_upper = (d_hidden * silu).astype(bf16)
    d_both = jnp.concatenate([d_gate, d_upper], axis=1)
    d_normed2 = own_rows_sum(dot_at(d_both, pair_weight, 1, 1).reshape(2, 2, rows, width))
    incoming = cotangent[0].astype(f32)
    d_middle = incoming + r2 * (
        d_normed2 - n2_own * jnp.mean(d_normed2 * n2_own, axis=-1, keepdims=True)
    )
    grad_down = dot_at(hidden, d_out, 0, 0).astype(bf16).reshape(count, ff_own, width)
    grad_both = dot_at(n2, d_both, 0, 0).astype(bf16).reshape(count, group, 2 * count * ff_own)
    owned_down, owned_both = ring_scatter([grad_down, grad_both], count)
    result = middle + own_rows_sum(dot_at(hidden, down_weight, 1, 0).reshape(2, 2, rows, width))

    d_mid = rows_of_group(d_middle.astype(bf16)).reshape(2 * seq_rows, width)
    d_mixed = dot_at(out_weight, d_mid, 1, 1).astype(bf16)
    d_mixed = d_mixed.reshape(count, half, 2, seq_rows).transpose(0, 2, 1, 3)
    d_mixed = all_to_all(d_mixed.reshape(2 * count, half, seq_rows), ("d", "y"))
    d_mixed = d_mixed.reshape(count, 2, half, seq_rows).transpose(1, 2, 0, 3)
    d_mixed = d_mixed.reshape(HEAD_SIZE, length)
    d_q, d_k, d_v = heads_backward(q, k, v, prob, mixed, d_mixed, step)
    core = lax.axis_index("core")
    d_kv = jnp.stack([rotate_back(d_k), d_v.reshape(2, half, length)], axis=1)
    away = lax.dynamic_index_in_dim(d_kv, 1 - core, 0, False).astype(bf16)
    kept = lax.dynamic_index_in_dim(d_kv, core, 0, False)
    d_kv = (kept + swap(away, "core").astype(f32)).astype(bf16)
    d_kv = d_kv.reshape(2, 2, quarter, count, seq_rows).transpose(3, 1, 0, 2, 4)
    d_kv = d_kv.reshape(count, 2, half, seq_rows)
    d_q = rotate_back(d_q).astype(bf16).reshape(2, half, count, seq_rows).transpose(2, 0, 1, 3)
    d_qkv = jnp.concatenate([d_q, d_kv], axis=2).reshape(2 * count, HEAD_SIZE, seq_rows)
    d_qkv = all_to_all(d_qkv, ("d", "y")).reshape(count, 2, HEAD_SIZE, seq_rows)
    d_qkv = d_qkv.transpose(0, 2, 1, 3).reshape(count * HEAD_SIZE, 2 * seq_rows)
    grad_out = dot_at(mixed_low, d_mid, 1, 0).astype(bf16).reshape(count, own, width)
    grad_qkv = dot_at(n1, d_qkv, 0, 1).astype(bf16).reshape(count, group, count * HEAD_SIZE)
    grad_out, grad_qkv, owned_down, owned_both = lax.optimization_barrier(
        (grad_out, grad_qkv, owned_down, owned_both)
    )
    owned_out, owned_qkv = ring_scatter([grad_out, grad_qkv], count)
    d_normed1 = own_rows_sum(dot_at(d_qkv, qkv_weight, 0, 1).reshape(2, 2, rows, width))
    n1_wide = inputs * r1
    input_grad = d_middle + r1 * (
        d_normed1 - n1_wide * jnp.mean(d_normed1 * n1_wide, axis=-1, keepdims=True)
    )

    own_both = all_to_all(owned_both.astype(bf16).reshape(4, own, -1), ("core", "y")).astype(f32)
    own_both = own_both.reshape(4, own, 2, count, ff_own).transpose(2, 1, 3, 0, 4)
    own_gate, own_up = own_both.reshape(2, own, 4 * count * ff_own)
    owned_gain2 = jnp.sum(own_gate * w_gate.astype(f32), axis=1) + jnp.sum(
        own_up * w_up.astype(f32), axis=1
    )
    own_qkv = all_to_all(owned_qkv.astype(bf16).reshape(4, own, -1), ("core", "y")).astype(f32)
    own_qkv = own_qkv.reshape(4, own, count, HEAD_SIZE).transpose(1, 2, 0, 3)
    own_query = own_qkv[..., :half].reshape(own, -1)
    own_key = own_qkv[..., half : half + quarter].reshape(own, -1)
    own_value = own_qkv[..., half + quarter :].reshape(own, -1)
    owned_gain1 = (
        jnp.sum(own_query * w_query.astype(f32), axis=1)
        + jnp.sum(own_key * key_weight.astype(f32), axis=1)
        + jnp.sum(own_value * value_weight.astype(f32), axis=1)
    )
    return (
        result.astype(bf16)[None],
        input_grad[None],
        owned_gain1,
        gain1 * own_query,
        gain1 * own_key,
        gain1 * own_value,
        owned_out,
        owned_gain2,
        gain2 * own_gate,
        gain2 * own_up,
        owned_down,
    )


def by_heads(mesh):
    count = mesh.shape["ctx"] // 2
    parts = Mesh(mesh.devices.reshape(count, 2, 2), ("d", "core", "y"))
    owner = ("d", "core", "y")
    row_spec = P("y", ("d", "core"), None)
    in_specs = (row_spec, row_spec) + (P(owner),) * 9
    out_specs = (row_spec, row_spec) + (P(owner),) * 9
    return jax.shard_map(
        functools.partial(head_layer, count),
        mesh=parts,
        in_specs=in_specs,
        out_specs=out_specs,
        check_vma=False,
    )


def solution(mesh):
    in_specs = (
        P("fsdp", "ctx", None),
        P("fsdp", "ctx", None),
        P(("ctx", "fsdp")),
        P(("ctx", "fsdp"), None),
        P(("ctx", "fsdp"), None),
        P(("ctx", "fsdp"), None),
        P(("ctx", "fsdp"), None),
        P(("ctx", "fsdp")),
        P(("ctx", "fsdp"), None),
        P(("ctx", "fsdp"), None),
        P(("ctx", "fsdp"), None),
    )
    out_specs = (
        P("fsdp", "ctx", None),
        P("fsdp", "ctx", None),
        P(("ctx", "fsdp")),
        P(("ctx", "fsdp"), None),
        P(("ctx", "fsdp"), None),
        P(("ctx", "fsdp"), None),
        P(("ctx", "fsdp"), None),
        P(("ctx", "fsdp")),
        P(("ctx", "fsdp"), None),
        P(("ctx", "fsdp"), None),
        P(("ctx", "fsdp"), None),
    )
    if mesh.shape["ctx"] == QUERY_HEADS and mesh.shape["fsdp"] == 2:
        return by_heads(mesh)
    return jax.shard_map(local, mesh=mesh, in_specs=in_specs, out_specs=out_specs, check_vma=False)
```

```python
import functools

import jax
import jax.numpy as jnp
import numpy as np
from jax import lax
from jax.experimental import pallas as pl
from jax.experimental.pallas import tpu as pltpu
from jax.sharding import Mesh
from jax.sharding import PartitionSpec as P

QUERY_HEADS = 16
KEY_VALUE_HEADS = 8
HEAD_SIZE = 96


rope_base = 100000.0
norm_eps = 1e-05
masked_value = -1e30
key_block = 512


def rms_norm(value_rows, gain):
    return (
        value_rows
        * lax.rsqrt(jnp.mean(value_rows * value_rows, axis=-1, keepdims=True) + norm_eps)
        * gain
    )


def apply_rotary(value_rows, token_position):
    half = value_rows.shape[-1] // 2
    exponent = jnp.arange(half, dtype=jnp.float32) * (2.0 / value_rows.shape[-1])
    freq = rope_base ** (-exponent)
    angle = token_position[:, None] * freq[None, :]
    cosine = jnp.cos(angle)[:, None, :]
    sine = jnp.sin(angle)[:, None, :]
    first = value_rows[..., :half]
    second = value_rows[..., half:]
    return jnp.concatenate(
        [first * cosine - second * sine, second * cosine + first * sine], axis=-1
    )


def matmul(left, right):
    return jnp.dot(left, right, preferred_element_type=jnp.float32)


def key_pieces(key_rows, value_rows, key_value_heads, head_dim):
    count = key_rows.shape[0]
    number = count // key_block
    key_sets = key_rows.reshape(number, key_block, key_value_heads, head_dim)
    value_sets = value_rows.reshape(number, key_block, key_value_heads, head_dim)
    starts = jnp.arange(number, dtype=jnp.int32) * key_block
    return (key_sets, value_sets, starts, key_block)


def fold_keys(carry, key_rows, value_rows, query_rows, query_pos):
    key_value_heads = query_rows.shape[1]
    head_dim = query_rows.shape[3]
    scale = head_dim ** (-0.5)
    key_sets, value_sets, starts, size = key_pieces(key_rows, value_rows, key_value_heads, head_dim)

    def fold_one_piece(state, item):
        key_set, value_set, begin = item

        def fold_live(state):
            top, total, summed = state
            scores = (
                jnp.einsum(
                    "tkgd,skd->kgts", query_rows, key_set, preferred_element_type=jnp.float32
                )
                * scale
            )
            visible = (begin + jnp.arange(size, dtype=jnp.int32))[None, :] <= query_pos[:, None]
            scores = jnp.where(visible, scores, masked_value)
            new_top = jnp.maximum(top, jnp.max(scores, axis=-1))
            weights = jnp.where(visible, jnp.exp(scores - new_top[..., None]), 0.0)
            factor = jnp.exp(top - new_top)
            total = total * factor + jnp.sum(weights, axis=-1)
            summed = summed * factor[..., None] + jnp.einsum(
                "kgts,skd->kgtd",
                weights.astype(jnp.bfloat16),
                value_set,
                preferred_element_type=jnp.float32,
            )
            return (new_top, total, summed)

        def fold_skipped(state):
            return state

        return (lax.cond(begin <= query_pos[-1], fold_live, fold_skipped, state), None)

    carry, _ = lax.scan(fold_one_piece, carry, (key_sets, value_sets, starts))
    return carry


def back_keys(key_rows, value_rows, query_rows, query_pos, d_heads, log_total, delta):
    rows, key_value_heads, groups, head_dim = query_rows.shape
    scale = head_dim ** (-0.5)
    key_sets, value_sets, starts, size = key_pieces(key_rows, value_rows, key_value_heads, head_dim)

    def back_one_piece(d_query, item):
        key_set, value_set, begin = item

        def back_live(d_query):
            scores = (
                jnp.einsum(
                    "tkgd,skd->kgts", query_rows, key_set, preferred_element_type=jnp.float32
                )
                * scale
            )
            visible = (begin + jnp.arange(size, dtype=jnp.int32))[None, :] <= query_pos[:, None]
            prob = jnp.where(visible, jnp.exp(scores - log_total[..., None]), 0.0)
            d_prob = jnp.einsum(
                "tkgd,skd->kgts", d_heads, value_set, preferred_element_type=jnp.float32
            )
            d_scores = (prob * (d_prob - delta[..., None])).astype(jnp.bfloat16)
            d_query = d_query + scale * jnp.einsum(
                "kgts,skd->tkgd", d_scores, key_set, preferred_element_type=jnp.float32
            )
            d_key = scale * jnp.einsum(
                "kgts,tkgd->skd", d_scores, query_rows, preferred_element_type=jnp.float32
            )
            d_value = jnp.einsum(
                "kgts,tkgd->skd",
                prob.astype(jnp.bfloat16),
                d_heads,
                preferred_element_type=jnp.float32,
            )
            return (
                d_query,
                (
                    d_key.reshape(size, key_value_heads * head_dim),
                    d_value.reshape(size, key_value_heads * head_dim),
                ),
            )

        def back_skipped(d_query):
            empty = jnp.zeros((size, key_value_heads * head_dim), jnp.float32)
            return (d_query, (empty, empty))

        return lax.cond(begin <= query_pos[-1], back_live, back_skipped, d_query)

    start_grad = jnp.zeros((rows, key_value_heads, groups, head_dim), jnp.float32)
    d_query, (d_keys, d_values) = lax.scan(
        back_one_piece, start_grad, (key_sets, value_sets, starts)
    )
    return (
        d_query,
        d_keys.reshape(key_rows.shape[0], key_value_heads * head_dim),
        d_values.reshape(key_rows.shape[0], key_value_heads * head_dim),
    )


def local(
    tokens,
    cotangent,
    norm_gain1,
    w_query,
    key_weight,
    value_weight,
    w_out,
    norm_gain2,
    w_gate,
    w_up,
    w_down,
):
    rows = tokens.shape[1]
    key_value_heads = KEY_VALUE_HEADS
    heads = QUERY_HEADS
    head_dim = HEAD_SIZE
    groups = heads // key_value_heads
    first_row = lax.axis_index("ctx") * rows
    query_pos = first_row + jnp.arange(rows, dtype=jnp.int32)
    token_position = query_pos.astype(jnp.float32)
    inputs = tokens[0].astype(jnp.float32)
    gathered = (
        lax.all_gather(norm_gain1, ("ctx", "fsdp"), axis=0, tiled=True),
        lax.all_gather(w_query, ("ctx", "fsdp"), axis=0, tiled=True),
        lax.all_gather(key_weight, ("ctx", "fsdp"), axis=0, tiled=True),
        lax.all_gather(value_weight, ("ctx", "fsdp"), axis=0, tiled=True),
        lax.all_gather(w_out, ("ctx", "fsdp"), axis=0, tiled=True),
        lax.all_gather(norm_gain2, ("ctx", "fsdp"), axis=0, tiled=True),
        lax.all_gather(w_gate, ("ctx", "fsdp"), axis=0, tiled=True),
        lax.all_gather(w_up, ("ctx", "fsdp"), axis=0, tiled=True),
        lax.all_gather(w_down, ("ctx", "fsdp"), axis=0, tiled=True),
    )
    gain_one = gathered[0].astype(jnp.float32)
    gain_two = gathered[5].astype(jnp.float32)
    normed1 = rms_norm(inputs, gain_one).astype(jnp.bfloat16)
    query_pre = matmul(normed1, gathered[1]).reshape(rows, heads, head_dim)
    key_pre = matmul(normed1, gathered[2]).reshape(rows, key_value_heads, head_dim)
    value = matmul(normed1, gathered[3]).astype(jnp.bfloat16)
    query_rows = (
        apply_rotary(query_pre, token_position)
        .astype(jnp.bfloat16)
        .reshape(rows, key_value_heads, groups, head_dim)
    )
    key_rows = (
        apply_rotary(key_pre, token_position)
        .reshape(rows, key_value_heads * head_dim)
        .astype(jnp.bfloat16)
    )
    start_state = (
        jnp.full((key_value_heads, groups, rows), masked_value, jnp.float32),
        jnp.zeros((key_value_heads, groups, rows), jnp.float32),
        jnp.zeros((key_value_heads, groups, rows, head_dim), jnp.float32),
    )
    top, total, summed = fold_keys(
        start_state,
        lax.all_gather(key_rows, "ctx", axis=0, tiled=True),
        lax.all_gather(value, "ctx", axis=0, tiled=True),
        query_rows,
        query_pos,
    )
    mixed_heads = jnp.transpose(summed / total[..., None], (2, 0, 1, 3))
    log_total = top + jnp.log(total)
    mixed_low = mixed_heads.reshape(rows, heads * head_dim).astype(jnp.bfloat16)
    middle = inputs + matmul(mixed_low, gathered[4])
    normed2 = rms_norm(middle, gain_two).astype(jnp.bfloat16)
    gate = matmul(normed2, gathered[6])
    upper = matmul(normed2, gathered[7])
    hidden = (jax.nn.silu(gate) * upper).astype(jnp.bfloat16)
    result = middle + matmul(hidden, gathered[8])
    gathered = (
        lax.all_gather(norm_gain1, ("ctx", "fsdp"), axis=0, tiled=True),
        lax.all_gather(w_query, ("ctx", "fsdp"), axis=0, tiled=True),
        lax.all_gather(key_weight, ("ctx", "fsdp"), axis=0, tiled=True),
        lax.all_gather(value_weight, ("ctx", "fsdp"), axis=0, tiled=True),
        lax.all_gather(w_out, ("ctx", "fsdp"), axis=0, tiled=True),
        lax.all_gather(norm_gain2, ("ctx", "fsdp"), axis=0, tiled=True),
        lax.all_gather(w_gate, ("ctx", "fsdp"), axis=0, tiled=True),
        lax.all_gather(w_up, ("ctx", "fsdp"), axis=0, tiled=True),
        lax.all_gather(w_down, ("ctx", "fsdp"), axis=0, tiled=True),
    )
    incoming = cotangent[0].astype(jnp.float32)
    incoming_low = incoming.astype(jnp.bfloat16)
    grad_down = matmul(hidden.T, incoming_low)
    d_hidden = matmul(incoming_low, gathered[8].T)
    _, swiglu_back = jax.vjp(lambda gate_in, upper_in: jax.nn.silu(gate_in) * upper_in, gate, upper)
    d_gate, d_upper = swiglu_back(d_hidden)
    d_gate = d_gate.astype(jnp.bfloat16)
    d_upper = d_upper.astype(jnp.bfloat16)
    grad_gate = matmul(normed2.T, d_gate)
    grad_up = matmul(normed2.T, d_upper)
    d_normed2 = matmul(d_gate, gathered[6].T) + matmul(d_upper, gathered[7].T)
    _, norm_back2 = jax.vjp(rms_norm, middle, gain_two)
    d_middle, grad_gain2 = norm_back2(d_normed2)
    d_middle = d_middle + incoming
    owned_gain2, owned_gate, owned_up, owned_down = (
        lax.psum_scatter(grad_gain2, ("ctx", "fsdp"), scatter_dimension=0, tiled=True),
        lax.psum_scatter(grad_gate, ("ctx", "fsdp"), scatter_dimension=0, tiled=True),
        lax.psum_scatter(grad_up, ("ctx", "fsdp"), scatter_dimension=0, tiled=True),
        lax.psum_scatter(grad_down, ("ctx", "fsdp"), scatter_dimension=0, tiled=True),
    )
    d_middle_low = d_middle.astype(jnp.bfloat16)
    grad_out = matmul(mixed_low.T, d_middle_low)
    d_mixed = matmul(d_middle_low, gathered[4].T).astype(jnp.bfloat16)
    d_heads = d_mixed.reshape(rows, key_value_heads, groups, head_dim)
    delta = jnp.transpose(jnp.sum(d_heads.astype(jnp.float32) * mixed_heads, axis=-1), (1, 2, 0))
    back_keys_all, back_values_all = (
        lax.all_gather(key_rows, "ctx", axis=0, tiled=True),
        lax.all_gather(value, "ctx", axis=0, tiled=True),
    )
    d_query_rot, d_keys_all, d_values_all = back_keys(
        back_keys_all, back_values_all, query_rows, query_pos, d_heads, log_total, delta
    )
    d_keys_rot, d_value = (
        lax.psum_scatter(d_keys_all, "ctx", scatter_dimension=0, tiled=True),
        lax.psum_scatter(d_values_all, "ctx", scatter_dimension=0, tiled=True),
    )
    _, rotate_back_query = jax.vjp(
        lambda values_in: apply_rotary(values_in, token_position), query_pre
    )
    _, rotate_back_key = jax.vjp(lambda values_in: apply_rotary(values_in, token_position), key_pre)
    d_query = (
        rotate_back_query(d_query_rot.reshape(rows, heads, head_dim))[0]
        .reshape(rows, heads * head_dim)
        .astype(jnp.bfloat16)
    )
    d_key = (
        rotate_back_key(d_keys_rot.reshape(rows, key_value_heads, head_dim))[0]
        .reshape(rows, key_value_heads * head_dim)
        .astype(jnp.bfloat16)
    )
    d_value = d_value.astype(jnp.bfloat16)
    grad_query = matmul(normed1.T, d_query)
    grad_key = matmul(normed1.T, d_key)
    grad_value = matmul(normed1.T, d_value)
    d_normed1 = (
        matmul(d_query, gathered[1].T)
        + matmul(d_key, gathered[2].T)
        + matmul(d_value, gathered[3].T)
    )
    _, norm_back1 = jax.vjp(rms_norm, inputs, gain_one)
    d_inputs, grad_gain1 = norm_back1(d_normed1)
    input_grad = d_inputs + d_middle
    owned_gain1, owned_query, owned_key, owned_value, owned_out = (
        lax.psum_scatter(grad_gain1, ("ctx", "fsdp"), scatter_dimension=0, tiled=True),
        lax.psum_scatter(grad_query, ("ctx", "fsdp"), scatter_dimension=0, tiled=True),
        lax.psum_scatter(grad_key, ("ctx", "fsdp"), scatter_dimension=0, tiled=True),
        lax.psum_scatter(grad_value, ("ctx", "fsdp"), scatter_dimension=0, tiled=True),
        lax.psum_scatter(grad_out, ("ctx", "fsdp"), scatter_dimension=0, tiled=True),
    )
    return (
        result.astype(jnp.bfloat16)[None],
        input_grad[None],
        owned_gain1,
        owned_query,
        owned_key,
        owned_value,
        owned_out,
        owned_gain2,
        owned_gate,
        owned_up,
        owned_down,
    )


bf16 = jnp.bfloat16
f32 = jnp.float32
score_scale = HEAD_SIZE ** (-0.5)
log2_e = 1.4426950408889634
ln_2 = 0.6931471805599453


def dot_at(left, right, left_dim, right_dim):
    return lax.dot_general(
        left, right, (((left_dim,), (right_dim,)), ((), ())), preferred_element_type=jnp.float32
    )


def heads_forward_kernel(step, q_ref, k_ref, v_ref, mixed_ref, prob_ref):
    tokens = q_ref.shape[1]
    offset = 0
    for begin in range(0, tokens, step):
        end = begin + step
        scores = dot_at(k_ref[:, 0:end], q_ref[:, begin:end], 0, 0)
        key = lax.broadcasted_iota(jnp.int32, (step, step), 0)
        query = lax.broadcasted_iota(jnp.int32, (step, step), 1)
        last = jnp.where(key <= query, scores[begin:end], masked_value)
        top = jnp.max(last, axis=0, keepdims=True)
        if begin:
            top = jnp.maximum(top, jnp.max(scores[:begin], axis=0, keepdims=True))
        last = jnp.exp2(last - top)
        total = jnp.sum(last, axis=0, keepdims=True)
        if begin:
            first = jnp.exp2(scores[:begin] - top)
            total = total + jnp.sum(first, axis=0, keepdims=True)
        inverse = 1.0 / total
        prob_ref[offset + begin : offset + end, :] = (last * inverse).astype(bf16)
        if begin:
            prob_ref[offset : offset + begin, :] = (first * inverse).astype(bf16)
        mixed_ref[:, begin:end] = dot_at(
            v_ref[:, 0:end], prob_ref[offset : offset + end, :], 1, 0
        )
        offset += end


def heads_backward_kernel(
    step, q_ref, k_ref, v_ref, prob_ref, mixed_ref, d_mixed_ref, d_q_ref, d_k_ref, d_v_ref
):
    tokens = q_ref.shape[1]
    offset = 0
    for begin in range(0, tokens, step):
        end = begin + step
        d_mixed = d_mixed_ref[:, begin:end]
        delta = jnp.sum(d_mixed.astype(f32) * mixed_ref[:, begin:end], axis=0, keepdims=True)
        prob = prob_ref[offset : offset + end, :]
        d_prob = dot_at(v_ref[:, 0:end], d_mixed, 0, 0)
        d_scores = (prob.astype(f32) * (d_prob - delta)).astype(bf16)
        d_q_ref[:, begin:end] = dot_at(k_ref[:, 0:end], d_scores, 1, 0) * score_scale
        d_v = dot_at(d_mixed, prob, 1, 1)
        d_k = dot_at(q_ref[:, begin:end], d_scores, 1, 1) * ln_2
        if begin:
            d_v_ref[:, 0:begin] += d_v[:, 0:begin]
            d_k_ref[:, 0:begin] += d_k[:, 0:begin]
        d_v_ref[:, begin:end] = d_v[:, begin:end]
        d_k_ref[:, begin:end] = d_k[:, begin:end]
        offset += end


def heads_forward(q, k, v, step):
    size, tokens = q.shape
    blocks = tokens // step
    pairs = step * blocks * (blocks + 1) // 2
    whole = pl.BlockSpec(memory_space=pltpu.VMEM)
    return pl.pallas_call(
        functools.partial(heads_forward_kernel, step),
        out_shape=(
            jax.ShapeDtypeStruct((size, tokens), f32),
            jax.ShapeDtypeStruct((pairs, step), bf16),
        ),
        in_specs=[whole] * 3,
        out_specs=(whole, whole),
        compiler_params=pltpu.CompilerParams(vmem_limit_bytes=40 * 2**20),
        cost_estimate=pl.CostEstimate(
            flops=4 * size * pairs * step, bytes_accessed=pairs * step * 2, transcendentals=pairs * step
        ),
        name="heads_forward",
    )(q, k, v)


def heads_backward(q, k, v, prob, mixed, d_mixed, step):
    size, tokens = q.shape
    whole = pl.BlockSpec(memory_space=pltpu.VMEM)
    return pl.pallas_call(
        functools.partial(heads_backward_kernel, step),
        out_shape=(jax.ShapeDtypeStruct((size, tokens), f32),) * 3,
        in_specs=[whole] * 6,
        out_specs=(whole,) * 3,
        compiler_params=pltpu.CompilerParams(vmem_limit_bytes=40 * 2**20),
        cost_estimate=pl.CostEstimate(
            flops=8 * size * prob.size, bytes_accessed=prob.size * 2, transcendentals=0
        ),
        name="heads_backward",
    )(q, k, v, prob, mixed, d_mixed)


def on_chip(kernel, out_shape, args, flops, blocks=(), scratch=(), name=None):
    moved = sum(a.size * a.dtype.itemsize for a in list(args) + list(blocks))
    moved += sum(o.size * o.dtype.itemsize for o in out_shape)
    near = pl.BlockSpec(memory_space=pltpu.VMEM)
    return pl.pallas_call(
        kernel,
        out_shape=tuple(out_shape),
        in_specs=[pl.BlockSpec(memory_space=pltpu.SMEM)]
        + [near] * (len(args) - 1)
        + [pl.BlockSpec(memory_space=pltpu.HBM)] * len(blocks),
        out_specs=(near,) * len(out_shape),
        scratch_shapes=scratch,
        compiler_params=pltpu.CompilerParams(vmem_limit_bytes=48 * 2**20),
        cost_estimate=pl.CostEstimate(flops=flops, bytes_accessed=moved, transcendentals=0),
        name=name,
    )(*args, *blocks)


def like(dtype, *shape):
    return jax.ShapeDtypeStruct(shape, dtype)


def block_copies(at_ref, block_refs, whole_ref, sem_ref, first=0):
    size = whole_ref.shape[0] // len(block_refs)
    copies = []
    for k, block_ref in enumerate(block_refs):
        start = pl.multiple_of(at_ref[k] * size, size)
        copies.append(
            pltpu.make_async_copy(
                block_ref.at[pl.ds(first, size), :], whole_ref.at[pl.ds(start, size), :], sem_ref.at[k]
            )
        )
    return copies


def core_rows(at_ref, count, rows, seq, other):
    core = at_ref[2 * count]
    start = seq * 2 * rows + (1 - core if other else core) * rows
    return pl.ds(pl.multiple_of(start, rows), rows)


def join_rows(at_ref, count, own_ref, other_ref, whole_ref):
    rows = own_ref.shape[1]
    for seq in range(2):
        whole_ref[core_rows(at_ref, count, rows, seq, False), :] = own_ref[seq]
        whole_ref[core_rows(at_ref, count, rows, seq, True), :] = other_ref[seq]


def part_rows(at_ref, count, whole_ref, kept_ref, away_ref):
    rows = kept_ref.shape[1]
    for seq in range(2):
        kept_ref[seq] = whole_ref[core_rows(at_ref, count, rows, seq, False), :]
        away_ref[seq] = whole_ref[core_rows(at_ref, count, rows, seq, True), :].astype(bf16)


def query_columns_kernel(at_ref, gain_ref, query_ref, key_ref, value_ref, out_ref):
    gain = gain_ref[...]
    query = query_ref[...].astype(f32) * gain
    key = key_ref[...].astype(f32) * gain
    value = value_ref[...].astype(f32) * gain
    half = HEAD_SIZE // 2
    quarter = HEAD_SIZE // 4
    groups = out_ref.shape[2] // HEAD_SIZE
    for t in range(4):
        pieces = []
        for group in range(groups):
            place = 4 * group + t
            pieces.append(query[:, place * half : (place + 1) * half])
            pieces.append(key[:, place * quarter : (place + 1) * quarter])
            pieces.append(value[:, place * quarter : (place + 1) * quarter])
        out_ref[t] = jnp.concatenate(pieces, axis=1).astype(bf16)


def query_columns(at, gain, query, key, value):
    own, width = query.shape
    (out,) = on_chip(
        query_columns_kernel,
        [like(bf16, 4, own, (width + 2 * key.shape[1]) // 4)],
        [at, gain, query, key, value],
        own * width,
        name="query_columns",
    )
    return out


def pair_columns_kernel(size, at_ref, gain_ref, gate_ref, up_ref, out_ref):
    gain = gain_ref[...]
    half = out_ref.shape[2] // 2
    for t in range(4):
        for position in range(half // size):
            columns = pl.ds((4 * position + t) * size, size)
            for side, ref in enumerate((gate_ref, up_ref)):
                out_ref[t, :, pl.ds(side * half + position * size, size)] = (
                    ref[:, columns].astype(f32) * gain
                ).astype(bf16)


def pair_columns(at, gain, gate, up, size):
    own, ff = gate.shape
    (out,) = on_chip(
        functools.partial(pair_columns_kernel, size),
        [like(bf16, 4, own, ff // 2)],
        [at, gain, gate, up],
        own * ff,
        name="pair_columns",
    )
    return out


def project_heads_kernel(at_ref, own_ref, other_ref, *refs):
    blocks, (n_ref, weight_ref, heads_ref, sem_ref) = refs[:-4], refs[-4:]
    copies = block_copies(at_ref, blocks, weight_ref, sem_ref)
    for copy in copies:
        copy.start()
    join_rows(at_ref, len(blocks), own_ref, other_ref, n_ref)
    for copy in copies:
        copy.wait()
    size, rows = heads_ref.shape[1:]
    for seq in range(2):
        part = dot_at(weight_ref[...], n_ref[seq * rows : (seq + 1) * rows, :], 0, 1).astype(bf16)
        for head in range(heads_ref.shape[0] // 2):
            heads_ref[2 * head + seq] = part[head * size : (head + 1) * size, :]


def project_heads(at, own, other, blocks):
    count = len(blocks)
    _, rows, width = own.shape
    columns = blocks[0].shape[1]
    return on_chip(
        project_heads_kernel,
        [
            like(bf16, 4 * rows, width),
            like(bf16, width, columns),
            like(bf16, 2 * count, columns // count, 2 * rows),
        ],
        [at, own, other],
        8 * rows * width * columns,
        blocks=blocks,
        scratch=[pltpu.SemaphoreType.DMA((count,))],
        name="project_heads",
    )


def join_heads(heads_ref, joined_ref):
    size, rows = heads_ref.shape[1:]
    for seq in range(2):
        for head in range(heads_ref.shape[0] // 2):
            joined_ref[head * size : (head + 1) * size, seq * rows : (seq + 1) * rows] = heads_ref[
                2 * head + seq
            ]


def project_out_kernel(first, at_ref, heads_ref, *refs):
    blocks, (weight_ref, joined_ref, kept_ref, away_ref, out_ref, sem_ref) = refs[:-6], refs[-6:]
    copies = block_copies(at_ref, blocks, weight_ref, sem_ref, first=first)
    for copy in copies:
        copy.start()
    join_heads(heads_ref, joined_ref)
    for copy in copies:
        copy.wait()
    out_ref[...] = dot_at(joined_ref[...], weight_ref[...], 0, 0)
    part_rows(at_ref, len(blocks), out_ref, kept_ref, away_ref)


def project_out(at, heads, blocks, first):
    count = len(blocks)
    own, width = blocks[0].shape
    own -= first
    rows = heads.shape[2] // 2
    return on_chip(
        functools.partial(project_out_kernel, first),
        [
            like(bf16, count * own, width),
            like(bf16, count * own, 4 * rows),
            like(f32, 2, rows, width),
            like(bf16, 2, rows, width),
        ],
        [at, heads],
        8 * rows * width * count * own,
        blocks=blocks,
        scratch=[pltpu.VMEM((4 * rows, width), f32), pltpu.SemaphoreType.DMA((count,))],
        name="project_out",
    )


def hidden_gradient_kernel(at_ref, own_ref, other_ref, *refs):
    blocks, (d_out_ref, weight_ref, d_hidden_ref, sem_ref) = refs[:-4], refs[-4:]
    copies = block_copies(at_ref, blocks, weight_ref, sem_ref)
    for copy in copies:
        copy.start()
    join_rows(at_ref, len(blocks), own_ref, other_ref, d_out_ref)
    for copy in copies:
        copy.wait()
    d_hidden_ref[...] = dot_at(d_out_ref[...], weight_ref[...], 1, 1).astype(bf16)


def hidden_gradient(at, d_out_own, d_out_other, blocks, own):
    count = len(blocks)
    _, rows, width = d_out_own.shape
    return on_chip(
        hidden_gradient_kernel,
        [
            like(bf16, 4 * rows, width),
            like(bf16, count * own, width),
            like(bf16, 4 * rows, count * own),
        ],
        [at, d_out_own, d_out_other],
        8 * rows * width * count * own,
        blocks=blocks,
        scratch=[pltpu.SemaphoreType.DMA((count,))],
        name="hidden_gradient",
    )


def feed_forward_kernel(step, at_ref, own_ref, other_ref, d_hidden_ref, *refs):
    blocks = refs[:-8]
    n_ref, hidden_ref, d_both_ref, kept_ref, away_ref, d_n_ref, whole_ref, sem_ref = refs[-8:]
    ff = hidden_ref.shape[1]
    copies = block_copies(at_ref, blocks, whole_ref, sem_ref)
    for copy in copies:
        copy.start()
    join_rows(at_ref, len(blocks), own_ref, other_ref, n_ref)
    for copy in copies:
        copy.wait()
    for begin in range(0, n_ref.shape[0], step):
        rows = slice(begin, begin + step)
        both = dot_at(n_ref[rows, :], whole_ref[...], 1, 0)
        gate = both[:, :ff]
        upper = both[:, ff:]
        sigma = 1.0 / (1.0 + jnp.exp(-gate))
        silu = gate * sigma
        hidden_ref[rows, :] = (silu * upper).astype(bf16)
        d_hidden = d_hidden_ref[rows, :].astype(f32)
        d_both_ref[rows, :ff] = (d_hidden * upper * (sigma + silu * (1.0 - sigma))).astype(bf16)
        d_both_ref[rows, ff:] = (d_hidden * silu).astype(bf16)
        d_n_ref[rows, :] = dot_at(d_both_ref[rows, :], whole_ref[...], 1, 1)
    part_rows(at_ref, len(blocks), d_n_ref, kept_ref, away_ref)


def feed_forward(at, own, other, d_hidden, blocks):
    _, rows, width = own.shape
    ff = d_hidden.shape[1]
    return on_chip(
        functools.partial(feed_forward_kernel, min(256, 4 * rows)),
        [
            like(bf16, 4 * rows, width),
            like(bf16, 4 * rows, ff),
            like(bf16, 4 * rows, 2 * ff),
            like(f32, 2, rows, width),
            like(bf16, 2, rows, width),
        ],
        [at, own, other, d_hidden],
        32 * rows * width * ff,
        blocks=blocks,
        scratch=[
            pltpu.VMEM((4 * rows, width), f32),
            pltpu.VMEM((width, 2 * ff), bf16),
            pltpu.SemaphoreType.DMA((len(blocks),)),
        ],
        name="feed_forward",
    )


def feed_forward_grads_kernel(at_ref, n_ref, d_both_ref, hidden_ref, d_out_ref, both_ref, down_ref):
    count, block, _ = both_ref.shape
    own = down_ref.shape[1]
    for k in range(count):
        down_ref[k] = dot_at(
            hidden_ref[:, pl.ds(pl.multiple_of(at_ref[k] * own, own), own)], d_out_ref[...], 0, 0
        ).astype(bf16)
    for position in range(count):
        columns = slice(position * block, (position + 1) * block)
        both_ref[at_ref[count + position]] = dot_at(
            n_ref[:, columns], d_both_ref[...], 0, 0
        ).astype(bf16)


def feed_forward_grads(at, n, d_both, hidden, d_out, count):
    rows, width = n.shape
    ff = hidden.shape[1]
    return on_chip(
        feed_forward_grads_kernel,
        [like(bf16, count, width // count, 2 * ff), like(bf16, count, ff // count, width)],
        [at, n, d_both, hidden, d_out],
        6 * rows * width * ff,
        name="feed_forward_grads",
    )


def split_heads_kernel(at_ref, own_ref, other_ref, weight_ref, d_mid_ref, heads_ref):
    join_rows(at_ref, heads_ref.shape[0] // 2, own_ref, other_ref, d_mid_ref)
    size, rows = heads_ref.shape[1:]
    for seq in range(2):
        part = dot_at(weight_ref[...], d_mid_ref[seq * rows : (seq + 1) * rows, :], 1, 1)
        part = part.astype(bf16)
        for head in range(heads_ref.shape[0] // 2):
            heads_ref[2 * head + seq] = part[head * size : (head + 1) * size, :]


def split_heads(at, own, other, weight, heads):
    _, rows, width = own.shape
    return on_chip(
        split_heads_kernel,
        [
            like(bf16, 4 * rows, width),
            like(bf16, 2 * heads, weight.shape[0] // heads, 2 * rows),
        ],
        [at, own, other, weight],
        8 * rows * width * weight.shape[0],
        name="split_heads",
    )


def heads_grad_kernel(at_ref, heads_ref, n_ref, joined_ref, grad_ref):
    join_heads(heads_ref, joined_ref)
    grad_ref[...] = dot_at(n_ref[...], joined_ref[...], 0, 1).astype(bf16)


def heads_grad(at, heads, n):
    rows, width = n.shape
    columns = heads.shape[0] // 2 * heads.shape[1]
    return on_chip(
        heads_grad_kernel,
        [like(bf16, columns, rows), like(bf16, width, columns)],
        [at, heads, n],
        2 * rows * width * columns,
        name="heads_grad",
    )


def heads_input_kernel(at_ref, joined_ref, weight_ref, kept_ref, away_ref, out_ref):
    out_ref[...] = dot_at(joined_ref[...], weight_ref[...], 0, 1)
    count = weight_ref.shape[1] // HEAD_SIZE
    part_rows(at_ref, count, out_ref, kept_ref, away_ref)


def heads_input(at, joined, weight):
    width, columns = weight.shape
    rows = joined.shape[1] // 4
    return on_chip(
        heads_input_kernel,
        [like(f32, 2, rows, width), like(bf16, 2, rows, width)],
        [at, joined, weight],
        0,
        scratch=[pltpu.VMEM((4 * rows, width), f32)],
        name="heads_input",
    )


def layer_output_kernel(count, at_ref, hidden_ref, weight_ref, kept_ref, away_ref, out_ref):
    out_ref[...] = dot_at(hidden_ref[...], weight_ref[...], 1, 0)
    part_rows(at_ref, count, out_ref, kept_ref, away_ref)


def layer_output(at, hidden, weight, count):
    ff, width = weight.shape
    rows = hidden.shape[0] // 4
    return on_chip(
        functools.partial(layer_output_kernel, count),
        [like(f32, 2, rows, width), like(bf16, 2, rows, width)],
        [at, hidden, weight],
        0,
        scratch=[pltpu.VMEM((4 * rows, width), f32)],
        name="layer_output",
    )


def query_rows_kernel(
    at_ref, terms_ref, gain_ref, query_ref, key_ref, value_ref, d_query, d_key, d_value, d_gain
):
    half = HEAD_SIZE // 2
    quarter = HEAD_SIZE // 4
    positions = terms_ref.shape[0] // 4
    groups = terms_ref.shape[2] // HEAD_SIZE
    parts = []
    for t in range(4):
        total = terms_ref[t].astype(f32)
        for position in range(1, positions):
            total = total + terms_ref[4 * position + t].astype(f32)
        parts.append(total)
    pieces = ([], [], [])
    for group in range(groups):
        for t in range(4):
            start = group * HEAD_SIZE
            pieces[0].append(parts[t][:, start : start + half])
            pieces[1].append(parts[t][:, start + half : start + half + quarter])
            pieces[2].append(parts[t][:, start + half + quarter : start + HEAD_SIZE])
    gain = gain_ref[...]
    rows_sum = None
    outs = (d_query, d_key, d_value)
    for pieces_of, weight_ref, out_ref in zip(pieces, (query_ref, key_ref, value_ref), outs):
        grad = jnp.concatenate(pieces_of, axis=1)
        out_ref[...] = gain * grad
        part = jnp.sum(grad * weight_ref[...].astype(f32), axis=1, keepdims=True)
        rows_sum = part if rows_sum is None else rows_sum + part
    d_gain[...] = rows_sum


def query_rows_grads(at, terms, gain, query, key, value):
    own = query.shape[0]
    return on_chip(
        query_rows_kernel,
        [
            like(f32, *query.shape),
            like(f32, *key.shape),
            like(f32, *value.shape),
            like(f32, own, 1),
        ],
        [at, terms, gain, query, key, value],
        terms.size,
        name="query_rows_grads",
    )


def pair_rows_kernel(
    size, count, at_ref, terms_ref, gain_ref, gate_ref, up_ref, d_gate, d_up, d_gain
):
    gain = gain_ref[...]
    core = at_ref[2 * count]
    seq = at_ref[2 * count + 1]
    half = terms_ref.shape[2] // 2
    rows_sum = jnp.zeros_like(gain)
    for side, (weight_ref, out_ref) in enumerate(((gate_ref, d_gate), (up_ref, d_up))):
        for position in range(half // size):
            for t in range(4):
                columns = slice((4 * position + t) * size, (4 * position + t + 1) * size)
                start = side * half + position * size
                block = (core + t // 2) % 2 * 2 + (seq + t % 2) % 2
                grad = terms_ref[block, :, start : start + size].astype(f32)
                out_ref[:, columns] = gain * grad
                rows_sum = rows_sum + jnp.sum(
                    grad * weight_ref[:, columns].astype(f32), axis=1, keepdims=True
                )
    d_gain[...] = rows_sum


def pair_rows_grads(at, terms, gain, gate, up, size, count):
    own = gate.shape[0]
    return on_chip(
        functools.partial(pair_rows_kernel, size, count),
        [like(f32, *gate.shape), like(f32, *up.shape), like(f32, own, 1)],
        [at, terms, gain, gate, up],
        terms.size,
        name="pair_rows_grads",
    )


def ring_of(count):
    order = list(range(0, count, 2)) + list(range(count - 1, 0, -2))
    forward = [(order[i], order[(i + 1) % count]) for i in range(count)]
    backward = [(there, here) for here, there in forward]
    return forward, backward


def place_of(position, count):
    return jnp.where(position % 2 == 0, position // 2, count - (position + 1) // 2)


def position_at(place, count):
    place = lax.rem(place, count)
    return jnp.where(place < count // 2, 2 * place, 2 * (count - place) - 1)


def tie(*values):
    return lax.optimization_barrier(values)


def after(value, *others):
    return lax.optimization_barrier((value,) + others)[0]


class GatherRing:
    def __init__(self, shard, count):
        self.count = count
        self.forward, self.backward = ring_of(count)
        self.parts = [shard] + [None] * (count - 1)
        self.ahead = self.behind = shard
        self.hops = 0

    def start(self, *others):
        self.hops += 1
        ahead, behind = self.ahead, self.behind
        if self.hops == self.count // 2:
            half = ahead.shape[0] // 2
            ahead, behind = ahead[:half], behind[half:]
        if others:
            ahead, behind = lax.optimization_barrier((ahead, behind) + others)[:2]
        self.ahead = lax.ppermute(ahead, "d", self.forward)
        self.behind = lax.ppermute(behind, "d", self.backward)

    def settle(self, *others):
        out = lax.optimization_barrier((self.ahead, self.behind) + others)
        self.ahead, self.behind = out[:2]
        if self.hops == self.count // 2:
            self.parts[self.hops] = jnp.concatenate(out[:2], axis=0)
        else:
            self.parts[self.count - self.hops] = self.ahead
            self.parts[self.hops] = self.behind
        return out[2] if len(others) == 1 else out[2:]


class ScatterRing:
    def __init__(self, terms, count):
        self.count = count
        self.terms = terms
        self.forward, self.backward = ring_of(count)
        self.ahead = [self.part(t, count - 1, 0) for t in terms]
        self.behind = [self.part(t, 1, 1) for t in terms]
        self.hops = 0

    def part(self, term, at, side):
        half = term.shape[1] // 2
        return term[at % self.count, side * half : (side + 1) * half]

    def start(self, *others):
        self.hops += 1
        ahead, behind = self.ahead, self.behind
        if others:
            ahead, behind = lax.optimization_barrier((ahead, behind) + others)[:2]
        self.ahead = [lax.ppermute(a, "d", self.forward) for a in ahead]
        self.behind = [lax.ppermute(b, "d", self.backward) for b in behind]

    def settle(self, *others):
        out = lax.optimization_barrier((self.ahead, self.behind) + others)
        ahead, behind = out[:2]
        kind = f32 if self.hops == self.count - 1 else bf16
        place = self.count - 1 - self.hops
        self.ahead = [
            (a.astype(f32) + self.part(t, place, 0).astype(f32)).astype(kind)
            for a, t in zip(ahead, self.terms)
        ]
        self.behind = [
            (b.astype(f32) + self.part(t, 1 + self.hops, 1).astype(f32)).astype(kind)
            for b, t in zip(behind, self.terms)
        ]
        return out[2] if len(others) == 1 else out[2:]

    def sums(self):
        return [jnp.concatenate([a, b], axis=0) for a, b in zip(self.ahead, self.behind)]


def swap(values, axis):
    return lax.ppermute(values, axis, [(0, 1), (1, 0)])


def rows_of_group(own):
    pair = lax.all_gather(own, "y", axis=0)
    return lax.all_gather(pair, "core", axis=1)


def core_sum(kept, away):
    return kept + swap(away, "core").astype(f32)


def both_rows_sum(pair):
    return pair + swap(pair.astype(bf16), "y").astype(f32)


def own_rows_sum(pair):
    seq = lax.axis_index("y")
    away = lax.dynamic_index_in_dim(pair, 1 - seq, 0, False).astype(bf16)
    return lax.dynamic_index_in_dim(pair, seq, 0, False) + swap(away, "y").astype(f32)


def own_columns(blocks):
    core = lax.axis_index("core")
    seq = lax.axis_index("y")
    away = lax.dynamic_index_in_dim(blocks, 1 - seq, 1, False)
    kept = lax.dynamic_index_in_dim(blocks, seq, 1, False)
    pair = jnp.stack([kept, swap(away, "y")])
    away = lax.dynamic_index_in_dim(pair, 1 - core, 1, False)
    kept = lax.dynamic_index_in_dim(pair, core, 1, False)
    return jnp.concatenate([kept, swap(away, "core")])


def both_rows(own, *others):
    other = after(swap(own, "y"), *others)
    first = lax.axis_index("y") == 0
    return jnp.stack([jnp.where(first, own, other), jnp.where(first, other, own)])


def all_to_all(values, axes):
    return lax.all_to_all(values, axes, 0, 0, tiled=True)


def inverse_rms(values):
    return lax.rsqrt(jnp.mean(values * values, axis=-1, keepdims=True) + norm_eps)


def head_layer(
    count,
    tokens,
    cotangent,
    norm_gain1,
    w_query,
    key_weight,
    value_weight,
    w_out,
    norm_gain2,
    w_gate,
    w_up,
    w_down,
):
    rows, width = tokens.shape[1:]
    own = w_query.shape[0]
    ff_own = w_down.shape[0]
    half = HEAD_SIZE // 2
    quarter = HEAD_SIZE // 4
    group = 4 * own
    seq_rows = 2 * rows
    length = count * seq_rows
    step = seq_rows

    gain1 = norm_gain1.astype(f32)[:, None]
    gain2 = norm_gain2.astype(f32)[:, None]

    place = place_of(lax.axis_index("d"), count)
    steps = jnp.arange(count, dtype=jnp.int32)
    core = lax.axis_index("core")
    seq = lax.axis_index("y")
    at = jnp.concatenate(
        [
            position_at(place + steps, count),
            lax.rem(place_of(steps, count) - place + count, count),
            jnp.stack([core, seq]).astype(jnp.int32),
        ]
    )

    out_down = GatherRing(jnp.concatenate([w_down, w_out], axis=0), count)
    out_down.start()
    qkv_cols = query_columns(at, gain1, w_query, key_weight, value_weight)
    qkv_rows = all_to_all(qkv_cols, ("core", "y")).reshape(group, count * HEAD_SIZE)
    qkv_rows = out_down.settle(qkv_rows)
    tokens_pair = both_rows(tokens[0], qkv_rows)
    qkv_ring = GatherRing(qkv_rows, count)
    qkv_ring.start()
    inputs = tokens_pair.astype(f32)
    r1 = inverse_rms(inputs)
    n1_own = (inputs * r1).astype(bf16)
    n1_other = swap(n1_own, "core")
    pair_cols = pair_columns(at, gain2, w_gate, w_up, ff_own)
    n1_own, n1_other, pair_cols = qkv_ring.settle(n1_own, n1_other, pair_cols)
    qkv_ring.start()
    pair_rows = all_to_all(pair_cols, ("core", "y")).reshape(group, 2 * count * ff_own)
    qkv_ring.settle()
    qkv_ring.start()
    pair_rows = qkv_ring.settle(pair_rows)
    qkv_ring.start()
    n1_own = qkv_ring.settle(n1_own)

    out_down.start(n1_own)
    n1, qkv_weight, qkv = project_heads(at, n1_own, n1_other, qkv_ring.parts)
    cotangent_pair = both_rows(after(cotangent[0], pair_rows), n1_own)
    cotangent_other = swap(cotangent_pair, "core")
    qkv = all_to_all(qkv, ("d", "y")).reshape(count, 2, HEAD_SIZE, seq_rows)
    out_down.settle()
    out_down.start()
    qkv, cotangent_other = out_down.settle(qkv, cotangent_other)
    out_down.start()
    q_parts = qkv[:, :, :half].transpose(1, 2, 0, 3).reshape(2, half, length)
    kv_own = qkv[:, :, half:].reshape(count, 2, 2, quarter, seq_rows).transpose(2, 1, 3, 0, 4)
    kv_own = kv_own.reshape(2, half, length)
    kv_other = swap(kv_own, "core")
    kv_first = jnp.where(core == 0, kv_own, kv_other)
    kv_second = jnp.where(core == 0, kv_other, kv_own)
    k_parts = (kv_first[0], kv_second[0])
    position = jnp.arange(length, dtype=f32)
    exponent = jnp.arange(half, dtype=f32) * (2.0 / HEAD_SIZE)
    angle = (rope_base ** (-exponent))[:, None] * position[None, :]
    cosine = jnp.cos(angle)
    sine = jnp.sin(angle)

    def rotate(first, second):
        return jnp.concatenate(
            [first * cosine - second * sine, second * cosine + first * sine], axis=0
        )

    def rotate_back(turned):
        first = turned[:half]
        second = turned[half:]
        return jnp.stack(
            [first * cosine + second * sine, second * cosine - first * sine], axis=0
        )

    q_parts = q_parts.astype(f32)
    k_parts = [part.astype(f32) for part in k_parts]
    q = (rotate(q_parts[0], q_parts[1]) * (score_scale * log2_e)).astype(bf16)
    k = rotate(k_parts[0], k_parts[1]).astype(bf16)
    v = jnp.concatenate([kv_first[1], kv_second[1]], axis=0)
    pair_ring = GatherRing(pair_rows, count)
    pair_ring.start(qkv)
    mixed, prob = heads_forward(q, k, v, step)
    mixed = out_down.settle(mixed)
    mixed = pair_ring.settle(mixed)
    pair_ring.start()
    mixed_send = mixed.astype(bf16).reshape(2, half, count, seq_rows).transpose(2, 0, 1, 3)
    mixed_low = all_to_all(mixed_send.reshape(2 * count, half, seq_rows), ("d", "y"))
    mixed_low = pair_ring.settle(mixed_low)
    pair_ring.start()
    out_weight, mixed_low, kept, away = project_out(at, mixed_low, out_down.parts, ff_own)
    branch = pair_ring.settle(core_sum(kept, away))
    pair_ring.start()
    branch = both_rows_sum(branch)
    d_out, down_weight, d_hidden = hidden_gradient(
        at, cotangent_pair, cotangent_other, out_down.parts, ff_own
    )
    branch, d_hidden = tie(branch, d_hidden)
    middle = inputs + branch

    r2 = inverse_rms(middle)
    n2_pair = middle * r2
    n2_own = n2_pair.astype(bf16)
    n2_other = swap(n2_own, "core")
    n2_own, n2_other = pair_ring.settle(n2_own, n2_other)
    n2, hidden, d_both, kept, away = feed_forward(at, n2_own, n2_other, d_hidden, pair_ring.parts)
    d_n2 = core_sum(kept, away)
    grad_both, grad_down = feed_forward_grads(
        at, n2, d_both, after(hidden, d_n2), d_out, count
    )
    d_normed2 = both_rows_sum(d_n2)
    ff_ring = ScatterRing([grad_both, grad_down], count)
    ff_ring.start()
    d_normed2 = ff_ring.settle(d_normed2)
    ff_ring.start()
    d_middle = cotangent_pair.astype(f32) + r2 * (
        d_normed2 - n2_pair * jnp.mean(d_normed2 * n2_pair, axis=-1, keepdims=True)
    )

    d_mid_own = d_middle.astype(bf16)
    d_mid_other = swap(d_mid_own, "core")
    d_mid, d_mixed = split_heads(at, d_mid_own, d_mid_other, out_weight, count)
    d_mixed = ff_ring.settle(d_mixed)
    ff_ring.start()
    d_mixed = all_to_all(d_mixed, ("d", "y"))
    d_mixed = ff_ring.settle(d_mixed)
    ff_ring.start()
    d_mixed = d_mixed.reshape(count, 2, half, seq_rows).transpose(1, 2, 0, 3)
    d_mixed = d_mixed.reshape(HEAD_SIZE, length)
    grad_out = dot_at(after(mixed_low, d_mixed), d_mid, 1, 0).astype(bf16)
    owned_out = all_to_all(grad_out.reshape(count, own, width), "d")
    d_q, d_k, d_v = heads_backward(q, k, v, prob, mixed, d_mixed, step)
    d_kv = jnp.stack([rotate_back(d_k), d_v.reshape(2, half, length)], axis=1)
    away = lax.dynamic_index_in_dim(d_kv, 1 - core, 0, False).astype(bf16)
    kept = lax.dynamic_index_in_dim(d_kv, core, 0, False)
    d_kv = core_sum(kept, away).astype(bf16)
    d_kv = d_kv.reshape(2, 2, quarter, count, seq_rows).transpose(3, 1, 0, 2, 4)
    d_kv = d_kv.reshape(count, 2, half, seq_rows)
    d_q = rotate_back(d_q).astype(bf16).reshape(2, half, count, seq_rows).transpose(2, 0, 1, 3)
    d_qkv = jnp.concatenate([d_q, d_kv], axis=2).reshape(2 * count, HEAD_SIZE, seq_rows)
    d_qkv, owned_out = ff_ring.settle(d_qkv, owned_out)
    ff_ring.start()
    d_qkv = all_to_all(d_qkv, ("d", "y"))
    ff_ring.settle()
    ff_ring.start()
    d_qkv = ff_ring.settle(d_qkv)
    d_qkv, grad_qkv = heads_grad(at, d_qkv, n1)
    grad_qkv = grad_qkv.reshape(4 * count, own, count * HEAD_SIZE)
    ff_ring.start(grad_qkv)
    own_qkv = all_to_all(grad_qkv, ("d", "core", "y"))
    ff_ring.settle()
    owned_both, owned_down = ff_ring.sums()
    own_both = own_columns(owned_both.astype(bf16).reshape(2, 2, own, -1))
    kept, away = heads_input(at, d_qkv, qkv_weight)
    d_normed1 = own_rows_sum(core_sum(kept, away))
    kept, away = layer_output(at, hidden, down_weight, count)
    n1_wide, r1_own, d_middle_own, middle_own = (
        lax.dynamic_index_in_dim(value, seq, 0, False)
        for value in (inputs * r1, r1, d_middle, middle)
    )
    input_grad = d_middle_own + r1_own * (
        d_normed1 - n1_wide * jnp.mean(d_normed1 * n1_wide, axis=-1, keepdims=True)
    )
    result = middle_own + own_rows_sum(core_sum(kept, away))
    own_qkv, own_both = tie(own_qkv, own_both)
    owned_out = jnp.sum(owned_out.astype(f32), axis=0)
    grad_gate, grad_up, grad_gain2 = pair_rows_grads(
        at, own_both, gain2, w_gate, w_up, ff_own, count
    )
    grad_query, grad_key, grad_value, grad_gain1 = query_rows_grads(
        at, own_qkv, gain1, w_query, key_weight, value_weight
    )
    return (
        result.astype(bf16)[None],
        input_grad[None],
        grad_gain1[:, 0],
        grad_query,
        grad_key,
        grad_value,
        owned_out,
        grad_gain2[:, 0],
        grad_gate,
        grad_up,
        owned_down,
    )


def by_heads(mesh):
    count = mesh.shape["ctx"] // 2
    parts = Mesh(mesh.devices.reshape(count, 2, 2), ("d", "core", "y"))
    owner = ("d", "core", "y")
    row_spec = P("y", ("d", "core"), None)
    in_specs = (row_spec, row_spec) + (P(owner),) * 9
    out_specs = (row_spec, row_spec) + (P(owner),) * 9
    return jax.shard_map(
        functools.partial(head_layer, count),
        mesh=parts,
        in_specs=in_specs,
        out_specs=out_specs,
        check_vma=False,
    )


def solution(mesh):
    in_specs = (
        P("fsdp", "ctx", None),
        P("fsdp", "ctx", None),
        P(("ctx", "fsdp")),
        P(("ctx", "fsdp"), None),
        P(("ctx", "fsdp"), None),
        P(("ctx", "fsdp"), None),
        P(("ctx", "fsdp"), None),
        P(("ctx", "fsdp")),
        P(("ctx", "fsdp"), None),
        P(("ctx", "fsdp"), None),
        P(("ctx", "fsdp"), None),
    )
    out_specs = (
        P("fsdp", "ctx", None),
        P("fsdp", "ctx", None),
        P(("ctx", "fsdp")),
        P(("ctx", "fsdp"), None),
        P(("ctx", "fsdp"), None),
        P(("ctx", "fsdp"), None),
        P(("ctx", "fsdp"), None),
        P(("ctx", "fsdp")),
        P(("ctx", "fsdp"), None),
        P(("ctx", "fsdp"), None),
        P(("ctx", "fsdp"), None),
    )
    if mesh.shape["ctx"] == QUERY_HEADS and mesh.shape["fsdp"] == 2:
        return by_heads(mesh)
    return jax.shard_map(local, mesh=mesh, in_specs=in_specs, out_specs=out_specs, check_vma=False)
```

```python
import functools

import jax
import jax.numpy as jnp
import numpy as np
from jax import lax
from jax.experimental import pallas as pl
from jax.experimental.pallas import tpu as pltpu
from jax.sharding import Mesh
from jax.sharding import PartitionSpec as P

QUERY_HEADS = 16
KEY_VALUE_HEADS = 8
HEAD_SIZE = 96


rope_base = 100000.0
norm_eps = 1e-05
masked_value = -1e30
key_block = 512


def rms_norm(value_rows, gain):
    return (
        value_rows
        * lax.rsqrt(jnp.mean(value_rows * value_rows, axis=-1, keepdims=True) + norm_eps)
        * gain
    )


def apply_rotary(value_rows, token_position):
    half = value_rows.shape[-1] // 2
    exponent = jnp.arange(half, dtype=jnp.float32) * (2.0 / value_rows.shape[-1])
    freq = rope_base ** (-exponent)
    angle = token_position[:, None] * freq[None, :]
    cosine = jnp.cos(angle)[:, None, :]
    sine = jnp.sin(angle)[:, None, :]
    first = value_rows[..., :half]
    second = value_rows[..., half:]
    return jnp.concatenate(
        [first * cosine - second * sine, second * cosine + first * sine], axis=-1
    )


def matmul(left, right):
    return jnp.dot(left, right, preferred_element_type=jnp.float32)


def key_pieces(key_rows, value_rows, key_value_heads, head_dim):
    count = key_rows.shape[0]
    number = count // key_block
    key_sets = key_rows.reshape(number, key_block, key_value_heads, head_dim)
    value_sets = value_rows.reshape(number, key_block, key_value_heads, head_dim)
    starts = jnp.arange(number, dtype=jnp.int32) * key_block
    return (key_sets, value_sets, starts, key_block)


def fold_keys(carry, key_rows, value_rows, query_rows, query_pos):
    key_value_heads = query_rows.shape[1]
    head_dim = query_rows.shape[3]
    scale = head_dim ** (-0.5)
    key_sets, value_sets, starts, size = key_pieces(key_rows, value_rows, key_value_heads, head_dim)

    def fold_one_piece(state, item):
        key_set, value_set, begin = item

        def fold_live(state):
            top, total, summed = state
            scores = (
                jnp.einsum(
                    "tkgd,skd->kgts", query_rows, key_set, preferred_element_type=jnp.float32
                )
                * scale
            )
            visible = (begin + jnp.arange(size, dtype=jnp.int32))[None, :] <= query_pos[:, None]
            scores = jnp.where(visible, scores, masked_value)
            new_top = jnp.maximum(top, jnp.max(scores, axis=-1))
            weights = jnp.where(visible, jnp.exp(scores - new_top[..., None]), 0.0)
            factor = jnp.exp(top - new_top)
            total = total * factor + jnp.sum(weights, axis=-1)
            summed = summed * factor[..., None] + jnp.einsum(
                "kgts,skd->kgtd",
                weights.astype(jnp.bfloat16),
                value_set,
                preferred_element_type=jnp.float32,
            )
            return (new_top, total, summed)

        def fold_skipped(state):
            return state

        return (lax.cond(begin <= query_pos[-1], fold_live, fold_skipped, state), None)

    carry, _ = lax.scan(fold_one_piece, carry, (key_sets, value_sets, starts))
    return carry


def back_keys(key_rows, value_rows, query_rows, query_pos, d_heads, log_total, delta):
    rows, key_value_heads, groups, head_dim = query_rows.shape
    scale = head_dim ** (-0.5)
    key_sets, value_sets, starts, size = key_pieces(key_rows, value_rows, key_value_heads, head_dim)

    def back_one_piece(d_query, item):
        key_set, value_set, begin = item

        def back_live(d_query):
            scores = (
                jnp.einsum(
                    "tkgd,skd->kgts", query_rows, key_set, preferred_element_type=jnp.float32
                )
                * scale
            )
            visible = (begin + jnp.arange(size, dtype=jnp.int32))[None, :] <= query_pos[:, None]
            prob = jnp.where(visible, jnp.exp(scores - log_total[..., None]), 0.0)
            d_prob = jnp.einsum(
                "tkgd,skd->kgts", d_heads, value_set, preferred_element_type=jnp.float32
            )
            d_scores = (prob * (d_prob - delta[..., None])).astype(jnp.bfloat16)
            d_query = d_query + scale * jnp.einsum(
                "kgts,skd->tkgd", d_scores, key_set, preferred_element_type=jnp.float32
            )
            d_key = scale * jnp.einsum(
                "kgts,tkgd->skd", d_scores, query_rows, preferred_element_type=jnp.float32
            )
            d_value = jnp.einsum(
                "kgts,tkgd->skd",
                prob.astype(jnp.bfloat16),
                d_heads,
                preferred_element_type=jnp.float32,
            )
            return (
                d_query,
                (
                    d_key.reshape(size, key_value_heads * head_dim),
                    d_value.reshape(size, key_value_heads * head_dim),
                ),
            )

        def back_skipped(d_query):
            empty = jnp.zeros((size, key_value_heads * head_dim), jnp.float32)
            return (d_query, (empty, empty))

        return lax.cond(begin <= query_pos[-1], back_live, back_skipped, d_query)

    start_grad = jnp.zeros((rows, key_value_heads, groups, head_dim), jnp.float32)
    d_query, (d_keys, d_values) = lax.scan(
        back_one_piece, start_grad, (key_sets, value_sets, starts)
    )
    return (
        d_query,
        d_keys.reshape(key_rows.shape[0], key_value_heads * head_dim),
        d_values.reshape(key_rows.shape[0], key_value_heads * head_dim),
    )


def local(
    tokens,
    cotangent,
    norm_gain1,
    w_query,
    key_weight,
    value_weight,
    w_out,
    norm_gain2,
    w_gate,
    w_up,
    w_down,
):
    rows = tokens.shape[1]
    key_value_heads = KEY_VALUE_HEADS
    heads = QUERY_HEADS
    head_dim = HEAD_SIZE
    groups = heads // key_value_heads
    first_row = lax.axis_index("ctx") * rows
    query_pos = first_row + jnp.arange(rows, dtype=jnp.int32)
    token_position = query_pos.astype(jnp.float32)
    inputs = tokens[0].astype(jnp.float32)
    gathered = (
        lax.all_gather(norm_gain1, ("ctx", "fsdp"), axis=0, tiled=True),
        lax.all_gather(w_query, ("ctx", "fsdp"), axis=0, tiled=True),
        lax.all_gather(key_weight, ("ctx", "fsdp"), axis=0, tiled=True),
        lax.all_gather(value_weight, ("ctx", "fsdp"), axis=0, tiled=True),
        lax.all_gather(w_out, ("ctx", "fsdp"), axis=0, tiled=True),
        lax.all_gather(norm_gain2, ("ctx", "fsdp"), axis=0, tiled=True),
        lax.all_gather(w_gate, ("ctx", "fsdp"), axis=0, tiled=True),
        lax.all_gather(w_up, ("ctx", "fsdp"), axis=0, tiled=True),
        lax.all_gather(w_down, ("ctx", "fsdp"), axis=0, tiled=True),
    )
    gain_one = gathered[0].astype(jnp.float32)
    gain_two = gathered[5].astype(jnp.float32)
    normed1 = rms_norm(inputs, gain_one).astype(jnp.bfloat16)
    query_pre = matmul(normed1, gathered[1]).reshape(rows, heads, head_dim)
    key_pre = matmul(normed1, gathered[2]).reshape(rows, key_value_heads, head_dim)
    value = matmul(normed1, gathered[3]).astype(jnp.bfloat16)
    query_rows = (
        apply_rotary(query_pre, token_position)
        .astype(jnp.bfloat16)
        .reshape(rows, key_value_heads, groups, head_dim)
    )
    key_rows = (
        apply_rotary(key_pre, token_position)
        .reshape(rows, key_value_heads * head_dim)
        .astype(jnp.bfloat16)
    )
    start_state = (
        jnp.full((key_value_heads, groups, rows), masked_value, jnp.float32),
        jnp.zeros((key_value_heads, groups, rows), jnp.float32),
        jnp.zeros((key_value_heads, groups, rows, head_dim), jnp.float32),
    )
    top, total, summed = fold_keys(
        start_state,
        lax.all_gather(key_rows, "ctx", axis=0, tiled=True),
        lax.all_gather(value, "ctx", axis=0, tiled=True),
        query_rows,
        query_pos,
    )
    mixed_heads = jnp.transpose(summed / total[..., None], (2, 0, 1, 3))
    log_total = top + jnp.log(total)
    mixed_low = mixed_heads.reshape(rows, heads * head_dim).astype(jnp.bfloat16)
    middle = inputs + matmul(mixed_low, gathered[4])
    normed2 = rms_norm(middle, gain_two).astype(jnp.bfloat16)
    gate = matmul(normed2, gathered[6])
    upper = matmul(normed2, gathered[7])
    hidden = (jax.nn.silu(gate) * upper).astype(jnp.bfloat16)
    result = middle + matmul(hidden, gathered[8])
    gathered = (
        lax.all_gather(norm_gain1, ("ctx", "fsdp"), axis=0, tiled=True),
        lax.all_gather(w_query, ("ctx", "fsdp"), axis=0, tiled=True),
        lax.all_gather(key_weight, ("ctx", "fsdp"), axis=0, tiled=True),
        lax.all_gather(value_weight, ("ctx", "fsdp"), axis=0, tiled=True),
        lax.all_gather(w_out, ("ctx", "fsdp"), axis=0, tiled=True),
        lax.all_gather(norm_gain2, ("ctx", "fsdp"), axis=0, tiled=True),
        lax.all_gather(w_gate, ("ctx", "fsdp"), axis=0, tiled=True),
        lax.all_gather(w_up, ("ctx", "fsdp"), axis=0, tiled=True),
        lax.all_gather(w_down, ("ctx", "fsdp"), axis=0, tiled=True),
    )
    incoming = cotangent[0].astype(jnp.float32)
    incoming_low = incoming.astype(jnp.bfloat16)
    grad_down = matmul(hidden.T, incoming_low)
    d_hidden = matmul(incoming_low, gathered[8].T)
    _, swiglu_back = jax.vjp(lambda gate_in, upper_in: jax.nn.silu(gate_in) * upper_in, gate, upper)
    d_gate, d_upper = swiglu_back(d_hidden)
    d_gate = d_gate.astype(jnp.bfloat16)
    d_upper = d_upper.astype(jnp.bfloat16)
    grad_gate = matmul(normed2.T, d_gate)
    grad_up = matmul(normed2.T, d_upper)
    d_normed2 = matmul(d_gate, gathered[6].T) + matmul(d_upper, gathered[7].T)
    _, norm_back2 = jax.vjp(rms_norm, middle, gain_two)
    d_middle, grad_gain2 = norm_back2(d_normed2)
    d_middle = d_middle + incoming
    owned_gain2, owned_gate, owned_up, owned_down = (
        lax.psum_scatter(grad_gain2, ("ctx", "fsdp"), scatter_dimension=0, tiled=True),
        lax.psum_scatter(grad_gate, ("ctx", "fsdp"), scatter_dimension=0, tiled=True),
        lax.psum_scatter(grad_up, ("ctx", "fsdp"), scatter_dimension=0, tiled=True),
        lax.psum_scatter(grad_down, ("ctx", "fsdp"), scatter_dimension=0, tiled=True),
    )
    d_middle_low = d_middle.astype(jnp.bfloat16)
    grad_out = matmul(mixed_low.T, d_middle_low)
    d_mixed = matmul(d_middle_low, gathered[4].T).astype(jnp.bfloat16)
    d_heads = d_mixed.reshape(rows, key_value_heads, groups, head_dim)
    delta = jnp.transpose(jnp.sum(d_heads.astype(jnp.float32) * mixed_heads, axis=-1), (1, 2, 0))
    back_keys_all, back_values_all = (
        lax.all_gather(key_rows, "ctx", axis=0, tiled=True),
        lax.all_gather(value, "ctx", axis=0, tiled=True),
    )
    d_query_rot, d_keys_all, d_values_all = back_keys(
        back_keys_all, back_values_all, query_rows, query_pos, d_heads, log_total, delta
    )
    d_keys_rot, d_value = (
        lax.psum_scatter(d_keys_all, "ctx", scatter_dimension=0, tiled=True),
        lax.psum_scatter(d_values_all, "ctx", scatter_dimension=0, tiled=True),
    )
    _, rotate_back_query = jax.vjp(
        lambda values_in: apply_rotary(values_in, token_position), query_pre
    )
    _, rotate_back_key = jax.vjp(lambda values_in: apply_rotary(values_in, token_position), key_pre)
    d_query = (
        rotate_back_query(d_query_rot.reshape(rows, heads, head_dim))[0]
        .reshape(rows, heads * head_dim)
        .astype(jnp.bfloat16)
    )
    d_key = (
        rotate_back_key(d_keys_rot.reshape(rows, key_value_heads, head_dim))[0]
        .reshape(rows, key_value_heads * head_dim)
        .astype(jnp.bfloat16)
    )
    d_value = d_value.astype(jnp.bfloat16)
    grad_query = matmul(normed1.T, d_query)
    grad_key = matmul(normed1.T, d_key)
    grad_value = matmul(normed1.T, d_value)
    d_normed1 = (
        matmul(d_query, gathered[1].T)
        + matmul(d_key, gathered[2].T)
        + matmul(d_value, gathered[3].T)
    )
    _, norm_back1 = jax.vjp(rms_norm, inputs, gain_one)
    d_inputs, grad_gain1 = norm_back1(d_normed1)
    input_grad = d_inputs + d_middle
    owned_gain1, owned_query, owned_key, owned_value, owned_out = (
        lax.psum_scatter(grad_gain1, ("ctx", "fsdp"), scatter_dimension=0, tiled=True),
        lax.psum_scatter(grad_query, ("ctx", "fsdp"), scatter_dimension=0, tiled=True),
        lax.psum_scatter(grad_key, ("ctx", "fsdp"), scatter_dimension=0, tiled=True),
        lax.psum_scatter(grad_value, ("ctx", "fsdp"), scatter_dimension=0, tiled=True),
        lax.psum_scatter(grad_out, ("ctx", "fsdp"), scatter_dimension=0, tiled=True),
    )
    return (
        result.astype(jnp.bfloat16)[None],
        input_grad[None],
        owned_gain1,
        owned_query,
        owned_key,
        owned_value,
        owned_out,
        owned_gain2,
        owned_gate,
        owned_up,
        owned_down,
    )


bf16 = jnp.bfloat16
f32 = jnp.float32
score_scale = HEAD_SIZE ** (-0.5)
log2_e = 1.4426950408889634
ln_2 = 0.6931471805599453


def dot_at(left, right, left_dim, right_dim):
    return lax.dot_general(
        left, right, (((left_dim,), (right_dim,)), ((), ())), preferred_element_type=jnp.float32
    )


def rotate(values, cosine, sine):
    half = values.shape[0] // 2
    first, second = values[:half], values[half:]
    return jnp.concatenate([first * cosine - second * sine, second * cosine + first * sine], axis=0)


def rotate_back(values, cosine, sine):
    half = values.shape[0] // 2
    first, second = values[:half], values[half:]
    return jnp.concatenate([first * cosine + second * sine, second * cosine - first * sine], axis=0)


def heads_forward_kernel(
    count, at_ref, q_ref, own_ref, other_ref, cos_ref, sin_ref,
    send_ref, mixed_ref, prob_ref, k_ref, v_ref, turn_ref,
):
    core = at_ref[2 * count]
    half = own_ref.shape[1]
    here = pl.ds(pl.multiple_of(core * half, half), half)
    there = pl.ds(pl.multiple_of((1 - core) * half, half), half)
    turn_ref[here, :] = own_ref[0].astype(f32)
    turn_ref[there, :] = other_ref[0].astype(f32)
    k_ref[...] = rotate(turn_ref[...], cos_ref[...], sin_ref[...]).astype(bf16)
    v_ref[here, :] = own_ref[1]
    v_ref[there, :] = other_ref[1]
    step = send_ref.shape[2]
    offset = 0
    for block in range(count):
        begin = block * step
        end = begin + step
        scores = dot_at(k_ref[:, 0:end], q_ref[:, begin:end], 0, 0)
        key = lax.broadcasted_iota(jnp.int32, (step, step), 0)
        query = lax.broadcasted_iota(jnp.int32, (step, step), 1)
        last = jnp.where(key <= query, scores[begin:end], masked_value)
        top = jnp.max(last, axis=0, keepdims=True)
        if begin:
            top = jnp.maximum(top, jnp.max(scores[:begin], axis=0, keepdims=True))
        last = jnp.exp2(last - top)
        total = jnp.sum(last, axis=0, keepdims=True)
        if begin:
            first = jnp.exp2(scores[:begin] - top)
            total = total + jnp.sum(first, axis=0, keepdims=True)
        inverse = 1.0 / total
        prob_ref[offset + begin : offset + end, :] = (last * inverse).astype(bf16)
        if begin:
            prob_ref[offset : offset + begin, :] = (first * inverse).astype(bf16)
        mixed = dot_at(v_ref[:, 0:end], prob_ref[offset : offset + end, :], 1, 0)
        mixed_ref[:, begin:end] = mixed
        send_ref[2 * block] = mixed[:half].astype(bf16)
        send_ref[2 * block + 1] = mixed[half:].astype(bf16)
        offset += end


def heads_forward(at, q, own, other, cosine, sine, count):
    size, tokens = q.shape
    step = tokens // count
    pairs = step * count * (count + 1) // 2
    return on_chip(
        functools.partial(heads_forward_kernel, count),
        [
            like(bf16, 2 * count, size // 2, step),
            like(f32, size, tokens),
            like(bf16, pairs, step),
            like(bf16, size, tokens),
            like(bf16, size, tokens),
        ],
        [at, q, own, other, cosine, sine],
        4 * size * pairs * step,
        scratch=[pltpu.VMEM((size, tokens), f32)],
        name="heads_forward",
    )


def heads_backward_kernel(
    count, at_ref, q_ref, k_ref, v_ref, prob_ref, mixed_ref, back_ref, cos_ref, sin_ref,
    d_q_ref, kept_ref, away_ref, d_k_ref, d_v_ref,
):
    core = at_ref[2 * count]
    half, step = back_ref.shape[1:]
    offset = 0
    for block in range(count):
        begin = block * step
        end = begin + step
        d_mixed = jnp.concatenate([back_ref[2 * block], back_ref[2 * block + 1]], axis=0)
        delta = jnp.sum(d_mixed.astype(f32) * mixed_ref[:, begin:end], axis=0, keepdims=True)
        prob = prob_ref[offset : offset + end, :]
        d_prob = dot_at(v_ref[:, 0:end], d_mixed, 0, 0)
        d_scores = (prob.astype(f32) * (d_prob - delta)).astype(bf16)
        d_q = dot_at(k_ref[:, 0:end], d_scores, 1, 0) * score_scale
        d_q_ref[:, begin:end] = rotate_back(d_q, cos_ref[:, begin:end], sin_ref[:, begin:end])
        d_v = dot_at(d_mixed, prob, 1, 1)
        d_k = dot_at(q_ref[:, begin:end], d_scores, 1, 1) * ln_2
        if begin:
            d_v_ref[:, 0:begin] += d_v[:, 0:begin]
            d_k_ref[:, 0:begin] += d_k[:, 0:begin]
        d_v_ref[:, begin:end] = d_v[:, begin:end]
        d_k_ref[:, begin:end] = d_k[:, begin:end]
        offset += end
    d_k_ref[...] = rotate_back(d_k_ref[...], cos_ref[...], sin_ref[...])
    here = pl.ds(pl.multiple_of(core * half, half), half)
    there = pl.ds(pl.multiple_of((1 - core) * half, half), half)
    kept_ref[0] = d_k_ref[here, :]
    kept_ref[1] = d_v_ref[here, :]
    away_ref[0] = d_k_ref[there, :].astype(bf16)
    away_ref[1] = d_v_ref[there, :].astype(bf16)


def heads_backward(at, q, k, v, prob, mixed, d_mixed, cosine, sine, count):
    size, tokens = q.shape
    return on_chip(
        functools.partial(heads_backward_kernel, count),
        [
            like(f32, size, tokens),
            like(f32, 2, size // 2, tokens),
            like(bf16, 2, size // 2, tokens),
        ],
        [at, q, k, v, prob, mixed, d_mixed, cosine, sine],
        8 * size * prob.size,
        scratch=[pltpu.VMEM((size, tokens), f32)] * 2,
        name="heads_backward",
    )


def heads_send_kernel(at_ref, d_q_ref, kept_ref, other_ref, send_ref, joined_ref):
    half = kept_ref.shape[1]
    quarter = half // 2
    step = send_ref.shape[2]
    d_kv = kept_ref[...] + other_ref[...].astype(f32)
    joined_ref[: 2 * half, :] = d_q_ref[...].astype(bf16)
    joined_ref[2 * half : 3 * half, :] = d_kv[0].astype(bf16)
    joined_ref[3 * half :, :] = d_kv[1].astype(bf16)
    for block in range(send_ref.shape[0] // 2):
        columns = slice(block * step, (block + 1) * step)
        for side in range(2):
            rows = slice(side * quarter, (side + 1) * quarter)
            send_ref[2 * block + side] = jnp.concatenate(
                [
                    d_q_ref[side * half : (side + 1) * half, columns],
                    d_kv[0, rows, columns],
                    d_kv[1, rows, columns],
                ],
                axis=0,
            ).astype(bf16)


def heads_send(at, d_q, kept, other, count):
    size, tokens = d_q.shape
    return on_chip(
        heads_send_kernel,
        [like(bf16, 2 * count, size, tokens // count), like(bf16, 2 * size, tokens)],
        [at, d_q, kept, other],
        8 * d_q.size,
        name="heads_send",
    )


def on_chip(kernel, out_shape, args, flops, blocks=(), scratch=(), name=None):
    moved = sum(a.size * a.dtype.itemsize for a in list(args) + list(blocks))
    moved += sum(o.size * o.dtype.itemsize for o in out_shape)
    near = pl.BlockSpec(memory_space=pltpu.VMEM)
    return pl.pallas_call(
        kernel,
        out_shape=tuple(out_shape),
        in_specs=[pl.BlockSpec(memory_space=pltpu.SMEM)]
        + [near] * (len(args) - 1)
        + [pl.BlockSpec(memory_space=pltpu.HBM)] * len(blocks),
        out_specs=(near,) * len(out_shape),
        scratch_shapes=scratch,
        compiler_params=pltpu.CompilerParams(vmem_limit_bytes=48 * 2**20),
        cost_estimate=pl.CostEstimate(flops=flops, bytes_accessed=moved, transcendentals=0),
        name=name,
    )(*args, *blocks)


def like(dtype, *shape):
    return jax.ShapeDtypeStruct(shape, dtype)


def block_copies(at_ref, block_refs, whole_ref, sem_ref, first=0):
    size = whole_ref.shape[0] // len(block_refs)
    copies = []
    for k, block_ref in enumerate(block_refs):
        start = pl.multiple_of(at_ref[k] * size, size)
        copies.append(
            pltpu.make_async_copy(
                block_ref.at[pl.ds(first, size), :], whole_ref.at[pl.ds(start, size), :], sem_ref.at[k]
            )
        )
    return copies


def core_rows(at_ref, count, rows, seq, other):
    core = at_ref[2 * count]
    start = seq * 2 * rows + (1 - core if other else core) * rows
    return pl.ds(pl.multiple_of(start, rows), rows)


def join_rows(at_ref, count, own_ref, other_ref, whole_ref):
    rows = own_ref.shape[1]
    for seq in range(2):
        whole_ref[core_rows(at_ref, count, rows, seq, False), :] = own_ref[seq]
        whole_ref[core_rows(at_ref, count, rows, seq, True), :] = other_ref[seq]


def part_rows(at_ref, count, whole_ref, kept_ref, away_ref):
    rows = kept_ref.shape[1]
    for seq in range(2):
        kept_ref[seq] = whole_ref[core_rows(at_ref, count, rows, seq, False), :]
        away_ref[seq] = whole_ref[core_rows(at_ref, count, rows, seq, True), :].astype(bf16)


def query_columns_kernel(at_ref, gain_ref, query_ref, key_ref, value_ref, out_ref):
    gain = gain_ref[...]
    query = query_ref[...].astype(f32) * gain
    key = key_ref[...].astype(f32) * gain
    value = value_ref[...].astype(f32) * gain
    half = HEAD_SIZE // 2
    quarter = HEAD_SIZE // 4
    groups = out_ref.shape[2] // HEAD_SIZE
    for t in range(4):
        pieces = []
        for group in range(groups):
            place = 4 * group + t
            pieces.append(query[:, place * half : (place + 1) * half])
            pieces.append(key[:, place * quarter : (place + 1) * quarter])
            pieces.append(value[:, place * quarter : (place + 1) * quarter])
        out_ref[t] = jnp.concatenate(pieces, axis=1).astype(bf16)


def query_columns(at, gain, query, key, value):
    own, width = query.shape
    (out,) = on_chip(
        query_columns_kernel,
        [like(bf16, 4, own, (width + 2 * key.shape[1]) // 4)],
        [at, gain, query, key, value],
        own * width,
        name="query_columns",
    )
    return out


def pair_columns_kernel(size, at_ref, gain_ref, gate_ref, up_ref, out_ref):
    gain = gain_ref[...]
    half = out_ref.shape[2] // 2
    for t in range(4):
        for position in range(half // size):
            columns = pl.ds((4 * position + t) * size, size)
            for side, ref in enumerate((gate_ref, up_ref)):
                out_ref[t, :, pl.ds(side * half + position * size, size)] = (
                    ref[:, columns].astype(f32) * gain
                ).astype(bf16)


def pair_columns(at, gain, gate, up, size):
    own, ff = gate.shape
    (out,) = on_chip(
        functools.partial(pair_columns_kernel, size),
        [like(bf16, 4, own, ff // 2)],
        [at, gain, gate, up],
        own * ff,
        name="pair_columns",
    )
    return out


def head_columns_kernel(at_ref, gain_ref, query_ref, key_ref, value_ref, out_ref):
    gain = gain_ref[...]
    query = query_ref[...].astype(f32) * gain
    key = key_ref[...].astype(f32) * gain
    value = value_ref[...].astype(f32) * gain
    half = HEAD_SIZE // 2
    for head in range(out_ref.shape[0] // 2):
        columns = jnp.concatenate(
            [
                query[:, head * HEAD_SIZE : (head + 1) * HEAD_SIZE],
                key[:, head * half : (head + 1) * half],
                value[:, head * half : (head + 1) * half],
            ],
            axis=1,
        ).astype(bf16)
        out_ref[2 * head] = columns
        out_ref[2 * head + 1] = columns


def head_columns(at, gain, query, key, value):
    own, width = query.shape
    (out,) = on_chip(
        head_columns_kernel,
        [like(bf16, 2 * (width // HEAD_SIZE), own, 2 * HEAD_SIZE)],
        [at, gain, query, key, value],
        own * width,
        name="head_columns",
    )
    return out


def sequence_copies(at_ref, block_refs, whole_ref, sem_ref):
    count = len(block_refs) // 2
    core = at_ref[2 * count]
    rows = block_refs[0].shape[0]
    copies = []
    for i, block_ref in enumerate(block_refs):
        side = core if i < count else 1 - core
        start = pl.multiple_of((2 * at_ref[i % count] + side) * rows, rows)
        copies.append(
            pltpu.make_async_copy(block_ref, whole_ref.at[pl.ds(start, rows), :], sem_ref.at[i])
        )
    return copies


def project_heads_kernel(at_ref, weight_ref, cos_ref, sin_ref, *refs):
    blocks, (q_ref, kv_ref, n_ref, sem_ref) = refs[:-4], refs[-4:]
    copies = sequence_copies(at_ref, blocks, n_ref, sem_ref)
    for copy in copies:
        copy.start()
    for copy in copies:
        copy.wait()
    half = kv_ref.shape[1]
    out = dot_at(weight_ref[...], n_ref[...], 0, 1)
    q = rotate(out[: 2 * half], cos_ref[...], sin_ref[...])
    q_ref[...] = (q * (score_scale * log2_e)).astype(bf16)
    kv_ref[0] = out[2 * half : 3 * half].astype(bf16)
    kv_ref[1] = out[3 * half :].astype(bf16)


def project_heads(at, weight, cosine, sine, blocks):
    half, tokens = cosine.shape
    rows, width = blocks[0].shape
    return on_chip(
        project_heads_kernel,
        [like(bf16, 2 * half, tokens), like(bf16, 2, half, tokens)],
        [at, weight, cosine, sine],
        8 * half * tokens * width,
        blocks=blocks,
        scratch=[pltpu.VMEM((tokens, width), bf16), pltpu.SemaphoreType.DMA((len(blocks),))],
        name="project_heads",
    )


def join_heads(heads_ref, joined_ref):
    size, rows = heads_ref.shape[1:]
    for seq in range(2):
        for head in range(heads_ref.shape[0] // 2):
            joined_ref[head * size : (head + 1) * size, seq * rows : (seq + 1) * rows] = heads_ref[
                2 * head + seq
            ]


def project_out_kernel(first, at_ref, heads_ref, *refs):
    blocks, (weight_ref, joined_ref, kept_ref, away_ref, out_ref, sem_ref) = refs[:-6], refs[-6:]
    copies = block_copies(at_ref, blocks, weight_ref, sem_ref, first=first)
    for copy in copies:
        copy.start()
    join_heads(heads_ref, joined_ref)
    for copy in copies:
        copy.wait()
    out_ref[...] = dot_at(joined_ref[...], weight_ref[...], 0, 0)
    part_rows(at_ref, len(blocks), out_ref, kept_ref, away_ref)


def project_out(at, heads, blocks, first):
    count = len(blocks)
    own, width = blocks[0].shape
    own -= first
    rows = heads.shape[2] // 2
    return on_chip(
        functools.partial(project_out_kernel, first),
        [
            like(bf16, count * own, width),
            like(bf16, count * own, 4 * rows),
            like(f32, 2, rows, width),
            like(bf16, 2, rows, width),
        ],
        [at, heads],
        8 * rows * width * count * own,
        blocks=blocks,
        scratch=[pltpu.VMEM((4 * rows, width), f32), pltpu.SemaphoreType.DMA((count,))],
        name="project_out",
    )


def hidden_gradient_kernel(at_ref, own_ref, other_ref, *refs):
    blocks, (d_out_ref, weight_ref, d_hidden_ref, sem_ref) = refs[:-4], refs[-4:]
    copies = block_copies(at_ref, blocks, weight_ref, sem_ref)
    for copy in copies:
        copy.start()
    join_rows(at_ref, len(blocks), own_ref, other_ref, d_out_ref)
    for copy in copies:
        copy.wait()
    d_hidden_ref[...] = dot_at(d_out_ref[...], weight_ref[...], 1, 1).astype(bf16)


def hidden_gradient(at, d_out_own, d_out_other, blocks, own):
    count = len(blocks)
    _, rows, width = d_out_own.shape
    return on_chip(
        hidden_gradient_kernel,
        [
            like(bf16, 4 * rows, width),
            like(bf16, count * own, width),
            like(bf16, 4 * rows, count * own),
        ],
        [at, d_out_own, d_out_other],
        8 * rows * width * count * own,
        blocks=blocks,
        scratch=[pltpu.SemaphoreType.DMA((count,))],
        name="hidden_gradient",
    )


def feed_forward_kernel(step, at_ref, own_ref, other_ref, d_hidden_ref, *refs):
    blocks = refs[:-8]
    n_ref, hidden_ref, d_both_ref, kept_ref, away_ref, d_n_ref, whole_ref, sem_ref = refs[-8:]
    ff = hidden_ref.shape[1]
    copies = block_copies(at_ref, blocks, whole_ref, sem_ref)
    for copy in copies:
        copy.start()
    join_rows(at_ref, len(blocks), own_ref, other_ref, n_ref)
    for copy in copies:
        copy.wait()
    for begin in range(0, n_ref.shape[0], step):
        rows = slice(begin, begin + step)
        both = dot_at(n_ref[rows, :], whole_ref[...], 1, 0)
        gate = both[:, :ff]
        upper = both[:, ff:]
        sigma = 1.0 / (1.0 + jnp.exp(-gate))
        silu = gate * sigma
        hidden_ref[rows, :] = (silu * upper).astype(bf16)
        d_hidden = d_hidden_ref[rows, :].astype(f32)
        d_both_ref[rows, :ff] = (d_hidden * upper * (sigma + silu * (1.0 - sigma))).astype(bf16)
        d_both_ref[rows, ff:] = (d_hidden * silu).astype(bf16)
        d_n_ref[rows, :] = dot_at(d_both_ref[rows, :], whole_ref[...], 1, 1)
    part_rows(at_ref, len(blocks), d_n_ref, kept_ref, away_ref)


def feed_forward(at, own, other, d_hidden, blocks):
    _, rows, width = own.shape
    ff = d_hidden.shape[1]
    return on_chip(
        functools.partial(feed_forward_kernel, min(256, 4 * rows)),
        [
            like(bf16, 4 * rows, width),
            like(bf16, 4 * rows, ff),
            like(bf16, 4 * rows, 2 * ff),
            like(f32, 2, rows, width),
            like(bf16, 2, rows, width),
        ],
        [at, own, other, d_hidden],
        32 * rows * width * ff,
        blocks=blocks,
        scratch=[
            pltpu.VMEM((4 * rows, width), f32),
            pltpu.VMEM((width, 2 * ff), bf16),
            pltpu.SemaphoreType.DMA((len(blocks),)),
        ],
        name="feed_forward",
    )


def feed_forward_grads_kernel(at_ref, n_ref, d_both_ref, hidden_ref, d_out_ref, both_ref, down_ref):
    count, block, _ = both_ref.shape
    own = down_ref.shape[1]
    for k in range(count):
        down_ref[k] = dot_at(
            hidden_ref[:, pl.ds(pl.multiple_of(at_ref[k] * own, own), own)], d_out_ref[...], 0, 0
        ).astype(bf16)
    for position in range(count):
        columns = slice(position * block, (position + 1) * block)
        both_ref[at_ref[count + position]] = dot_at(
            n_ref[:, columns], d_both_ref[...], 0, 0
        ).astype(bf16)


def feed_forward_grads(at, n, d_both, hidden, d_out, count):
    rows, width = n.shape
    ff = hidden.shape[1]
    return on_chip(
        feed_forward_grads_kernel,
        [like(bf16, count, width // count, 2 * ff), like(bf16, count, ff // count, width)],
        [at, n, d_both, hidden, d_out],
        6 * rows * width * ff,
        name="feed_forward_grads",
    )


def split_heads_kernel(at_ref, own_ref, other_ref, weight_ref, d_mid_ref, heads_ref):
    join_rows(at_ref, heads_ref.shape[0] // 2, own_ref, other_ref, d_mid_ref)
    size, rows = heads_ref.shape[1:]
    for seq in range(2):
        part = dot_at(weight_ref[...], d_mid_ref[seq * rows : (seq + 1) * rows, :], 1, 1)
        part = part.astype(bf16)
        for head in range(heads_ref.shape[0] // 2):
            heads_ref[2 * head + seq] = part[head * size : (head + 1) * size, :]


def split_heads(at, own, other, weight, heads):
    _, rows, width = own.shape
    return on_chip(
        split_heads_kernel,
        [
            like(bf16, 4 * rows, width),
            like(bf16, 2 * heads, weight.shape[0] // heads, 2 * rows),
        ],
        [at, own, other, weight],
        8 * rows * width * weight.shape[0],
        name="split_heads",
    )


def heads_grad_kernel(at_ref, joined_ref, *refs):
    blocks, (grad_ref, n_ref, sem_ref) = refs[:-3], refs[-3:]
    copies = sequence_copies(at_ref, blocks, n_ref, sem_ref)
    for copy in copies:
        copy.start()
    for copy in copies:
        copy.wait()
    grad_ref[...] = dot_at(n_ref[...], joined_ref[...], 0, 1).astype(bf16)


def heads_grad(at, joined, blocks):
    columns, tokens = joined.shape
    width = blocks[0].shape[1]
    (out,) = on_chip(
        heads_grad_kernel,
        [like(bf16, width, columns)],
        [at, joined],
        2 * tokens * width * columns,
        blocks=blocks,
        scratch=[pltpu.VMEM((tokens, width), bf16), pltpu.SemaphoreType.DMA((len(blocks),))],
        name="heads_grad",
    )
    return out


def heads_input_kernel(at_ref, heads_ref, *refs):
    blocks = refs[:-6]
    kept_ref, away_ref, out_ref, joined_ref, weight_ref, sem_ref = refs[-6:]
    copies = block_copies(at_ref, blocks, weight_ref, sem_ref)
    for copy in copies:
        copy.start()
    join_heads(heads_ref, joined_ref)
    for copy in copies:
        copy.wait()
    out_ref[...] = dot_at(joined_ref[...], weight_ref[...], 0, 1)
    part_rows(at_ref, len(blocks), out_ref, kept_ref, away_ref)


def heads_input(at, heads, blocks):
    count = len(blocks)
    block, columns = blocks[0].shape
    rows = heads.shape[2] // 2
    width = count * block
    return on_chip(
        heads_input_kernel,
        [like(f32, 2, rows, width), like(bf16, 2, rows, width)],
        [at, heads],
        0,
        blocks=blocks,
        scratch=[
            pltpu.VMEM((4 * rows, width), f32),
            pltpu.VMEM((columns, 4 * rows), bf16),
            pltpu.VMEM((width, columns), bf16),
            pltpu.SemaphoreType.DMA((count,)),
        ],
        name="heads_input",
    )


def layer_output_kernel(count, at_ref, hidden_ref, weight_ref, kept_ref, away_ref, out_ref):
    out_ref[...] = dot_at(hidden_ref[...], weight_ref[...], 1, 0)
    part_rows(at_ref, count, out_ref, kept_ref, away_ref)


def layer_output(at, hidden, weight, count):
    ff, width = weight.shape
    rows = hidden.shape[0] // 4
    return on_chip(
        functools.partial(layer_output_kernel, count),
        [like(f32, 2, rows, width), like(bf16, 2, rows, width)],
        [at, hidden, weight],
        0,
        scratch=[pltpu.VMEM((4 * rows, width), f32)],
        name="layer_output",
    )


def query_rows_kernel(
    at_ref, terms_ref, gain_ref, query_ref, key_ref, value_ref, d_query, d_key, d_value, d_gain
):
    half = HEAD_SIZE // 2
    pieces = ([], [], [])
    for head in range(terms_ref.shape[0] // 2):
        part = terms_ref[2 * head].astype(f32) + terms_ref[2 * head + 1].astype(f32)
        pieces[0].append(part[:, :HEAD_SIZE])
        pieces[1].append(part[:, HEAD_SIZE : HEAD_SIZE + half])
        pieces[2].append(part[:, HEAD_SIZE + half :])
    gain = gain_ref[...]
    rows_sum = None
    outs = (d_query, d_key, d_value)
    for pieces_of, weight_ref, out_ref in zip(pieces, (query_ref, key_ref, value_ref), outs):
        grad = jnp.concatenate(pieces_of, axis=1)
        out_ref[...] = gain * grad
        part = jnp.sum(grad * weight_ref[...].astype(f32), axis=1, keepdims=True)
        rows_sum = part if rows_sum is None else rows_sum + part
    d_gain[...] = rows_sum


def query_rows_grads(at, terms, gain, query, key, value):
    own = query.shape[0]
    return on_chip(
        query_rows_kernel,
        [
            like(f32, *query.shape),
            like(f32, *key.shape),
            like(f32, *value.shape),
            like(f32, own, 1),
        ],
        [at, terms, gain, query, key, value],
        terms.size,
        name="query_rows_grads",
    )


def pair_rows_kernel(
    size, count, at_ref, terms_ref, gain_ref, gate_ref, up_ref, d_gate, d_up, d_gain
):
    gain = gain_ref[...]
    core = at_ref[2 * count]
    seq = at_ref[2 * count + 1]
    half = terms_ref.shape[2] // 2
    rows_sum = jnp.zeros_like(gain)
    for side, (weight_ref, out_ref) in enumerate(((gate_ref, d_gate), (up_ref, d_up))):
        for position in range(half // size):
            for t in range(4):
                columns = slice((4 * position + t) * size, (4 * position + t + 1) * size)
                start = side * half + position * size
                block = (core + t // 2) % 2 * 2 + (seq + t % 2) % 2
                grad = terms_ref[block, :, start : start + size].astype(f32)
                out_ref[:, columns] = gain * grad
                rows_sum = rows_sum + jnp.sum(
                    grad * weight_ref[:, columns].astype(f32), axis=1, keepdims=True
                )
    d_gain[...] = rows_sum


def pair_rows_grads(at, terms, gain, gate, up, size, count):
    own = gate.shape[0]
    return on_chip(
        functools.partial(pair_rows_kernel, size, count),
        [like(f32, *gate.shape), like(f32, *up.shape), like(f32, own, 1)],
        [at, terms, gain, gate, up],
        terms.size,
        name="pair_rows_grads",
    )


def ring_of(count):
    order = list(range(0, count, 2)) + list(range(count - 1, 0, -2))
    forward = [(order[i], order[(i + 1) % count]) for i in range(count)]
    backward = [(there, here) for here, there in forward]
    return forward, backward


def place_of(position, count):
    return jnp.where(position % 2 == 0, position // 2, count - (position + 1) // 2)


def position_at(place, count):
    place = lax.rem(place, count)
    return jnp.where(place < count // 2, 2 * place, 2 * (count - place) - 1)


def tie(*values):
    return lax.optimization_barrier(values)


def after(value, *others):
    return lax.optimization_barrier((value,) + others)[0]


class GatherRing:
    def __init__(self, shard, count):
        self.count = count
        self.forward, self.backward = ring_of(count)
        self.parts = [shard] + [None] * (count - 1)
        self.ahead = self.behind = shard
        self.hops = 0

    def start(self, *others):
        self.hops += 1
        ahead, behind = self.ahead, self.behind
        if self.hops == self.count // 2:
            half = ahead.shape[0] // 2
            ahead, behind = ahead[:half], behind[half:]
        if others:
            ahead, behind = lax.optimization_barrier((ahead, behind) + others)[:2]
        self.ahead = lax.ppermute(ahead, "d", self.forward)
        self.behind = lax.ppermute(behind, "d", self.backward)

    def settle(self, *others):
        out = lax.optimization_barrier((self.ahead, self.behind) + others)
        self.ahead, self.behind = out[:2]
        if self.hops == self.count // 2:
            self.parts[self.hops] = jnp.concatenate(out[:2], axis=0)
        else:
            self.parts[self.count - self.hops] = self.ahead
            self.parts[self.hops] = self.behind
        return out[2] if len(others) == 1 else out[2:]


class ScatterRing:
    def __init__(self, terms, count):
        self.count = count
        self.terms = terms
        self.forward, self.backward = ring_of(count)
        self.ahead = [self.part(t, count - 1, 0) for t in terms]
        self.behind = [self.part(t, 1, 1) for t in terms]
        self.hops = 0

    def part(self, term, at, side):
        half = term.shape[1] // 2
        return term[at % self.count, side * half : (side + 1) * half]

    def start(self, *others):
        self.hops += 1
        ahead, behind = self.ahead, self.behind
        if others:
            ahead, behind = lax.optimization_barrier((ahead, behind) + others)[:2]
        self.ahead = [lax.ppermute(a, "d", self.forward) for a in ahead]
        self.behind = [lax.ppermute(b, "d", self.backward) for b in behind]

    def settle(self, *others):
        out = lax.optimization_barrier((self.ahead, self.behind) + others)
        ahead, behind = out[:2]
        kind = f32 if self.hops == self.count - 1 else bf16
        place = self.count - 1 - self.hops
        self.ahead = [
            (a.astype(f32) + self.part(t, place, 0).astype(f32)).astype(kind)
            for a, t in zip(ahead, self.terms)
        ]
        self.behind = [
            (b.astype(f32) + self.part(t, 1 + self.hops, 1).astype(f32)).astype(kind)
            for b, t in zip(behind, self.terms)
        ]
        return out[2] if len(others) == 1 else out[2:]

    def sums(self):
        return [jnp.concatenate([a, b], axis=0) for a, b in zip(self.ahead, self.behind)]


def swap(values, axis):
    return lax.ppermute(values, axis, [(0, 1), (1, 0)])


def rows_of_group(own):
    pair = lax.all_gather(own, "y", axis=0)
    return lax.all_gather(pair, "core", axis=1)


def core_sum(kept, away):
    return kept + swap(away, "core").astype(f32)


def both_rows_sum(pair):
    return pair + swap(pair.astype(bf16), "y").astype(f32)


def own_rows_sum(pair):
    seq = lax.axis_index("y")
    away = lax.dynamic_index_in_dim(pair, 1 - seq, 0, False).astype(bf16)
    return lax.dynamic_index_in_dim(pair, seq, 0, False) + swap(away, "y").astype(f32)


def own_columns(blocks):
    core = lax.axis_index("core")
    seq = lax.axis_index("y")
    away = lax.dynamic_index_in_dim(blocks, 1 - seq, 1, False)
    kept = lax.dynamic_index_in_dim(blocks, seq, 1, False)
    pair = jnp.stack([kept, swap(away, "y")])
    away = lax.dynamic_index_in_dim(pair, 1 - core, 1, False)
    kept = lax.dynamic_index_in_dim(pair, core, 1, False)
    return jnp.concatenate([kept, swap(away, "core")])


def both_rows(own, *others):
    other = after(swap(own, "y"), *others)
    first = lax.axis_index("y") == 0
    return jnp.stack([jnp.where(first, own, other), jnp.where(first, other, own)])


def all_to_all(values, axes):
    return lax.all_to_all(values, axes, 0, 0, tiled=True)


def inverse_rms(values):
    return lax.rsqrt(jnp.mean(values * values, axis=-1, keepdims=True) + norm_eps)


def head_layer(
    count,
    tokens,
    cotangent,
    norm_gain1,
    w_query,
    key_weight,
    value_weight,
    w_out,
    norm_gain2,
    w_gate,
    w_up,
    w_down,
):
    rows, width = tokens.shape[1:]
    own = w_query.shape[0]
    ff_own = w_down.shape[0]
    half = HEAD_SIZE // 2
    quarter = HEAD_SIZE // 4
    group = 4 * own
    seq_rows = 2 * rows
    length = count * seq_rows
    step = seq_rows

    gain1 = norm_gain1.astype(f32)[:, None]
    gain2 = norm_gain2.astype(f32)[:, None]

    place = place_of(lax.axis_index("d"), count)
    steps = jnp.arange(count, dtype=jnp.int32)
    core = lax.axis_index("core")
    seq = lax.axis_index("y")
    at = jnp.concatenate(
        [
            position_at(place + steps, count),
            lax.rem(place_of(steps, count) - place + count, count),
            jnp.stack([core, seq]).astype(jnp.int32),
        ]
    )

    position = jnp.arange(length, dtype=f32)
    exponent = jnp.arange(half, dtype=f32) * (2.0 / HEAD_SIZE)
    angle = (rope_base ** (-exponent))[:, None] * position[None, :]
    cosine = jnp.cos(angle)
    sine = jnp.sin(angle)

    own_rows = tokens[0].astype(f32)
    n1_ring = GatherRing((own_rows * inverse_rms(own_rows)).astype(bf16), count)
    n1_ring.start()
    out_ring = GatherRing(w_out, count)
    out_ring.start()
    head_cols = head_columns(at, gain1, w_query, key_weight, value_weight)
    head_weight = all_to_all(head_cols, ("d", "core", "y")).reshape(width, 2 * HEAD_SIZE)
    out_ring.settle()
    head_cols = n1_ring.settle(head_cols)
    n1_ring.start()
    out_ring.start()
    tokens_pair = both_rows(tokens[0], head_cols)
    pair_cols = pair_columns(at, gain2, w_gate, w_up, ff_own)
    out_ring.settle()
    head_weight, tokens_pair, pair_cols = n1_ring.settle(head_weight, tokens_pair, pair_cols)
    n1_ring.start()
    out_ring.start()
    pair_rows = all_to_all(pair_cols, ("core", "y")).reshape(group, 2 * count * ff_own)
    out_ring.settle()
    n1_ring.settle()
    n1_ring.start()
    out_ring.start()
    out_ring.settle()
    pair_rows = n1_ring.settle(pair_rows)
    n1_blocks = n1_ring.parts + [swap(part, "core") for part in n1_ring.parts]

    pair_ring = GatherRing(pair_rows, count)
    pair_ring.start(n1_blocks[count // 2])
    down_ring = GatherRing(w_down, count)
    down_ring.start(n1_blocks[count // 2])
    q, kv_own = project_heads(at, head_weight, cosine, sine, n1_blocks)
    kv_other = swap(kv_own, "core")
    cotangent_pair = both_rows(after(cotangent[0], pair_rows), kv_own)
    cotangent_other = swap(cotangent_pair, "core")
    mixed_send, mixed, prob, k, v = heads_forward(at, q, kv_own, kv_other, cosine, sine, count)
    mixed_send = pair_ring.settle(mixed_send)
    down_ring.settle()
    pair_ring.start()
    down_ring.start()
    mixed_low = all_to_all(mixed_send, ("d", "y"))
    mixed_low, cotangent_other = pair_ring.settle(mixed_low, cotangent_other)
    down_ring.settle()
    pair_ring.start()
    down_ring.start()
    out_weight, mixed_low, kept, away = project_out(at, mixed_low, out_ring.parts, 0)
    branch = core_sum(kept, away)
    branch = both_rows_sum(branch)
    down_ring.settle()
    branch = pair_ring.settle(branch)
    pair_ring.start()
    down_ring.start()
    inputs = tokens_pair.astype(f32)
    middle = inputs + branch

    r2 = inverse_rms(middle)
    n2_pair = middle * r2
    n2_own = n2_pair.astype(bf16)
    n2_other = swap(n2_own, "core")
    down_ring.settle()
    d_out, down_weight, d_hidden = hidden_gradient(
        at, cotangent_pair, cotangent_other, down_ring.parts, ff_own
    )
    n2_own, n2_other, d_hidden = pair_ring.settle(n2_own, n2_other, d_hidden)
    qkv_cols = query_columns(at, gain1, w_query, key_weight, value_weight)
    qkv_rows = all_to_all(after(qkv_cols, pair_rows), ("core", "y"))
    qkv_rows = qkv_rows.reshape(group, count * HEAD_SIZE)
    n2_own, qkv_rows = tie(n2_own, qkv_rows)
    qkv_ring = GatherRing(qkv_rows, count)
    qkv_ring.start()
    n2, hidden, d_both, kept, away = feed_forward(at, n2_own, n2_other, d_hidden, pair_ring.parts)
    d_n2 = qkv_ring.settle(core_sum(kept, away))
    qkv_ring.start()
    grad_both, grad_down = feed_forward_grads(
        at, n2, d_both, after(hidden, d_n2), d_out, count
    )
    d_normed2 = both_rows_sum(d_n2)
    grad_down = qkv_ring.settle(grad_down)
    qkv_ring.start()
    ff_ring = ScatterRing([grad_both, grad_down], count)
    qkv_ring.settle()
    qkv_ring.start()
    ff_ring.start()
    qkv_ring.settle()
    d_normed2 = ff_ring.settle(d_normed2)
    ff_ring.start()
    d_middle = cotangent_pair.astype(f32) + r2 * (
        d_normed2 - n2_pair * jnp.mean(d_normed2 * n2_pair, axis=-1, keepdims=True)
    )

    d_mid_own = d_middle.astype(bf16)
    d_mid_other = swap(d_mid_own, "core")
    d_mid, d_mixed = split_heads(at, d_mid_own, d_mid_other, out_weight, count)
    d_mixed = all_to_all(d_mixed, ("d", "y"))
    d_mixed = ff_ring.settle(d_mixed)
    ff_ring.start()
    grad_out = dot_at(after(mixed_low, d_mixed), d_mid, 1, 0).astype(bf16)
    owned_out = all_to_all(grad_out.reshape(count, own, width), "d")
    d_q, kept, away = heads_backward(at, q, k, v, prob, mixed, d_mixed, cosine, sine, count)
    d_qkv, joined = heads_send(at, d_q, kept, swap(away, "core"), count)
    d_qkv, owned_out = ff_ring.settle(d_qkv, owned_out)
    ff_ring.start()
    d_qkv = all_to_all(d_qkv, ("d", "y"))
    grad_heads = heads_grad(at, joined, n1_blocks)
    grad_heads = ff_ring.settle(grad_heads)
    ff_ring.start()
    grad_heads, d_qkv = ff_ring.settle(grad_heads, d_qkv)
    ff_ring.start()
    grad_heads = all_to_all(grad_heads.reshape(4 * count, own, 2 * HEAD_SIZE), ("d", "core", "y"))
    kept, away = heads_input(at, d_qkv, qkv_ring.parts)
    d_normed1 = own_rows_sum(core_sum(kept, away))
    ff_ring.settle()
    ff_ring.start()
    ff_ring.settle()
    owned_both, owned_down = ff_ring.sums()
    own_both = own_columns(owned_both.astype(bf16).reshape(2, 2, own, -1))
    kept, away = layer_output(at, hidden, down_weight, count)
    d_middle_own, middle_own = (
        lax.dynamic_index_in_dim(value, seq, 0, False) for value in (d_middle, middle)
    )
    r1 = inverse_rms(own_rows)
    n1_wide = own_rows * r1
    input_grad = d_middle_own + r1 * (
        d_normed1 - n1_wide * jnp.mean(d_normed1 * n1_wide, axis=-1, keepdims=True)
    )
    result = middle_own + own_rows_sum(core_sum(kept, away))
    grad_heads, own_both = tie(grad_heads, own_both)
    owned_out = jnp.sum(owned_out.astype(f32), axis=0)
    grad_gate, grad_up, grad_gain2 = pair_rows_grads(
        at, own_both, gain2, w_gate, w_up, ff_own, count
    )
    grad_query, grad_key, grad_value, grad_gain1 = query_rows_grads(
        at, grad_heads, gain1, w_query, key_weight, value_weight
    )
    return (
        result.astype(bf16)[None],
        input_grad[None],
        grad_gain1[:, 0],
        grad_query,
        grad_key,
        grad_value,
        owned_out,
        grad_gain2[:, 0],
        grad_gate,
        grad_up,
        owned_down,
    )


def by_heads(mesh):
    count = mesh.shape["ctx"] // 2
    parts = Mesh(mesh.devices.reshape(count, 2, 2), ("d", "core", "y"))
    owner = ("d", "core", "y")
    row_spec = P("y", ("d", "core"), None)
    in_specs = (row_spec, row_spec) + (P(owner),) * 9
    out_specs = (row_spec, row_spec) + (P(owner),) * 9
    return jax.shard_map(
        functools.partial(head_layer, count),
        mesh=parts,
        in_specs=in_specs,
        out_specs=out_specs,
        check_vma=False,
    )


def solution(mesh):
    in_specs = (
        P("fsdp", "ctx", None),
        P("fsdp", "ctx", None),
        P(("ctx", "fsdp")),
        P(("ctx", "fsdp"), None),
        P(("ctx", "fsdp"), None),
        P(("ctx", "fsdp"), None),
        P(("ctx", "fsdp"), None),
        P(("ctx", "fsdp")),
        P(("ctx", "fsdp"), None),
        P(("ctx", "fsdp"), None),
        P(("ctx", "fsdp"), None),
    )
    out_specs = (
        P("fsdp", "ctx", None),
        P("fsdp", "ctx", None),
        P(("ctx", "fsdp")),
        P(("ctx", "fsdp"), None),
        P(("ctx", "fsdp"), None),
        P(("ctx", "fsdp"), None),
        P(("ctx", "fsdp"), None),
        P(("ctx", "fsdp")),
        P(("ctx", "fsdp"), None),
        P(("ctx", "fsdp"), None),
        P(("ctx", "fsdp"), None),
    )
    if mesh.shape["ctx"] == QUERY_HEADS and mesh.shape["fsdp"] == 2:
        return by_heads(mesh)
    return jax.shard_map(local, mesh=mesh, in_specs=in_specs, out_specs=out_specs, check_vma=False)
```

```python
import functools

import jax
import jax.numpy as jnp
import numpy as np
from jax import lax
from jax.experimental import pallas as pl
from jax.experimental.pallas import tpu as pltpu
from jax.sharding import Mesh
from jax.sharding import PartitionSpec as P

QUERY_HEADS = 16
KEY_VALUE_HEADS = 8
HEAD_SIZE = 96


rope_base = 100000.0
norm_eps = 1e-05
masked_value = -1e30
key_block = 512


def rms_norm(value_rows, gain):
    return (
        value_rows
        * lax.rsqrt(jnp.mean(value_rows * value_rows, axis=-1, keepdims=True) + norm_eps)
        * gain
    )


def apply_rotary(value_rows, token_position):
    half = value_rows.shape[-1] // 2
    exponent = jnp.arange(half, dtype=jnp.float32) * (2.0 / value_rows.shape[-1])
    freq = rope_base ** (-exponent)
    angle = token_position[:, None] * freq[None, :]
    cosine = jnp.cos(angle)[:, None, :]
    sine = jnp.sin(angle)[:, None, :]
    first = value_rows[..., :half]
    second = value_rows[..., half:]
    return jnp.concatenate(
        [first * cosine - second * sine, second * cosine + first * sine], axis=-1
    )


def matmul(left, right):
    return jnp.dot(left, right, preferred_element_type=jnp.float32)


def key_pieces(key_rows, value_rows, key_value_heads, head_dim):
    count = key_rows.shape[0]
    number = count // key_block
    key_sets = key_rows.reshape(number, key_block, key_value_heads, head_dim)
    value_sets = value_rows.reshape(number, key_block, key_value_heads, head_dim)
    starts = jnp.arange(number, dtype=jnp.int32) * key_block
    return (key_sets, value_sets, starts, key_block)


def fold_keys(carry, key_rows, value_rows, query_rows, query_pos):
    key_value_heads = query_rows.shape[1]
    head_dim = query_rows.shape[3]
    scale = head_dim ** (-0.5)
    key_sets, value_sets, starts, size = key_pieces(key_rows, value_rows, key_value_heads, head_dim)

    def fold_one_piece(state, item):
        key_set, value_set, begin = item

        def fold_live(state):
            top, total, summed = state
            scores = (
                jnp.einsum(
                    "tkgd,skd->kgts", query_rows, key_set, preferred_element_type=jnp.float32
                )
                * scale
            )
            visible = (begin + jnp.arange(size, dtype=jnp.int32))[None, :] <= query_pos[:, None]
            scores = jnp.where(visible, scores, masked_value)
            new_top = jnp.maximum(top, jnp.max(scores, axis=-1))
            weights = jnp.where(visible, jnp.exp(scores - new_top[..., None]), 0.0)
            factor = jnp.exp(top - new_top)
            total = total * factor + jnp.sum(weights, axis=-1)
            summed = summed * factor[..., None] + jnp.einsum(
                "kgts,skd->kgtd",
                weights.astype(jnp.bfloat16),
                value_set,
                preferred_element_type=jnp.float32,
            )
            return (new_top, total, summed)

        def fold_skipped(state):
            return state

        return (lax.cond(begin <= query_pos[-1], fold_live, fold_skipped, state), None)

    carry, _ = lax.scan(fold_one_piece, carry, (key_sets, value_sets, starts))
    return carry


def back_keys(key_rows, value_rows, query_rows, query_pos, d_heads, log_total, delta):
    rows, key_value_heads, groups, head_dim = query_rows.shape
    scale = head_dim ** (-0.5)
    key_sets, value_sets, starts, size = key_pieces(key_rows, value_rows, key_value_heads, head_dim)

    def back_one_piece(d_query, item):
        key_set, value_set, begin = item

        def back_live(d_query):
            scores = (
                jnp.einsum(
                    "tkgd,skd->kgts", query_rows, key_set, preferred_element_type=jnp.float32
                )
                * scale
            )
            visible = (begin + jnp.arange(size, dtype=jnp.int32))[None, :] <= query_pos[:, None]
            prob = jnp.where(visible, jnp.exp(scores - log_total[..., None]), 0.0)
            d_prob = jnp.einsum(
                "tkgd,skd->kgts", d_heads, value_set, preferred_element_type=jnp.float32
            )
            d_scores = (prob * (d_prob - delta[..., None])).astype(jnp.bfloat16)
            d_query = d_query + scale * jnp.einsum(
                "kgts,skd->tkgd", d_scores, key_set, preferred_element_type=jnp.float32
            )
            d_key = scale * jnp.einsum(
                "kgts,tkgd->skd", d_scores, query_rows, preferred_element_type=jnp.float32
            )
            d_value = jnp.einsum(
                "kgts,tkgd->skd",
                prob.astype(jnp.bfloat16),
                d_heads,
                preferred_element_type=jnp.float32,
            )
            return (
                d_query,
                (
                    d_key.reshape(size, key_value_heads * head_dim),
                    d_value.reshape(size, key_value_heads * head_dim),
                ),
            )

        def back_skipped(d_query):
            empty = jnp.zeros((size, key_value_heads * head_dim), jnp.float32)
            return (d_query, (empty, empty))

        return lax.cond(begin <= query_pos[-1], back_live, back_skipped, d_query)

    start_grad = jnp.zeros((rows, key_value_heads, groups, head_dim), jnp.float32)
    d_query, (d_keys, d_values) = lax.scan(
        back_one_piece, start_grad, (key_sets, value_sets, starts)
    )
    return (
        d_query,
        d_keys.reshape(key_rows.shape[0], key_value_heads * head_dim),
        d_values.reshape(key_rows.shape[0], key_value_heads * head_dim),
    )


def local(
    tokens,
    cotangent,
    norm_gain1,
    w_query,
    key_weight,
    value_weight,
    w_out,
    norm_gain2,
    w_gate,
    w_up,
    w_down,
):
    rows = tokens.shape[1]
    key_value_heads = KEY_VALUE_HEADS
    heads = QUERY_HEADS
    head_dim = HEAD_SIZE
    groups = heads // key_value_heads
    first_row = lax.axis_index("ctx") * rows
    query_pos = first_row + jnp.arange(rows, dtype=jnp.int32)
    token_position = query_pos.astype(jnp.float32)
    inputs = tokens[0].astype(jnp.float32)
    gathered = (
        lax.all_gather(norm_gain1, ("ctx", "fsdp"), axis=0, tiled=True),
        lax.all_gather(w_query, ("ctx", "fsdp"), axis=0, tiled=True),
        lax.all_gather(key_weight, ("ctx", "fsdp"), axis=0, tiled=True),
        lax.all_gather(value_weight, ("ctx", "fsdp"), axis=0, tiled=True),
        lax.all_gather(w_out, ("ctx", "fsdp"), axis=0, tiled=True),
        lax.all_gather(norm_gain2, ("ctx", "fsdp"), axis=0, tiled=True),
        lax.all_gather(w_gate, ("ctx", "fsdp"), axis=0, tiled=True),
        lax.all_gather(w_up, ("ctx", "fsdp"), axis=0, tiled=True),
        lax.all_gather(w_down, ("ctx", "fsdp"), axis=0, tiled=True),
    )
    gain_one = gathered[0].astype(jnp.float32)
    gain_two = gathered[5].astype(jnp.float32)
    normed1 = rms_norm(inputs, gain_one).astype(jnp.bfloat16)
    query_pre = matmul(normed1, gathered[1]).reshape(rows, heads, head_dim)
    key_pre = matmul(normed1, gathered[2]).reshape(rows, key_value_heads, head_dim)
    value = matmul(normed1, gathered[3]).astype(jnp.bfloat16)
    query_rows = (
        apply_rotary(query_pre, token_position)
        .astype(jnp.bfloat16)
        .reshape(rows, key_value_heads, groups, head_dim)
    )
    key_rows = (
        apply_rotary(key_pre, token_position)
        .reshape(rows, key_value_heads * head_dim)
        .astype(jnp.bfloat16)
    )
    start_state = (
        jnp.full((key_value_heads, groups, rows), masked_value, jnp.float32),
        jnp.zeros((key_value_heads, groups, rows), jnp.float32),
        jnp.zeros((key_value_heads, groups, rows, head_dim), jnp.float32),
    )
    top, total, summed = fold_keys(
        start_state,
        lax.all_gather(key_rows, "ctx", axis=0, tiled=True),
        lax.all_gather(value, "ctx", axis=0, tiled=True),
        query_rows,
        query_pos,
    )
    mixed_heads = jnp.transpose(summed / total[..., None], (2, 0, 1, 3))
    log_total = top + jnp.log(total)
    mixed_low = mixed_heads.reshape(rows, heads * head_dim).astype(jnp.bfloat16)
    middle = inputs + matmul(mixed_low, gathered[4])
    normed2 = rms_norm(middle, gain_two).astype(jnp.bfloat16)
    gate = matmul(normed2, gathered[6])
    upper = matmul(normed2, gathered[7])
    hidden = (jax.nn.silu(gate) * upper).astype(jnp.bfloat16)
    result = middle + matmul(hidden, gathered[8])
    gathered = (
        lax.all_gather(norm_gain1, ("ctx", "fsdp"), axis=0, tiled=True),
        lax.all_gather(w_query, ("ctx", "fsdp"), axis=0, tiled=True),
        lax.all_gather(key_weight, ("ctx", "fsdp"), axis=0, tiled=True),
        lax.all_gather(value_weight, ("ctx", "fsdp"), axis=0, tiled=True),
        lax.all_gather(w_out, ("ctx", "fsdp"), axis=0, tiled=True),
        lax.all_gather(norm_gain2, ("ctx", "fsdp"), axis=0, tiled=True),
        lax.all_gather(w_gate, ("ctx", "fsdp"), axis=0, tiled=True),
        lax.all_gather(w_up, ("ctx", "fsdp"), axis=0, tiled=True),
        lax.all_gather(w_down, ("ctx", "fsdp"), axis=0, tiled=True),
    )
    incoming = cotangent[0].astype(jnp.float32)
    incoming_low = incoming.astype(jnp.bfloat16)
    grad_down = matmul(hidden.T, incoming_low)
    d_hidden = matmul(incoming_low, gathered[8].T)
    _, swiglu_back = jax.vjp(lambda gate_in, upper_in: jax.nn.silu(gate_in) * upper_in, gate, upper)
    d_gate, d_upper = swiglu_back(d_hidden)
    d_gate = d_gate.astype(jnp.bfloat16)
    d_upper = d_upper.astype(jnp.bfloat16)
    grad_gate = matmul(normed2.T, d_gate)
    grad_up = matmul(normed2.T, d_upper)
    d_normed2 = matmul(d_gate, gathered[6].T) + matmul(d_upper, gathered[7].T)
    _, norm_back2 = jax.vjp(rms_norm, middle, gain_two)
    d_middle, grad_gain2 = norm_back2(d_normed2)
    d_middle = d_middle + incoming
    owned_gain2, owned_gate, owned_up, owned_down = (
        lax.psum_scatter(grad_gain2, ("ctx", "fsdp"), scatter_dimension=0, tiled=True),
        lax.psum_scatter(grad_gate, ("ctx", "fsdp"), scatter_dimension=0, tiled=True),
        lax.psum_scatter(grad_up, ("ctx", "fsdp"), scatter_dimension=0, tiled=True),
        lax.psum_scatter(grad_down, ("ctx", "fsdp"), scatter_dimension=0, tiled=True),
    )
    d_middle_low = d_middle.astype(jnp.bfloat16)
    grad_out = matmul(mixed_low.T, d_middle_low)
    d_mixed = matmul(d_middle_low, gathered[4].T).astype(jnp.bfloat16)
    d_heads = d_mixed.reshape(rows, key_value_heads, groups, head_dim)
    delta = jnp.transpose(jnp.sum(d_heads.astype(jnp.float32) * mixed_heads, axis=-1), (1, 2, 0))
    back_keys_all, back_values_all = (
        lax.all_gather(key_rows, "ctx", axis=0, tiled=True),
        lax.all_gather(value, "ctx", axis=0, tiled=True),
    )
    d_query_rot, d_keys_all, d_values_all = back_keys(
        back_keys_all, back_values_all, query_rows, query_pos, d_heads, log_total, delta
    )
    d_keys_rot, d_value = (
        lax.psum_scatter(d_keys_all, "ctx", scatter_dimension=0, tiled=True),
        lax.psum_scatter(d_values_all, "ctx", scatter_dimension=0, tiled=True),
    )
    _, rotate_back_query = jax.vjp(
        lambda values_in: apply_rotary(values_in, token_position), query_pre
    )
    _, rotate_back_key = jax.vjp(lambda values_in: apply_rotary(values_in, token_position), key_pre)
    d_query = (
        rotate_back_query(d_query_rot.reshape(rows, heads, head_dim))[0]
        .reshape(rows, heads * head_dim)
        .astype(jnp.bfloat16)
    )
    d_key = (
        rotate_back_key(d_keys_rot.reshape(rows, key_value_heads, head_dim))[0]
        .reshape(rows, key_value_heads * head_dim)
        .astype(jnp.bfloat16)
    )
    d_value = d_value.astype(jnp.bfloat16)
    grad_query = matmul(normed1.T, d_query)
    grad_key = matmul(normed1.T, d_key)
    grad_value = matmul(normed1.T, d_value)
    d_normed1 = (
        matmul(d_query, gathered[1].T)
        + matmul(d_key, gathered[2].T)
        + matmul(d_value, gathered[3].T)
    )
    _, norm_back1 = jax.vjp(rms_norm, inputs, gain_one)
    d_inputs, grad_gain1 = norm_back1(d_normed1)
    input_grad = d_inputs + d_middle
    owned_gain1, owned_query, owned_key, owned_value, owned_out = (
        lax.psum_scatter(grad_gain1, ("ctx", "fsdp"), scatter_dimension=0, tiled=True),
        lax.psum_scatter(grad_query, ("ctx", "fsdp"), scatter_dimension=0, tiled=True),
        lax.psum_scatter(grad_key, ("ctx", "fsdp"), scatter_dimension=0, tiled=True),
        lax.psum_scatter(grad_value, ("ctx", "fsdp"), scatter_dimension=0, tiled=True),
        lax.psum_scatter(grad_out, ("ctx", "fsdp"), scatter_dimension=0, tiled=True),
    )
    return (
        result.astype(jnp.bfloat16)[None],
        input_grad[None],
        owned_gain1,
        owned_query,
        owned_key,
        owned_value,
        owned_out,
        owned_gain2,
        owned_gate,
        owned_up,
        owned_down,
    )


bf16 = jnp.bfloat16
f32 = jnp.float32
score_scale = HEAD_SIZE ** (-0.5)
log2_e = 1.4426950408889634
ln_2 = 0.6931471805599453


def dot_at(left, right, left_dim, right_dim):
    return lax.dot_general(
        left, right, (((left_dim,), (right_dim,)), ((), ())), preferred_element_type=jnp.float32
    )


def rotate(values, cosine, sine):
    half = values.shape[0] // 2
    first, second = values[:half], values[half:]
    return jnp.concatenate([first * cosine - second * sine, second * cosine + first * sine], axis=0)


def rotate_back(values, cosine, sine):
    half = values.shape[0] // 2
    first, second = values[:half], values[half:]
    return jnp.concatenate([first * cosine + second * sine, second * cosine - first * sine], axis=0)


def heads_forward_kernel(
    count, at_ref, kept_ref, other_ref, cos_ref, sin_ref,
    send_ref, mixed_ref, prob_ref, q_ref, k_ref, v_ref,
):
    size = q_ref.shape[0]
    half = size // 2
    rows = kept_ref[...] + other_ref[...].astype(f32)
    q = rotate(rows[:size], cos_ref[...], sin_ref[...])
    q_ref[...] = (q * (score_scale * log2_e)).astype(bf16)
    k_ref[...] = rotate(rows[size : 2 * size], cos_ref[...], sin_ref[...]).astype(bf16)
    v_ref[...] = rows[2 * size :].astype(bf16)
    step = send_ref.shape[2]
    offset = 0
    for block in range(count):
        begin = block * step
        end = begin + step
        scores = dot_at(k_ref[:, 0:end], q_ref[:, begin:end], 0, 0)
        key = lax.broadcasted_iota(jnp.int32, (step, step), 0)
        query = lax.broadcasted_iota(jnp.int32, (step, step), 1)
        last = jnp.where(key <= query, scores[begin:end], masked_value)
        top = jnp.max(last, axis=0, keepdims=True)
        if begin:
            top = jnp.maximum(top, jnp.max(scores[:begin], axis=0, keepdims=True))
        last = jnp.exp2(last - top)
        total = jnp.sum(last, axis=0, keepdims=True)
        if begin:
            first = jnp.exp2(scores[:begin] - top)
            total = total + jnp.sum(first, axis=0, keepdims=True)
        inverse = 1.0 / total
        prob_ref[offset + begin : offset + end, :] = (last * inverse).astype(bf16)
        if begin:
            prob_ref[offset : offset + begin, :] = (first * inverse).astype(bf16)
        mixed = dot_at(v_ref[:, 0:end], prob_ref[offset : offset + end, :], 1, 0)
        mixed_ref[:, begin:end] = mixed
        send_ref[2 * block] = mixed[:half].astype(bf16)
        send_ref[2 * block + 1] = mixed[half:].astype(bf16)
        offset += end


def heads_forward(at, kept, other, cosine, sine, count):
    tokens = kept.shape[1]
    size = kept.shape[0] // 3
    step = tokens // count
    pairs = step * count * (count + 1) // 2
    return on_chip(
        functools.partial(heads_forward_kernel, count),
        [
            like(bf16, 2 * count, size // 2, step),
            like(f32, size, tokens),
            like(bf16, pairs, step),
            like(bf16, size, tokens),
            like(bf16, size, tokens),
            like(bf16, size, tokens),
        ],
        [at, kept, other, cosine, sine],
        4 * size * pairs * step,
        name="heads_forward",
        room=32,
    )


def heads_backward_kernel(
    count, at_ref, q_ref, k_ref, v_ref, prob_ref, mixed_ref, back_ref, cos_ref, sin_ref,
    kept_ref, away_ref,
):
    half, step = back_ref.shape[1:]
    size = 2 * half
    d_k_ref = kept_ref.at[size : 2 * size]
    d_v_ref = kept_ref.at[2 * size :]
    offset = 0
    for block in range(count):
        begin = block * step
        end = begin + step
        d_mixed = jnp.concatenate([back_ref[2 * block], back_ref[2 * block + 1]], axis=0)
        delta = jnp.sum(d_mixed.astype(f32) * mixed_ref[:, begin:end], axis=0, keepdims=True)
        prob = prob_ref[offset : offset + end, :]
        d_prob = dot_at(v_ref[:, 0:end], d_mixed, 0, 0)
        d_scores = (prob.astype(f32) * (d_prob - delta)).astype(bf16)
        d_q = dot_at(k_ref[:, 0:end], d_scores, 1, 0) * score_scale
        kept_ref[:size, begin:end] = rotate_back(d_q, cos_ref[:, begin:end], sin_ref[:, begin:end])
        d_v = dot_at(d_mixed, prob, 1, 1)
        d_k = dot_at(q_ref[:, begin:end], d_scores, 1, 1) * ln_2
        if begin:
            d_v_ref[:, 0:begin] += d_v[:, 0:begin]
            d_k_ref[:, 0:begin] += d_k[:, 0:begin]
        d_v_ref[:, begin:end] = d_v[:, begin:end]
        d_k_ref[:, begin:end] = d_k[:, begin:end]
        offset += end
    d_k_ref[...] = rotate_back(d_k_ref[...], cos_ref[...], sin_ref[...])
    away_ref[...] = kept_ref[...].astype(bf16)


def heads_backward(at, q, k, v, prob, mixed, d_mixed, cosine, sine, count):
    size, tokens = q.shape
    return on_chip(
        functools.partial(heads_backward_kernel, count),
        [like(f32, 3 * size, tokens), like(bf16, 3 * size, tokens)],
        [at, q, k, v, prob, mixed, d_mixed, cosine, sine],
        8 * size * prob.size,
        name="heads_backward",
        room=32,
    )


def heads_send_kernel(count, at_ref, kept_ref, other_ref, send_ref, joined_ref, d_kv_ref):
    core = at_ref[2 * count]
    size = kept_ref.shape[0] // 3
    half = size // 2
    quarter = half // 2
    step = send_ref.shape[2]
    d_kv_ref[...] = kept_ref[size:, :] + other_ref[size:, :].astype(f32)
    joined_ref[pl.ds(pl.multiple_of(core * size, size), size), :] = kept_ref[:size, :].astype(bf16)
    joined_ref[pl.ds(pl.multiple_of((1 - core) * size, size), size), :] = other_ref[:size, :]
    joined_ref[2 * size :, :] = d_kv_ref[...].astype(bf16)
    for block in range(count):
        columns = slice(block * step, (block + 1) * step)
        for side in range(2):
            start = pl.multiple_of(core * half + side * quarter, quarter)
            send_ref[2 * block + side] = jnp.concatenate(
                [
                    kept_ref[side * half : (side + 1) * half, columns],
                    d_kv_ref[pl.ds(start, quarter), columns],
                    d_kv_ref[pl.ds(start + size, quarter), columns],
                ],
                axis=0,
            ).astype(bf16)


def heads_send(at, kept, other, count):
    size, tokens = kept.shape
    size = size // 3
    return on_chip(
        functools.partial(heads_send_kernel, count),
        [like(bf16, 2 * count, size, tokens // count), like(bf16, 4 * size, tokens)],
        [at, kept, other],
        8 * kept.size,
        scratch=[pltpu.VMEM((2 * size, tokens), f32)],
        name="heads_send",
    )


def on_chip(kernel, out_shape, args, flops, blocks=(), scratch=(), name=None, room=24):
    moved = sum(a.size * a.dtype.itemsize for a in list(args) + list(blocks))
    moved += sum(o.size * o.dtype.itemsize for o in out_shape)
    near = pl.BlockSpec(memory_space=pltpu.VMEM)
    return pl.pallas_call(
        kernel,
        out_shape=tuple(out_shape),
        in_specs=[pl.BlockSpec(memory_space=pltpu.SMEM)]
        + [near] * (len(args) - 1)
        + [pl.BlockSpec(memory_space=pltpu.HBM)] * len(blocks),
        out_specs=(near,) * len(out_shape),
        scratch_shapes=scratch,
        compiler_params=pltpu.CompilerParams(vmem_limit_bytes=room * 2**20),
        cost_estimate=pl.CostEstimate(flops=flops, bytes_accessed=moved, transcendentals=0),
        name=name,
    )(*args, *blocks)


def like(dtype, *shape):
    return jax.ShapeDtypeStruct(shape, dtype)


def block_copies(at_ref, block_refs, whole_ref, sem_ref, first=0):
    size = whole_ref.shape[0] // len(block_refs)
    copies = []
    for k, block_ref in enumerate(block_refs):
        start = pl.multiple_of(at_ref[k] * size, size)
        copies.append(
            pltpu.make_async_copy(
                block_ref.at[pl.ds(first, size), :], whole_ref.at[pl.ds(start, size), :], sem_ref.at[k]
            )
        )
    return copies


def core_rows(at_ref, count, rows, seq, other):
    core = at_ref[2 * count]
    start = seq * 2 * rows + (1 - core if other else core) * rows
    return pl.ds(pl.multiple_of(start, rows), rows)


def join_rows(at_ref, count, own_ref, other_ref, whole_ref):
    rows = own_ref.shape[1]
    for seq in range(2):
        whole_ref[core_rows(at_ref, count, rows, seq, False), :] = own_ref[seq]
        whole_ref[core_rows(at_ref, count, rows, seq, True), :] = other_ref[seq]


def part_rows(at_ref, count, whole_ref, kept_ref, away_ref):
    rows = kept_ref.shape[1]
    for seq in range(2):
        kept_ref[seq] = whole_ref[core_rows(at_ref, count, rows, seq, False), :]
        away_ref[seq] = whole_ref[core_rows(at_ref, count, rows, seq, True), :].astype(bf16)


def query_columns_kernel(at_ref, gain_ref, query_ref, key_ref, value_ref, out_ref):
    gain = gain_ref[...]
    query = query_ref[...].astype(f32) * gain
    key = key_ref[...].astype(f32) * gain
    value = value_ref[...].astype(f32) * gain
    half = HEAD_SIZE // 2
    quarter = HEAD_SIZE // 4
    groups = out_ref.shape[2] // HEAD_SIZE
    for t in range(4):
        pieces = []
        for group in range(groups):
            place = 4 * group + t
            pieces.append(query[:, place * half : (place + 1) * half])
            pieces.append(key[:, place * quarter : (place + 1) * quarter])
            pieces.append(value[:, place * quarter : (place + 1) * quarter])
        out_ref[t] = jnp.concatenate(pieces, axis=1).astype(bf16)


def query_columns(at, gain, query, key, value):
    own, width = query.shape
    (out,) = on_chip(
        query_columns_kernel,
        [like(bf16, 4, own, (width + 2 * key.shape[1]) // 4)],
        [at, gain, query, key, value],
        own * width,
        name="query_columns",
    )
    return out


def pair_columns_kernel(size, at_ref, gain_ref, gate_ref, up_ref, out_ref):
    gain = gain_ref[...]
    half = out_ref.shape[2] // 2
    for t in range(4):
        for position in range(half // size):
            columns = pl.ds((4 * position + t) * size, size)
            for side, ref in enumerate((gate_ref, up_ref)):
                out_ref[t, :, pl.ds(side * half + position * size, size)] = (
                    ref[:, columns].astype(f32) * gain
                ).astype(bf16)


def pair_columns(at, gain, gate, up, size):
    own, ff = gate.shape
    (out,) = on_chip(
        functools.partial(pair_columns_kernel, size),
        [like(bf16, 4, own, ff // 2)],
        [at, gain, gate, up],
        own * ff,
        name="pair_columns",
    )
    return out


def head_columns_kernel(at_ref, gain_ref, query_ref, key_ref, value_ref, out_ref):
    gain = gain_ref[...]
    query = query_ref[...].astype(f32) * gain
    key = key_ref[...].astype(f32) * gain
    value = value_ref[...].astype(f32) * gain
    for group in range(out_ref.shape[0] // 2):
        shared = slice(group * HEAD_SIZE, (group + 1) * HEAD_SIZE)
        columns = jnp.concatenate(
            [
                query[:, 2 * group * HEAD_SIZE : 2 * (group + 1) * HEAD_SIZE],
                key[:, shared],
                value[:, shared],
            ],
            axis=1,
        ).astype(bf16)
        out_ref[2 * group] = columns
        out_ref[2 * group + 1] = columns


def head_columns(at, gain, query, key, value):
    own, width = query.shape
    (out,) = on_chip(
        head_columns_kernel,
        [like(bf16, width // HEAD_SIZE, own, 4 * HEAD_SIZE)],
        [at, gain, query, key, value],
        own * width,
        name="head_columns",
    )
    return out


def normed_halves_kernel(count, at_ref, rows_ref, kept_ref, away_ref):
    core = at_ref[2 * count]
    rows = rows_ref[...].astype(f32)
    mean = jnp.mean(rows * rows, axis=-1, keepdims=True)
    normed = rows * lax.rsqrt(mean + norm_eps)
    size = rows.shape[1] // (2 * count)
    halves = [
        jnp.concatenate(
            [normed[:, (2 * i + c) * size : (2 * i + c + 1) * size] for i in range(count)], axis=1
        )
        for c in range(2)
    ]
    kept_ref[...] = jnp.where(core == 0, halves[0], halves[1]).astype(bf16)
    away_ref[...] = jnp.where(core == 0, halves[1], halves[0]).astype(bf16)


def normed_halves(at, rows, count):
    tokens, width = rows.shape
    return on_chip(
        functools.partial(normed_halves_kernel, count),
        [like(bf16, tokens, width // 2), like(bf16, tokens, width // 2)],
        [at, rows],
        8 * rows.size,
        name="normed_halves",
    )


def sequence_copies(at_ref, block_refs, whole_ref, sem_ref):
    count = len(block_refs)
    core = at_ref[2 * count]
    rows = whole_ref.shape[0] // (2 * count)
    copies = []
    for i, block_ref in enumerate(block_refs):
        for k, side in enumerate((core, 1 - core)):
            start = pl.multiple_of((2 * at_ref[i] + side) * rows, rows)
            copies.append(
                pltpu.make_async_copy(
                    block_ref.at[pl.ds(k * rows, rows), :],
                    whole_ref.at[pl.ds(start, rows), :],
                    sem_ref.at[2 * i + k],
                )
            )
    return copies


def project_heads_kernel(at_ref, weight_ref, *refs):
    blocks, (kept_ref, away_ref, n_ref, out_ref, sem_ref) = refs[:-5], refs[-5:]
    copies = sequence_copies(at_ref, blocks, n_ref, sem_ref)
    for copy in copies:
        copy.start()
    for copy in copies:
        copy.wait()
    core = at_ref[2 * len(blocks)]
    size = kept_ref.shape[0] // 3
    out_ref[...] = dot_at(weight_ref[...], n_ref[...], 0, 1)
    kept_ref[:size, :] = out_ref[pl.ds(pl.multiple_of(core * size, size), size), :]
    kept_ref[size:, :] = out_ref[2 * size :, :]
    there = pl.ds(pl.multiple_of((1 - core) * size, size), size)
    away_ref[:size, :] = out_ref[there, :].astype(bf16)
    away_ref[size:, :] = out_ref[2 * size :, :].astype(bf16)


def project_heads(at, weight, blocks, rows):
    count = len(blocks)
    width, columns = weight.shape
    tokens = 2 * count * rows
    size = columns // 4
    return on_chip(
        project_heads_kernel,
        [like(f32, 3 * size, tokens), like(bf16, 3 * size, tokens)],
        [at, weight],
        2 * columns * tokens * width,
        blocks=blocks,
        scratch=[
            pltpu.VMEM((tokens, width), bf16),
            pltpu.VMEM((columns, tokens), f32),
            pltpu.SemaphoreType.DMA((2 * count,)),
        ],
        name="project_heads",
    )


def join_heads(heads_ref, joined_ref):
    size, rows = heads_ref.shape[1:]
    for seq in range(2):
        for head in range(heads_ref.shape[0] // 2):
            joined_ref[head * size : (head + 1) * size, seq * rows : (seq + 1) * rows] = heads_ref[
                2 * head + seq
            ]


def project_out_kernel(first, at_ref, heads_ref, *refs):
    blocks, (weight_ref, joined_ref, kept_ref, away_ref, out_ref, sem_ref) = refs[:-6], refs[-6:]
    count = len(blocks)
    own = weight_ref.shape[0] // count
    width = weight_ref.shape[1] // 2
    copies = []
    for i, block_ref in enumerate(blocks):
        start = pl.multiple_of(at_ref[i] * own, own)
        for k in range(2):
            copies.append(
                pltpu.make_async_copy(
                    block_ref.at[pl.ds(first + k * own, own), :],
                    weight_ref.at[pl.ds(start, own), pl.ds(k * width, width)],
                    sem_ref.at[2 * i + k],
                )
            )
    for copy in copies:
        copy.start()
    join_heads(heads_ref, joined_ref)
    for copy in copies:
        copy.wait()
    out_ref[...] = dot_at(joined_ref[...], weight_ref[...], 0, 0)
    part_rows(at_ref, count, out_ref, kept_ref, away_ref)


def project_out(at, heads, blocks, first, own):
    count = len(blocks)
    width = 2 * blocks[0].shape[1]
    rows = heads.shape[2] // 2
    return on_chip(
        functools.partial(project_out_kernel, first),
        [
            like(bf16, count * own, width),
            like(bf16, count * own, 4 * rows),
            like(f32, 2, rows, width),
            like(bf16, 2, rows, width),
        ],
        [at, heads],
        8 * rows * width * count * own,
        blocks=blocks,
        scratch=[pltpu.VMEM((4 * rows, width), f32), pltpu.SemaphoreType.DMA((2 * count,))],
        name="project_out",
    )


def down_pieces(rows, width, wide):
    left = wide // 2
    right = width - left
    pieces = [(i * rows // 2, 0, rows // 2, left, 0, i * left) for i in range(2)]
    parts = wide // right
    size = rows // parts
    pieces += [(i * size, left, size, right, rows // 2, i * right) for i in range(parts)]
    return pieces


def pack_down_kernel(at_ref, down_ref, pair_ref, out_ref):
    first = pair_ref.shape[0]
    out_ref[:first, :] = pair_ref[...]
    for row, column, rows, columns, to, place in down_pieces(*down_ref.shape, out_ref.shape[1]):
        out_ref[first + to : first + to + rows, place : place + columns] = down_ref[
            row : row + rows, column : column + columns
        ]


def pack_down(at, down, pair):
    first, wide = pair.shape
    (out,) = on_chip(
        pack_down_kernel,
        [like(bf16, first + down.size // wide, wide)],
        [at, down, pair],
        0,
        name="pack_down",
    )
    return out


def down_copies(at_ref, block_refs, first, down_ref, sem_ref):
    own = down_ref.shape[0] // len(block_refs)
    pieces = down_pieces(own, down_ref.shape[1], block_refs[0].shape[1])
    copies = []
    for i, block_ref in enumerate(block_refs):
        for k, (row, column, rows, columns, to, place) in enumerate(pieces):
            start = pl.multiple_of(at_ref[i] * own + row, rows)
            copies.append(
                pltpu.make_async_copy(
                    block_ref.at[pl.ds(first + to, rows), pl.ds(place, columns)],
                    down_ref.at[pl.ds(start, rows), pl.ds(column, columns)],
                    sem_ref.at[i * len(pieces) + k],
                )
            )
    return copies


def feed_forward_kernel(step, at_ref, own_ref, other_ref, d_own_ref, d_other_ref, *refs):
    blocks = refs[:-11]
    n_ref, d_out_ref, hidden_ref, d_both_ref, kept_ref, away_ref = refs[-11:-5]
    d_n_ref, whole_ref, down_ref, sem_ref, down_sem_ref = refs[-5:]
    ff = hidden_ref.shape[1]
    first = whole_ref.shape[0] // len(blocks)
    copies = down_copies(at_ref, blocks, first, down_ref, down_sem_ref)
    copies += block_copies(at_ref, blocks, whole_ref, sem_ref)
    for copy in copies:
        copy.start()
    join_rows(at_ref, len(blocks), own_ref, other_ref, n_ref)
    join_rows(at_ref, len(blocks), d_own_ref, d_other_ref, d_out_ref)
    for copy in copies:
        copy.wait()
    for begin in range(0, n_ref.shape[0], step):
        rows = slice(begin, begin + step)
        d_hidden = dot_at(d_out_ref[rows, :], down_ref[...], 1, 1)
        both = dot_at(n_ref[rows, :], whole_ref[...], 1, 0)
        gate = both[:, :ff]
        upper = both[:, ff:]
        sigma = 1.0 / (1.0 + jnp.exp(-gate))
        silu = gate * sigma
        hidden_ref[rows, :] = (silu * upper).astype(bf16)
        d_both_ref[rows, :ff] = (d_hidden * upper * (sigma + silu * (1.0 - sigma))).astype(bf16)
        d_both_ref[rows, ff:] = (d_hidden * silu).astype(bf16)
        d_n_ref[rows, :] = dot_at(d_both_ref[rows, :], whole_ref[...], 1, 1)
    part_rows(at_ref, len(blocks), d_n_ref, kept_ref, away_ref)


def feed_forward(at, own, other, d_own, d_other, blocks, ff):
    _, rows, width = own.shape
    count = len(blocks)
    pieces = len(down_pieces(ff // count, width, 2 * ff))
    return on_chip(
        functools.partial(feed_forward_kernel, min(256, 4 * rows)),
        [
            like(bf16, 4 * rows, width),
            like(bf16, 4 * rows, width),
            like(bf16, 4 * rows, ff),
            like(bf16, 4 * rows, 2 * ff),
            like(f32, 2, rows, width),
            like(bf16, 2, rows, width),
        ],
        [at, own, other, d_own, d_other],
        40 * rows * width * ff,
        blocks=blocks,
        scratch=[
            pltpu.VMEM((4 * rows, width), f32),
            pltpu.VMEM((width, 2 * ff), bf16),
            pltpu.VMEM((ff, width), bf16),
            pltpu.SemaphoreType.DMA((count,)),
            pltpu.SemaphoreType.DMA((count * pieces,)),
        ],
        name="feed_forward",
        room=40,
    )


def feed_forward_grads_kernel(at_ref, n_ref, d_both_ref, hidden_ref, d_out_ref, grad_ref):
    count, _, wide = grad_ref.shape
    block = n_ref.shape[1] // count
    own = hidden_ref.shape[1] // count
    for position in range(count):
        place = at_ref[count + position]
        columns = slice(position * block, (position + 1) * block)
        grad_ref[place, :block, :] = dot_at(n_ref[:, columns], d_both_ref[...], 0, 0).astype(bf16)
        columns = slice(position * own, (position + 1) * own)
        down = dot_at(hidden_ref[:, columns], d_out_ref[...], 0, 0).astype(bf16)
        for row, column, rows, width, to, start in down_pieces(own, n_ref.shape[1], wide):
            grad_ref[place, block + to : block + to + rows, start : start + width] = down[
                row : row + rows, column : column + width
            ]


def feed_forward_grads(at, n, d_both, hidden, d_out, count):
    rows, width = n.shape
    ff = hidden.shape[1]
    (out,) = on_chip(
        feed_forward_grads_kernel,
        [like(bf16, count, width // count + ff // count * width // (2 * ff), 2 * ff)],
        [at, n, d_both, hidden, d_out],
        6 * rows * width * ff,
        name="feed_forward_grads",
        room=32,
    )
    return out


def joined_grads_kernel(at_ref, left_ref, right_ref, grad_ref):
    count, block, _ = grad_ref.shape
    for position in range(count):
        rows = slice(position * block, (position + 1) * block)
        grad_ref[at_ref[count + position]] = dot_at(
            left_ref[rows, :], right_ref[...], 1, 0
        ).astype(bf16)


def joined_grads(at, left, right, count):
    width, rows = left.shape
    (out,) = on_chip(
        joined_grads_kernel,
        [like(bf16, count, width // count, right.shape[1])],
        [at, left, right],
        2 * rows * width * right.shape[1],
        name="joined_grads",
    )
    return out


def split_heads_kernel(at_ref, own_ref, other_ref, weight_ref, d_mid_ref, heads_ref):
    join_rows(at_ref, heads_ref.shape[0] // 2, own_ref, other_ref, d_mid_ref)
    size, rows = heads_ref.shape[1:]
    for seq in range(2):
        part = dot_at(weight_ref[...], d_mid_ref[seq * rows : (seq + 1) * rows, :], 1, 1)
        part = part.astype(bf16)
        for head in range(heads_ref.shape[0] // 2):
            heads_ref[2 * head + seq] = part[head * size : (head + 1) * size, :]


def split_heads(at, own, other, weight, heads):
    _, rows, width = own.shape
    return on_chip(
        split_heads_kernel,
        [
            like(bf16, 4 * rows, width),
            like(bf16, 2 * heads, weight.shape[0] // heads, 2 * rows),
        ],
        [at, own, other, weight],
        8 * rows * width * weight.shape[0],
        name="split_heads",
    )


def heads_grad_kernel(at_ref, joined_ref, *refs):
    blocks, (grad_ref, n_ref, sem_ref) = refs[:-3], refs[-3:]
    copies = sequence_copies(at_ref, blocks, n_ref, sem_ref)
    for copy in copies:
        copy.start()
    for copy in copies:
        copy.wait()
    grad_ref[...] = dot_at(n_ref[...], joined_ref[...], 0, 1).astype(bf16)


def heads_grad(at, joined, blocks):
    columns, tokens = joined.shape
    width = blocks[0].shape[1]
    (out,) = on_chip(
        heads_grad_kernel,
        [like(bf16, width, columns)],
        [at, joined],
        2 * tokens * width * columns,
        blocks=blocks,
        scratch=[pltpu.VMEM((tokens, width), bf16), pltpu.SemaphoreType.DMA((2 * len(blocks),))],
        name="heads_grad",
    )
    return out


def heads_input_kernel(at_ref, heads_ref, *refs):
    blocks = refs[:-6]
    kept_ref, away_ref, out_ref, joined_ref, weight_ref, sem_ref = refs[-6:]
    copies = block_copies(at_ref, blocks, weight_ref, sem_ref)
    for copy in copies:
        copy.start()
    join_heads(heads_ref, joined_ref)
    for copy in copies:
        copy.wait()
    out_ref[...] = dot_at(joined_ref[...], weight_ref[...], 0, 1)
    part_rows(at_ref, len(blocks), out_ref, kept_ref, away_ref)


def heads_input(at, heads, blocks):
    count = len(blocks)
    block, columns = blocks[0].shape
    rows = heads.shape[2] // 2
    width = count * block
    return on_chip(
        heads_input_kernel,
        [like(f32, 2, rows, width), like(bf16, 2, rows, width)],
        [at, heads],
        0,
        blocks=blocks,
        scratch=[
            pltpu.VMEM((4 * rows, width), f32),
            pltpu.VMEM((columns, 4 * rows), bf16),
            pltpu.VMEM((width, columns), bf16),
            pltpu.SemaphoreType.DMA((count,)),
        ],
        name="heads_input",
    )


def layer_output_kernel(first, at_ref, hidden_ref, *refs):
    blocks, (kept_ref, away_ref, out_ref, down_ref, sem_ref) = refs[:-5], refs[-5:]
    copies = down_copies(at_ref, blocks, first, down_ref, sem_ref)
    for copy in copies:
        copy.start()
    for copy in copies:
        copy.wait()
    out_ref[...] = dot_at(hidden_ref[...], down_ref[...], 1, 0)
    part_rows(at_ref, len(blocks), out_ref, kept_ref, away_ref)


def layer_output(at, hidden, blocks, first, width):
    ff = hidden.shape[1]
    rows = hidden.shape[0] // 4
    count = len(blocks)
    pieces = len(down_pieces(ff // count, width, 2 * ff))
    return on_chip(
        functools.partial(layer_output_kernel, first),
        [like(f32, 2, rows, width), like(bf16, 2, rows, width)],
        [at, hidden],
        0,
        blocks=blocks,
        scratch=[
            pltpu.VMEM((4 * rows, width), f32),
            pltpu.VMEM((ff, width), bf16),
            pltpu.SemaphoreType.DMA((count * pieces,)),
        ],
        name="layer_output",
    )


def query_rows_kernel(
    at_ref, terms_ref, gain_ref, query_ref, key_ref, value_ref, d_query, d_key, d_value, d_gain
):
    pieces = ([], [], [])
    for group in range(terms_ref.shape[0] // 2):
        part = terms_ref[2 * group].astype(f32) + terms_ref[2 * group + 1].astype(f32)
        pieces[0].append(part[:, : 2 * HEAD_SIZE])
        pieces[1].append(part[:, 2 * HEAD_SIZE : 3 * HEAD_SIZE])
        pieces[2].append(part[:, 3 * HEAD_SIZE :])
    gain = gain_ref[...]
    rows_sum = None
    outs = (d_query, d_key, d_value)
    for pieces_of, weight_ref, out_ref in zip(pieces, (query_ref, key_ref, value_ref), outs):
        grad = jnp.concatenate(pieces_of, axis=1)
        out_ref[...] = gain * grad
        part = jnp.sum(grad * weight_ref[...].astype(f32), axis=1, keepdims=True)
        rows_sum = part if rows_sum is None else rows_sum + part
    d_gain[...] = rows_sum


def query_rows_grads(at, terms, gain, query, key, value):
    own = query.shape[0]
    return on_chip(
        query_rows_kernel,
        [
            like(f32, *query.shape),
            like(f32, *key.shape),
            like(f32, *value.shape),
            like(f32, own, 1),
        ],
        [at, terms, gain, query, key, value],
        terms.size,
        name="query_rows_grads",
    )


def pair_rows_kernel(
    size, count, at_ref, terms_ref, down_terms, gain_ref, gate_ref, up_ref,
    d_gate, d_up, d_gain, d_down,
):
    gain = gain_ref[...]
    core = at_ref[2 * count]
    seq = at_ref[2 * count + 1]
    half = terms_ref.shape[2] // 2
    rows_sum = jnp.zeros_like(gain)
    for side, (weight_ref, out_ref) in enumerate(((gate_ref, d_gate), (up_ref, d_up))):
        for position in range(half // size):
            for t in range(4):
                columns = slice((4 * position + t) * size, (4 * position + t + 1) * size)
                start = side * half + position * size
                block = (core + t // 2) % 2 * 2 + (seq + t % 2) % 2
                grad = terms_ref[block, :, start : start + size].astype(f32)
                out_ref[:, columns] = gain * grad
                rows_sum = rows_sum + jnp.sum(
                    grad * weight_ref[:, columns].astype(f32), axis=1, keepdims=True
                )
    d_gain[...] = rows_sum
    for row, column, rows, columns, to, place in down_pieces(*d_down.shape, down_terms.shape[1]):
        d_down[row : row + rows, column : column + columns] = down_terms[
            to : to + rows, place : place + columns
        ]


def pair_rows_grads(at, terms, down_terms, gain, gate, up, size, count):
    own = gate.shape[0]
    return on_chip(
        functools.partial(pair_rows_kernel, size, count),
        [
            like(f32, *gate.shape),
            like(f32, *up.shape),
            like(f32, own, 1),
            like(f32, size, down_terms.size // size),
        ],
        [at, terms, down_terms, gain, gate, up],
        terms.size,
        name="pair_rows_grads",
    )


ring_axes = ("z", "x")
owner_axes = ("z", "x", "core", "y")
head_axes = ("z", "x", "y")


def ring_of(count):
    order = list(range(0, count, 2)) + list(range(count - 1, 0, -2))
    forward = [(order[i], order[(i + 1) % count]) for i in range(count)]
    backward = [(there, here) for here, there in forward]
    return forward, backward


def place_of(position, count):
    return jnp.where(position % 2 == 0, position // 2, count - (position + 1) // 2)


def position_at(place, count):
    place = lax.rem(place, count)
    return jnp.where(place < count // 2, 2 * place, 2 * (count - place) - 1)


def tie(*values):
    return lax.optimization_barrier(values)


def after(value, *others):
    return lax.optimization_barrier((value,) + others)[0]


class GatherRing:
    def __init__(self, shard, count):
        self.count = count
        self.forward, self.backward = ring_of(count)
        self.parts = [shard] + [None] * (count - 1)
        self.ahead = self.behind = shard
        self.hops = 0

    def start(self, *others):
        self.hops += 1
        ahead, behind = self.ahead, self.behind
        if self.hops == self.count // 2:
            half = ahead.shape[0] // 2
            ahead, behind = ahead[:half], behind[half:]
        if others:
            ahead, behind = lax.optimization_barrier((ahead, behind) + others)[:2]
        self.pending = [
            lax.ppermute(ahead, ring_axes, self.forward),
            lax.ppermute(behind, ring_axes, self.backward),
        ]

    def land(self, arrived):
        self.ahead, self.behind = arrived
        if self.hops == self.count // 2:
            self.parts[self.hops] = jnp.concatenate(arrived, axis=0)
        else:
            self.parts[self.count - self.hops] = self.ahead
            self.parts[self.hops] = self.behind


class ScatterRing:
    def __init__(self, term, count):
        self.count = count
        self.term = term
        self.forward, self.backward = ring_of(count)
        self.rows = term.shape[1] // 2
        far = term[count // 2]
        self.ahead, self.behind = far[: self.rows], far[self.rows :]
        self.hops = 0

    def start(self):
        self.hops += 1
        self.pending = [
            lax.ppermute(self.ahead, ring_axes, self.forward),
            lax.ppermute(self.behind, ring_axes, self.backward),
        ]

    def land(self, arrived):
        ahead, behind = (value.astype(f32) for value in arrived)
        left = self.count // 2 - self.hops
        if left == 0:
            self.total = self.term[0].astype(f32) + ahead + behind
            return
        if self.hops == 1:
            edges = ((0, self.rows, 0), (self.rows, 0, 0))
            ahead, behind = (
                lax.pad(value, jnp.float32(0), (edge,) + ((0, 0, 0),) * (value.ndim - 1))
                for value, edge in zip((ahead, behind), (edges[0], edges[1]))
            )
        self.ahead = (self.term[left].astype(f32) + ahead).astype(bf16)
        self.behind = (self.term[self.count - left].astype(f32) + behind).astype(bf16)


def settle(moves, *others):
    moving = tuple(tuple(move.pending) for move in moves)
    out = lax.optimization_barrier((moving, others))
    for move, arrived in zip(moves, out[0]):
        move.land(list(arrived))
    return out[1][0] if len(others) == 1 else out[1]


def swap(values, axis):
    return lax.ppermute(values, axis, [(0, 1), (1, 0)])


def rows_of_group(own):
    pair = lax.all_gather(own, "y", axis=0)
    return lax.all_gather(pair, "core", axis=1)


def core_sum(kept, away):
    return kept + swap(away, "core").astype(f32)


def both_rows_sum(pair):
    return pair + swap(pair.astype(bf16), "y").astype(f32)


def own_rows_sum(pair):
    seq = lax.axis_index("y")
    away = lax.dynamic_index_in_dim(pair, 1 - seq, 0, False).astype(bf16)
    return lax.dynamic_index_in_dim(pair, seq, 0, False) + swap(away, "y").astype(f32)


def own_columns(blocks):
    core = lax.axis_index("core")
    seq = lax.axis_index("y")
    away = lax.dynamic_index_in_dim(blocks, 1 - seq, 1, False)
    kept = lax.dynamic_index_in_dim(blocks, seq, 1, False)
    pair = jnp.stack([kept, swap(away, "y")])
    away = lax.dynamic_index_in_dim(pair, 1 - core, 1, False)
    kept = lax.dynamic_index_in_dim(pair, core, 1, False)
    return jnp.concatenate([kept, swap(away, "core")])


def both_rows(own, *others):
    other = after(swap(own, "y"), *others)
    first = lax.axis_index("y") == 0
    return jnp.stack([jnp.where(first, own, other), jnp.where(first, other, own)])


def all_to_all(values, axes):
    return lax.all_to_all(values, axes, 0, 0, tiled=True)


def inverse_rms(values):
    return lax.rsqrt(jnp.mean(values * values, axis=-1, keepdims=True) + norm_eps)


def head_layer(
    count,
    tokens,
    cotangent,
    norm_gain1,
    w_query,
    key_weight,
    value_weight,
    w_out,
    norm_gain2,
    w_gate,
    w_up,
    w_down,
):
    rows, width = tokens.shape[1:]
    own = w_query.shape[0]
    ff_own = w_down.shape[0]
    half = HEAD_SIZE // 2
    quarter = HEAD_SIZE // 4
    group = 4 * own
    seq_rows = 2 * rows
    length = count * seq_rows
    step = seq_rows

    gain1 = norm_gain1.astype(f32)[:, None]
    gain2 = norm_gain2.astype(f32)[:, None]

    place = place_of(lax.axis_index(ring_axes), count)
    steps = jnp.arange(count, dtype=jnp.int32)
    core = lax.axis_index("core")
    seq = lax.axis_index("y")
    at = jnp.concatenate(
        [
            position_at(place + steps, count),
            lax.rem(place_of(steps, count) - place + count, count),
            jnp.stack([core, seq]).astype(jnp.int32),
        ]
    )

    position = jnp.arange(length, dtype=f32)
    exponent = jnp.arange(half, dtype=f32) * (2.0 / HEAD_SIZE)
    angle = (rope_base ** (-exponent))[:, None] * position[None, :]
    cosine = jnp.cos(angle)
    sine = jnp.sin(angle)

    own_rows = tokens[0].astype(f32)
    n1_kept, n1_away = normed_halves(at, tokens[0], count)
    n1_other = swap(n1_away, "core")
    half_width = width // 2
    n1_ring = GatherRing(
        jnp.concatenate([n1_kept, n1_other, w_out[:, :half_width], w_out[:, half_width:]], axis=0),
        count,
    )
    n1_ring.start()
    head_cols = head_columns(at, gain1, w_query, key_weight, value_weight)
    head_weight = all_to_all(head_cols, head_axes).reshape(half_width, 4 * HEAD_SIZE)
    pair_cols = pair_columns(at, gain2, w_gate, w_up, ff_own)
    head_cols, pair_cols = settle([n1_ring], head_cols, pair_cols)
    n1_ring.start()
    tokens_pair = both_rows(tokens[0], head_cols)
    head_weight, tokens_pair = settle([n1_ring], head_weight, tokens_pair)
    n1_ring.start()
    pair_rows = all_to_all(pair_cols, ("core", "y")).reshape(group, 2 * count * ff_own)
    settle([n1_ring])
    n1_ring.start()
    ff_rows = pack_down(at, w_down, pair_rows)
    ff_rows = settle([n1_ring], ff_rows)

    gather = GatherRing(ff_rows, count)
    gather.start()
    kept, away = project_heads(at, head_weight, n1_ring.parts, rows)
    cotangent_pair = both_rows(after(cotangent[0], ff_rows), kept)
    mixed_send, mixed, prob, q, k, v = heads_forward(
        at, kept, swap(away, "core"), cosine, sine, count
    )
    mixed_send, cotangent_pair = settle([gather], mixed_send, cotangent_pair)
    gather.start()
    mixed_low = all_to_all(mixed_send, head_axes)
    cotangent_other = swap(cotangent_pair, "core")
    mixed_low, cotangent_other = settle([gather], mixed_low, cotangent_other)
    gather.start()
    out_weight, mixed_low, kept, away = project_out(at, mixed_low, n1_ring.parts, 2 * rows, own)
    branch = both_rows_sum(core_sum(kept, away))
    qkv_cols = query_columns(at, gain1, w_query, key_weight, value_weight)
    qkv_rows = all_to_all(after(qkv_cols, mixed_low), ("core", "y"))
    branch, qkv_rows = settle([gather], branch, qkv_rows)
    gather.start()
    inputs = tokens_pair.astype(f32)
    middle = inputs + branch

    r2 = inverse_rms(middle)
    n2_pair = middle * r2
    n2_own = n2_pair.astype(bf16)
    n2_other = swap(n2_own, "core")
    n2_own, n2_other = settle([gather], n2_own, n2_other)
    qkv_ring = GatherRing(qkv_rows.reshape(group, count * HEAD_SIZE), count)
    qkv_ring.start(n2_own)
    n2, d_out, hidden, d_both, kept, away = feed_forward(
        at, n2_own, n2_other, cotangent_pair, cotangent_other, gather.parts, count * ff_own
    )
    kept, away = settle([qkv_ring], kept, away)
    qkv_ring.start()
    d_n2 = core_sum(kept, away)
    grads = feed_forward_grads(at, n2, d_both, after(hidden, d_n2), d_out, count)
    d_normed2 = both_rows_sum(d_n2)
    grads = settle([qkv_ring], grads)
    scatter = ScatterRing(grads, count)
    scatter.start()
    d_normed2 = settle([scatter], d_normed2)
    scatter.start()
    qkv_ring.start()
    d_middle = cotangent_pair.astype(f32) + r2 * (
        d_normed2 - n2_pair * jnp.mean(d_normed2 * n2_pair, axis=-1, keepdims=True)
    )

    d_mid_own = d_middle.astype(bf16)
    d_mid_other = swap(d_mid_own, "core")
    d_mid, d_mixed = split_heads(at, d_mid_own, d_mid_other, out_weight, count)
    d_mixed = all_to_all(d_mixed, head_axes)
    out_grads = joined_grads(at, mixed_low, d_mid, count)
    kept_out, away_out = layer_output(
        at, after(hidden, d_mid), gather.parts, group, width
    )
    d_mixed, out_grads, kept_out, away_out = settle(
        [scatter, qkv_ring], d_mixed, out_grads, kept_out, away_out
    )
    out_scatter = ScatterRing(out_grads, count)
    scatter.start()
    out_scatter.start()
    qkv_ring.start()
    kept, away = heads_backward(at, q, k, v, prob, mixed, d_mixed, cosine, sine, count)
    out_rows = own_rows_sum(core_sum(kept_out, away_out))
    kept, away, out_rows = settle([scatter, out_scatter, qkv_ring], kept, away, out_rows)
    scatter.start()
    out_scatter.start()
    d_qkv, joined = heads_send(at, kept, swap(away, "core"), count)
    d_qkv = all_to_all(d_qkv, head_axes)
    grad_heads = heads_grad(at, joined, n1_ring.parts)
    grad_heads, d_qkv = settle([out_scatter], grad_heads, d_qkv)
    out_scatter.start()
    grad_heads = all_to_all(grad_heads.reshape(2 * count, own, 4 * HEAD_SIZE), head_axes)
    kept, away = heads_input(at, d_qkv, qkv_ring.parts)
    kept, away = settle([scatter, out_scatter], kept, away)
    out_scatter.start()
    own_both = own_columns(scatter.total[:group].astype(bf16).reshape(2, 2, own, -1))
    d_normed1 = own_rows_sum(core_sum(kept, away))
    d_middle_own, middle_own = (
        lax.dynamic_index_in_dim(value, seq, 0, False) for value in (d_middle, middle)
    )
    r1 = inverse_rms(own_rows)
    n1_wide = own_rows * r1
    input_grad = d_middle_own + r1 * (
        d_normed1 - n1_wide * jnp.mean(d_normed1 * n1_wide, axis=-1, keepdims=True)
    )
    result = middle_own + out_rows
    grad_heads, own_both = settle([out_scatter], grad_heads, own_both)
    owned_out = out_scatter.total
    grad_gate, grad_up, grad_gain2, owned_down = pair_rows_grads(
        at, own_both, scatter.total[group:], gain2, w_gate, w_up, ff_own, count
    )
    grad_query, grad_key, grad_value, grad_gain1 = query_rows_grads(
        at, grad_heads, gain1, w_query, key_weight, value_weight
    )
    return (
        result.astype(bf16)[None],
        input_grad[None],
        grad_gain1[:, 0],
        grad_query,
        grad_key,
        grad_value,
        owned_out,
        grad_gain2[:, 0],
        grad_gate,
        grad_up,
        owned_down,
    )


def by_heads(mesh):
    count = mesh.shape["ctx"] // 2
    parts = Mesh(mesh.devices.reshape(count // 2, 2, 2, 2), owner_axes)
    row_spec = P("y", ("z", "x", "core"), None)
    in_specs = (row_spec, row_spec) + (P(owner_axes),) * 9
    out_specs = (row_spec, row_spec) + (P(owner_axes),) * 9
    return jax.shard_map(
        functools.partial(head_layer, count),
        mesh=parts,
        in_specs=in_specs,
        out_specs=out_specs,
        check_vma=False,
    )


def solution(mesh):
    in_specs = (
        P("fsdp", "ctx", None),
        P("fsdp", "ctx", None),
        P(("ctx", "fsdp")),
        P(("ctx", "fsdp"), None),
        P(("ctx", "fsdp"), None),
        P(("ctx", "fsdp"), None),
        P(("ctx", "fsdp"), None),
        P(("ctx", "fsdp")),
        P(("ctx", "fsdp"), None),
        P(("ctx", "fsdp"), None),
        P(("ctx", "fsdp"), None),
    )
    out_specs = (
        P("fsdp", "ctx", None),
        P("fsdp", "ctx", None),
        P(("ctx", "fsdp")),
        P(("ctx", "fsdp"), None),
        P(("ctx", "fsdp"), None),
        P(("ctx", "fsdp"), None),
        P(("ctx", "fsdp"), None),
        P(("ctx", "fsdp")),
        P(("ctx", "fsdp"), None),
        P(("ctx", "fsdp"), None),
        P(("ctx", "fsdp"), None),
    )
    if mesh.shape["ctx"] == QUERY_HEADS and mesh.shape["fsdp"] == 2:
        return by_heads(mesh)
    return jax.shard_map(local, mesh=mesh, in_specs=in_specs, out_specs=out_specs, check_vma=False)
```

```python
import functools

import jax
import jax.numpy as jnp
import numpy as np
from jax import lax
from jax.experimental import pallas as pl
from jax.experimental.pallas import tpu as pltpu
from jax.sharding import Mesh
from jax.sharding import PartitionSpec as P

QUERY_HEADS = 16
KEY_VALUE_HEADS = 8
HEAD_SIZE = 96


rope_base = 100000.0
norm_eps = 1e-05
masked_value = -1e30
key_block = 512


def rms_norm(value_rows, gain):
    return (
        value_rows
        * lax.rsqrt(jnp.mean(value_rows * value_rows, axis=-1, keepdims=True) + norm_eps)
        * gain
    )


def apply_rotary(value_rows, token_position):
    half = value_rows.shape[-1] // 2
    exponent = jnp.arange(half, dtype=jnp.float32) * (2.0 / value_rows.shape[-1])
    freq = rope_base ** (-exponent)
    angle = token_position[:, None] * freq[None, :]
    cosine = jnp.cos(angle)[:, None, :]
    sine = jnp.sin(angle)[:, None, :]
    first = value_rows[..., :half]
    second = value_rows[..., half:]
    return jnp.concatenate(
        [first * cosine - second * sine, second * cosine + first * sine], axis=-1
    )


def matmul(left, right):
    return jnp.dot(left, right, preferred_element_type=jnp.float32)


def key_pieces(key_rows, value_rows, key_value_heads, head_dim):
    count = key_rows.shape[0]
    number = count // key_block
    key_sets = key_rows.reshape(number, key_block, key_value_heads, head_dim)
    value_sets = value_rows.reshape(number, key_block, key_value_heads, head_dim)
    starts = jnp.arange(number, dtype=jnp.int32) * key_block
    return (key_sets, value_sets, starts, key_block)


def fold_keys(carry, key_rows, value_rows, query_rows, query_pos):
    key_value_heads = query_rows.shape[1]
    head_dim = query_rows.shape[3]
    scale = head_dim ** (-0.5)
    key_sets, value_sets, starts, size = key_pieces(key_rows, value_rows, key_value_heads, head_dim)

    def fold_one_piece(state, item):
        key_set, value_set, begin = item

        def fold_live(state):
            top, total, summed = state
            scores = (
                jnp.einsum(
                    "tkgd,skd->kgts", query_rows, key_set, preferred_element_type=jnp.float32
                )
                * scale
            )
            visible = (begin + jnp.arange(size, dtype=jnp.int32))[None, :] <= query_pos[:, None]
            scores = jnp.where(visible, scores, masked_value)
            new_top = jnp.maximum(top, jnp.max(scores, axis=-1))
            weights = jnp.where(visible, jnp.exp(scores - new_top[..., None]), 0.0)
            factor = jnp.exp(top - new_top)
            total = total * factor + jnp.sum(weights, axis=-1)
            summed = summed * factor[..., None] + jnp.einsum(
                "kgts,skd->kgtd",
                weights.astype(jnp.bfloat16),
                value_set,
                preferred_element_type=jnp.float32,
            )
            return (new_top, total, summed)

        def fold_skipped(state):
            return state

        return (lax.cond(begin <= query_pos[-1], fold_live, fold_skipped, state), None)

    carry, _ = lax.scan(fold_one_piece, carry, (key_sets, value_sets, starts))
    return carry


def back_keys(key_rows, value_rows, query_rows, query_pos, d_heads, log_total, delta):
    rows, key_value_heads, groups, head_dim = query_rows.shape
    scale = head_dim ** (-0.5)
    key_sets, value_sets, starts, size = key_pieces(key_rows, value_rows, key_value_heads, head_dim)

    def back_one_piece(d_query, item):
        key_set, value_set, begin = item

        def back_live(d_query):
            scores = (
                jnp.einsum(
                    "tkgd,skd->kgts", query_rows, key_set, preferred_element_type=jnp.float32
                )
                * scale
            )
            visible = (begin + jnp.arange(size, dtype=jnp.int32))[None, :] <= query_pos[:, None]
            prob = jnp.where(visible, jnp.exp(scores - log_total[..., None]), 0.0)
            d_prob = jnp.einsum(
                "tkgd,skd->kgts", d_heads, value_set, preferred_element_type=jnp.float32
            )
            d_scores = (prob * (d_prob - delta[..., None])).astype(jnp.bfloat16)
            d_query = d_query + scale * jnp.einsum(
                "kgts,skd->tkgd", d_scores, key_set, preferred_element_type=jnp.float32
            )
            d_key = scale * jnp.einsum(
                "kgts,tkgd->skd", d_scores, query_rows, preferred_element_type=jnp.float32
            )
            d_value = jnp.einsum(
                "kgts,tkgd->skd",
                prob.astype(jnp.bfloat16),
                d_heads,
                preferred_element_type=jnp.float32,
            )
            return (
                d_query,
                (
                    d_key.reshape(size, key_value_heads * head_dim),
                    d_value.reshape(size, key_value_heads * head_dim),
                ),
            )

        def back_skipped(d_query):
            empty = jnp.zeros((size, key_value_heads * head_dim), jnp.float32)
            return (d_query, (empty, empty))

        return lax.cond(begin <= query_pos[-1], back_live, back_skipped, d_query)

    start_grad = jnp.zeros((rows, key_value_heads, groups, head_dim), jnp.float32)
    d_query, (d_keys, d_values) = lax.scan(
        back_one_piece, start_grad, (key_sets, value_sets, starts)
    )
    return (
        d_query,
        d_keys.reshape(key_rows.shape[0], key_value_heads * head_dim),
        d_values.reshape(key_rows.shape[0], key_value_heads * head_dim),
    )


def local(
    tokens,
    cotangent,
    norm_gain1,
    w_query,
    key_weight,
    value_weight,
    w_out,
    norm_gain2,
    w_gate,
    w_up,
    w_down,
):
    rows = tokens.shape[1]
    key_value_heads = KEY_VALUE_HEADS
    heads = QUERY_HEADS
    head_dim = HEAD_SIZE
    groups = heads // key_value_heads
    first_row = lax.axis_index("ctx") * rows
    query_pos = first_row + jnp.arange(rows, dtype=jnp.int32)
    token_position = query_pos.astype(jnp.float32)
    inputs = tokens[0].astype(jnp.float32)
    gathered = (
        lax.all_gather(norm_gain1, ("ctx", "fsdp"), axis=0, tiled=True),
        lax.all_gather(w_query, ("ctx", "fsdp"), axis=0, tiled=True),
        lax.all_gather(key_weight, ("ctx", "fsdp"), axis=0, tiled=True),
        lax.all_gather(value_weight, ("ctx", "fsdp"), axis=0, tiled=True),
        lax.all_gather(w_out, ("ctx", "fsdp"), axis=0, tiled=True),
        lax.all_gather(norm_gain2, ("ctx", "fsdp"), axis=0, tiled=True),
        lax.all_gather(w_gate, ("ctx", "fsdp"), axis=0, tiled=True),
        lax.all_gather(w_up, ("ctx", "fsdp"), axis=0, tiled=True),
        lax.all_gather(w_down, ("ctx", "fsdp"), axis=0, tiled=True),
    )
    gain_one = gathered[0].astype(jnp.float32)
    gain_two = gathered[5].astype(jnp.float32)
    normed1 = rms_norm(inputs, gain_one).astype(jnp.bfloat16)
    query_pre = matmul(normed1, gathered[1]).reshape(rows, heads, head_dim)
    key_pre = matmul(normed1, gathered[2]).reshape(rows, key_value_heads, head_dim)
    value = matmul(normed1, gathered[3]).astype(jnp.bfloat16)
    query_rows = (
        apply_rotary(query_pre, token_position)
        .astype(jnp.bfloat16)
        .reshape(rows, key_value_heads, groups, head_dim)
    )
    key_rows = (
        apply_rotary(key_pre, token_position)
        .reshape(rows, key_value_heads * head_dim)
        .astype(jnp.bfloat16)
    )
    start_state = (
        jnp.full((key_value_heads, groups, rows), masked_value, jnp.float32),
        jnp.zeros((key_value_heads, groups, rows), jnp.float32),
        jnp.zeros((key_value_heads, groups, rows, head_dim), jnp.float32),
    )
    top, total, summed = fold_keys(
        start_state,
        lax.all_gather(key_rows, "ctx", axis=0, tiled=True),
        lax.all_gather(value, "ctx", axis=0, tiled=True),
        query_rows,
        query_pos,
    )
    mixed_heads = jnp.transpose(summed / total[..., None], (2, 0, 1, 3))
    log_total = top + jnp.log(total)
    mixed_low = mixed_heads.reshape(rows, heads * head_dim).astype(jnp.bfloat16)
    middle = inputs + matmul(mixed_low, gathered[4])
    normed2 = rms_norm(middle, gain_two).astype(jnp.bfloat16)
    gate = matmul(normed2, gathered[6])
    upper = matmul(normed2, gathered[7])
    hidden = (jax.nn.silu(gate) * upper).astype(jnp.bfloat16)
    result = middle + matmul(hidden, gathered[8])
    gathered = (
        lax.all_gather(norm_gain1, ("ctx", "fsdp"), axis=0, tiled=True),
        lax.all_gather(w_query, ("ctx", "fsdp"), axis=0, tiled=True),
        lax.all_gather(key_weight, ("ctx", "fsdp"), axis=0, tiled=True),
        lax.all_gather(value_weight, ("ctx", "fsdp"), axis=0, tiled=True),
        lax.all_gather(w_out, ("ctx", "fsdp"), axis=0, tiled=True),
        lax.all_gather(norm_gain2, ("ctx", "fsdp"), axis=0, tiled=True),
        lax.all_gather(w_gate, ("ctx", "fsdp"), axis=0, tiled=True),
        lax.all_gather(w_up, ("ctx", "fsdp"), axis=0, tiled=True),
        lax.all_gather(w_down, ("ctx", "fsdp"), axis=0, tiled=True),
    )
    incoming = cotangent[0].astype(jnp.float32)
    incoming_low = incoming.astype(jnp.bfloat16)
    grad_down = matmul(hidden.T, incoming_low)
    d_hidden = matmul(incoming_low, gathered[8].T)
    _, swiglu_back = jax.vjp(lambda gate_in, upper_in: jax.nn.silu(gate_in) * upper_in, gate, upper)
    d_gate, d_upper = swiglu_back(d_hidden)
    d_gate = d_gate.astype(jnp.bfloat16)
    d_upper = d_upper.astype(jnp.bfloat16)
    grad_gate = matmul(normed2.T, d_gate)
    grad_up = matmul(normed2.T, d_upper)
    d_normed2 = matmul(d_gate, gathered[6].T) + matmul(d_upper, gathered[7].T)
    _, norm_back2 = jax.vjp(rms_norm, middle, gain_two)
    d_middle, grad_gain2 = norm_back2(d_normed2)
    d_middle = d_middle + incoming
    owned_gain2, owned_gate, owned_up, owned_down = (
        lax.psum_scatter(grad_gain2, ("ctx", "fsdp"), scatter_dimension=0, tiled=True),
        lax.psum_scatter(grad_gate, ("ctx", "fsdp"), scatter_dimension=0, tiled=True),
        lax.psum_scatter(grad_up, ("ctx", "fsdp"), scatter_dimension=0, tiled=True),
        lax.psum_scatter(grad_down, ("ctx", "fsdp"), scatter_dimension=0, tiled=True),
    )
    d_middle_low = d_middle.astype(jnp.bfloat16)
    grad_out = matmul(mixed_low.T, d_middle_low)
    d_mixed = matmul(d_middle_low, gathered[4].T).astype(jnp.bfloat16)
    d_heads = d_mixed.reshape(rows, key_value_heads, groups, head_dim)
    delta = jnp.transpose(jnp.sum(d_heads.astype(jnp.float32) * mixed_heads, axis=-1), (1, 2, 0))
    back_keys_all, back_values_all = (
        lax.all_gather(key_rows, "ctx", axis=0, tiled=True),
        lax.all_gather(value, "ctx", axis=0, tiled=True),
    )
    d_query_rot, d_keys_all, d_values_all = back_keys(
        back_keys_all, back_values_all, query_rows, query_pos, d_heads, log_total, delta
    )
    d_keys_rot, d_value = (
        lax.psum_scatter(d_keys_all, "ctx", scatter_dimension=0, tiled=True),
        lax.psum_scatter(d_values_all, "ctx", scatter_dimension=0, tiled=True),
    )
    _, rotate_back_query = jax.vjp(
        lambda values_in: apply_rotary(values_in, token_position), query_pre
    )
    _, rotate_back_key = jax.vjp(lambda values_in: apply_rotary(values_in, token_position), key_pre)
    d_query = (
        rotate_back_query(d_query_rot.reshape(rows, heads, head_dim))[0]
        .reshape(rows, heads * head_dim)
        .astype(jnp.bfloat16)
    )
    d_key = (
        rotate_back_key(d_keys_rot.reshape(rows, key_value_heads, head_dim))[0]
        .reshape(rows, key_value_heads * head_dim)
        .astype(jnp.bfloat16)
    )
    d_value = d_value.astype(jnp.bfloat16)
    grad_query = matmul(normed1.T, d_query)
    grad_key = matmul(normed1.T, d_key)
    grad_value = matmul(normed1.T, d_value)
    d_normed1 = (
        matmul(d_query, gathered[1].T)
        + matmul(d_key, gathered[2].T)
        + matmul(d_value, gathered[3].T)
    )
    _, norm_back1 = jax.vjp(rms_norm, inputs, gain_one)
    d_inputs, grad_gain1 = norm_back1(d_normed1)
    input_grad = d_inputs + d_middle
    owned_gain1, owned_query, owned_key, owned_value, owned_out = (
        lax.psum_scatter(grad_gain1, ("ctx", "fsdp"), scatter_dimension=0, tiled=True),
        lax.psum_scatter(grad_query, ("ctx", "fsdp"), scatter_dimension=0, tiled=True),
        lax.psum_scatter(grad_key, ("ctx", "fsdp"), scatter_dimension=0, tiled=True),
        lax.psum_scatter(grad_value, ("ctx", "fsdp"), scatter_dimension=0, tiled=True),
        lax.psum_scatter(grad_out, ("ctx", "fsdp"), scatter_dimension=0, tiled=True),
    )
    return (
        result.astype(jnp.bfloat16)[None],
        input_grad[None],
        owned_gain1,
        owned_query,
        owned_key,
        owned_value,
        owned_out,
        owned_gain2,
        owned_gate,
        owned_up,
        owned_down,
    )


bf16 = jnp.bfloat16
f32 = jnp.float32
score_scale = HEAD_SIZE ** (-0.5)
log2_e = 1.4426950408889634
ln_2 = 0.6931471805599453


def dot_at(left, right, left_dim, right_dim):
    return lax.dot_general(
        left, right, (((left_dim,), (right_dim,)), ((), ())), preferred_element_type=jnp.float32
    )


def rotate(values, cosine, sine):
    half = values.shape[0] // 2
    first, second = values[:half], values[half:]
    return jnp.concatenate([first * cosine - second * sine, second * cosine + first * sine], axis=0)


def rotate_back(values, cosine, sine):
    half = values.shape[0] // 2
    first, second = values[:half], values[half:]
    return jnp.concatenate([first * cosine + second * sine, second * cosine - first * sine], axis=0)


def heads_forward_kernel(
    count, at_ref, kept_ref, other_ref, cos_ref, sin_ref,
    send_ref, mixed_ref, prob_ref, q_ref, k_ref, v_ref,
):
    size = q_ref.shape[0]
    half = size // 2
    rows = kept_ref[...] + other_ref[...].astype(f32)
    q = rotate(rows[:size], cos_ref[...], sin_ref[...])
    q_ref[...] = (q * (score_scale * log2_e)).astype(bf16)
    k_ref[...] = rotate(rows[size : 2 * size], cos_ref[...], sin_ref[...]).astype(bf16)
    v_ref[...] = rows[2 * size :].astype(bf16)
    step = send_ref.shape[2]
    offset = 0
    for block in range(count):
        begin = block * step
        end = begin + step
        scores = dot_at(k_ref[:, 0:end], q_ref[:, begin:end], 0, 0)
        key = lax.broadcasted_iota(jnp.int32, (step, step), 0)
        query = lax.broadcasted_iota(jnp.int32, (step, step), 1)
        last = jnp.where(key <= query, scores[begin:end], masked_value)
        top = jnp.max(last, axis=0, keepdims=True)
        if begin:
            top = jnp.maximum(top, jnp.max(scores[:begin], axis=0, keepdims=True))
        last = jnp.exp2(last - top)
        total = jnp.sum(last, axis=0, keepdims=True)
        if begin:
            first = jnp.exp2(scores[:begin] - top)
            total = total + jnp.sum(first, axis=0, keepdims=True)
        inverse = 1.0 / total
        prob_ref[offset + begin : offset + end, :] = (last * inverse).astype(bf16)
        if begin:
            prob_ref[offset : offset + begin, :] = (first * inverse).astype(bf16)
        mixed = dot_at(v_ref[:, 0:end], prob_ref[offset : offset + end, :], 1, 0)
        mixed_ref[:, begin:end] = mixed
        send_ref[2 * block] = mixed[:half].astype(bf16)
        send_ref[2 * block + 1] = mixed[half:].astype(bf16)
        offset += end


def heads_forward(at, kept, other, cosine, sine, count):
    tokens = kept.shape[1]
    size = kept.shape[0] // 3
    step = tokens // count
    pairs = step * count * (count + 1) // 2
    return on_chip(
        functools.partial(heads_forward_kernel, count),
        [
            like(bf16, 2 * count, size // 2, step),
            like(f32, size, tokens),
            like(bf16, pairs, step),
            like(bf16, size, tokens),
            like(bf16, size, tokens),
            like(bf16, size, tokens),
        ],
        [at, kept, other, cosine, sine],
        4 * size * pairs * step,
        name="heads_forward",
        room=32,
    )


def heads_backward_kernel(
    count, at_ref, q_ref, k_ref, v_ref, prob_ref, mixed_ref, back_ref, cos_ref, sin_ref,
    kept_ref, away_ref,
):
    half, step = back_ref.shape[1:]
    size = 2 * half
    d_k_ref = kept_ref.at[size : 2 * size]
    d_v_ref = kept_ref.at[2 * size :]
    offset = 0
    for block in range(count):
        begin = block * step
        end = begin + step
        d_mixed = jnp.concatenate([back_ref[2 * block], back_ref[2 * block + 1]], axis=0)
        delta = jnp.sum(d_mixed.astype(f32) * mixed_ref[:, begin:end], axis=0, keepdims=True)
        prob = prob_ref[offset : offset + end, :]
        d_prob = dot_at(v_ref[:, 0:end], d_mixed, 0, 0)
        d_scores = (prob.astype(f32) * (d_prob - delta)).astype(bf16)
        d_q = dot_at(k_ref[:, 0:end], d_scores, 1, 0) * score_scale
        kept_ref[:size, begin:end] = rotate_back(d_q, cos_ref[:, begin:end], sin_ref[:, begin:end])
        d_v = dot_at(d_mixed, prob, 1, 1)
        d_k = dot_at(q_ref[:, begin:end], d_scores, 1, 1) * ln_2
        if begin:
            d_v_ref[:, 0:begin] += d_v[:, 0:begin]
            d_k_ref[:, 0:begin] += d_k[:, 0:begin]
        d_v_ref[:, begin:end] = d_v[:, begin:end]
        d_k_ref[:, begin:end] = d_k[:, begin:end]
        offset += end
    d_k_ref[...] = rotate_back(d_k_ref[...], cos_ref[...], sin_ref[...])
    away_ref[...] = kept_ref[...].astype(bf16)


def heads_backward(at, q, k, v, prob, mixed, d_mixed, cosine, sine, count):
    size, tokens = q.shape
    return on_chip(
        functools.partial(heads_backward_kernel, count),
        [like(f32, 3 * size, tokens), like(bf16, 3 * size, tokens)],
        [at, q, k, v, prob, mixed, d_mixed, cosine, sine],
        8 * size * prob.size,
        name="heads_backward",
        room=32,
    )


def heads_join_kernel(count, at_ref, kept_ref, other_ref, joined_ref):
    core = at_ref[2 * count]
    size = kept_ref.shape[0] // 3
    joined_ref[pl.ds(pl.multiple_of(core * size, size), size), :] = kept_ref[:size, :].astype(bf16)
    joined_ref[pl.ds(pl.multiple_of((1 - core) * size, size), size), :] = other_ref[:size, :]
    d_kv = kept_ref[size:, :] + other_ref[size:, :].astype(f32)
    joined_ref[2 * size :, :] = d_kv.astype(bf16)


def heads_join(at, kept, other, count):
    size, tokens = kept.shape
    (out,) = on_chip(
        functools.partial(heads_join_kernel, count),
        [like(bf16, size // 3 * 4, tokens)],
        [at, kept, other],
        4 * kept.size,
        name="heads_join",
    )
    return out


def on_chip(kernel, out_shape, args, flops, blocks=(), scratch=(), name=None, room=24):
    moved = sum(a.size * a.dtype.itemsize for a in list(args) + list(blocks))
    moved += sum(o.size * o.dtype.itemsize for o in out_shape)
    near = pl.BlockSpec(memory_space=pltpu.VMEM)
    return pl.pallas_call(
        kernel,
        out_shape=tuple(out_shape),
        in_specs=[pl.BlockSpec(memory_space=pltpu.SMEM)]
        + [near] * (len(args) - 1)
        + [pl.BlockSpec(memory_space=pltpu.HBM)] * len(blocks),
        out_specs=(near,) * len(out_shape),
        scratch_shapes=scratch,
        compiler_params=pltpu.CompilerParams(vmem_limit_bytes=room * 2**20),
        cost_estimate=pl.CostEstimate(flops=flops, bytes_accessed=moved, transcendentals=0),
        name=name,
    )(*args, *blocks)


def like(dtype, *shape):
    return jax.ShapeDtypeStruct(shape, dtype)


def block_copies(at_ref, block_refs, whole_ref, sem_ref, first=0):
    size = whole_ref.shape[0] // len(block_refs)
    copies = []
    for k, block_ref in enumerate(block_refs):
        start = pl.multiple_of(at_ref[k] * size, size)
        copies.append(
            pltpu.make_async_copy(
                block_ref.at[pl.ds(first, size), :], whole_ref.at[pl.ds(start, size), :], sem_ref.at[k]
            )
        )
    return copies


def core_rows(at_ref, count, rows, seq, other):
    core = at_ref[2 * count]
    start = seq * 2 * rows + (1 - core if other else core) * rows
    return pl.ds(pl.multiple_of(start, rows), rows)


def join_rows(at_ref, count, own_ref, other_ref, whole_ref):
    rows = own_ref.shape[1]
    for seq in range(2):
        whole_ref[core_rows(at_ref, count, rows, seq, False), :] = own_ref[seq]
        whole_ref[core_rows(at_ref, count, rows, seq, True), :] = other_ref[seq]


def part_rows(at_ref, count, whole_ref, kept_ref, away_ref):
    rows = kept_ref.shape[1]
    for seq in range(2):
        kept_ref[seq] = whole_ref[core_rows(at_ref, count, rows, seq, False), :]
        away_ref[seq] = whole_ref[core_rows(at_ref, count, rows, seq, True), :].astype(bf16)


def pair_columns_kernel(size, at_ref, gain_ref, gate_ref, up_ref, out_ref):
    gain = gain_ref[...]
    half = out_ref.shape[2] // 2
    for t in range(4):
        for position in range(half // size):
            columns = pl.ds((4 * position + t) * size, size)
            for side, ref in enumerate((gate_ref, up_ref)):
                out_ref[t, :, pl.ds(side * half + position * size, size)] = (
                    ref[:, columns].astype(f32) * gain
                ).astype(bf16)


def pair_columns(at, gain, gate, up, size):
    own, ff = gate.shape
    (out,) = on_chip(
        functools.partial(pair_columns_kernel, size),
        [like(bf16, 4, own, ff // 2)],
        [at, gain, gate, up],
        own * ff,
        name="pair_columns",
    )
    return out


def head_columns_kernel(at_ref, gain_ref, query_ref, key_ref, value_ref, out_ref):
    gain = gain_ref[...]
    query = query_ref[...].astype(f32) * gain
    key = key_ref[...].astype(f32) * gain
    value = value_ref[...].astype(f32) * gain
    for group in range(out_ref.shape[0]):
        shared = slice(group * HEAD_SIZE, (group + 1) * HEAD_SIZE)
        out_ref[group] = jnp.concatenate(
            [
                query[:, 2 * group * HEAD_SIZE : 2 * (group + 1) * HEAD_SIZE],
                key[:, shared],
                value[:, shared],
            ],
            axis=1,
        ).astype(bf16)


def head_columns(at, gain, query, key, value):
    own, width = query.shape
    (out,) = on_chip(
        head_columns_kernel,
        [like(bf16, width // HEAD_SIZE // 2, own, 4 * HEAD_SIZE)],
        [at, gain, query, key, value],
        own * width,
        name="head_columns",
    )
    return out


def normed_halves_kernel(count, at_ref, rows_ref, kept_ref, away_ref):
    core = at_ref[2 * count]
    rows = rows_ref[...].astype(f32)
    mean = jnp.mean(rows * rows, axis=-1, keepdims=True)
    normed = rows * lax.rsqrt(mean + norm_eps)
    size = rows.shape[1] // (2 * count)
    halves = [
        jnp.concatenate(
            [normed[:, (2 * i + c) * size : (2 * i + c + 1) * size] for i in range(count)], axis=1
        )
        for c in range(2)
    ]
    kept_ref[...] = jnp.where(core == 0, halves[0], halves[1]).astype(bf16)
    away_ref[...] = jnp.where(core == 0, halves[1], halves[0]).astype(bf16)


def normed_halves(at, rows, count):
    tokens, width = rows.shape
    return on_chip(
        functools.partial(normed_halves_kernel, count),
        [like(bf16, tokens, width // 2), like(bf16, tokens, width // 2)],
        [at, rows],
        8 * rows.size,
        name="normed_halves",
    )


def sequence_copies(at_ref, block_refs, whole_ref, sem_ref):
    count = len(block_refs)
    core = at_ref[2 * count]
    rows = whole_ref.shape[0] // (2 * count)
    copies = []
    for i, block_ref in enumerate(block_refs):
        for k, side in enumerate((core, 1 - core)):
            start = pl.multiple_of((2 * at_ref[i] + side) * rows, rows)
            copies.append(
                pltpu.make_async_copy(
                    block_ref.at[pl.ds(k * rows, rows), :],
                    whole_ref.at[pl.ds(start, rows), :],
                    sem_ref.at[2 * i + k],
                )
            )
    return copies


def project_heads_kernel(at_ref, own_ref, other_ref, *refs):
    blocks, (kept_ref, away_ref, weight_ref, n_ref, out_ref, sem_ref) = refs[:-6], refs[-6:]
    copies = sequence_copies(at_ref, blocks, n_ref, sem_ref)
    for copy in copies:
        copy.start()
    core = at_ref[2 * len(blocks)]
    seq = at_ref[2 * len(blocks) + 1]
    own = own_ref.shape[1]
    for position in range(len(blocks)):
        for ref, side in ((own_ref, seq), (other_ref, 1 - seq)):
            start = pl.multiple_of((2 * position + side) * own, own)
            weight_ref[pl.ds(start, own), :] = ref[position]
    for copy in copies:
        copy.wait()
    size = kept_ref.shape[0] // 3
    out_ref[...] = dot_at(weight_ref[...], n_ref[...], 0, 1)
    kept_ref[:size, :] = out_ref[pl.ds(pl.multiple_of(core * size, size), size), :]
    kept_ref[size:, :] = out_ref[2 * size :, :]
    there = pl.ds(pl.multiple_of((1 - core) * size, size), size)
    away_ref[:size, :] = out_ref[there, :].astype(bf16)
    away_ref[size:, :] = out_ref[2 * size :, :].astype(bf16)


def project_heads(at, weight_own, weight_other, blocks, rows):
    count = len(blocks)
    _, own, columns = weight_own.shape
    width = 2 * count * own
    tokens = 2 * count * rows
    size = columns // 4
    return on_chip(
        project_heads_kernel,
        [
            like(f32, 3 * size, tokens),
            like(bf16, 3 * size, tokens),
            like(bf16, width, columns),
        ],
        [at, weight_own, weight_other],
        2 * columns * tokens * width,
        blocks=blocks,
        scratch=[
            pltpu.VMEM((tokens, width), bf16),
            pltpu.VMEM((columns, tokens), f32),
            pltpu.SemaphoreType.DMA((2 * count,)),
        ],
        name="project_heads",
    )


def join_heads(heads_ref, joined_ref):
    size, rows = heads_ref.shape[1:]
    for seq in range(2):
        for head in range(heads_ref.shape[0] // 2):
            joined_ref[head * size : (head + 1) * size, seq * rows : (seq + 1) * rows] = heads_ref[
                2 * head + seq
            ]


def project_out_kernel(first, at_ref, heads_ref, *refs):
    blocks, (weight_ref, joined_ref, kept_ref, away_ref, out_ref, sem_ref) = refs[:-6], refs[-6:]
    count = len(blocks)
    own = weight_ref.shape[0] // count
    width = weight_ref.shape[1] // 2
    copies = []
    for i, block_ref in enumerate(blocks):
        start = pl.multiple_of(at_ref[i] * own, own)
        for k in range(2):
            copies.append(
                pltpu.make_async_copy(
                    block_ref.at[pl.ds(first + k * own, own), :],
                    weight_ref.at[pl.ds(start, own), pl.ds(k * width, width)],
                    sem_ref.at[2 * i + k],
                )
            )
    for copy in copies:
        copy.start()
    join_heads(heads_ref, joined_ref)
    for copy in copies:
        copy.wait()
    out_ref[...] = dot_at(joined_ref[...], weight_ref[...], 0, 0)
    part_rows(at_ref, count, out_ref, kept_ref, away_ref)


def project_out(at, heads, blocks, first, own):
    count = len(blocks)
    width = 2 * blocks[0].shape[1]
    rows = heads.shape[2] // 2
    return on_chip(
        functools.partial(project_out_kernel, first),
        [
            like(bf16, count * own, width),
            like(bf16, count * own, 4 * rows),
            like(f32, 2, rows, width),
            like(bf16, 2, rows, width),
        ],
        [at, heads],
        8 * rows * width * count * own,
        blocks=blocks,
        scratch=[pltpu.VMEM((4 * rows, width), f32), pltpu.SemaphoreType.DMA((2 * count,))],
        name="project_out",
    )


def down_pieces(rows, width, wide):
    left = wide // 2
    right = width - left
    pieces = [(i * rows // 2, 0, rows // 2, left, 0, i * left) for i in range(2)]
    parts = wide // right
    size = rows // parts
    pieces += [(i * size, left, size, right, rows // 2, i * right) for i in range(parts)]
    return pieces


def pack_down_kernel(at_ref, down_ref, pair_ref, out_ref):
    first = pair_ref.shape[0]
    out_ref[:first, :] = pair_ref[...]
    for row, column, rows, columns, to, place in down_pieces(*down_ref.shape, out_ref.shape[1]):
        out_ref[first + to : first + to + rows, place : place + columns] = down_ref[
            row : row + rows, column : column + columns
        ]


def pack_down(at, down, pair):
    first, wide = pair.shape
    (out,) = on_chip(
        pack_down_kernel,
        [like(bf16, first + down.size // wide, wide)],
        [at, down, pair],
        0,
        name="pack_down",
    )
    return out


def down_copies(at_ref, block_refs, first, down_ref, sem_ref):
    own = down_ref.shape[0] // len(block_refs)
    pieces = down_pieces(own, down_ref.shape[1], block_refs[0].shape[1])
    copies = []
    for i, block_ref in enumerate(block_refs):
        for k, (row, column, rows, columns, to, place) in enumerate(pieces):
            start = pl.multiple_of(at_ref[i] * own + row, rows)
            copies.append(
                pltpu.make_async_copy(
                    block_ref.at[pl.ds(first + to, rows), pl.ds(place, columns)],
                    down_ref.at[pl.ds(start, rows), pl.ds(column, columns)],
                    sem_ref.at[i * len(pieces) + k],
                )
            )
    return copies


def feed_forward_kernel(step, at_ref, own_ref, other_ref, d_own_ref, d_other_ref, *refs):
    blocks = refs[:-12]
    n_ref, d_out_ref, hidden_ref, d_both_ref, kept_ref, away_ref = refs[-12:-6]
    d_n_ref, d_hidden_ref, whole_ref, down_ref, sem_ref, down_sem_ref = refs[-6:]
    ff = hidden_ref.shape[1]
    first = whole_ref.shape[0] // len(blocks)
    down = down_copies(at_ref, blocks, first, down_ref, down_sem_ref)
    whole = block_copies(at_ref, blocks, whole_ref, sem_ref)
    for copy in down + whole:
        copy.start()
    join_rows(at_ref, len(blocks), own_ref, other_ref, n_ref)
    join_rows(at_ref, len(blocks), d_own_ref, d_other_ref, d_out_ref)
    for copy in down:
        copy.wait()
    d_hidden_ref[...] = dot_at(d_out_ref[...], down_ref[...], 1, 1).astype(bf16)
    for copy in whole:
        copy.wait()
    for begin in range(0, n_ref.shape[0], step):
        rows = slice(begin, begin + step)
        d_hidden = d_hidden_ref[rows, :].astype(f32)
        both = dot_at(n_ref[rows, :], whole_ref[...], 1, 0)
        gate = both[:, :ff]
        upper = both[:, ff:]
        sigma = 1.0 / (1.0 + jnp.exp(-gate))
        silu = gate * sigma
        hidden_ref[rows, :] = (silu * upper).astype(bf16)
        d_both_ref[rows, :ff] = (d_hidden * upper * (sigma + silu * (1.0 - sigma))).astype(bf16)
        d_both_ref[rows, ff:] = (d_hidden * silu).astype(bf16)
        d_n_ref[rows, :] = dot_at(d_both_ref[rows, :], whole_ref[...], 1, 1)
    part_rows(at_ref, len(blocks), d_n_ref, kept_ref, away_ref)


def feed_forward(at, own, other, d_own, d_other, blocks, ff):
    _, rows, width = own.shape
    count = len(blocks)
    pieces = len(down_pieces(ff // count, width, 2 * ff))
    return on_chip(
        functools.partial(feed_forward_kernel, min(256, 4 * rows)),
        [
            like(bf16, 4 * rows, width),
            like(bf16, 4 * rows, width),
            like(bf16, 4 * rows, ff),
            like(bf16, 4 * rows, 2 * ff),
            like(f32, 2, rows, width),
            like(bf16, 2, rows, width),
        ],
        [at, own, other, d_own, d_other],
        40 * rows * width * ff,
        blocks=blocks,
        scratch=[
            pltpu.VMEM((4 * rows, width), f32),
            pltpu.VMEM((4 * rows, ff), bf16),
            pltpu.VMEM((width, 2 * ff), bf16),
            pltpu.VMEM((ff, width), bf16),
            pltpu.SemaphoreType.DMA((count,)),
            pltpu.SemaphoreType.DMA((count * pieces,)),
        ],
        name="feed_forward",
        room=40,
    )


def feed_forward_grads_kernel(at_ref, n_ref, d_both_ref, hidden_ref, d_out_ref, grad_ref):
    count, _, wide = grad_ref.shape
    block = n_ref.shape[1] // count
    own = hidden_ref.shape[1] // count
    for position in range(count):
        place = at_ref[count + position]
        columns = slice(position * block, (position + 1) * block)
        grad_ref[place, :block, :] = dot_at(n_ref[:, columns], d_both_ref[...], 0, 0).astype(bf16)
        columns = slice(position * own, (position + 1) * own)
        down = dot_at(hidden_ref[:, columns], d_out_ref[...], 0, 0).astype(bf16)
        for row, column, rows, width, to, start in down_pieces(own, n_ref.shape[1], wide):
            grad_ref[place, block + to : block + to + rows, start : start + width] = down[
                row : row + rows, column : column + width
            ]


def feed_forward_grads(at, n, d_both, hidden, d_out, count):
    rows, width = n.shape
    ff = hidden.shape[1]
    (out,) = on_chip(
        feed_forward_grads_kernel,
        [like(bf16, count, width // count + ff // count * width // (2 * ff), 2 * ff)],
        [at, n, d_both, hidden, d_out],
        6 * rows * width * ff,
        name="feed_forward_grads",
        room=32,
    )
    return out


def joined_grads_kernel(at_ref, left_ref, right_ref, grad_ref):
    count, block, _ = grad_ref.shape
    for position in range(count):
        rows = slice(position * block, (position + 1) * block)
        grad_ref[at_ref[count + position]] = dot_at(
            left_ref[rows, :], right_ref[...], 1, 0
        ).astype(bf16)


def joined_grads(at, left, right, count):
    width, rows = left.shape
    (out,) = on_chip(
        joined_grads_kernel,
        [like(bf16, count, width // count, right.shape[1])],
        [at, left, right],
        2 * rows * width * right.shape[1],
        name="joined_grads",
    )
    return out


def split_heads_kernel(at_ref, own_ref, other_ref, weight_ref, d_mid_ref, heads_ref):
    join_rows(at_ref, heads_ref.shape[0] // 2, own_ref, other_ref, d_mid_ref)
    size, rows = heads_ref.shape[1:]
    for seq in range(2):
        part = dot_at(weight_ref[...], d_mid_ref[seq * rows : (seq + 1) * rows, :], 1, 1)
        part = part.astype(bf16)
        for head in range(heads_ref.shape[0] // 2):
            heads_ref[2 * head + seq] = part[head * size : (head + 1) * size, :]


def split_heads(at, own, other, weight, heads):
    _, rows, width = own.shape
    return on_chip(
        split_heads_kernel,
        [
            like(bf16, 4 * rows, width),
            like(bf16, 2 * heads, weight.shape[0] // heads, 2 * rows),
        ],
        [at, own, other, weight],
        8 * rows * width * weight.shape[0],
        name="split_heads",
    )


def heads_grad_kernel(at_ref, joined_ref, *refs):
    blocks, (grad_ref, n_ref, sem_ref) = refs[:-3], refs[-3:]
    copies = sequence_copies(at_ref, blocks, n_ref, sem_ref)
    for copy in copies:
        copy.start()
    for copy in copies:
        copy.wait()
    grad_ref[...] = dot_at(n_ref[...], joined_ref[...], 0, 1).astype(bf16)


def heads_grad(at, joined, blocks):
    columns, tokens = joined.shape
    width = blocks[0].shape[1]
    (out,) = on_chip(
        heads_grad_kernel,
        [like(bf16, width, columns)],
        [at, joined],
        2 * tokens * width * columns,
        blocks=blocks,
        scratch=[pltpu.VMEM((tokens, width), bf16), pltpu.SemaphoreType.DMA((2 * len(blocks),))],
        name="heads_grad",
    )
    return out


def heads_input_kernel(at_ref, joined_ref, weight_ref, out_ref):
    count, rows, _ = out_ref.shape
    for position in range(count):
        columns = slice(position * rows, (position + 1) * rows)
        out_ref[at_ref[count + position]] = dot_at(
            joined_ref[:, columns], weight_ref[...], 0, 1
        ).astype(bf16)


def heads_input(at, joined, weight, count):
    width, columns = weight.shape
    tokens = joined.shape[1]
    (out,) = on_chip(
        heads_input_kernel,
        [like(bf16, count, tokens // count, width)],
        [at, joined, weight],
        2 * tokens * width * columns,
        name="heads_input",
    )
    return out


def input_rows_kernel(count, at_ref, kept_ref, other_ref, rows_ref, d_middle_ref, out_ref):
    core = at_ref[2 * count]
    kept = kept_ref[...]
    other = other_ref[...].astype(f32)
    first = jnp.where(core == 0, kept, other)
    second = jnp.where(core == 0, other, kept)
    size = kept.shape[1] // count
    pieces = []
    for i in range(count):
        pieces.append(first[:, i * size : (i + 1) * size])
        pieces.append(second[:, i * size : (i + 1) * size])
    d_normed = jnp.concatenate(pieces, axis=1)
    rows = rows_ref[...].astype(f32)
    inverse = lax.rsqrt(jnp.mean(rows * rows, axis=-1, keepdims=True) + norm_eps)
    normed = rows * inverse
    mean = jnp.mean(d_normed * normed, axis=-1, keepdims=True)
    out_ref[...] = d_middle_ref[...] + inverse * (d_normed - normed * mean)


def input_rows(at, kept, other, rows, d_middle, count):
    (out,) = on_chip(
        functools.partial(input_rows_kernel, count),
        [like(f32, *rows.shape)],
        [at, kept, other, rows, d_middle],
        8 * rows.size,
        name="input_rows",
    )
    return out


def layer_output_kernel(first, at_ref, hidden_ref, *refs):
    blocks, (kept_ref, away_ref, out_ref, down_ref, sem_ref) = refs[:-5], refs[-5:]
    copies = down_copies(at_ref, blocks, first, down_ref, sem_ref)
    for copy in copies:
        copy.start()
    for copy in copies:
        copy.wait()
    out_ref[...] = dot_at(hidden_ref[...], down_ref[...], 1, 0)
    part_rows(at_ref, len(blocks), out_ref, kept_ref, away_ref)


def layer_output(at, hidden, blocks, first, width):
    ff = hidden.shape[1]
    rows = hidden.shape[0] // 4
    count = len(blocks)
    pieces = len(down_pieces(ff // count, width, 2 * ff))
    return on_chip(
        functools.partial(layer_output_kernel, first),
        [like(f32, 2, rows, width), like(bf16, 2, rows, width)],
        [at, hidden],
        0,
        blocks=blocks,
        scratch=[
            pltpu.VMEM((4 * rows, width), f32),
            pltpu.VMEM((ff, width), bf16),
            pltpu.SemaphoreType.DMA((count * pieces,)),
        ],
        name="layer_output",
    )


def query_rows_kernel(
    at_ref, terms_ref, gain_ref, query_ref, key_ref, value_ref, d_query, d_key, d_value, d_gain
):
    pieces = ([], [], [])
    for group in range(terms_ref.shape[0] // 2):
        part = terms_ref[2 * group].astype(f32) + terms_ref[2 * group + 1].astype(f32)
        pieces[0].append(part[:, : 2 * HEAD_SIZE])
        pieces[1].append(part[:, 2 * HEAD_SIZE : 3 * HEAD_SIZE])
        pieces[2].append(part[:, 3 * HEAD_SIZE :])
    gain = gain_ref[...]
    rows_sum = None
    outs = (d_query, d_key, d_value)
    for pieces_of, weight_ref, out_ref in zip(pieces, (query_ref, key_ref, value_ref), outs):
        grad = jnp.concatenate(pieces_of, axis=1)
        out_ref[...] = gain * grad
        part = jnp.sum(grad * weight_ref[...].astype(f32), axis=1, keepdims=True)
        rows_sum = part if rows_sum is None else rows_sum + part
    d_gain[...] = rows_sum


def query_rows_grads(at, terms, gain, query, key, value):
    own = query.shape[0]
    return on_chip(
        query_rows_kernel,
        [
            like(f32, *query.shape),
            like(f32, *key.shape),
            like(f32, *value.shape),
            like(f32, own, 1),
        ],
        [at, terms, gain, query, key, value],
        terms.size,
        name="query_rows_grads",
    )


def pair_rows_kernel(
    size, count, at_ref, terms_ref, down_terms, gain_ref, gate_ref, up_ref,
    d_gate, d_up, d_gain, d_down,
):
    gain = gain_ref[...]
    core = at_ref[2 * count]
    seq = at_ref[2 * count + 1]
    half = terms_ref.shape[2] // 2
    rows_sum = jnp.zeros_like(gain)
    for side, (weight_ref, out_ref) in enumerate(((gate_ref, d_gate), (up_ref, d_up))):
        for position in range(half // size):
            for t in range(4):
                columns = slice((4 * position + t) * size, (4 * position + t + 1) * size)
                start = side * half + position * size
                block = (core + t // 2) % 2 * 2 + (seq + t % 2) % 2
                grad = terms_ref[block, :, start : start + size].astype(f32)
                out_ref[:, columns] = gain * grad
                rows_sum = rows_sum + jnp.sum(
                    grad * weight_ref[:, columns].astype(f32), axis=1, keepdims=True
                )
    d_gain[...] = rows_sum
    for row, column, rows, columns, to, place in down_pieces(*d_down.shape, down_terms.shape[1]):
        d_down[row : row + rows, column : column + columns] = down_terms[
            to : to + rows, place : place + columns
        ]


def pair_rows_grads(at, terms, down_terms, gain, gate, up, size, count):
    own = gate.shape[0]
    return on_chip(
        functools.partial(pair_rows_kernel, size, count),
        [
            like(f32, *gate.shape),
            like(f32, *up.shape),
            like(f32, own, 1),
            like(f32, size, down_terms.size // size),
        ],
        [at, terms, down_terms, gain, gate, up],
        terms.size,
        name="pair_rows_grads",
    )


ring_axes = ("z", "x")
owner_axes = ("z", "x", "core", "y")
head_axes = ("z", "x", "y")


def ring_of(count):
    order = list(range(0, count, 2)) + list(range(count - 1, 0, -2))
    forward = [(order[i], order[(i + 1) % count]) for i in range(count)]
    backward = [(there, here) for here, there in forward]
    return forward, backward


def place_of(position, count):
    return jnp.where(position % 2 == 0, position // 2, count - (position + 1) // 2)


def position_at(place, count):
    place = lax.rem(place, count)
    return jnp.where(place < count // 2, 2 * place, 2 * (count - place) - 1)


def tie(*values):
    return lax.optimization_barrier(values)


def after(value, *others):
    return lax.optimization_barrier((value,) + others)[0]


class GatherRing:
    def __init__(self, shard, count):
        self.count = count
        self.forward, self.backward = ring_of(count)
        self.parts = [shard] + [None] * (count - 1)
        self.ahead = self.behind = shard
        self.hops = 0

    def start(self, *others):
        self.hops += 1
        ahead, behind = self.ahead, self.behind
        if self.hops == self.count // 2:
            half = ahead.shape[0] // 2
            ahead, behind = ahead[:half], behind[half:]
        if others:
            ahead, behind = lax.optimization_barrier((ahead, behind) + others)[:2]
        self.pending = [
            lax.ppermute(ahead, ring_axes, self.forward),
            lax.ppermute(behind, ring_axes, self.backward),
        ]

    def land(self, arrived):
        self.ahead, self.behind = arrived
        if self.hops == self.count // 2:
            self.parts[self.hops] = jnp.concatenate(arrived, axis=0)
        else:
            self.parts[self.count - self.hops] = self.ahead
            self.parts[self.hops] = self.behind


class ScatterRing:
    def __init__(self, term, count, pieces=1):
        self.count = count
        self.pieces = pieces
        self.term = term
        self.forward, self.backward = ring_of(count)
        self.rows = term.shape[1] // 2
        far = term[count // 2]
        self.ahead, self.behind = far[: self.rows], far[self.rows :]
        self.hops = 0

    def start(self):
        self.hops += 1
        self.pending = [
            lax.ppermute(self.ahead, ring_axes, self.forward),
            lax.ppermute(self.behind, ring_axes, self.backward),
        ]

    def land(self, arrived):
        ahead, behind = (value.astype(f32) for value in arrived)
        left = self.count // 2 - self.hops
        if self.hops == 1:
            edges = ((0, self.rows, 0), (self.rows, 0, 0))
            ahead, behind = (
                lax.pad(value, jnp.float32(0), (edge,) + ((0, 0, 0),) * (value.ndim - 1))
                for value, edge in zip((ahead, behind), (edges[0], edges[1]))
            )
        sides = ((self.term[left], ahead), (self.term[self.count - left], behind))
        if left > 1:
            self.ahead, self.behind = ((t.astype(f32) + v).astype(bf16) for t, v in sides)
            return
        rows = self.term.shape[1]
        self.lasts = []
        for piece in range(self.pieces):
            cut = slice(piece * rows // self.pieces, (piece + 1) * rows // self.pieces)
            ends = [(t[cut].astype(f32) + v[cut]).astype(bf16) for t, v in sides]
            self.lasts.append(LastHop(self, self.term[0, cut], ends))


class LastHop:
    def __init__(self, ring, own, ends):
        self.ring, self.own, self.ends = ring, own, ends

    def start(self):
        ahead, behind = self.ends
        self.pending = [
            lax.ppermute(ahead, ring_axes, self.ring.forward),
            lax.ppermute(behind, ring_axes, self.ring.backward),
        ]

    def land(self, arrived):
        self.total = self.own.astype(f32) + arrived[0].astype(f32) + arrived[1].astype(f32)


def settle(moves, *others):
    moving = tuple(tuple(move.pending) for move in moves)
    out = lax.optimization_barrier((moving, others))
    for move, arrived in zip(moves, out[0]):
        move.land(list(arrived))
    return out[1][0] if len(others) == 1 else out[1]


def swap(values, axis):
    return lax.ppermute(values, axis, [(0, 1), (1, 0)])


def rows_of_group(own):
    pair = lax.all_gather(own, "y", axis=0)
    return lax.all_gather(pair, "core", axis=1)


def core_sum(kept, away):
    return kept + swap(away, "core").astype(f32)


def both_rows_sum(pair):
    return pair + swap(pair.astype(bf16), "y").astype(f32)


def own_rows_sum(pair):
    seq = lax.axis_index("y")
    away = lax.dynamic_index_in_dim(pair, 1 - seq, 0, False).astype(bf16)
    return lax.dynamic_index_in_dim(pair, seq, 0, False) + swap(away, "y").astype(f32)


def own_columns(blocks):
    core = lax.axis_index("core")
    seq = lax.axis_index("y")
    away = lax.dynamic_index_in_dim(blocks, 1 - seq, 1, False)
    kept = lax.dynamic_index_in_dim(blocks, seq, 1, False)
    pair = jnp.stack([kept, swap(away, "y")])
    away = lax.dynamic_index_in_dim(pair, 1 - core, 1, False)
    kept = lax.dynamic_index_in_dim(pair, core, 1, False)
    return jnp.concatenate([kept, swap(away, "core")])


def both_rows(own, *others):
    other = after(swap(own, "y"), *others)
    first = lax.axis_index("y") == 0
    return jnp.stack([jnp.where(first, own, other), jnp.where(first, other, own)])


def all_to_all(values, axes):
    return lax.all_to_all(values, axes, 0, 0, tiled=True)


def inverse_rms(values):
    return lax.rsqrt(jnp.mean(values * values, axis=-1, keepdims=True) + norm_eps)


def head_layer(
    count,
    tokens,
    cotangent,
    norm_gain1,
    w_query,
    key_weight,
    value_weight,
    w_out,
    norm_gain2,
    w_gate,
    w_up,
    w_down,
):
    rows, width = tokens.shape[1:]
    own = w_query.shape[0]
    ff_own = w_down.shape[0]
    half = HEAD_SIZE // 2
    quarter = HEAD_SIZE // 4
    group = 4 * own
    seq_rows = 2 * rows
    length = count * seq_rows
    step = seq_rows

    gain1 = norm_gain1.astype(f32)[:, None]
    gain2 = norm_gain2.astype(f32)[:, None]

    place = place_of(lax.axis_index(ring_axes), count)
    steps = jnp.arange(count, dtype=jnp.int32)
    core = lax.axis_index("core")
    seq = lax.axis_index("y")
    at = jnp.concatenate(
        [
            position_at(place + steps, count),
            lax.rem(place_of(steps, count) - place + count, count),
            jnp.stack([core, seq]).astype(jnp.int32),
        ]
    )

    position = jnp.arange(length, dtype=f32)
    exponent = jnp.arange(half, dtype=f32) * (2.0 / HEAD_SIZE)
    angle = (rope_base ** (-exponent))[:, None] * position[None, :]
    cosine = jnp.cos(angle)
    sine = jnp.sin(angle)

    own_rows = tokens[0].astype(f32)
    n1_kept, n1_away = normed_halves(at, tokens[0], count)
    n1_other = swap(n1_away, "core")
    half_width = width // 2
    n1_ring = GatherRing(
        jnp.concatenate([n1_kept, n1_other, w_out[:, :half_width], w_out[:, half_width:]], axis=0),
        count,
    )
    n1_ring.start()
    head_cols = head_columns(at, gain1, w_query, key_weight, value_weight)
    weight_own = all_to_all(head_cols, ring_axes)
    pair_cols = pair_columns(at, gain2, w_gate, w_up, ff_own)
    head_cols, pair_cols = settle([n1_ring], head_cols, pair_cols)
    n1_ring.start()
    tokens_pair = both_rows(tokens[0], head_cols)
    weight_own, tokens_pair = settle([n1_ring], weight_own, tokens_pair)
    n1_ring.start()
    weight_other = swap(weight_own, "y")
    pair_rows = all_to_all(pair_cols, ("core", "y")).reshape(group, 2 * count * ff_own)
    settle([n1_ring])
    n1_ring.start()
    ff_rows = pack_down(at, w_down, pair_rows)
    ff_rows, weight_other = settle([n1_ring], ff_rows, weight_other)

    gather = GatherRing(ff_rows, count)
    gather.start()
    kept, away, head_weight = project_heads(at, weight_own, weight_other, n1_ring.parts, rows)
    cotangent_pair = both_rows(after(cotangent[0], ff_rows), kept)
    mixed_send, mixed, prob, q, k, v = heads_forward(
        at, kept, swap(away, "core"), cosine, sine, count
    )
    mixed_send, cotangent_pair = settle([gather], mixed_send, cotangent_pair)
    gather.start()
    mixed_low = all_to_all(mixed_send, head_axes)
    cotangent_other = swap(cotangent_pair, "core")
    mixed_low, cotangent_other = settle([gather], mixed_low, cotangent_other)
    gather.start()
    out_weight, mixed_low, kept, away = project_out(at, mixed_low, n1_ring.parts, 2 * rows, own)
    branch = both_rows_sum(core_sum(kept, away))
    branch = settle([gather], branch)
    gather.start()
    inputs = tokens_pair.astype(f32)
    middle = inputs + branch

    r2 = inverse_rms(middle)
    n2_pair = middle * r2
    n2_own = n2_pair.astype(bf16)
    n2_other = swap(n2_own, "core")
    n2_own, n2_other = settle([gather], n2_own, n2_other)
    n2, d_out, hidden, d_both, kept, away = feed_forward(
        at, n2_own, n2_other, cotangent_pair, cotangent_other, gather.parts, count * ff_own
    )
    d_n2 = core_sum(kept, away)
    grads = feed_forward_grads(at, n2, d_both, after(hidden, d_n2), d_out, count)
    d_normed2 = both_rows_sum(d_n2)
    scatter = ScatterRing(grads, count, pieces=2)
    scatter.start()
    d_normed2 = settle([scatter], d_normed2)
    scatter.start()
    d_middle = cotangent_pair.astype(f32) + r2 * (
        d_normed2 - n2_pair * jnp.mean(d_normed2 * n2_pair, axis=-1, keepdims=True)
    )

    d_mid_own = d_middle.astype(bf16)
    d_mid_other = swap(d_mid_own, "core")
    d_mid, d_mixed = split_heads(at, d_mid_own, d_mid_other, out_weight, count)
    d_mixed = all_to_all(d_mixed, head_axes)
    out_grads = joined_grads(at, mixed_low, d_mid, count)
    kept_out, away_out = layer_output(
        at, after(hidden, d_mid), gather.parts, group, width
    )
    d_mixed, out_grads, kept_out, away_out = settle(
        [scatter], d_mixed, out_grads, kept_out, away_out
    )
    out_scatter = ScatterRing(out_grads, count)
    scatter.start()
    out_scatter.start()
    kept, away = heads_backward(at, q, k, v, prob, mixed, d_mixed, cosine, sine, count)
    out_rows = own_rows_sum(core_sum(kept_out, away_out))
    kept, away, out_rows = settle([scatter, out_scatter], kept, away, out_rows)
    early, late = scatter.lasts
    early.start()
    out_scatter.start()
    joined = heads_join(at, kept, swap(away, "core"), count)
    d_n1 = heads_input(at, joined, head_weight, count)
    grad_heads = heads_grad(at, joined, n1_ring.parts)
    d_n1, grad_heads = settle([early, out_scatter], d_n1, grad_heads)
    d_n1_ring = ScatterRing(d_n1, count)
    d_n1_ring.start()
    late.start()
    out_scatter.start()
    grad_heads = all_to_all(grad_heads.reshape(2 * count, own, 4 * HEAD_SIZE), head_axes)
    settle([d_n1_ring])
    d_n1_ring.start()
    grad_heads = settle([late, out_scatter, d_n1_ring], grad_heads)
    d_n1_ring.start()
    (out_last,) = out_scatter.lasts
    out_last.start()
    owned = jnp.concatenate([early.total, late.total], axis=0)
    own_both = own_columns(owned[:group].astype(bf16).reshape(2, 2, own, -1))
    grad_query, grad_key, grad_value, grad_gain1 = query_rows_grads(
        at, grad_heads, gain1, w_query, key_weight, value_weight
    )
    grad_query, own_both = settle([d_n1_ring, out_last], grad_query, own_both)
    (d_n1_last,) = d_n1_ring.lasts
    d_n1_last.start()
    grad_gate, grad_up, grad_gain2, owned_down = pair_rows_grads(
        at, own_both, owned[group:], gain2, w_gate, w_up, ff_own, count
    )
    grad_gate = settle([d_n1_last], grad_gate)
    d_middle_own, middle_own = (
        lax.dynamic_index_in_dim(value, seq, 0, False) for value in (d_middle, middle)
    )
    by_core = d_n1_last.total.reshape(2, rows, half_width)
    other = swap(lax.dynamic_index_in_dim(by_core, 1 - core, 0, False).astype(bf16), "core")
    kept = lax.dynamic_index_in_dim(by_core, core, 0, False)
    input_grad = input_rows(at, kept, other, tokens[0], d_middle_own, count)
    result = middle_own + out_rows
    owned_out = out_last.total
    return (
        result.astype(bf16)[None],
        input_grad[None],
        grad_gain1[:, 0],
        grad_query,
        grad_key,
        grad_value,
        owned_out,
        grad_gain2[:, 0],
        grad_gate,
        grad_up,
        owned_down,
    )


def by_heads(mesh):
    count = mesh.shape["ctx"] // 2
    parts = Mesh(mesh.devices.reshape(count // 2, 2, 2, 2), owner_axes)
    row_spec = P("y", ("z", "x", "core"), None)
    in_specs = (row_spec, row_spec) + (P(owner_axes),) * 9
    out_specs = (row_spec, row_spec) + (P(owner_axes),) * 9
    return jax.shard_map(
        functools.partial(head_layer, count),
        mesh=parts,
        in_specs=in_specs,
        out_specs=out_specs,
        check_vma=False,
    )


def solution(mesh):
    in_specs = (
        P("fsdp", "ctx", None),
        P("fsdp", "ctx", None),
        P(("ctx", "fsdp")),
        P(("ctx", "fsdp"), None),
        P(("ctx", "fsdp"), None),
        P(("ctx", "fsdp"), None),
        P(("ctx", "fsdp"), None),
        P(("ctx", "fsdp")),
        P(("ctx", "fsdp"), None),
        P(("ctx", "fsdp"), None),
        P(("ctx", "fsdp"), None),
    )
    out_specs = (
        P("fsdp", "ctx", None),
        P("fsdp", "ctx", None),
        P(("ctx", "fsdp")),
        P(("ctx", "fsdp"), None),
        P(("ctx", "fsdp"), None),
        P(("ctx", "fsdp"), None),
        P(("ctx", "fsdp"), None),
        P(("ctx", "fsdp")),
        P(("ctx", "fsdp"), None),
        P(("ctx", "fsdp"), None),
        P(("ctx", "fsdp"), None),
    )
    if mesh.shape["ctx"] == QUERY_HEADS and mesh.shape["fsdp"] == 2:
        return by_heads(mesh)
    return jax.shard_map(local, mesh=mesh, in_specs=in_specs, out_specs=out_specs, check_vma=False)
```

```python
import functools

import jax
import jax.numpy as jnp
import numpy as np
from jax import lax
from jax.experimental import pallas as pl
from jax.experimental.pallas import tpu as pltpu
from jax.sharding import Mesh
from jax.sharding import PartitionSpec as P

QUERY_HEADS = 16
KEY_VALUE_HEADS = 8
HEAD_SIZE = 96


rope_base = 100000.0
norm_eps = 1e-05
masked_value = -1e30
key_block = 512


def rms_norm(value_rows, gain):
    return (
        value_rows
        * lax.rsqrt(jnp.mean(value_rows * value_rows, axis=-1, keepdims=True) + norm_eps)
        * gain
    )


def apply_rotary(value_rows, token_position):
    half = value_rows.shape[-1] // 2
    exponent = jnp.arange(half, dtype=jnp.float32) * (2.0 / value_rows.shape[-1])
    freq = rope_base ** (-exponent)
    angle = token_position[:, None] * freq[None, :]
    cosine = jnp.cos(angle)[:, None, :]
    sine = jnp.sin(angle)[:, None, :]
    first = value_rows[..., :half]
    second = value_rows[..., half:]
    return jnp.concatenate(
        [first * cosine - second * sine, second * cosine + first * sine], axis=-1
    )


def matmul(left, right):
    return jnp.dot(left, right, preferred_element_type=jnp.float32)


def key_pieces(key_rows, value_rows, key_value_heads, head_dim):
    count = key_rows.shape[0]
    number = count // key_block
    key_sets = key_rows.reshape(number, key_block, key_value_heads, head_dim)
    value_sets = value_rows.reshape(number, key_block, key_value_heads, head_dim)
    starts = jnp.arange(number, dtype=jnp.int32) * key_block
    return (key_sets, value_sets, starts, key_block)


def fold_keys(carry, key_rows, value_rows, query_rows, query_pos):
    key_value_heads = query_rows.shape[1]
    head_dim = query_rows.shape[3]
    scale = head_dim ** (-0.5)
    key_sets, value_sets, starts, size = key_pieces(key_rows, value_rows, key_value_heads, head_dim)

    def fold_one_piece(state, item):
        key_set, value_set, begin = item

        def fold_live(state):
            top, total, summed = state
            scores = (
                jnp.einsum(
                    "tkgd,skd->kgts", query_rows, key_set, preferred_element_type=jnp.float32
                )
                * scale
            )
            visible = (begin + jnp.arange(size, dtype=jnp.int32))[None, :] <= query_pos[:, None]
            scores = jnp.where(visible, scores, masked_value)
            new_top = jnp.maximum(top, jnp.max(scores, axis=-1))
            weights = jnp.where(visible, jnp.exp(scores - new_top[..., None]), 0.0)
            factor = jnp.exp(top - new_top)
            total = total * factor + jnp.sum(weights, axis=-1)
            summed = summed * factor[..., None] + jnp.einsum(
                "kgts,skd->kgtd",
                weights.astype(jnp.bfloat16),
                value_set,
                preferred_element_type=jnp.float32,
            )
            return (new_top, total, summed)

        def fold_skipped(state):
            return state

        return (lax.cond(begin <= query_pos[-1], fold_live, fold_skipped, state), None)

    carry, _ = lax.scan(fold_one_piece, carry, (key_sets, value_sets, starts))
    return carry


def back_keys(key_rows, value_rows, query_rows, query_pos, d_heads, log_total, delta):
    rows, key_value_heads, groups, head_dim = query_rows.shape
    scale = head_dim ** (-0.5)
    key_sets, value_sets, starts, size = key_pieces(key_rows, value_rows, key_value_heads, head_dim)

    def back_one_piece(d_query, item):
        key_set, value_set, begin = item

        def back_live(d_query):
            scores = (
                jnp.einsum(
                    "tkgd,skd->kgts", query_rows, key_set, preferred_element_type=jnp.float32
                )
                * scale
            )
            visible = (begin + jnp.arange(size, dtype=jnp.int32))[None, :] <= query_pos[:, None]
            prob = jnp.where(visible, jnp.exp(scores - log_total[..., None]), 0.0)
            d_prob = jnp.einsum(
                "tkgd,skd->kgts", d_heads, value_set, preferred_element_type=jnp.float32
            )
            d_scores = (prob * (d_prob - delta[..., None])).astype(jnp.bfloat16)
            d_query = d_query + scale * jnp.einsum(
                "kgts,skd->tkgd", d_scores, key_set, preferred_element_type=jnp.float32
            )
            d_key = scale * jnp.einsum(
                "kgts,tkgd->skd", d_scores, query_rows, preferred_element_type=jnp.float32
            )
            d_value = jnp.einsum(
                "kgts,tkgd->skd",
                prob.astype(jnp.bfloat16),
                d_heads,
                preferred_element_type=jnp.float32,
            )
            return (
                d_query,
                (
                    d_key.reshape(size, key_value_heads * head_dim),
                    d_value.reshape(size, key_value_heads * head_dim),
                ),
            )

        def back_skipped(d_query):
            empty = jnp.zeros((size, key_value_heads * head_dim), jnp.float32)
            return (d_query, (empty, empty))

        return lax.cond(begin <= query_pos[-1], back_live, back_skipped, d_query)

    start_grad = jnp.zeros((rows, key_value_heads, groups, head_dim), jnp.float32)
    d_query, (d_keys, d_values) = lax.scan(
        back_one_piece, start_grad, (key_sets, value_sets, starts)
    )
    return (
        d_query,
        d_keys.reshape(key_rows.shape[0], key_value_heads * head_dim),
        d_values.reshape(key_rows.shape[0], key_value_heads * head_dim),
    )


def local(
    tokens,
    cotangent,
    norm_gain1,
    w_query,
    key_weight,
    value_weight,
    w_out,
    norm_gain2,
    w_gate,
    w_up,
    w_down,
):
    rows = tokens.shape[1]
    key_value_heads = KEY_VALUE_HEADS
    heads = QUERY_HEADS
    head_dim = HEAD_SIZE
    groups = heads // key_value_heads
    first_row = lax.axis_index("ctx") * rows
    query_pos = first_row + jnp.arange(rows, dtype=jnp.int32)
    token_position = query_pos.astype(jnp.float32)
    inputs = tokens[0].astype(jnp.float32)
    gathered = (
        lax.all_gather(norm_gain1, ("ctx", "fsdp"), axis=0, tiled=True),
        lax.all_gather(w_query, ("ctx", "fsdp"), axis=0, tiled=True),
        lax.all_gather(key_weight, ("ctx", "fsdp"), axis=0, tiled=True),
        lax.all_gather(value_weight, ("ctx", "fsdp"), axis=0, tiled=True),
        lax.all_gather(w_out, ("ctx", "fsdp"), axis=0, tiled=True),
        lax.all_gather(norm_gain2, ("ctx", "fsdp"), axis=0, tiled=True),
        lax.all_gather(w_gate, ("ctx", "fsdp"), axis=0, tiled=True),
        lax.all_gather(w_up, ("ctx", "fsdp"), axis=0, tiled=True),
        lax.all_gather(w_down, ("ctx", "fsdp"), axis=0, tiled=True),
    )
    gain_one = gathered[0].astype(jnp.float32)
    gain_two = gathered[5].astype(jnp.float32)
    normed1 = rms_norm(inputs, gain_one).astype(jnp.bfloat16)
    query_pre = matmul(normed1, gathered[1]).reshape(rows, heads, head_dim)
    key_pre = matmul(normed1, gathered[2]).reshape(rows, key_value_heads, head_dim)
    value = matmul(normed1, gathered[3]).astype(jnp.bfloat16)
    query_rows = (
        apply_rotary(query_pre, token_position)
        .astype(jnp.bfloat16)
        .reshape(rows, key_value_heads, groups, head_dim)
    )
    key_rows = (
        apply_rotary(key_pre, token_position)
        .reshape(rows, key_value_heads * head_dim)
        .astype(jnp.bfloat16)
    )
    start_state = (
        jnp.full((key_value_heads, groups, rows), masked_value, jnp.float32),
        jnp.zeros((key_value_heads, groups, rows), jnp.float32),
        jnp.zeros((key_value_heads, groups, rows, head_dim), jnp.float32),
    )
    top, total, summed = fold_keys(
        start_state,
        lax.all_gather(key_rows, "ctx", axis=0, tiled=True),
        lax.all_gather(value, "ctx", axis=0, tiled=True),
        query_rows,
        query_pos,
    )
    mixed_heads = jnp.transpose(summed / total[..., None], (2, 0, 1, 3))
    log_total = top + jnp.log(total)
    mixed_low = mixed_heads.reshape(rows, heads * head_dim).astype(jnp.bfloat16)
    middle = inputs + matmul(mixed_low, gathered[4])
    normed2 = rms_norm(middle, gain_two).astype(jnp.bfloat16)
    gate = matmul(normed2, gathered[6])
    upper = matmul(normed2, gathered[7])
    hidden = (jax.nn.silu(gate) * upper).astype(jnp.bfloat16)
    result = middle + matmul(hidden, gathered[8])
    gathered = (
        lax.all_gather(norm_gain1, ("ctx", "fsdp"), axis=0, tiled=True),
        lax.all_gather(w_query, ("ctx", "fsdp"), axis=0, tiled=True),
        lax.all_gather(key_weight, ("ctx", "fsdp"), axis=0, tiled=True),
        lax.all_gather(value_weight, ("ctx", "fsdp"), axis=0, tiled=True),
        lax.all_gather(w_out, ("ctx", "fsdp"), axis=0, tiled=True),
        lax.all_gather(norm_gain2, ("ctx", "fsdp"), axis=0, tiled=True),
        lax.all_gather(w_gate, ("ctx", "fsdp"), axis=0, tiled=True),
        lax.all_gather(w_up, ("ctx", "fsdp"), axis=0, tiled=True),
        lax.all_gather(w_down, ("ctx", "fsdp"), axis=0, tiled=True),
    )
    incoming = cotangent[0].astype(jnp.float32)
    incoming_low = incoming.astype(jnp.bfloat16)
    grad_down = matmul(hidden.T, incoming_low)
    d_hidden = matmul(incoming_low, gathered[8].T)
    _, swiglu_back = jax.vjp(lambda gate_in, upper_in: jax.nn.silu(gate_in) * upper_in, gate, upper)
    d_gate, d_upper = swiglu_back(d_hidden)
    d_gate = d_gate.astype(jnp.bfloat16)
    d_upper = d_upper.astype(jnp.bfloat16)
    grad_gate = matmul(normed2.T, d_gate)
    grad_up = matmul(normed2.T, d_upper)
    d_normed2 = matmul(d_gate, gathered[6].T) + matmul(d_upper, gathered[7].T)
    _, norm_back2 = jax.vjp(rms_norm, middle, gain_two)
    d_middle, grad_gain2 = norm_back2(d_normed2)
    d_middle = d_middle + incoming
    owned_gain2, owned_gate, owned_up, owned_down = (
        lax.psum_scatter(grad_gain2, ("ctx", "fsdp"), scatter_dimension=0, tiled=True),
        lax.psum_scatter(grad_gate, ("ctx", "fsdp"), scatter_dimension=0, tiled=True),
        lax.psum_scatter(grad_up, ("ctx", "fsdp"), scatter_dimension=0, tiled=True),
        lax.psum_scatter(grad_down, ("ctx", "fsdp"), scatter_dimension=0, tiled=True),
    )
    d_middle_low = d_middle.astype(jnp.bfloat16)
    grad_out = matmul(mixed_low.T, d_middle_low)
    d_mixed = matmul(d_middle_low, gathered[4].T).astype(jnp.bfloat16)
    d_heads = d_mixed.reshape(rows, key_value_heads, groups, head_dim)
    delta = jnp.transpose(jnp.sum(d_heads.astype(jnp.float32) * mixed_heads, axis=-1), (1, 2, 0))
    back_keys_all, back_values_all = (
        lax.all_gather(key_rows, "ctx", axis=0, tiled=True),
        lax.all_gather(value, "ctx", axis=0, tiled=True),
    )
    d_query_rot, d_keys_all, d_values_all = back_keys(
        back_keys_all, back_values_all, query_rows, query_pos, d_heads, log_total, delta
    )
    d_keys_rot, d_value = (
        lax.psum_scatter(d_keys_all, "ctx", scatter_dimension=0, tiled=True),
        lax.psum_scatter(d_values_all, "ctx", scatter_dimension=0, tiled=True),
    )
    _, rotate_back_query = jax.vjp(
        lambda values_in: apply_rotary(values_in, token_position), query_pre
    )
    _, rotate_back_key = jax.vjp(lambda values_in: apply_rotary(values_in, token_position), key_pre)
    d_query = (
        rotate_back_query(d_query_rot.reshape(rows, heads, head_dim))[0]
        .reshape(rows, heads * head_dim)
        .astype(jnp.bfloat16)
    )
    d_key = (
        rotate_back_key(d_keys_rot.reshape(rows, key_value_heads, head_dim))[0]
        .reshape(rows, key_value_heads * head_dim)
        .astype(jnp.bfloat16)
    )
    d_value = d_value.astype(jnp.bfloat16)
    grad_query = matmul(normed1.T, d_query)
    grad_key = matmul(normed1.T, d_key)
    grad_value = matmul(normed1.T, d_value)
    d_normed1 = (
        matmul(d_query, gathered[1].T)
        + matmul(d_key, gathered[2].T)
        + matmul(d_value, gathered[3].T)
    )
    _, norm_back1 = jax.vjp(rms_norm, inputs, gain_one)
    d_inputs, grad_gain1 = norm_back1(d_normed1)
    input_grad = d_inputs + d_middle
    owned_gain1, owned_query, owned_key, owned_value, owned_out = (
        lax.psum_scatter(grad_gain1, ("ctx", "fsdp"), scatter_dimension=0, tiled=True),
        lax.psum_scatter(grad_query, ("ctx", "fsdp"), scatter_dimension=0, tiled=True),
        lax.psum_scatter(grad_key, ("ctx", "fsdp"), scatter_dimension=0, tiled=True),
        lax.psum_scatter(grad_value, ("ctx", "fsdp"), scatter_dimension=0, tiled=True),
        lax.psum_scatter(grad_out, ("ctx", "fsdp"), scatter_dimension=0, tiled=True),
    )
    return (
        result.astype(jnp.bfloat16)[None],
        input_grad[None],
        owned_gain1,
        owned_query,
        owned_key,
        owned_value,
        owned_out,
        owned_gain2,
        owned_gate,
        owned_up,
        owned_down,
    )


bf16 = jnp.bfloat16
f32 = jnp.float32
score_scale = HEAD_SIZE ** (-0.5)
log2_e = 1.4426950408889634
ln_2 = 0.6931471805599453


def dot_at(left, right, left_dim, right_dim):
    return lax.dot_general(
        left, right, (((left_dim,), (right_dim,)), ((), ())), preferred_element_type=jnp.float32
    )


def rotate(values, cosine, sine):
    half = values.shape[0] // 2
    first, second = values[:half], values[half:]
    return jnp.concatenate([first * cosine - second * sine, second * cosine + first * sine], axis=0)


def rotate_back(values, cosine, sine):
    half = values.shape[0] // 2
    first, second = values[:half], values[half:]
    return jnp.concatenate([first * cosine + second * sine, second * cosine - first * sine], axis=0)


def heads_forward_kernel(
    count, at_ref, kept_ref, other_ref, cos_ref, sin_ref,
    send_ref, mixed_ref, prob_ref, q_ref, k_ref, v_ref,
):
    size = q_ref.shape[0]
    half = size // 2
    rows = kept_ref[...] + other_ref[...].astype(f32)
    q = rotate(rows[:size], cos_ref[...], sin_ref[...])
    q_ref[...] = (q * (score_scale * log2_e)).astype(bf16)
    k_ref[...] = rotate(rows[size : 2 * size], cos_ref[...], sin_ref[...]).astype(bf16)
    v_ref[...] = rows[2 * size :].astype(bf16)
    step = send_ref.shape[2]
    offset = 0
    for block in range(count):
        begin = block * step
        end = begin + step
        scores = dot_at(k_ref[:, 0:end], q_ref[:, begin:end], 0, 0)
        key = lax.broadcasted_iota(jnp.int32, (step, step), 0)
        query = lax.broadcasted_iota(jnp.int32, (step, step), 1)
        last = jnp.where(key <= query, scores[begin:end], masked_value)
        top = jnp.max(last, axis=0, keepdims=True)
        if begin:
            top = jnp.maximum(top, jnp.max(scores[:begin], axis=0, keepdims=True))
        last = jnp.exp2(last - top)
        total = jnp.sum(last, axis=0, keepdims=True)
        if begin:
            first = jnp.exp2(scores[:begin] - top)
            total = total + jnp.sum(first, axis=0, keepdims=True)
        inverse = 1.0 / total
        prob_ref[offset + begin : offset + end, :] = (last * inverse).astype(bf16)
        if begin:
            prob_ref[offset : offset + begin, :] = (first * inverse).astype(bf16)
        mixed = dot_at(v_ref[:, 0:end], prob_ref[offset : offset + end, :], 1, 0)
        mixed_ref[:, begin:end] = mixed
        send_ref[2 * block] = mixed[:half].astype(bf16)
        send_ref[2 * block + 1] = mixed[half:].astype(bf16)
        offset += end


def heads_forward(at, kept, other, cosine, sine, count):
    tokens = kept.shape[1]
    size = kept.shape[0] // 3
    step = tokens // count
    pairs = step * count * (count + 1) // 2
    return on_chip(
        functools.partial(heads_forward_kernel, count),
        [
            like(bf16, 2 * count, size // 2, step),
            like(f32, size, tokens),
            like(bf16, pairs, step),
            like(bf16, size, tokens),
            like(bf16, size, tokens),
            like(bf16, size, tokens),
        ],
        [at, kept, other, cosine, sine],
        4 * size * pairs * step,
        name="heads_forward",
        room=32,
    )


def heads_backward_kernel(
    count, at_ref, q_ref, k_ref, v_ref, prob_ref, mixed_ref, back_ref, cos_ref, sin_ref,
    kept_ref, away_ref,
):
    half, step = back_ref.shape[1:]
    size = 2 * half
    d_k_ref = kept_ref.at[size : 2 * size]
    d_v_ref = kept_ref.at[2 * size :]
    offset = 0
    for block in range(count):
        begin = block * step
        end = begin + step
        d_mixed = jnp.concatenate([back_ref[2 * block], back_ref[2 * block + 1]], axis=0)
        delta = jnp.sum(d_mixed.astype(f32) * mixed_ref[:, begin:end], axis=0, keepdims=True)
        prob = prob_ref[offset : offset + end, :]
        d_prob = dot_at(v_ref[:, 0:end], d_mixed, 0, 0)
        d_scores = (prob.astype(f32) * (d_prob - delta)).astype(bf16)
        d_q = dot_at(k_ref[:, 0:end], d_scores, 1, 0) * score_scale
        kept_ref[:size, begin:end] = rotate_back(d_q, cos_ref[:, begin:end], sin_ref[:, begin:end])
        d_v = dot_at(d_mixed, prob, 1, 1)
        d_k = dot_at(q_ref[:, begin:end], d_scores, 1, 1) * ln_2
        if begin:
            d_v_ref[:, 0:begin] += d_v[:, 0:begin]
            d_k_ref[:, 0:begin] += d_k[:, 0:begin]
        d_v_ref[:, begin:end] = d_v[:, begin:end]
        d_k_ref[:, begin:end] = d_k[:, begin:end]
        offset += end
    d_k_ref[...] = rotate_back(d_k_ref[...], cos_ref[...], sin_ref[...])
    away_ref[...] = kept_ref[...].astype(bf16)


def heads_backward(at, q, k, v, prob, mixed, d_mixed, cosine, sine, count):
    size, tokens = q.shape
    return on_chip(
        functools.partial(heads_backward_kernel, count),
        [like(f32, 3 * size, tokens), like(bf16, 3 * size, tokens)],
        [at, q, k, v, prob, mixed, d_mixed, cosine, sine],
        8 * size * prob.size,
        name="heads_backward",
        room=32,
    )


def heads_join_kernel(count, at_ref, kept_ref, other_ref, joined_ref):
    core = at_ref[2 * count]
    size = kept_ref.shape[0] // 3
    joined_ref[pl.ds(pl.multiple_of(core * size, size), size), :] = kept_ref[:size, :].astype(bf16)
    joined_ref[pl.ds(pl.multiple_of((1 - core) * size, size), size), :] = other_ref[:size, :]
    d_kv = kept_ref[size:, :] + other_ref[size:, :].astype(f32)
    joined_ref[2 * size :, :] = d_kv.astype(bf16)


def heads_join(at, kept, other, count):
    size, tokens = kept.shape
    (out,) = on_chip(
        functools.partial(heads_join_kernel, count),
        [like(bf16, size // 3 * 4, tokens)],
        [at, kept, other],
        4 * kept.size,
        name="heads_join",
    )
    return out


def on_chip(kernel, out_shape, args, flops, blocks=(), scratch=(), name=None, room=24):
    moved = sum(a.size * a.dtype.itemsize for a in list(args) + list(blocks))
    moved += sum(o.size * o.dtype.itemsize for o in out_shape)
    near = pl.BlockSpec(memory_space=pltpu.VMEM)
    return pl.pallas_call(
        kernel,
        out_shape=tuple(out_shape),
        in_specs=[pl.BlockSpec(memory_space=pltpu.SMEM)]
        + [near] * (len(args) - 1)
        + [pl.BlockSpec(memory_space=pltpu.HBM)] * len(blocks),
        out_specs=(near,) * len(out_shape),
        scratch_shapes=scratch,
        compiler_params=pltpu.CompilerParams(vmem_limit_bytes=room * 2**20),
        cost_estimate=pl.CostEstimate(flops=flops, bytes_accessed=moved, transcendentals=0),
        name=name,
    )(*args, *blocks)


def like(dtype, *shape):
    return jax.ShapeDtypeStruct(shape, dtype)


def block_copies(at_ref, block_refs, whole_ref, sem_ref, first=0):
    size = whole_ref.shape[0] // len(block_refs)
    copies = []
    for k, block_ref in enumerate(block_refs):
        start = pl.multiple_of(at_ref[k] * size, size)
        copies.append(
            pltpu.make_async_copy(
                block_ref.at[pl.ds(first, size), :], whole_ref.at[pl.ds(start, size), :], sem_ref.at[k]
            )
        )
    return copies


def core_rows(at_ref, count, rows, seq, other):
    core = at_ref[2 * count]
    start = seq * 2 * rows + (1 - core if other else core) * rows
    return pl.ds(pl.multiple_of(start, rows), rows)


def join_rows(at_ref, count, own_ref, other_ref, whole_ref):
    rows = own_ref.shape[1]
    for seq in range(2):
        whole_ref[core_rows(at_ref, count, rows, seq, False), :] = own_ref[seq]
        whole_ref[core_rows(at_ref, count, rows, seq, True), :] = other_ref[seq]


def part_rows(at_ref, count, whole_ref, kept_ref, away_ref):
    rows = kept_ref.shape[1]
    for seq in range(2):
        kept_ref[seq] = whole_ref[core_rows(at_ref, count, rows, seq, False), :]
        away_ref[seq] = whole_ref[core_rows(at_ref, count, rows, seq, True), :].astype(bf16)


def pair_columns_kernel(size, at_ref, gain_ref, gate_ref, up_ref, out_ref):
    gain = gain_ref[...]
    half = out_ref.shape[2] // 2
    for t in range(4):
        for position in range(half // size):
            columns = pl.ds((4 * position + t) * size, size)
            for side, ref in enumerate((gate_ref, up_ref)):
                out_ref[t, :, pl.ds(side * half + position * size, size)] = (
                    ref[:, columns].astype(f32) * gain
                ).astype(bf16)


def pair_columns(at, gain, gate, up, size):
    own, ff = gate.shape
    (out,) = on_chip(
        functools.partial(pair_columns_kernel, size),
        [like(bf16, 4, own, ff // 2)],
        [at, gain, gate, up],
        own * ff,
        name="pair_columns",
    )
    return out


def head_columns_kernel(at_ref, gain_ref, query_ref, key_ref, value_ref, out_ref):
    gain = gain_ref[...]
    query = query_ref[...].astype(f32) * gain
    key = key_ref[...].astype(f32) * gain
    value = value_ref[...].astype(f32) * gain
    for group in range(out_ref.shape[0]):
        shared = slice(group * HEAD_SIZE, (group + 1) * HEAD_SIZE)
        out_ref[group] = jnp.concatenate(
            [
                query[:, 2 * group * HEAD_SIZE : 2 * (group + 1) * HEAD_SIZE],
                key[:, shared],
                value[:, shared],
            ],
            axis=1,
        ).astype(bf16)


def head_columns(at, gain, query, key, value):
    own, width = query.shape
    (out,) = on_chip(
        head_columns_kernel,
        [like(bf16, width // HEAD_SIZE // 2, own, 4 * HEAD_SIZE)],
        [at, gain, query, key, value],
        own * width,
        name="head_columns",
    )
    return out


def normed_halves_kernel(count, at_ref, rows_ref, kept_ref, away_ref):
    core = at_ref[2 * count]
    rows = rows_ref[...].astype(f32)
    mean = jnp.mean(rows * rows, axis=-1, keepdims=True)
    normed = rows * lax.rsqrt(mean + norm_eps)
    size = rows.shape[1] // (2 * count)
    halves = [
        jnp.concatenate(
            [normed[:, (2 * i + c) * size : (2 * i + c + 1) * size] for i in range(count)], axis=1
        )
        for c in range(2)
    ]
    kept_ref[...] = jnp.where(core == 0, halves[0], halves[1]).astype(bf16)
    away_ref[...] = jnp.where(core == 0, halves[1], halves[0]).astype(bf16)


def normed_halves(at, rows, count):
    tokens, width = rows.shape
    return on_chip(
        functools.partial(normed_halves_kernel, count),
        [like(bf16, tokens, width // 2), like(bf16, tokens, width // 2)],
        [at, rows],
        8 * rows.size,
        name="normed_halves",
    )


def sequence_copies(at_ref, block_refs, whole_ref, sem_ref):
    count = len(block_refs)
    core = at_ref[2 * count]
    rows = whole_ref.shape[0] // (2 * count)
    copies = []
    for i, block_ref in enumerate(block_refs):
        for k, side in enumerate((core, 1 - core)):
            start = pl.multiple_of((2 * at_ref[i] + side) * rows, rows)
            copies.append(
                pltpu.make_async_copy(
                    block_ref.at[pl.ds(k * rows, rows), :],
                    whole_ref.at[pl.ds(start, rows), :],
                    sem_ref.at[2 * i + k],
                )
            )
    return copies


def project_heads_kernel(at_ref, own_ref, other_ref, *refs):
    blocks, (kept_ref, away_ref, weight_ref, n_ref, out_ref, sem_ref) = refs[:-6], refs[-6:]
    copies = sequence_copies(at_ref, blocks, n_ref, sem_ref)
    for copy in copies:
        copy.start()
    core = at_ref[2 * len(blocks)]
    seq = at_ref[2 * len(blocks) + 1]
    own = own_ref.shape[1]
    for position in range(len(blocks)):
        for ref, side in ((own_ref, seq), (other_ref, 1 - seq)):
            start = pl.multiple_of((2 * position + side) * own, own)
            weight_ref[pl.ds(start, own), :] = ref[position]
    for copy in copies:
        copy.wait()
    size = kept_ref.shape[0] // 3
    out_ref[...] = dot_at(weight_ref[...], n_ref[...], 0, 1)
    kept_ref[:size, :] = out_ref[pl.ds(pl.multiple_of(core * size, size), size), :]
    kept_ref[size:, :] = out_ref[2 * size :, :]
    there = pl.ds(pl.multiple_of((1 - core) * size, size), size)
    away_ref[:size, :] = out_ref[there, :].astype(bf16)
    away_ref[size:, :] = out_ref[2 * size :, :].astype(bf16)


def project_heads(at, weight_own, weight_other, blocks, rows):
    count = len(blocks)
    _, own, columns = weight_own.shape
    width = 2 * count * own
    tokens = 2 * count * rows
    size = columns // 4
    return on_chip(
        project_heads_kernel,
        [
            like(f32, 3 * size, tokens),
            like(bf16, 3 * size, tokens),
            like(bf16, width, columns),
        ],
        [at, weight_own, weight_other],
        2 * columns * tokens * width,
        blocks=blocks,
        scratch=[
            pltpu.VMEM((tokens, width), bf16),
            pltpu.VMEM((columns, tokens), f32),
            pltpu.SemaphoreType.DMA((2 * count,)),
        ],
        name="project_heads",
    )


def join_heads(heads_ref, joined_ref):
    size, rows = heads_ref.shape[1:]
    for seq in range(2):
        for head in range(heads_ref.shape[0] // 2):
            joined_ref[head * size : (head + 1) * size, seq * rows : (seq + 1) * rows] = heads_ref[
                2 * head + seq
            ]


def project_out_kernel(first, at_ref, heads_ref, *refs):
    blocks, (weight_ref, joined_ref, kept_ref, away_ref, out_ref, sem_ref) = refs[:-6], refs[-6:]
    count = len(blocks)
    own = weight_ref.shape[0] // count
    width = weight_ref.shape[1] // 2
    copies = []
    for i, block_ref in enumerate(blocks):
        start = pl.multiple_of(at_ref[i] * own, own)
        for k in range(2):
            copies.append(
                pltpu.make_async_copy(
                    block_ref.at[pl.ds(first + k * own, own), :],
                    weight_ref.at[pl.ds(start, own), pl.ds(k * width, width)],
                    sem_ref.at[2 * i + k],
                )
            )
    for copy in copies:
        copy.start()
    join_heads(heads_ref, joined_ref)
    for copy in copies:
        copy.wait()
    out_ref[...] = dot_at(joined_ref[...], weight_ref[...], 0, 0)
    part_rows(at_ref, count, out_ref, kept_ref, away_ref)


def project_out(at, heads, blocks, first, own):
    count = len(blocks)
    width = 2 * blocks[0].shape[1]
    rows = heads.shape[2] // 2
    return on_chip(
        functools.partial(project_out_kernel, first),
        [
            like(bf16, count * own, width),
            like(bf16, count * own, 4 * rows),
            like(f32, 2, rows, width),
            like(bf16, 2, rows, width),
        ],
        [at, heads],
        8 * rows * width * count * own,
        blocks=blocks,
        scratch=[pltpu.VMEM((4 * rows, width), f32), pltpu.SemaphoreType.DMA((2 * count,))],
        name="project_out",
    )


def down_pieces(rows, width, wide):
    left = wide // 2
    right = width - left
    pieces = [(i * rows // 2, 0, rows // 2, left, 0, i * left) for i in range(2)]
    parts = wide // right
    size = rows // parts
    pieces += [(i * size, left, size, right, rows // 2, i * right) for i in range(parts)]
    return pieces


def pack_down_kernel(at_ref, down_ref, pair_ref, out_ref):
    first = pair_ref.shape[0]
    out_ref[:first, :] = pair_ref[...]
    for row, column, rows, columns, to, place in down_pieces(*down_ref.shape, out_ref.shape[1]):
        out_ref[first + to : first + to + rows, place : place + columns] = down_ref[
            row : row + rows, column : column + columns
        ]


def pack_down(at, down, pair):
    first, wide = pair.shape
    (out,) = on_chip(
        pack_down_kernel,
        [like(bf16, first + down.size // wide, wide)],
        [at, down, pair],
        0,
        name="pack_down",
    )
    return out


def down_copies(at_ref, block_refs, first, down_ref, sem_ref):
    own = down_ref.shape[0] // len(block_refs)
    pieces = down_pieces(own, down_ref.shape[1], block_refs[0].shape[1])
    copies = []
    for i, block_ref in enumerate(block_refs):
        for k, (row, column, rows, columns, to, place) in enumerate(pieces):
            start = pl.multiple_of(at_ref[i] * own + row, rows)
            copies.append(
                pltpu.make_async_copy(
                    block_ref.at[pl.ds(first + to, rows), pl.ds(place, columns)],
                    down_ref.at[pl.ds(start, rows), pl.ds(column, columns)],
                    sem_ref.at[i * len(pieces) + k],
                )
            )
    return copies


def feed_forward_kernel(step, at_ref, own_ref, other_ref, d_own_ref, d_other_ref, *refs):
    blocks = refs[:-12]
    n_ref, d_out_ref, hidden_ref, d_both_ref, kept_ref, away_ref = refs[-12:-6]
    d_n_ref, d_hidden_ref, whole_ref, down_ref, sem_ref, down_sem_ref = refs[-6:]
    ff = hidden_ref.shape[1]
    first = whole_ref.shape[0] // len(blocks)
    down = down_copies(at_ref, blocks, first, down_ref, down_sem_ref)
    whole = block_copies(at_ref, blocks, whole_ref, sem_ref)
    for copy in down + whole:
        copy.start()
    join_rows(at_ref, len(blocks), own_ref, other_ref, n_ref)
    join_rows(at_ref, len(blocks), d_own_ref, d_other_ref, d_out_ref)
    for copy in down:
        copy.wait()
    d_hidden_ref[...] = dot_at(d_out_ref[...], down_ref[...], 1, 1).astype(bf16)
    for copy in whole:
        copy.wait()
    for begin in range(0, n_ref.shape[0], step):
        rows = slice(begin, begin + step)
        d_hidden = d_hidden_ref[rows, :].astype(f32)
        both = dot_at(n_ref[rows, :], whole_ref[...], 1, 0)
        gate = both[:, :ff]
        upper = both[:, ff:]
        sigma = 1.0 / (1.0 + jnp.exp(-gate))
        silu = gate * sigma
        hidden_ref[rows, :] = (silu * upper).astype(bf16)
        d_both_ref[rows, :ff] = (d_hidden * upper * (sigma + silu * (1.0 - sigma))).astype(bf16)
        d_both_ref[rows, ff:] = (d_hidden * silu).astype(bf16)
        d_n_ref[rows, :] = dot_at(d_both_ref[rows, :], whole_ref[...], 1, 1)
    part_rows(at_ref, len(blocks), d_n_ref, kept_ref, away_ref)


def feed_forward(at, own, other, d_own, d_other, blocks, ff):
    _, rows, width = own.shape
    count = len(blocks)
    pieces = len(down_pieces(ff // count, width, 2 * ff))
    return on_chip(
        functools.partial(feed_forward_kernel, min(256, 4 * rows)),
        [
            like(bf16, 4 * rows, width),
            like(bf16, 4 * rows, width),
            like(bf16, 4 * rows, ff),
            like(bf16, 4 * rows, 2 * ff),
            like(f32, 2, rows, width),
            like(bf16, 2, rows, width),
        ],
        [at, own, other, d_own, d_other],
        40 * rows * width * ff,
        blocks=blocks,
        scratch=[
            pltpu.VMEM((4 * rows, width), f32),
            pltpu.VMEM((4 * rows, ff), bf16),
            pltpu.VMEM((width, 2 * ff), bf16),
            pltpu.VMEM((ff, width), bf16),
            pltpu.SemaphoreType.DMA((count,)),
            pltpu.SemaphoreType.DMA((count * pieces,)),
        ],
        name="feed_forward",
        room=40,
    )


def feed_forward_grads_kernel(at_ref, n_ref, d_both_ref, hidden_ref, d_out_ref, grad_ref):
    count, _, wide = grad_ref.shape
    block = n_ref.shape[1] // count
    own = hidden_ref.shape[1] // count
    for position in range(count):
        place = at_ref[count + position]
        columns = slice(position * block, (position + 1) * block)
        grad_ref[place, :block, :] = dot_at(n_ref[:, columns], d_both_ref[...], 0, 0).astype(bf16)
        columns = slice(position * own, (position + 1) * own)
        down = dot_at(hidden_ref[:, columns], d_out_ref[...], 0, 0).astype(bf16)
        for row, column, rows, width, to, start in down_pieces(own, n_ref.shape[1], wide):
            grad_ref[place, block + to : block + to + rows, start : start + width] = down[
                row : row + rows, column : column + width
            ]


def feed_forward_grads(at, n, d_both, hidden, d_out, count):
    rows, width = n.shape
    ff = hidden.shape[1]
    (out,) = on_chip(
        feed_forward_grads_kernel,
        [like(bf16, count, width // count + ff // count * width // (2 * ff), 2 * ff)],
        [at, n, d_both, hidden, d_out],
        6 * rows * width * ff,
        name="feed_forward_grads",
        room=32,
    )
    return out


def joined_grads_kernel(at_ref, left_ref, right_ref, grad_ref):
    count, block, _ = grad_ref.shape
    for position in range(count):
        rows = slice(position * block, (position + 1) * block)
        grad_ref[at_ref[count + position]] = dot_at(
            left_ref[rows, :], right_ref[...], 1, 0
        ).astype(bf16)


def joined_grads(at, left, right, count):
    width, rows = left.shape
    (out,) = on_chip(
        joined_grads_kernel,
        [like(bf16, count, width // count, right.shape[1])],
        [at, left, right],
        2 * rows * width * right.shape[1],
        name="joined_grads",
    )
    return out


def split_heads_kernel(at_ref, own_ref, other_ref, weight_ref, d_mid_ref, heads_ref):
    join_rows(at_ref, heads_ref.shape[0] // 2, own_ref, other_ref, d_mid_ref)
    size, rows = heads_ref.shape[1:]
    for seq in range(2):
        part = dot_at(weight_ref[...], d_mid_ref[seq * rows : (seq + 1) * rows, :], 1, 1)
        part = part.astype(bf16)
        for head in range(heads_ref.shape[0] // 2):
            heads_ref[2 * head + seq] = part[head * size : (head + 1) * size, :]


def split_heads(at, own, other, weight, heads):
    _, rows, width = own.shape
    return on_chip(
        split_heads_kernel,
        [
            like(bf16, 4 * rows, width),
            like(bf16, 2 * heads, weight.shape[0] // heads, 2 * rows),
        ],
        [at, own, other, weight],
        8 * rows * width * weight.shape[0],
        name="split_heads",
    )


def heads_grad_kernel(at_ref, joined_ref, *refs):
    blocks, (grad_ref, n_ref, sem_ref) = refs[:-3], refs[-3:]
    copies = sequence_copies(at_ref, blocks, n_ref, sem_ref)
    for copy in copies:
        copy.start()
    for copy in copies:
        copy.wait()
    grad_ref[...] = dot_at(n_ref[...], joined_ref[...], 0, 1).astype(bf16)


def heads_grad(at, joined, blocks):
    columns, tokens = joined.shape
    width = blocks[0].shape[1]
    (out,) = on_chip(
        heads_grad_kernel,
        [like(bf16, width, columns)],
        [at, joined],
        2 * tokens * width * columns,
        blocks=blocks,
        scratch=[pltpu.VMEM((tokens, width), bf16), pltpu.SemaphoreType.DMA((2 * len(blocks),))],
        name="heads_grad",
    )
    return out


def heads_input_kernel(at_ref, joined_ref, weight_ref, out_ref):
    count, rows, _ = out_ref.shape
    for position in range(count):
        columns = slice(position * rows, (position + 1) * rows)
        out_ref[at_ref[count + position]] = dot_at(
            joined_ref[:, columns], weight_ref[...], 0, 1
        ).astype(bf16)


def heads_input(at, joined, weight, count):
    width, columns = weight.shape
    tokens = joined.shape[1]
    (out,) = on_chip(
        heads_input_kernel,
        [like(bf16, count, tokens // count, width)],
        [at, joined, weight],
        2 * tokens * width * columns,
        name="heads_input",
    )
    return out


def input_rows_kernel(count, at_ref, kept_ref, other_ref, rows_ref, d_middle_ref, out_ref):
    core = at_ref[2 * count]
    kept = kept_ref[core]
    other = other_ref[...].astype(f32)
    first = jnp.where(core == 0, kept, other)
    second = jnp.where(core == 0, other, kept)
    size = kept.shape[1] // count
    pieces = []
    for i in range(count):
        pieces.append(first[:, i * size : (i + 1) * size])
        pieces.append(second[:, i * size : (i + 1) * size])
    d_normed = jnp.concatenate(pieces, axis=1)
    rows = rows_ref[...].astype(f32)
    inverse = lax.rsqrt(jnp.mean(rows * rows, axis=-1, keepdims=True) + norm_eps)
    normed = rows * inverse
    mean = jnp.mean(d_normed * normed, axis=-1, keepdims=True)
    d_middle = d_middle_ref[at_ref[2 * count + 1]]
    out_ref[...] = d_middle + inverse * (d_normed - normed * mean)


def input_rows(at, kept, other, rows, d_middle, count):
    (out,) = on_chip(
        functools.partial(input_rows_kernel, count),
        [like(f32, *rows.shape)],
        [at, kept, other, rows, d_middle],
        8 * rows.size,
        name="input_rows",
    )
    return out


def layer_output_kernel(first, at_ref, hidden_ref, *refs):
    blocks, (kept_ref, away_ref, out_ref, down_ref, sem_ref) = refs[:-5], refs[-5:]
    copies = down_copies(at_ref, blocks, first, down_ref, sem_ref)
    for copy in copies:
        copy.start()
    for copy in copies:
        copy.wait()
    out_ref[...] = dot_at(hidden_ref[...], down_ref[...], 1, 0)
    part_rows(at_ref, len(blocks), out_ref, kept_ref, away_ref)


def layer_output(at, hidden, blocks, first, width):
    ff = hidden.shape[1]
    rows = hidden.shape[0] // 4
    count = len(blocks)
    pieces = len(down_pieces(ff // count, width, 2 * ff))
    return on_chip(
        functools.partial(layer_output_kernel, first),
        [like(f32, 2, rows, width), like(bf16, 2, rows, width)],
        [at, hidden],
        0,
        blocks=blocks,
        scratch=[
            pltpu.VMEM((4 * rows, width), f32),
            pltpu.VMEM((ff, width), bf16),
            pltpu.SemaphoreType.DMA((count * pieces,)),
        ],
        name="layer_output",
    )


def query_rows_kernel(
    at_ref, terms_ref, gain_ref, query_ref, key_ref, value_ref, d_query, d_key, d_value, d_gain
):
    pieces = ([], [], [])
    for group in range(terms_ref.shape[0] // 2):
        part = terms_ref[2 * group].astype(f32) + terms_ref[2 * group + 1].astype(f32)
        pieces[0].append(part[:, : 2 * HEAD_SIZE])
        pieces[1].append(part[:, 2 * HEAD_SIZE : 3 * HEAD_SIZE])
        pieces[2].append(part[:, 3 * HEAD_SIZE :])
    gain = gain_ref[...]
    rows_sum = None
    outs = (d_query, d_key, d_value)
    for pieces_of, weight_ref, out_ref in zip(pieces, (query_ref, key_ref, value_ref), outs):
        grad = jnp.concatenate(pieces_of, axis=1)
        out_ref[...] = gain * grad
        part = jnp.sum(grad * weight_ref[...].astype(f32), axis=1, keepdims=True)
        rows_sum = part if rows_sum is None else rows_sum + part
    d_gain[...] = rows_sum


def query_rows_grads(at, terms, gain, query, key, value):
    own = query.shape[0]
    return on_chip(
        query_rows_kernel,
        [
            like(f32, *query.shape),
            like(f32, *key.shape),
            like(f32, *value.shape),
            like(f32, own, 1),
        ],
        [at, terms, gain, query, key, value],
        terms.size,
        name="query_rows_grads",
    )


def pair_rows_kernel(
    size, count, at_ref, terms_ref, down_terms, gain_ref, gate_ref, up_ref,
    d_gate, d_up, d_gain, d_down,
):
    gain = gain_ref[...]
    core = at_ref[2 * count]
    seq = at_ref[2 * count + 1]
    half = terms_ref.shape[2] // 2
    rows_sum = jnp.zeros_like(gain)
    for side, (weight_ref, out_ref) in enumerate(((gate_ref, d_gate), (up_ref, d_up))):
        for position in range(half // size):
            for t in range(4):
                columns = slice((4 * position + t) * size, (4 * position + t + 1) * size)
                start = side * half + position * size
                block = (core + t // 2) % 2 * 2 + (seq + t % 2) % 2
                grad = terms_ref[block, :, start : start + size].astype(f32)
                out_ref[:, columns] = gain * grad
                rows_sum = rows_sum + jnp.sum(
                    grad * weight_ref[:, columns].astype(f32), axis=1, keepdims=True
                )
    d_gain[...] = rows_sum
    for row, column, rows, columns, to, place in down_pieces(*d_down.shape, down_terms.shape[1]):
        d_down[row : row + rows, column : column + columns] = down_terms[
            to : to + rows, place : place + columns
        ]


def pair_rows_grads(at, terms, down_terms, gain, gate, up, size, count):
    own = gate.shape[0]
    return on_chip(
        functools.partial(pair_rows_kernel, size, count),
        [
            like(f32, *gate.shape),
            like(f32, *up.shape),
            like(f32, own, 1),
            like(f32, size, down_terms.size // size),
        ],
        [at, terms, down_terms, gain, gate, up],
        terms.size,
        name="pair_rows_grads",
    )


ring_axes = ("z", "x")
owner_axes = ("z", "x", "core", "y")
head_axes = ("z", "x", "y")


def ring_of(count):
    order = list(range(0, count, 2)) + list(range(count - 1, 0, -2))
    forward = [(order[i], order[(i + 1) % count]) for i in range(count)]
    backward = [(there, here) for here, there in forward]
    return forward, backward


def place_of(position, count):
    return jnp.where(position % 2 == 0, position // 2, count - (position + 1) // 2)


def position_at(place, count):
    place = lax.rem(place, count)
    return jnp.where(place < count // 2, 2 * place, 2 * (count - place) - 1)


def tie(*values):
    return lax.optimization_barrier(values)


def after(value, *others):
    return lax.optimization_barrier((value,) + others)[0]


class GatherRing:
    def __init__(self, shard, count):
        self.count = count
        self.forward, self.backward = ring_of(count)
        self.parts = [shard] + [None] * (count - 1)
        self.ahead = self.behind = shard
        self.hops = 0

    def start(self, *others):
        self.hops += 1
        ahead, behind = self.ahead, self.behind
        if self.hops == self.count // 2:
            half = ahead.shape[0] // 2
            ahead, behind = ahead[:half], behind[half:]
        if others:
            ahead, behind = lax.optimization_barrier((ahead, behind) + others)[:2]
        self.pending = [
            lax.ppermute(ahead, ring_axes, self.forward),
            lax.ppermute(behind, ring_axes, self.backward),
        ]

    def land(self, arrived):
        self.ahead, self.behind = arrived
        if self.hops == self.count // 2:
            self.parts[self.hops] = jnp.concatenate(arrived, axis=0)
        else:
            self.parts[self.count - self.hops] = self.ahead
            self.parts[self.hops] = self.behind


class ScatterRing:
    def __init__(self, term, count, pieces=1):
        self.count = count
        self.pieces = pieces
        self.term = term
        self.forward, self.backward = ring_of(count)
        self.rows = term.shape[1] // 2
        far = term[count // 2]
        self.ahead, self.behind = far[: self.rows], far[self.rows :]
        self.hops = 0

    def start(self):
        self.hops += 1
        self.pending = [
            lax.ppermute(self.ahead, ring_axes, self.forward),
            lax.ppermute(self.behind, ring_axes, self.backward),
        ]

    def land(self, arrived):
        ahead, behind = arrived
        left = self.count // 2 - self.hops
        if self.hops == 1:
            rest = ((0, 0, 0),) * (ahead.ndim - 1)
            ahead = lax.pad(ahead, bf16(0), ((0, self.rows, 0),) + rest)
            behind = lax.pad(behind, bf16(0), ((self.rows, 0, 0),) + rest)
        sides = ((self.term[left], ahead), (self.term[self.count - left], behind))
        if left > 1:
            self.ahead, self.behind = (t + v for t, v in sides)
            return
        rows = self.term.shape[1]
        self.lasts = []
        for piece in range(self.pieces):
            cut = slice(piece * rows // self.pieces, (piece + 1) * rows // self.pieces)
            ends = [t[cut] + v[cut] for t, v in sides]
            self.lasts.append(LastHop(self, self.term[0, cut], ends))


class LastHop:
    def __init__(self, ring, own, ends):
        self.ring, self.own, self.ends = ring, own, ends

    def start(self):
        ahead, behind = self.ends
        self.pending = [
            lax.ppermute(ahead, ring_axes, self.ring.forward),
            lax.ppermute(behind, ring_axes, self.ring.backward),
        ]

    def land(self, arrived):
        self.total = self.own.astype(f32) + arrived[0].astype(f32) + arrived[1].astype(f32)


def settle(moves, *others):
    moving = tuple(tuple(move.pending) for move in moves)
    out = lax.optimization_barrier((moving, others))
    for move, arrived in zip(moves, out[0]):
        move.land(list(arrived))
    return out[1][0] if len(others) == 1 else out[1]


def swap(values, axis):
    return lax.ppermute(values, axis, [(0, 1), (1, 0)])


def rows_of_group(own):
    pair = lax.all_gather(own, "y", axis=0)
    return lax.all_gather(pair, "core", axis=1)


def core_sum(kept, away):
    return kept + swap(away, "core").astype(f32)


def both_rows_sum(pair):
    return pair + swap(pair.astype(bf16), "y").astype(f32)


def own_rows_sum(pair):
    seq = lax.axis_index("y")
    away = lax.dynamic_index_in_dim(pair, 1 - seq, 0, False).astype(bf16)
    return lax.dynamic_index_in_dim(pair, seq, 0, False) + swap(away, "y").astype(f32)


def own_columns(blocks):
    core = lax.axis_index("core")
    seq = lax.axis_index("y")
    away = lax.dynamic_index_in_dim(blocks, 1 - seq, 1, False)
    kept = lax.dynamic_index_in_dim(blocks, seq, 1, False)
    pair = jnp.stack([kept, swap(away, "y")])
    away = lax.dynamic_index_in_dim(pair, 1 - core, 1, False)
    kept = lax.dynamic_index_in_dim(pair, core, 1, False)
    return jnp.concatenate([kept, swap(away, "core")])


def both_rows(own, *others):
    other = after(swap(own, "y"), *others)
    first = lax.axis_index("y") == 0
    return jnp.stack([jnp.where(first, own, other), jnp.where(first, other, own)])


def all_to_all(values, axes):
    return lax.all_to_all(values, axes, 0, 0, tiled=True)


def inverse_rms(values):
    return lax.rsqrt(jnp.mean(values * values, axis=-1, keepdims=True) + norm_eps)


def head_layer(
    count,
    tokens,
    cotangent,
    norm_gain1,
    w_query,
    key_weight,
    value_weight,
    w_out,
    norm_gain2,
    w_gate,
    w_up,
    w_down,
):
    rows, width = tokens.shape[1:]
    own = w_query.shape[0]
    ff_own = w_down.shape[0]
    half = HEAD_SIZE // 2
    quarter = HEAD_SIZE // 4
    group = 4 * own
    seq_rows = 2 * rows
    length = count * seq_rows
    step = seq_rows

    gain1 = norm_gain1.astype(f32)[:, None]
    gain2 = norm_gain2.astype(f32)[:, None]

    place = place_of(lax.axis_index(ring_axes), count)
    steps = jnp.arange(count, dtype=jnp.int32)
    core = lax.axis_index("core")
    seq = lax.axis_index("y")
    at = jnp.concatenate(
        [
            position_at(place + steps, count),
            lax.rem(place_of(steps, count) - place + count, count),
            jnp.stack([core, seq]).astype(jnp.int32),
        ]
    )

    position = jnp.arange(length, dtype=f32)
    exponent = jnp.arange(half, dtype=f32) * (2.0 / HEAD_SIZE)
    angle = (rope_base ** (-exponent))[:, None] * position[None, :]
    cosine = jnp.cos(angle)
    sine = jnp.sin(angle)

    own_rows = tokens[0].astype(f32)
    n1_kept, n1_away = normed_halves(at, tokens[0], count)
    n1_other = swap(n1_away, "core")
    half_width = width // 2
    n1_ring = GatherRing(
        jnp.concatenate([n1_kept, n1_other, w_out[:, :half_width], w_out[:, half_width:]], axis=0),
        count,
    )
    n1_ring.start()
    head_cols = head_columns(at, gain1, w_query, key_weight, value_weight)
    weight_own = all_to_all(head_cols, ring_axes)
    pair_cols = pair_columns(at, gain2, w_gate, w_up, ff_own)
    head_cols, pair_cols = settle([n1_ring], head_cols, pair_cols)
    n1_ring.start()
    tokens_pair = both_rows(tokens[0], head_cols)
    weight_own, tokens_pair = settle([n1_ring], weight_own, tokens_pair)
    n1_ring.start()
    weight_other = swap(weight_own, "y")
    pair_rows = all_to_all(pair_cols, ("core", "y")).reshape(group, 2 * count * ff_own)
    pair_rows = settle([n1_ring], pair_rows)
    n1_ring.start()
    ff_rows = pack_down(at, w_down, pair_rows)
    ff_rows = settle([n1_ring], ff_rows)

    gather = GatherRing(ff_rows, count)
    gather.start()
    kept, away, head_weight = project_heads(at, weight_own, weight_other, n1_ring.parts, rows)
    cotangent_pair = both_rows(after(cotangent[0], ff_rows), kept)
    mixed_send, mixed, prob, q, k, v = heads_forward(
        at, kept, swap(away, "core"), cosine, sine, count
    )
    mixed_send, cotangent_pair = settle([gather], mixed_send, cotangent_pair)
    gather.start()
    mixed_low = all_to_all(mixed_send, head_axes)
    cotangent_other = swap(cotangent_pair, "core")
    mixed_low, cotangent_other = settle([gather], mixed_low, cotangent_other)
    gather.start()
    out_weight, mixed_low, kept, away = project_out(at, mixed_low, n1_ring.parts, 2 * rows, own)
    branch = both_rows_sum(core_sum(kept, away))
    branch = settle([gather], branch)
    gather.start()
    inputs = tokens_pair.astype(f32)
    middle = inputs + branch

    r2 = inverse_rms(middle)
    n2_pair = middle * r2
    n2_own = n2_pair.astype(bf16)
    n2_other = swap(n2_own, "core")
    n2_own, n2_other = settle([gather], n2_own, n2_other)
    n2, d_out, hidden, d_both, kept, away = feed_forward(
        at, n2_own, n2_other, cotangent_pair, cotangent_other, gather.parts, count * ff_own
    )
    d_n2 = core_sum(kept, away)
    grads = feed_forward_grads(at, n2, d_both, after(hidden, d_n2), d_out, count)
    d_normed2 = both_rows_sum(d_n2)
    scatter = ScatterRing(grads, count, pieces=2)
    scatter.start()
    d_normed2 = settle([scatter], d_normed2)
    scatter.start()
    d_middle = cotangent_pair.astype(f32) + r2 * (
        d_normed2 - n2_pair * jnp.mean(d_normed2 * n2_pair, axis=-1, keepdims=True)
    )

    d_mid_own = d_middle.astype(bf16)
    d_mid_other = swap(d_mid_own, "core")
    d_mid, d_mixed = split_heads(at, d_mid_own, d_mid_other, out_weight, count)
    d_mixed = all_to_all(d_mixed, head_axes)
    out_grads = joined_grads(at, mixed_low, d_mid, count)
    kept_out, away_out = layer_output(
        at, after(hidden, d_mid), gather.parts, group, width
    )
    d_mixed, out_grads, kept_out, away_out = settle(
        [scatter], d_mixed, out_grads, kept_out, away_out
    )
    out_scatter = ScatterRing(out_grads, count)
    scatter.start()
    out_scatter.start()
    kept, away = heads_backward(at, q, k, v, prob, mixed, d_mixed, cosine, sine, count)
    out_rows = own_rows_sum(core_sum(kept_out, away_out))
    kept, away, out_rows = settle([scatter, out_scatter], kept, away, out_rows)
    early, late = scatter.lasts
    early.start()
    out_scatter.start()
    joined = heads_join(at, kept, swap(away, "core"), count)
    grad_heads = heads_grad(at, joined, n1_ring.parts)
    d_n1 = heads_input(at, after(joined, grad_heads), head_weight, count)
    d_n1_ring = ScatterRing(d_n1, count)
    d_n1_ring.start()
    grad_heads = settle([early, out_scatter, d_n1_ring], grad_heads)
    late.start()
    d_n1_ring.start()
    out_scatter.start()
    grad_heads = settle([late, d_n1_ring, out_scatter], grad_heads)
    d_n1_ring.start()
    (out_last,) = out_scatter.lasts
    out_last.start()
    grad_heads = all_to_all(grad_heads.reshape(2 * count, own, 4 * HEAD_SIZE), head_axes)
    owned = jnp.concatenate([early.total, late.total], axis=0)
    owned = after(owned, d_n1_ring.ahead, d_n1_ring.behind)
    own_both = own_columns(owned[:group].astype(bf16).reshape(2, 2, own, -1))
    own_both = settle([d_n1_ring], own_both)
    (d_n1_last,) = d_n1_ring.lasts
    d_n1_last.start()
    grad_gate, grad_up, grad_gain2, owned_down = pair_rows_grads(
        at, own_both, owned[group:], gain2, w_gate, w_up, ff_own, count
    )
    grad_gate, grad_heads = settle([d_n1_last, out_last], grad_gate, grad_heads)
    grad_query, grad_key, grad_value, grad_gain1 = query_rows_grads(
        at, grad_heads, gain1, w_query, key_weight, value_weight
    )
    by_core = d_n1_last.total.reshape(2, rows, half_width)
    other = swap(lax.dynamic_index_in_dim(by_core, 1 - core, 0, False).astype(bf16), "core")
    input_grad = input_rows(at, by_core, other, tokens[0], d_middle, count)
    result = lax.dynamic_index_in_dim(middle, seq, 0, False) + out_rows
    owned_out = out_last.total
    return (
        result.astype(bf16)[None],
        input_grad[None],
        grad_gain1[:, 0],
        grad_query,
        grad_key,
        grad_value,
        owned_out,
        grad_gain2[:, 0],
        grad_gate,
        grad_up,
        owned_down,
    )


def by_heads(mesh):
    count = mesh.shape["ctx"] // 2
    parts = Mesh(mesh.devices.reshape(count // 2, 2, 2, 2), owner_axes)
    row_spec = P("y", ("z", "x", "core"), None)
    in_specs = (row_spec, row_spec) + (P(owner_axes),) * 9
    out_specs = (row_spec, row_spec) + (P(owner_axes),) * 9
    return jax.shard_map(
        functools.partial(head_layer, count),
        mesh=parts,
        in_specs=in_specs,
        out_specs=out_specs,
        check_vma=False,
    )


def solution(mesh):
    in_specs = (
        P("fsdp", "ctx", None),
        P("fsdp", "ctx", None),
        P(("ctx", "fsdp")),
        P(("ctx", "fsdp"), None),
        P(("ctx", "fsdp"), None),
        P(("ctx", "fsdp"), None),
        P(("ctx", "fsdp"), None),
        P(("ctx", "fsdp")),
        P(("ctx", "fsdp"), None),
        P(("ctx", "fsdp"), None),
        P(("ctx", "fsdp"), None),
    )
    out_specs = (
        P("fsdp", "ctx", None),
        P("fsdp", "ctx", None),
        P(("ctx", "fsdp")),
        P(("ctx", "fsdp"), None),
        P(("ctx", "fsdp"), None),
        P(("ctx", "fsdp"), None),
        P(("ctx", "fsdp"), None),
        P(("ctx", "fsdp")),
        P(("ctx", "fsdp"), None),
        P(("ctx", "fsdp"), None),
        P(("ctx", "fsdp"), None),
    )
    if mesh.shape["ctx"] == QUERY_HEADS and mesh.shape["fsdp"] == 2:
        return by_heads(mesh)
    return jax.shard_map(local, mesh=mesh, in_specs=in_specs, out_specs=out_specs, check_vma=False)
```

```python
import functools

import jax
import jax.numpy as jnp
import numpy as np
from jax import lax
from jax.experimental import pallas as pl
from jax.experimental.pallas import tpu as pltpu
from jax.sharding import Mesh
from jax.sharding import PartitionSpec as P

QUERY_HEADS = 16
KEY_VALUE_HEADS = 8
HEAD_SIZE = 96


rope_base = 100000.0
norm_eps = 1e-05
masked_value = -1e30
key_block = 512


def rms_norm(value_rows, gain):
    return (
        value_rows
        * lax.rsqrt(jnp.mean(value_rows * value_rows, axis=-1, keepdims=True) + norm_eps)
        * gain
    )


def apply_rotary(value_rows, token_position):
    half = value_rows.shape[-1] // 2
    exponent = jnp.arange(half, dtype=jnp.float32) * (2.0 / value_rows.shape[-1])
    freq = rope_base ** (-exponent)
    angle = token_position[:, None] * freq[None, :]
    cosine = jnp.cos(angle)[:, None, :]
    sine = jnp.sin(angle)[:, None, :]
    first = value_rows[..., :half]
    second = value_rows[..., half:]
    return jnp.concatenate(
        [first * cosine - second * sine, second * cosine + first * sine], axis=-1
    )


def matmul(left, right):
    return jnp.dot(left, right, preferred_element_type=jnp.float32)


def key_pieces(key_rows, value_rows, key_value_heads, head_dim):
    count = key_rows.shape[0]
    number = count // key_block
    key_sets = key_rows.reshape(number, key_block, key_value_heads, head_dim)
    value_sets = value_rows.reshape(number, key_block, key_value_heads, head_dim)
    starts = jnp.arange(number, dtype=jnp.int32) * key_block
    return (key_sets, value_sets, starts, key_block)


def fold_keys(carry, key_rows, value_rows, query_rows, query_pos):
    key_value_heads = query_rows.shape[1]
    head_dim = query_rows.shape[3]
    scale = head_dim ** (-0.5)
    key_sets, value_sets, starts, size = key_pieces(key_rows, value_rows, key_value_heads, head_dim)

    def fold_one_piece(state, item):
        key_set, value_set, begin = item

        def fold_live(state):
            top, total, summed = state
            scores = (
                jnp.einsum(
                    "tkgd,skd->kgts", query_rows, key_set, preferred_element_type=jnp.float32
                )
                * scale
            )
            visible = (begin + jnp.arange(size, dtype=jnp.int32))[None, :] <= query_pos[:, None]
            scores = jnp.where(visible, scores, masked_value)
            new_top = jnp.maximum(top, jnp.max(scores, axis=-1))
            weights = jnp.where(visible, jnp.exp(scores - new_top[..., None]), 0.0)
            factor = jnp.exp(top - new_top)
            total = total * factor + jnp.sum(weights, axis=-1)
            summed = summed * factor[..., None] + jnp.einsum(
                "kgts,skd->kgtd",
                weights.astype(jnp.bfloat16),
                value_set,
                preferred_element_type=jnp.float32,
            )
            return (new_top, total, summed)

        def fold_skipped(state):
            return state

        return (lax.cond(begin <= query_pos[-1], fold_live, fold_skipped, state), None)

    carry, _ = lax.scan(fold_one_piece, carry, (key_sets, value_sets, starts))
    return carry


def back_keys(key_rows, value_rows, query_rows, query_pos, d_heads, log_total, delta):
    rows, key_value_heads, groups, head_dim = query_rows.shape
    scale = head_dim ** (-0.5)
    key_sets, value_sets, starts, size = key_pieces(key_rows, value_rows, key_value_heads, head_dim)

    def back_one_piece(d_query, item):
        key_set, value_set, begin = item

        def back_live(d_query):
            scores = (
                jnp.einsum(
                    "tkgd,skd->kgts", query_rows, key_set, preferred_element_type=jnp.float32
                )
                * scale
            )
            visible = (begin + jnp.arange(size, dtype=jnp.int32))[None, :] <= query_pos[:, None]
            prob = jnp.where(visible, jnp.exp(scores - log_total[..., None]), 0.0)
            d_prob = jnp.einsum(
                "tkgd,skd->kgts", d_heads, value_set, preferred_element_type=jnp.float32
            )
            d_scores = (prob * (d_prob - delta[..., None])).astype(jnp.bfloat16)
            d_query = d_query + scale * jnp.einsum(
                "kgts,skd->tkgd", d_scores, key_set, preferred_element_type=jnp.float32
            )
            d_key = scale * jnp.einsum(
                "kgts,tkgd->skd", d_scores, query_rows, preferred_element_type=jnp.float32
            )
            d_value = jnp.einsum(
                "kgts,tkgd->skd",
                prob.astype(jnp.bfloat16),
                d_heads,
                preferred_element_type=jnp.float32,
            )
            return (
                d_query,
                (
                    d_key.reshape(size, key_value_heads * head_dim),
                    d_value.reshape(size, key_value_heads * head_dim),
                ),
            )

        def back_skipped(d_query):
            empty = jnp.zeros((size, key_value_heads * head_dim), jnp.float32)
            return (d_query, (empty, empty))

        return lax.cond(begin <= query_pos[-1], back_live, back_skipped, d_query)

    start_grad = jnp.zeros((rows, key_value_heads, groups, head_dim), jnp.float32)
    d_query, (d_keys, d_values) = lax.scan(
        back_one_piece, start_grad, (key_sets, value_sets, starts)
    )
    return (
        d_query,
        d_keys.reshape(key_rows.shape[0], key_value_heads * head_dim),
        d_values.reshape(key_rows.shape[0], key_value_heads * head_dim),
    )


def local(
    tokens,
    cotangent,
    norm_gain1,
    w_query,
    key_weight,
    value_weight,
    w_out,
    norm_gain2,
    w_gate,
    w_up,
    w_down,
):
    rows = tokens.shape[1]
    key_value_heads = KEY_VALUE_HEADS
    heads = QUERY_HEADS
    head_dim = HEAD_SIZE
    groups = heads // key_value_heads
    first_row = lax.axis_index("ctx") * rows
    query_pos = first_row + jnp.arange(rows, dtype=jnp.int32)
    token_position = query_pos.astype(jnp.float32)
    inputs = tokens[0].astype(jnp.float32)
    gathered = (
        lax.all_gather(norm_gain1, ("ctx", "fsdp"), axis=0, tiled=True),
        lax.all_gather(w_query, ("ctx", "fsdp"), axis=0, tiled=True),
        lax.all_gather(key_weight, ("ctx", "fsdp"), axis=0, tiled=True),
        lax.all_gather(value_weight, ("ctx", "fsdp"), axis=0, tiled=True),
        lax.all_gather(w_out, ("ctx", "fsdp"), axis=0, tiled=True),
        lax.all_gather(norm_gain2, ("ctx", "fsdp"), axis=0, tiled=True),
        lax.all_gather(w_gate, ("ctx", "fsdp"), axis=0, tiled=True),
        lax.all_gather(w_up, ("ctx", "fsdp"), axis=0, tiled=True),
        lax.all_gather(w_down, ("ctx", "fsdp"), axis=0, tiled=True),
    )
    gain_one = gathered[0].astype(jnp.float32)
    gain_two = gathered[5].astype(jnp.float32)
    normed1 = rms_norm(inputs, gain_one).astype(jnp.bfloat16)
    query_pre = matmul(normed1, gathered[1]).reshape(rows, heads, head_dim)
    key_pre = matmul(normed1, gathered[2]).reshape(rows, key_value_heads, head_dim)
    value = matmul(normed1, gathered[3]).astype(jnp.bfloat16)
    query_rows = (
        apply_rotary(query_pre, token_position)
        .astype(jnp.bfloat16)
        .reshape(rows, key_value_heads, groups, head_dim)
    )
    key_rows = (
        apply_rotary(key_pre, token_position)
        .reshape(rows, key_value_heads * head_dim)
        .astype(jnp.bfloat16)
    )
    start_state = (
        jnp.full((key_value_heads, groups, rows), masked_value, jnp.float32),
        jnp.zeros((key_value_heads, groups, rows), jnp.float32),
        jnp.zeros((key_value_heads, groups, rows, head_dim), jnp.float32),
    )
    top, total, summed = fold_keys(
        start_state,
        lax.all_gather(key_rows, "ctx", axis=0, tiled=True),
        lax.all_gather(value, "ctx", axis=0, tiled=True),
        query_rows,
        query_pos,
    )
    mixed_heads = jnp.transpose(summed / total[..., None], (2, 0, 1, 3))
    log_total = top + jnp.log(total)
    mixed_low = mixed_heads.reshape(rows, heads * head_dim).astype(jnp.bfloat16)
    middle = inputs + matmul(mixed_low, gathered[4])
    normed2 = rms_norm(middle, gain_two).astype(jnp.bfloat16)
    gate = matmul(normed2, gathered[6])
    upper = matmul(normed2, gathered[7])
    hidden = (jax.nn.silu(gate) * upper).astype(jnp.bfloat16)
    result = middle + matmul(hidden, gathered[8])
    gathered = (
        lax.all_gather(norm_gain1, ("ctx", "fsdp"), axis=0, tiled=True),
        lax.all_gather(w_query, ("ctx", "fsdp"), axis=0, tiled=True),
        lax.all_gather(key_weight, ("ctx", "fsdp"), axis=0, tiled=True),
        lax.all_gather(value_weight, ("ctx", "fsdp"), axis=0, tiled=True),
        lax.all_gather(w_out, ("ctx", "fsdp"), axis=0, tiled=True),
        lax.all_gather(norm_gain2, ("ctx", "fsdp"), axis=0, tiled=True),
        lax.all_gather(w_gate, ("ctx", "fsdp"), axis=0, tiled=True),
        lax.all_gather(w_up, ("ctx", "fsdp"), axis=0, tiled=True),
        lax.all_gather(w_down, ("ctx", "fsdp"), axis=0, tiled=True),
    )
    incoming = cotangent[0].astype(jnp.float32)
    incoming_low = incoming.astype(jnp.bfloat16)
    grad_down = matmul(hidden.T, incoming_low)
    d_hidden = matmul(incoming_low, gathered[8].T)
    _, swiglu_back = jax.vjp(lambda gate_in, upper_in: jax.nn.silu(gate_in) * upper_in, gate, upper)
    d_gate, d_upper = swiglu_back(d_hidden)
    d_gate = d_gate.astype(jnp.bfloat16)
    d_upper = d_upper.astype(jnp.bfloat16)
    grad_gate = matmul(normed2.T, d_gate)
    grad_up = matmul(normed2.T, d_upper)
    d_normed2 = matmul(d_gate, gathered[6].T) + matmul(d_upper, gathered[7].T)
    _, norm_back2 = jax.vjp(rms_norm, middle, gain_two)
    d_middle, grad_gain2 = norm_back2(d_normed2)
    d_middle = d_middle + incoming
    owned_gain2, owned_gate, owned_up, owned_down = (
        lax.psum_scatter(grad_gain2, ("ctx", "fsdp"), scatter_dimension=0, tiled=True),
        lax.psum_scatter(grad_gate, ("ctx", "fsdp"), scatter_dimension=0, tiled=True),
        lax.psum_scatter(grad_up, ("ctx", "fsdp"), scatter_dimension=0, tiled=True),
        lax.psum_scatter(grad_down, ("ctx", "fsdp"), scatter_dimension=0, tiled=True),
    )
    d_middle_low = d_middle.astype(jnp.bfloat16)
    grad_out = matmul(mixed_low.T, d_middle_low)
    d_mixed = matmul(d_middle_low, gathered[4].T).astype(jnp.bfloat16)
    d_heads = d_mixed.reshape(rows, key_value_heads, groups, head_dim)
    delta = jnp.transpose(jnp.sum(d_heads.astype(jnp.float32) * mixed_heads, axis=-1), (1, 2, 0))
    back_keys_all, back_values_all = (
        lax.all_gather(key_rows, "ctx", axis=0, tiled=True),
        lax.all_gather(value, "ctx", axis=0, tiled=True),
    )
    d_query_rot, d_keys_all, d_values_all = back_keys(
        back_keys_all, back_values_all, query_rows, query_pos, d_heads, log_total, delta
    )
    d_keys_rot, d_value = (
        lax.psum_scatter(d_keys_all, "ctx", scatter_dimension=0, tiled=True),
        lax.psum_scatter(d_values_all, "ctx", scatter_dimension=0, tiled=True),
    )
    _, rotate_back_query = jax.vjp(
        lambda values_in: apply_rotary(values_in, token_position), query_pre
    )
    _, rotate_back_key = jax.vjp(lambda values_in: apply_rotary(values_in, token_position), key_pre)
    d_query = (
        rotate_back_query(d_query_rot.reshape(rows, heads, head_dim))[0]
        .reshape(rows, heads * head_dim)
        .astype(jnp.bfloat16)
    )
    d_key = (
        rotate_back_key(d_keys_rot.reshape(rows, key_value_heads, head_dim))[0]
        .reshape(rows, key_value_heads * head_dim)
        .astype(jnp.bfloat16)
    )
    d_value = d_value.astype(jnp.bfloat16)
    grad_query = matmul(normed1.T, d_query)
    grad_key = matmul(normed1.T, d_key)
    grad_value = matmul(normed1.T, d_value)
    d_normed1 = (
        matmul(d_query, gathered[1].T)
        + matmul(d_key, gathered[2].T)
        + matmul(d_value, gathered[3].T)
    )
    _, norm_back1 = jax.vjp(rms_norm, inputs, gain_one)
    d_inputs, grad_gain1 = norm_back1(d_normed1)
    input_grad = d_inputs + d_middle
    owned_gain1, owned_query, owned_key, owned_value, owned_out = (
        lax.psum_scatter(grad_gain1, ("ctx", "fsdp"), scatter_dimension=0, tiled=True),
        lax.psum_scatter(grad_query, ("ctx", "fsdp"), scatter_dimension=0, tiled=True),
        lax.psum_scatter(grad_key, ("ctx", "fsdp"), scatter_dimension=0, tiled=True),
        lax.psum_scatter(grad_value, ("ctx", "fsdp"), scatter_dimension=0, tiled=True),
        lax.psum_scatter(grad_out, ("ctx", "fsdp"), scatter_dimension=0, tiled=True),
    )
    return (
        result.astype(jnp.bfloat16)[None],
        input_grad[None],
        owned_gain1,
        owned_query,
        owned_key,
        owned_value,
        owned_out,
        owned_gain2,
        owned_gate,
        owned_up,
        owned_down,
    )


bf16 = jnp.bfloat16
f32 = jnp.float32
score_scale = HEAD_SIZE ** (-0.5)
log2_e = 1.4426950408889634
ln_2 = 0.6931471805599453


def dot_at(left, right, left_dim, right_dim):
    return lax.dot_general(
        left, right, (((left_dim,), (right_dim,)), ((), ())), preferred_element_type=jnp.float32
    )


def rotate(values, cosine, sine):
    half = values.shape[0] // 2
    first, second = values[:half], values[half:]
    return jnp.concatenate([first * cosine - second * sine, second * cosine + first * sine], axis=0)


def rotate_back(values, cosine, sine):
    half = values.shape[0] // 2
    first, second = values[:half], values[half:]
    return jnp.concatenate([first * cosine + second * sine, second * cosine - first * sine], axis=0)


def heads_forward_kernel(
    count, at_ref, kept_ref, other_ref, cos_ref, sin_ref,
    send_ref, mixed_ref, prob_ref, q_ref, k_ref, v_ref,
):
    size = q_ref.shape[0]
    half = size // 2
    rows = kept_ref[...] + other_ref[...].astype(f32)
    q = rotate(rows[:size], cos_ref[...], sin_ref[...])
    q_ref[...] = (q * (score_scale * log2_e)).astype(bf16)
    k_ref[...] = rotate(rows[size : 2 * size], cos_ref[...], sin_ref[...]).astype(bf16)
    v_ref[...] = rows[2 * size :].astype(bf16)
    step = send_ref.shape[2]
    offset = 0
    for block in range(count):
        begin = block * step
        end = begin + step
        scores = dot_at(k_ref[:, 0:end], q_ref[:, begin:end], 0, 0)
        key = lax.broadcasted_iota(jnp.int32, (step, step), 0)
        query = lax.broadcasted_iota(jnp.int32, (step, step), 1)
        last = jnp.where(key <= query, scores[begin:end], masked_value)
        top = jnp.max(last, axis=0, keepdims=True)
        if begin:
            top = jnp.maximum(top, jnp.max(scores[:begin], axis=0, keepdims=True))
        last = jnp.exp2(last - top)
        total = jnp.sum(last, axis=0, keepdims=True)
        if begin:
            first = jnp.exp2(scores[:begin] - top)
            total = total + jnp.sum(first, axis=0, keepdims=True)
        inverse = 1.0 / total
        prob_ref[offset + begin : offset + end, :] = (last * inverse).astype(bf16)
        if begin:
            prob_ref[offset : offset + begin, :] = (first * inverse).astype(bf16)
        mixed = dot_at(v_ref[:, 0:end], prob_ref[offset : offset + end, :], 1, 0)
        mixed_ref[:, begin:end] = mixed
        send_ref[2 * block] = mixed[:half].astype(bf16)
        send_ref[2 * block + 1] = mixed[half:].astype(bf16)
        offset += end


def heads_forward(at, kept, other, cosine, sine, count):
    tokens = kept.shape[1]
    size = kept.shape[0] // 3
    step = tokens // count
    pairs = step * count * (count + 1) // 2
    return on_chip(
        functools.partial(heads_forward_kernel, count),
        [
            like(bf16, 2 * count, size // 2, step),
            like(f32, size, tokens),
            like(bf16, pairs, step),
            like(bf16, size, tokens),
            like(bf16, size, tokens),
            like(bf16, size, tokens),
        ],
        [at, kept, other, cosine, sine],
        4 * size * pairs * step,
        name="heads_forward",
        room=32,
    )


def heads_backward_kernel(
    count, at_ref, q_ref, k_ref, v_ref, prob_ref, mixed_ref, back_ref, cos_ref, sin_ref,
    kept_ref, away_ref,
):
    half, step = back_ref.shape[1:]
    size = 2 * half
    d_k_ref = kept_ref.at[size : 2 * size]
    d_v_ref = kept_ref.at[2 * size :]
    offset = 0
    for block in range(count):
        begin = block * step
        end = begin + step
        d_mixed = jnp.concatenate([back_ref[2 * block], back_ref[2 * block + 1]], axis=0)
        delta = jnp.sum(d_mixed.astype(f32) * mixed_ref[:, begin:end], axis=0, keepdims=True)
        prob = prob_ref[offset : offset + end, :]
        d_prob = dot_at(v_ref[:, 0:end], d_mixed, 0, 0)
        d_scores = (prob.astype(f32) * (d_prob - delta)).astype(bf16)
        d_q = dot_at(k_ref[:, 0:end], d_scores, 1, 0) * score_scale
        kept_ref[:size, begin:end] = rotate_back(d_q, cos_ref[:, begin:end], sin_ref[:, begin:end])
        d_v = dot_at(d_mixed, prob, 1, 1)
        d_k = dot_at(q_ref[:, begin:end], d_scores, 1, 1) * ln_2
        if begin:
            d_v_ref[:, 0:begin] += d_v[:, 0:begin]
            d_k_ref[:, 0:begin] += d_k[:, 0:begin]
        d_v_ref[:, begin:end] = d_v[:, begin:end]
        d_k_ref[:, begin:end] = d_k[:, begin:end]
        offset += end
    d_k_ref[...] = rotate_back(d_k_ref[...], cos_ref[...], sin_ref[...])
    away_ref[...] = kept_ref[...].astype(bf16)


def heads_backward(at, q, k, v, prob, mixed, d_mixed, cosine, sine, count):
    size, tokens = q.shape
    return on_chip(
        functools.partial(heads_backward_kernel, count),
        [like(f32, 3 * size, tokens), like(bf16, 3 * size, tokens)],
        [at, q, k, v, prob, mixed, d_mixed, cosine, sine],
        8 * size * prob.size,
        name="heads_backward",
        room=32,
    )


def heads_join_kernel(count, at_ref, kept_ref, other_ref, joined_ref):
    core = at_ref[2 * count]
    size = kept_ref.shape[0] // 3
    joined_ref[pl.ds(pl.multiple_of(core * size, size), size), :] = kept_ref[:size, :].astype(bf16)
    joined_ref[pl.ds(pl.multiple_of((1 - core) * size, size), size), :] = other_ref[:size, :]
    d_kv = kept_ref[size:, :] + other_ref[size:, :].astype(f32)
    joined_ref[2 * size :, :] = d_kv.astype(bf16)


def heads_join(at, kept, other, count):
    size, tokens = kept.shape
    (out,) = on_chip(
        functools.partial(heads_join_kernel, count),
        [like(bf16, size // 3 * 4, tokens)],
        [at, kept, other],
        4 * kept.size,
        name="heads_join",
    )
    return out


def on_chip(kernel, out_shape, args, flops, blocks=(), scratch=(), name=None, room=24):
    moved = sum(a.size * a.dtype.itemsize for a in list(args) + list(blocks))
    moved += sum(o.size * o.dtype.itemsize for o in out_shape)
    near = pl.BlockSpec(memory_space=pltpu.VMEM)
    return pl.pallas_call(
        kernel,
        out_shape=tuple(out_shape),
        in_specs=[pl.BlockSpec(memory_space=pltpu.SMEM)]
        + [near] * (len(args) - 1)
        + [pl.BlockSpec(memory_space=pltpu.HBM)] * len(blocks),
        out_specs=(near,) * len(out_shape),
        scratch_shapes=scratch,
        compiler_params=pltpu.CompilerParams(vmem_limit_bytes=room * 2**20),
        cost_estimate=pl.CostEstimate(flops=flops, bytes_accessed=moved, transcendentals=0),
        name=name,
    )(*args, *blocks)


def like(dtype, *shape):
    return jax.ShapeDtypeStruct(shape, dtype)


def block_copies(at_ref, block_refs, whole_ref, sem_ref, first=0):
    size = whole_ref.shape[0] // len(block_refs)
    copies = []
    for k, block_ref in enumerate(block_refs):
        start = pl.multiple_of(at_ref[k] * size, size)
        copies.append(
            pltpu.make_async_copy(
                block_ref.at[pl.ds(first, size), :], whole_ref.at[pl.ds(start, size), :], sem_ref.at[k]
            )
        )
    return copies


def core_rows(at_ref, count, rows, seq, other):
    core = at_ref[2 * count]
    start = seq * 2 * rows + (1 - core if other else core) * rows
    return pl.ds(pl.multiple_of(start, rows), rows)


def join_rows(at_ref, count, own_ref, other_ref, whole_ref):
    rows = own_ref.shape[1]
    for seq in range(2):
        whole_ref[core_rows(at_ref, count, rows, seq, False), :] = own_ref[seq]
        whole_ref[core_rows(at_ref, count, rows, seq, True), :] = other_ref[seq]


def part_rows(at_ref, count, whole_ref, kept_ref, away_ref):
    rows = kept_ref.shape[1]
    for seq in range(2):
        kept_ref[seq] = whole_ref[core_rows(at_ref, count, rows, seq, False), :]
        away_ref[seq] = whole_ref[core_rows(at_ref, count, rows, seq, True), :].astype(bf16)


def pair_columns_kernel(size, at_ref, gain_ref, gate_ref, up_ref, out_ref):
    gain = gain_ref[...]
    half = out_ref.shape[2] // 2
    for t in range(4):
        for position in range(half // size):
            columns = pl.ds((4 * position + t) * size, size)
            for side, ref in enumerate((gate_ref, up_ref)):
                out_ref[t, :, pl.ds(side * half + position * size, size)] = (
                    ref[:, columns].astype(f32) * gain
                ).astype(bf16)


def pair_columns(at, gain, gate, up, size):
    own, ff = gate.shape
    (out,) = on_chip(
        functools.partial(pair_columns_kernel, size),
        [like(bf16, 4, own, ff // 2)],
        [at, gain, gate, up],
        own * ff,
        name="pair_columns",
    )
    return out


def head_columns_kernel(at_ref, gain_ref, query_ref, key_ref, value_ref, out_ref):
    gain = gain_ref[...]
    query = query_ref[...].astype(f32) * gain
    key = key_ref[...].astype(f32) * gain
    value = value_ref[...].astype(f32) * gain
    for group in range(out_ref.shape[0]):
        shared = slice(group * HEAD_SIZE, (group + 1) * HEAD_SIZE)
        out_ref[group] = jnp.concatenate(
            [
                query[:, 2 * group * HEAD_SIZE : 2 * (group + 1) * HEAD_SIZE],
                key[:, shared],
                value[:, shared],
            ],
            axis=1,
        ).astype(bf16)


def head_columns(at, gain, query, key, value):
    own, width = query.shape
    (out,) = on_chip(
        head_columns_kernel,
        [like(bf16, width // HEAD_SIZE // 2, own, 4 * HEAD_SIZE)],
        [at, gain, query, key, value],
        own * width,
        name="head_columns",
    )
    return out


def normed_halves_kernel(count, at_ref, rows_ref, kept_ref, away_ref):
    core = at_ref[2 * count]
    rows = rows_ref[...].astype(f32)
    mean = jnp.mean(rows * rows, axis=-1, keepdims=True)
    normed = rows * lax.rsqrt(mean + norm_eps)
    size = rows.shape[1] // (2 * count)
    halves = [
        jnp.concatenate(
            [normed[:, (2 * i + c) * size : (2 * i + c + 1) * size] for i in range(count)], axis=1
        )
        for c in range(2)
    ]
    kept_ref[...] = jnp.where(core == 0, halves[0], halves[1]).astype(bf16)
    away_ref[...] = jnp.where(core == 0, halves[1], halves[0]).astype(bf16)


def normed_halves(at, rows, count):
    tokens, width = rows.shape
    return on_chip(
        functools.partial(normed_halves_kernel, count),
        [like(bf16, tokens, width // 2), like(bf16, tokens, width // 2)],
        [at, rows],
        8 * rows.size,
        name="normed_halves",
    )


def sequence_copies(at_ref, block_refs, whole_ref, sem_ref):
    count = len(block_refs)
    core = at_ref[2 * count]
    rows = whole_ref.shape[0] // (2 * count)
    copies = []
    for i, block_ref in enumerate(block_refs):
        for k, side in enumerate((core, 1 - core)):
            start = pl.multiple_of((2 * at_ref[i] + side) * rows, rows)
            copies.append(
                pltpu.make_async_copy(
                    block_ref.at[pl.ds(k * rows, rows), :],
                    whole_ref.at[pl.ds(start, rows), :],
                    sem_ref.at[2 * i + k],
                )
            )
    return copies


def project_heads_kernel(at_ref, own_ref, other_ref, *refs):
    blocks, (kept_ref, away_ref, weight_ref, n_ref, out_ref, sem_ref) = refs[:-6], refs[-6:]
    copies = sequence_copies(at_ref, blocks, n_ref, sem_ref)
    for copy in copies:
        copy.start()
    core = at_ref[2 * len(blocks)]
    seq = at_ref[2 * len(blocks) + 1]
    own = own_ref.shape[1]
    for position in range(len(blocks)):
        for ref, side in ((own_ref, seq), (other_ref, 1 - seq)):
            start = pl.multiple_of((2 * position + side) * own, own)
            weight_ref[pl.ds(start, own), :] = ref[position]
    for copy in copies:
        copy.wait()
    size = kept_ref.shape[0] // 3
    out_ref[...] = dot_at(weight_ref[...], n_ref[...], 0, 1)
    kept_ref[:size, :] = out_ref[pl.ds(pl.multiple_of(core * size, size), size), :]
    kept_ref[size:, :] = out_ref[2 * size :, :]
    there = pl.ds(pl.multiple_of((1 - core) * size, size), size)
    away_ref[:size, :] = out_ref[there, :].astype(bf16)
    away_ref[size:, :] = out_ref[2 * size :, :].astype(bf16)


def project_heads(at, weight_own, weight_other, blocks, rows):
    count = len(blocks)
    _, own, columns = weight_own.shape
    width = 2 * count * own
    tokens = 2 * count * rows
    size = columns // 4
    return on_chip(
        project_heads_kernel,
        [
            like(f32, 3 * size, tokens),
            like(bf16, 3 * size, tokens),
            like(bf16, width, columns),
        ],
        [at, weight_own, weight_other],
        2 * columns * tokens * width,
        blocks=blocks,
        scratch=[
            pltpu.VMEM((tokens, width), bf16),
            pltpu.VMEM((columns, tokens), f32),
            pltpu.SemaphoreType.DMA((2 * count,)),
        ],
        name="project_heads",
    )


def join_heads(heads_ref, joined_ref):
    size, rows = heads_ref.shape[1:]
    for seq in range(2):
        for head in range(heads_ref.shape[0] // 2):
            joined_ref[head * size : (head + 1) * size, seq * rows : (seq + 1) * rows] = heads_ref[
                2 * head + seq
            ]


def project_out_kernel(first, at_ref, heads_ref, *refs):
    blocks, (weight_ref, joined_ref, kept_ref, away_ref, out_ref, sem_ref) = refs[:-6], refs[-6:]
    count = len(blocks)
    own = weight_ref.shape[0] // count
    width = weight_ref.shape[1] // 2
    copies = []
    for i, block_ref in enumerate(blocks):
        start = pl.multiple_of(at_ref[i] * own, own)
        for k in range(2):
            copies.append(
                pltpu.make_async_copy(
                    block_ref.at[pl.ds(first + k * own, own), :],
                    weight_ref.at[pl.ds(start, own), pl.ds(k * width, width)],
                    sem_ref.at[2 * i + k],
                )
            )
    for copy in copies:
        copy.start()
    join_heads(heads_ref, joined_ref)
    for copy in copies:
        copy.wait()
    out_ref[...] = dot_at(joined_ref[...], weight_ref[...], 0, 0)
    part_rows(at_ref, count, out_ref, kept_ref, away_ref)


def project_out(at, heads, blocks, first, own):
    count = len(blocks)
    width = 2 * blocks[0].shape[1]
    rows = heads.shape[2] // 2
    return on_chip(
        functools.partial(project_out_kernel, first),
        [
            like(bf16, count * own, width),
            like(bf16, count * own, 4 * rows),
            like(f32, 2, rows, width),
            like(bf16, 2, rows, width),
        ],
        [at, heads],
        8 * rows * width * count * own,
        blocks=blocks,
        scratch=[pltpu.VMEM((4 * rows, width), f32), pltpu.SemaphoreType.DMA((2 * count,))],
        name="project_out",
    )


def down_pieces(rows, width, wide):
    left = wide // 2
    right = width - left
    pieces = [(i * rows // 2, 0, rows // 2, left, 0, i * left) for i in range(2)]
    parts = wide // right
    size = rows // parts
    pieces += [(i * size, left, size, right, rows // 2, i * right) for i in range(parts)]
    return pieces


def pack_down_kernel(at_ref, down_ref, pair_ref, out_ref):
    first = pair_ref.shape[0]
    out_ref[:first, :] = pair_ref[...]
    for row, column, rows, columns, to, place in down_pieces(*down_ref.shape, out_ref.shape[1]):
        out_ref[first + to : first + to + rows, place : place + columns] = down_ref[
            row : row + rows, column : column + columns
        ]


def pack_down(at, down, pair):
    first, wide = pair.shape
    (out,) = on_chip(
        pack_down_kernel,
        [like(bf16, first + down.size // wide, wide)],
        [at, down, pair],
        0,
        name="pack_down",
    )
    return out


def down_copies(at_ref, block_refs, first, down_ref, sem_ref):
    own = down_ref.shape[0] // len(block_refs)
    pieces = down_pieces(own, down_ref.shape[1], block_refs[0].shape[1])
    copies = []
    for i, block_ref in enumerate(block_refs):
        for k, (row, column, rows, columns, to, place) in enumerate(pieces):
            start = pl.multiple_of(at_ref[i] * own + row, rows)
            copies.append(
                pltpu.make_async_copy(
                    block_ref.at[pl.ds(first + to, rows), pl.ds(place, columns)],
                    down_ref.at[pl.ds(start, rows), pl.ds(column, columns)],
                    sem_ref.at[i * len(pieces) + k],
                )
            )
    return copies


def feed_forward_kernel(step, at_ref, own_ref, other_ref, d_own_ref, d_other_ref, *refs):
    blocks = refs[:-12]
    n_ref, d_out_ref, hidden_ref, d_both_ref, kept_ref, away_ref = refs[-12:-6]
    d_n_ref, d_hidden_ref, whole_ref, down_ref, sem_ref, down_sem_ref = refs[-6:]
    ff = hidden_ref.shape[1]
    first = whole_ref.shape[0] // len(blocks)
    down = down_copies(at_ref, blocks, first, down_ref, down_sem_ref)
    whole = block_copies(at_ref, blocks, whole_ref, sem_ref)
    for copy in down + whole:
        copy.start()
    join_rows(at_ref, len(blocks), own_ref, other_ref, n_ref)
    join_rows(at_ref, len(blocks), d_own_ref, d_other_ref, d_out_ref)
    for copy in down:
        copy.wait()
    d_hidden_ref[...] = dot_at(d_out_ref[...], down_ref[...], 1, 1).astype(bf16)
    for copy in whole:
        copy.wait()
    for begin in range(0, n_ref.shape[0], step):
        rows = slice(begin, begin + step)
        d_hidden = d_hidden_ref[rows, :].astype(f32)
        both = dot_at(n_ref[rows, :], whole_ref[...], 1, 0)
        gate = both[:, :ff]
        upper = both[:, ff:]
        sigma = 1.0 / (1.0 + jnp.exp(-gate))
        silu = gate * sigma
        hidden_ref[rows, :] = (silu * upper).astype(bf16)
        d_both_ref[rows, :ff] = (d_hidden * upper * (sigma + silu * (1.0 - sigma))).astype(bf16)
        d_both_ref[rows, ff:] = (d_hidden * silu).astype(bf16)
        d_n_ref[rows, :] = dot_at(d_both_ref[rows, :], whole_ref[...], 1, 1)
    part_rows(at_ref, len(blocks), d_n_ref, kept_ref, away_ref)


def feed_forward(at, own, other, d_own, d_other, blocks, ff):
    _, rows, width = own.shape
    count = len(blocks)
    pieces = len(down_pieces(ff // count, width, 2 * ff))
    return on_chip(
        functools.partial(feed_forward_kernel, min(256, 4 * rows)),
        [
            like(bf16, 4 * rows, width),
            like(bf16, 4 * rows, width),
            like(bf16, 4 * rows, ff),
            like(bf16, 4 * rows, 2 * ff),
            like(f32, 2, rows, width),
            like(bf16, 2, rows, width),
        ],
        [at, own, other, d_own, d_other],
        40 * rows * width * ff,
        blocks=blocks,
        scratch=[
            pltpu.VMEM((4 * rows, width), f32),
            pltpu.VMEM((4 * rows, ff), bf16),
            pltpu.VMEM((width, 2 * ff), bf16),
            pltpu.VMEM((ff, width), bf16),
            pltpu.SemaphoreType.DMA((count,)),
            pltpu.SemaphoreType.DMA((count * pieces,)),
        ],
        name="feed_forward",
        room=40,
    )


def packed_grads(n_ref, d_both_ref, hidden_ref, d_out_ref, position, block, own, wide):
    columns = slice(position * block, (position + 1) * block)
    yield 0, block, 0, wide, dot_at(n_ref[:, columns], d_both_ref[...], 0, 0).astype(bf16)
    columns = slice(position * own, (position + 1) * own)
    down = dot_at(hidden_ref[:, columns], d_out_ref[...], 0, 0).astype(bf16)
    for row, column, rows, width, to, start in down_pieces(own, n_ref.shape[1], wide):
        yield block + to, rows, start, width, down[row : row + rows, column : column + width]


def far_grads_kernel(count, at_ref, n_ref, d_both_ref, hidden_ref, d_out_ref, grad_ref):
    wide = grad_ref.shape[1]
    block = n_ref.shape[1] // count
    own = hidden_ref.shape[1] // count
    for position in range(count):

        @pl.when(at_ref[count // 2] == position)
        def _(position=position):
            refs = (n_ref, d_both_ref, hidden_ref, d_out_ref)
            for to, rows, start, width, part in packed_grads(*refs, position, block, own, wide):
                grad_ref[to : to + rows, start : start + width] = part


def far_grads(at, n, d_both, hidden, d_out, count):
    rows, width = n.shape
    ff = hidden.shape[1]
    (out,) = on_chip(
        functools.partial(far_grads_kernel, count),
        [like(bf16, width // count + ff // count * width // (2 * ff), 2 * ff)],
        [at, n, d_both, hidden, d_out],
        6 * rows * width * ff // count,
        name="far_grads",
    )
    return out


def feed_forward_grads_kernel(at_ref, n_ref, d_both_ref, hidden_ref, d_out_ref, grad_ref):
    count, _, wide = grad_ref.shape
    block = n_ref.shape[1] // count
    own = hidden_ref.shape[1] // count
    for position in range(count):
        place = at_ref[count + position]
        refs = (n_ref, d_both_ref, hidden_ref, d_out_ref)
        for to, rows, start, width, part in packed_grads(*refs, position, block, own, wide):
            grad_ref[place, to : to + rows, start : start + width] = part


def feed_forward_grads(at, n, d_both, hidden, d_out, count):
    rows, width = n.shape
    ff = hidden.shape[1]
    (out,) = on_chip(
        feed_forward_grads_kernel,
        [like(bf16, count, width // count + ff // count * width // (2 * ff), 2 * ff)],
        [at, n, d_both, hidden, d_out],
        6 * rows * width * ff,
        name="feed_forward_grads",
        room=32,
    )
    return out


def joined_grads_kernel(at_ref, left_ref, right_ref, grad_ref):
    count, block, _ = grad_ref.shape
    for position in range(count):
        rows = slice(position * block, (position + 1) * block)
        grad_ref[at_ref[count + position]] = dot_at(
            left_ref[rows, :], right_ref[...], 1, 0
        ).astype(bf16)


def joined_grads(at, left, right, count):
    width, rows = left.shape
    (out,) = on_chip(
        joined_grads_kernel,
        [like(bf16, count, width // count, right.shape[1])],
        [at, left, right],
        2 * rows * width * right.shape[1],
        name="joined_grads",
    )
    return out


def split_heads_kernel(at_ref, own_ref, other_ref, weight_ref, d_mid_ref, heads_ref):
    join_rows(at_ref, heads_ref.shape[0] // 2, own_ref, other_ref, d_mid_ref)
    size, rows = heads_ref.shape[1:]
    for seq in range(2):
        part = dot_at(weight_ref[...], d_mid_ref[seq * rows : (seq + 1) * rows, :], 1, 1)
        part = part.astype(bf16)
        for head in range(heads_ref.shape[0] // 2):
            heads_ref[2 * head + seq] = part[head * size : (head + 1) * size, :]


def split_heads(at, own, other, weight, heads):
    _, rows, width = own.shape
    return on_chip(
        split_heads_kernel,
        [
            like(bf16, 4 * rows, width),
            like(bf16, 2 * heads, weight.shape[0] // heads, 2 * rows),
        ],
        [at, own, other, weight],
        8 * rows * width * weight.shape[0],
        name="split_heads",
    )


def heads_grad_kernel(at_ref, joined_ref, *refs):
    blocks, (grad_ref, n_ref, sem_ref) = refs[:-3], refs[-3:]
    copies = sequence_copies(at_ref, blocks, n_ref, sem_ref)
    for copy in copies:
        copy.start()
    for copy in copies:
        copy.wait()
    grad_ref[...] = dot_at(n_ref[...], joined_ref[...], 0, 1).astype(bf16)


def heads_grad(at, joined, blocks):
    columns, tokens = joined.shape
    width = blocks[0].shape[1]
    (out,) = on_chip(
        heads_grad_kernel,
        [like(bf16, width, columns)],
        [at, joined],
        2 * tokens * width * columns,
        blocks=blocks,
        scratch=[pltpu.VMEM((tokens, width), bf16), pltpu.SemaphoreType.DMA((2 * len(blocks),))],
        name="heads_grad",
    )
    return out


def heads_input_kernel(at_ref, joined_ref, weight_ref, out_ref):
    count, rows, _ = out_ref.shape
    for position in range(count):
        columns = slice(position * rows, (position + 1) * rows)
        out_ref[at_ref[count + position]] = dot_at(
            joined_ref[:, columns], weight_ref[...], 0, 1
        ).astype(bf16)


def heads_input(at, joined, weight, count):
    width, columns = weight.shape
    tokens = joined.shape[1]
    (out,) = on_chip(
        heads_input_kernel,
        [like(bf16, count, tokens // count, width)],
        [at, joined, weight],
        2 * tokens * width * columns,
        name="heads_input",
    )
    return out


def input_rows_kernel(count, at_ref, kept_ref, other_ref, rows_ref, d_middle_ref, out_ref):
    core = at_ref[2 * count]
    kept = kept_ref[core]
    other = other_ref[...].astype(f32)
    first = jnp.where(core == 0, kept, other)
    second = jnp.where(core == 0, other, kept)
    size = kept.shape[1] // count
    pieces = []
    for i in range(count):
        pieces.append(first[:, i * size : (i + 1) * size])
        pieces.append(second[:, i * size : (i + 1) * size])
    d_normed = jnp.concatenate(pieces, axis=1)
    rows = rows_ref[...].astype(f32)
    inverse = lax.rsqrt(jnp.mean(rows * rows, axis=-1, keepdims=True) + norm_eps)
    normed = rows * inverse
    mean = jnp.mean(d_normed * normed, axis=-1, keepdims=True)
    d_middle = d_middle_ref[at_ref[2 * count + 1]]
    out_ref[...] = d_middle + inverse * (d_normed - normed * mean)


def input_rows(at, kept, other, rows, d_middle, count):
    (out,) = on_chip(
        functools.partial(input_rows_kernel, count),
        [like(f32, *rows.shape)],
        [at, kept, other, rows, d_middle],
        8 * rows.size,
        name="input_rows",
    )
    return out


def layer_output_kernel(first, at_ref, hidden_ref, *refs):
    blocks, (kept_ref, away_ref, out_ref, down_ref, sem_ref) = refs[:-5], refs[-5:]
    copies = down_copies(at_ref, blocks, first, down_ref, sem_ref)
    for copy in copies:
        copy.start()
    for copy in copies:
        copy.wait()
    out_ref[...] = dot_at(hidden_ref[...], down_ref[...], 1, 0)
    part_rows(at_ref, len(blocks), out_ref, kept_ref, away_ref)


def layer_output(at, hidden, blocks, first, width):
    ff = hidden.shape[1]
    rows = hidden.shape[0] // 4
    count = len(blocks)
    pieces = len(down_pieces(ff // count, width, 2 * ff))
    return on_chip(
        functools.partial(layer_output_kernel, first),
        [like(f32, 2, rows, width), like(bf16, 2, rows, width)],
        [at, hidden],
        0,
        blocks=blocks,
        scratch=[
            pltpu.VMEM((4 * rows, width), f32),
            pltpu.VMEM((ff, width), bf16),
            pltpu.SemaphoreType.DMA((count * pieces,)),
        ],
        name="layer_output",
    )


def query_rows_kernel(
    at_ref, terms_ref, gain_ref, query_ref, key_ref, value_ref, d_query, d_key, d_value, d_gain
):
    pieces = ([], [], [])
    for group in range(terms_ref.shape[0] // 2):
        part = terms_ref[2 * group].astype(f32) + terms_ref[2 * group + 1].astype(f32)
        pieces[0].append(part[:, : 2 * HEAD_SIZE])
        pieces[1].append(part[:, 2 * HEAD_SIZE : 3 * HEAD_SIZE])
        pieces[2].append(part[:, 3 * HEAD_SIZE :])
    gain = gain_ref[...]
    rows_sum = None
    outs = (d_query, d_key, d_value)
    for pieces_of, weight_ref, out_ref in zip(pieces, (query_ref, key_ref, value_ref), outs):
        grad = jnp.concatenate(pieces_of, axis=1)
        out_ref[...] = gain * grad
        part = jnp.sum(grad * weight_ref[...].astype(f32), axis=1, keepdims=True)
        rows_sum = part if rows_sum is None else rows_sum + part
    d_gain[...] = rows_sum


def query_rows_grads(at, terms, gain, query, key, value):
    own = query.shape[0]
    return on_chip(
        query_rows_kernel,
        [
            like(f32, *query.shape),
            like(f32, *key.shape),
            like(f32, *value.shape),
            like(f32, own, 1),
        ],
        [at, terms, gain, query, key, value],
        terms.size,
        name="query_rows_grads",
    )


def pair_rows_kernel(
    size, count, at_ref, terms_ref, down_terms, gain_ref, gate_ref, up_ref,
    d_gate, d_up, d_gain, d_down,
):
    gain = gain_ref[...]
    core = at_ref[2 * count]
    seq = at_ref[2 * count + 1]
    half = terms_ref.shape[2] // 2
    rows_sum = jnp.zeros_like(gain)
    for side, (weight_ref, out_ref) in enumerate(((gate_ref, d_gate), (up_ref, d_up))):
        for position in range(half // size):
            for t in range(4):
                columns = slice((4 * position + t) * size, (4 * position + t + 1) * size)
                start = side * half + position * size
                block = (core + t // 2) % 2 * 2 + (seq + t % 2) % 2
                grad = terms_ref[block, :, start : start + size].astype(f32)
                out_ref[:, columns] = gain * grad
                rows_sum = rows_sum + jnp.sum(
                    grad * weight_ref[:, columns].astype(f32), axis=1, keepdims=True
                )
    d_gain[...] = rows_sum
    for row, column, rows, columns, to, place in down_pieces(*d_down.shape, down_terms.shape[1]):
        d_down[row : row + rows, column : column + columns] = down_terms[
            to : to + rows, place : place + columns
        ]


def pair_rows_grads(at, terms, down_terms, gain, gate, up, size, count):
    own = gate.shape[0]
    return on_chip(
        functools.partial(pair_rows_kernel, size, count),
        [
            like(f32, *gate.shape),
            like(f32, *up.shape),
            like(f32, own, 1),
            like(f32, size, down_terms.size // size),
        ],
        [at, terms, down_terms, gain, gate, up],
        terms.size,
        name="pair_rows_grads",
    )


ring_axes = ("z", "x")
owner_axes = ("z", "x", "core", "y")
head_axes = ("z", "x", "y")


def ring_of(count):
    order = list(range(0, count, 2)) + list(range(count - 1, 0, -2))
    forward = [(order[i], order[(i + 1) % count]) for i in range(count)]
    backward = [(there, here) for here, there in forward]
    return forward, backward


def place_of(position, count):
    return jnp.where(position % 2 == 0, position // 2, count - (position + 1) // 2)


def position_at(place, count):
    place = lax.rem(place, count)
    return jnp.where(place < count // 2, 2 * place, 2 * (count - place) - 1)


def tie(*values):
    return lax.optimization_barrier(values)


def after(value, *others):
    return lax.optimization_barrier((value,) + others)[0]


class GatherRing:
    def __init__(self, shard, count):
        self.count = count
        self.forward, self.backward = ring_of(count)
        self.parts = [shard] + [None] * (count - 1)
        self.ahead = self.behind = shard
        self.hops = 0

    def start(self, *others):
        self.hops += 1
        ahead, behind = self.ahead, self.behind
        if self.hops == self.count // 2:
            half = ahead.shape[0] // 2
            ahead, behind = ahead[:half], behind[half:]
        if others:
            ahead, behind = lax.optimization_barrier((ahead, behind) + others)[:2]
        self.pending = [
            lax.ppermute(ahead, ring_axes, self.forward),
            lax.ppermute(behind, ring_axes, self.backward),
        ]

    def land(self, arrived):
        self.ahead, self.behind = arrived
        if self.hops == self.count // 2:
            self.parts[self.hops] = jnp.concatenate(arrived, axis=0)
        else:
            self.parts[self.count - self.hops] = self.ahead
            self.parts[self.hops] = self.behind


class ScatterRing:
    def __init__(self, far, count, pieces=1):
        self.count = count
        self.pieces = pieces
        self.forward, self.backward = ring_of(count)
        self.rows = far.shape[0] // 2
        self.ahead, self.behind = far[: self.rows], far[self.rows :]
        self.hops = 0

    def start(self):
        self.hops += 1
        self.pending = [
            lax.ppermute(self.ahead, ring_axes, self.forward),
            lax.ppermute(self.behind, ring_axes, self.backward),
        ]

    def land(self, arrived):
        ahead, behind = arrived
        left = self.count // 2 - self.hops
        if self.hops == 1:
            rest = ((0, 0, 0),) * (ahead.ndim - 1)
            ahead = lax.pad(ahead, bf16(0), ((0, self.rows, 0),) + rest)
            behind = lax.pad(behind, bf16(0), ((self.rows, 0, 0),) + rest)
        sides = ((self.term[left], ahead), (self.term[self.count - left], behind))
        if left > 1:
            self.ahead, self.behind = (t + v for t, v in sides)
            return
        rows = self.term.shape[1]
        self.lasts = []
        for piece in range(self.pieces):
            cut = slice(piece * rows // self.pieces, (piece + 1) * rows // self.pieces)
            ends = [t[cut] + v[cut] for t, v in sides]
            self.lasts.append(LastHop(self, self.term[0, cut], ends))


class LastHop:
    def __init__(self, ring, own, ends):
        self.ring, self.own, self.ends = ring, own, ends

    def start(self):
        ahead, behind = self.ends
        self.pending = [
            lax.ppermute(ahead, ring_axes, self.ring.forward),
            lax.ppermute(behind, ring_axes, self.ring.backward),
        ]

    def land(self, arrived):
        self.arrived = arrived

    def total(self, *others):
        ahead, behind = lax.optimization_barrier(tuple(self.arrived) + others)[:2]
        return self.own.astype(f32) + ahead.astype(f32) + behind.astype(f32)


def settle(moves, *others):
    moving = tuple(tuple(move.pending) for move in moves)
    out = lax.optimization_barrier((moving, others))
    for move, arrived in zip(moves, out[0]):
        move.land(list(arrived))
    return out[1][0] if len(others) == 1 else out[1]


def swap(values, axis):
    return lax.ppermute(values, axis, [(0, 1), (1, 0)])


def rows_of_group(own):
    pair = lax.all_gather(own, "y", axis=0)
    return lax.all_gather(pair, "core", axis=1)


def core_sum(kept, away):
    return kept + swap(away, "core").astype(f32)


def both_rows_sum(pair):
    return pair + swap(pair.astype(bf16), "y").astype(f32)


def own_rows_sum(pair):
    seq = lax.axis_index("y")
    away = lax.dynamic_index_in_dim(pair, 1 - seq, 0, False).astype(bf16)
    return lax.dynamic_index_in_dim(pair, seq, 0, False) + swap(away, "y").astype(f32)


def own_columns(blocks):
    core = lax.axis_index("core")
    seq = lax.axis_index("y")
    away = lax.dynamic_index_in_dim(blocks, 1 - seq, 1, False)
    kept = lax.dynamic_index_in_dim(blocks, seq, 1, False)
    pair = jnp.stack([kept, swap(away, "y")])
    away = lax.dynamic_index_in_dim(pair, 1 - core, 1, False)
    kept = lax.dynamic_index_in_dim(pair, core, 1, False)
    return jnp.concatenate([kept, swap(away, "core")])


def both_rows(own, *others):
    other = after(swap(own, "y"), *others)
    first = lax.axis_index("y") == 0
    return jnp.stack([jnp.where(first, own, other), jnp.where(first, other, own)])


def all_to_all(values, axes):
    return lax.all_to_all(values, axes, 0, 0, tiled=True)


def inverse_rms(values):
    return lax.rsqrt(jnp.mean(values * values, axis=-1, keepdims=True) + norm_eps)


def head_layer(
    count,
    tokens,
    cotangent,
    norm_gain1,
    w_query,
    key_weight,
    value_weight,
    w_out,
    norm_gain2,
    w_gate,
    w_up,
    w_down,
):
    rows, width = tokens.shape[1:]
    own = w_query.shape[0]
    ff_own = w_down.shape[0]
    half = HEAD_SIZE // 2
    quarter = HEAD_SIZE // 4
    group = 4 * own
    seq_rows = 2 * rows
    length = count * seq_rows
    step = seq_rows

    gain1 = norm_gain1.astype(f32)[:, None]
    gain2 = norm_gain2.astype(f32)[:, None]

    place = place_of(lax.axis_index(ring_axes), count)
    steps = jnp.arange(count, dtype=jnp.int32)
    core = lax.axis_index("core")
    seq = lax.axis_index("y")
    at = jnp.concatenate(
        [
            position_at(place + steps, count),
            lax.rem(place_of(steps, count) - place + count, count),
            jnp.stack([core, seq]).astype(jnp.int32),
        ]
    )

    position = jnp.arange(length, dtype=f32)
    exponent = jnp.arange(half, dtype=f32) * (2.0 / HEAD_SIZE)
    angle = (rope_base ** (-exponent))[:, None] * position[None, :]
    cosine = jnp.cos(angle)
    sine = jnp.sin(angle)

    own_rows = tokens[0].astype(f32)
    n1_kept, n1_away = normed_halves(at, tokens[0], count)
    n1_other = swap(n1_away, "core")
    half_width = width // 2
    n1_ring = GatherRing(
        jnp.concatenate([n1_kept, n1_other, w_out[:, :half_width], w_out[:, half_width:]], axis=0),
        count,
    )
    n1_ring.start()
    head_cols = head_columns(at, gain1, w_query, key_weight, value_weight)
    weight_own = all_to_all(head_cols, ring_axes)
    pair_cols = pair_columns(at, gain2, w_gate, w_up, ff_own)
    head_cols, pair_cols = settle([n1_ring], head_cols, pair_cols)
    n1_ring.start()
    tokens_pair = both_rows(tokens[0], head_cols)
    weight_own, tokens_pair = settle([n1_ring], weight_own, tokens_pair)
    n1_ring.start()
    weight_other = swap(weight_own, "y")
    pair_rows = all_to_all(pair_cols, ("core", "y")).reshape(group, 2 * count * ff_own)
    pair_rows = settle([n1_ring], pair_rows)
    n1_ring.start()
    ff_rows = pack_down(at, w_down, pair_rows)
    ff_rows = settle([n1_ring], ff_rows)

    gather = GatherRing(ff_rows, count)
    gather.start()
    kept, away, head_weight = project_heads(at, weight_own, weight_other, n1_ring.parts, rows)
    cotangent_pair = both_rows(after(cotangent[0], ff_rows), kept)
    mixed_send, mixed, prob, q, k, v = heads_forward(
        at, kept, swap(away, "core"), cosine, sine, count
    )
    mixed_send, cotangent_pair = settle([gather], mixed_send, cotangent_pair)
    gather.start()
    mixed_low = all_to_all(mixed_send, head_axes)
    cotangent_other = swap(cotangent_pair, "core")
    mixed_low, cotangent_other = settle([gather], mixed_low, cotangent_other)
    gather.start()
    out_weight, mixed_low, kept, away = project_out(at, mixed_low, n1_ring.parts, 2 * rows, own)
    branch = both_rows_sum(core_sum(kept, away))
    branch = settle([gather], branch)
    gather.start()
    inputs = tokens_pair.astype(f32)
    middle = inputs + branch

    r2 = inverse_rms(middle)
    n2_pair = middle * r2
    n2_own = n2_pair.astype(bf16)
    n2_other = swap(n2_own, "core")
    n2_own, n2_other = settle([gather], n2_own, n2_other)
    n2, d_out, hidden, d_both, kept, away = feed_forward(
        at, n2_own, n2_other, cotangent_pair, cotangent_other, gather.parts, count * ff_own
    )
    d_n2 = core_sum(kept, away)
    hidden = after(hidden, d_n2)
    d_normed2 = both_rows_sum(d_n2)
    far = far_grads(at, n2, d_both, hidden, d_out, count)
    scatter = ScatterRing(far, count, pieces=2)
    scatter.start()
    scatter.term = feed_forward_grads(at, n2, d_both, after(hidden, far), d_out, count)
    scatter.term = settle([scatter], scatter.term)
    scatter.start()
    d_middle = cotangent_pair.astype(f32) + r2 * (
        d_normed2 - n2_pair * jnp.mean(d_normed2 * n2_pair, axis=-1, keepdims=True)
    )

    d_mid_own = d_middle.astype(bf16)
    d_mid_other = swap(d_mid_own, "core")
    d_mid, d_mixed = split_heads(at, d_mid_own, d_mid_other, out_weight, count)
    d_mixed = all_to_all(d_mixed, head_axes)
    out_grads = joined_grads(at, mixed_low, d_mid, count)
    kept_out, away_out = layer_output(
        at, after(hidden, d_mid), gather.parts, group, width
    )
    d_mixed, out_grads, kept_out, away_out = settle(
        [scatter], d_mixed, out_grads, kept_out, away_out
    )
    out_scatter = ScatterRing(out_grads[count // 2], count)
    out_scatter.term = out_grads
    scatter.start()
    out_scatter.start()
    kept, away = heads_backward(at, q, k, v, prob, mixed, d_mixed, cosine, sine, count)
    kept, away = settle([scatter, out_scatter], kept, away)
    early, late = scatter.lasts
    early.start()
    out_scatter.start()
    away = after(away, *early.ends)
    joined = heads_join(at, kept, swap(away, "core"), count)
    grad_heads = heads_grad(at, joined, n1_ring.parts)
    d_n1 = heads_input(at, after(joined, grad_heads), head_weight, count)
    d_n1_ring = ScatterRing(d_n1[count // 2], count)
    d_n1_ring.term = d_n1
    d_n1_ring.start()
    away_out = after(away_out, joined)
    out_rows = core_sum(kept_out, away_out)
    grad_heads, out_rows = settle([early, out_scatter, d_n1_ring], grad_heads, out_rows)
    late.start()
    d_n1_ring.start()
    out_scatter.start()
    out_rows = own_rows_sum(out_rows)
    grad_heads, out_rows = settle([late, d_n1_ring, out_scatter], grad_heads, out_rows)
    d_n1_ring.start()
    (out_last,) = out_scatter.lasts
    out_last.start()
    grad_heads = all_to_all(grad_heads.reshape(2 * count, own, 4 * HEAD_SIZE), head_axes)
    sent = (d_n1_ring.ahead, d_n1_ring.behind)
    owned = jnp.concatenate([early.total(*sent), late.total(*sent)], axis=0)
    own_both = own_columns(owned[:group].astype(bf16).reshape(2, 2, own, -1))
    own_both = settle([d_n1_ring], own_both)
    (d_n1_last,) = d_n1_ring.lasts
    d_n1_last.start()
    grad_gate, grad_up, grad_gain2, owned_down = pair_rows_grads(
        at, own_both, owned[group:], gain2, w_gate, w_up, ff_own, count
    )
    grad_gate, grad_heads = settle([d_n1_last, out_last], grad_gate, grad_heads)
    grad_query, grad_key, grad_value, grad_gain1 = query_rows_grads(
        at, grad_heads, gain1, w_query, key_weight, value_weight
    )
    by_core = d_n1_last.total().reshape(2, rows, half_width)
    other = swap(lax.dynamic_index_in_dim(by_core, 1 - core, 0, False).astype(bf16), "core")
    input_grad = input_rows(at, by_core, other, tokens[0], d_middle, count)
    result = lax.dynamic_index_in_dim(middle, seq, 0, False) + out_rows
    owned_out = out_last.total()
    return (
        result.astype(bf16)[None],
        input_grad[None],
        grad_gain1[:, 0],
        grad_query,
        grad_key,
        grad_value,
        owned_out,
        grad_gain2[:, 0],
        grad_gate,
        grad_up,
        owned_down,
    )


def by_heads(mesh):
    count = mesh.shape["ctx"] // 2
    parts = Mesh(mesh.devices.reshape(count // 2, 2, 2, 2), owner_axes)
    row_spec = P("y", ("z", "x", "core"), None)
    in_specs = (row_spec, row_spec) + (P(owner_axes),) * 9
    out_specs = (row_spec, row_spec) + (P(owner_axes),) * 9
    return jax.shard_map(
        functools.partial(head_layer, count),
        mesh=parts,
        in_specs=in_specs,
        out_specs=out_specs,
        check_vma=False,
    )


def solution(mesh):
    in_specs = (
        P("fsdp", "ctx", None),
        P("fsdp", "ctx", None),
        P(("ctx", "fsdp")),
        P(("ctx", "fsdp"), None),
        P(("ctx", "fsdp"), None),
        P(("ctx", "fsdp"), None),
        P(("ctx", "fsdp"), None),
        P(("ctx", "fsdp")),
        P(("ctx", "fsdp"), None),
        P(("ctx", "fsdp"), None),
        P(("ctx", "fsdp"), None),
    )
    out_specs = (
        P("fsdp", "ctx", None),
        P("fsdp", "ctx", None),
        P(("ctx", "fsdp")),
        P(("ctx", "fsdp"), None),
        P(("ctx", "fsdp"), None),
        P(("ctx", "fsdp"), None),
        P(("ctx", "fsdp"), None),
        P(("ctx", "fsdp")),
        P(("ctx", "fsdp"), None),
        P(("ctx", "fsdp"), None),
        P(("ctx", "fsdp"), None),
    )
    if mesh.shape["ctx"] == QUERY_HEADS and mesh.shape["fsdp"] == 2:
        return by_heads(mesh)
    return jax.shard_map(local, mesh=mesh, in_specs=in_specs, out_specs=out_specs, check_vma=False)
```

```python
import functools

import jax
import jax.numpy as jnp
import numpy as np
from jax import lax
from jax.experimental import pallas as pl
from jax.experimental.pallas import tpu as pltpu
from jax.sharding import Mesh
from jax.sharding import PartitionSpec as P

QUERY_HEADS = 16
KEY_VALUE_HEADS = 8
HEAD_SIZE = 96


rope_base = 100000.0
norm_eps = 1e-05
masked_value = -1e30
key_block = 512


def rms_norm(value_rows, gain):
    return (
        value_rows
        * lax.rsqrt(jnp.mean(value_rows * value_rows, axis=-1, keepdims=True) + norm_eps)
        * gain
    )


def apply_rotary(value_rows, token_position):
    half = value_rows.shape[-1] // 2
    exponent = jnp.arange(half, dtype=jnp.float32) * (2.0 / value_rows.shape[-1])
    freq = rope_base ** (-exponent)
    angle = token_position[:, None] * freq[None, :]
    cosine = jnp.cos(angle)[:, None, :]
    sine = jnp.sin(angle)[:, None, :]
    first = value_rows[..., :half]
    second = value_rows[..., half:]
    return jnp.concatenate(
        [first * cosine - second * sine, second * cosine + first * sine], axis=-1
    )


def matmul(left, right):
    return jnp.dot(left, right, preferred_element_type=jnp.float32)


def key_pieces(key_rows, value_rows, key_value_heads, head_dim):
    count = key_rows.shape[0]
    number = count // key_block
    key_sets = key_rows.reshape(number, key_block, key_value_heads, head_dim)
    value_sets = value_rows.reshape(number, key_block, key_value_heads, head_dim)
    starts = jnp.arange(number, dtype=jnp.int32) * key_block
    return (key_sets, value_sets, starts, key_block)


def fold_keys(carry, key_rows, value_rows, query_rows, query_pos):
    key_value_heads = query_rows.shape[1]
    head_dim = query_rows.shape[3]
    scale = head_dim ** (-0.5)
    key_sets, value_sets, starts, size = key_pieces(key_rows, value_rows, key_value_heads, head_dim)

    def fold_one_piece(state, item):
        key_set, value_set, begin = item

        def fold_live(state):
            top, total, summed = state
            scores = (
                jnp.einsum(
                    "tkgd,skd->kgts", query_rows, key_set, preferred_element_type=jnp.float32
                )
                * scale
            )
            visible = (begin + jnp.arange(size, dtype=jnp.int32))[None, :] <= query_pos[:, None]
            scores = jnp.where(visible, scores, masked_value)
            new_top = jnp.maximum(top, jnp.max(scores, axis=-1))
            weights = jnp.where(visible, jnp.exp(scores - new_top[..., None]), 0.0)
            factor = jnp.exp(top - new_top)
            total = total * factor + jnp.sum(weights, axis=-1)
            summed = summed * factor[..., None] + jnp.einsum(
                "kgts,skd->kgtd",
                weights.astype(jnp.bfloat16),
                value_set,
                preferred_element_type=jnp.float32,
            )
            return (new_top, total, summed)

        def fold_skipped(state):
            return state

        return (lax.cond(begin <= query_pos[-1], fold_live, fold_skipped, state), None)

    carry, _ = lax.scan(fold_one_piece, carry, (key_sets, value_sets, starts))
    return carry


def back_keys(key_rows, value_rows, query_rows, query_pos, d_heads, log_total, delta):
    rows, key_value_heads, groups, head_dim = query_rows.shape
    scale = head_dim ** (-0.5)
    key_sets, value_sets, starts, size = key_pieces(key_rows, value_rows, key_value_heads, head_dim)

    def back_one_piece(d_query, item):
        key_set, value_set, begin = item

        def back_live(d_query):
            scores = (
                jnp.einsum(
                    "tkgd,skd->kgts", query_rows, key_set, preferred_element_type=jnp.float32
                )
                * scale
            )
            visible = (begin + jnp.arange(size, dtype=jnp.int32))[None, :] <= query_pos[:, None]
            prob = jnp.where(visible, jnp.exp(scores - log_total[..., None]), 0.0)
            d_prob = jnp.einsum(
                "tkgd,skd->kgts", d_heads, value_set, preferred_element_type=jnp.float32
            )
            d_scores = (prob * (d_prob - delta[..., None])).astype(jnp.bfloat16)
            d_query = d_query + scale * jnp.einsum(
                "kgts,skd->tkgd", d_scores, key_set, preferred_element_type=jnp.float32
            )
            d_key = scale * jnp.einsum(
                "kgts,tkgd->skd", d_scores, query_rows, preferred_element_type=jnp.float32
            )
            d_value = jnp.einsum(
                "kgts,tkgd->skd",
                prob.astype(jnp.bfloat16),
                d_heads,
                preferred_element_type=jnp.float32,
            )
            return (
                d_query,
                (
                    d_key.reshape(size, key_value_heads * head_dim),
                    d_value.reshape(size, key_value_heads * head_dim),
                ),
            )

        def back_skipped(d_query):
            empty = jnp.zeros((size, key_value_heads * head_dim), jnp.float32)
            return (d_query, (empty, empty))

        return lax.cond(begin <= query_pos[-1], back_live, back_skipped, d_query)

    start_grad = jnp.zeros((rows, key_value_heads, groups, head_dim), jnp.float32)
    d_query, (d_keys, d_values) = lax.scan(
        back_one_piece, start_grad, (key_sets, value_sets, starts)
    )
    return (
        d_query,
        d_keys.reshape(key_rows.shape[0], key_value_heads * head_dim),
        d_values.reshape(key_rows.shape[0], key_value_heads * head_dim),
    )


def local(
    tokens,
    cotangent,
    norm_gain1,
    w_query,
    key_weight,
    value_weight,
    w_out,
    norm_gain2,
    w_gate,
    w_up,
    w_down,
):
    rows = tokens.shape[1]
    key_value_heads = KEY_VALUE_HEADS
    heads = QUERY_HEADS
    head_dim = HEAD_SIZE
    groups = heads // key_value_heads
    first_row = lax.axis_index("ctx") * rows
    query_pos = first_row + jnp.arange(rows, dtype=jnp.int32)
    token_position = query_pos.astype(jnp.float32)
    inputs = tokens[0].astype(jnp.float32)
    gathered = (
        lax.all_gather(norm_gain1, ("ctx", "fsdp"), axis=0, tiled=True),
        lax.all_gather(w_query, ("ctx", "fsdp"), axis=0, tiled=True),
        lax.all_gather(key_weight, ("ctx", "fsdp"), axis=0, tiled=True),
        lax.all_gather(value_weight, ("ctx", "fsdp"), axis=0, tiled=True),
        lax.all_gather(w_out, ("ctx", "fsdp"), axis=0, tiled=True),
        lax.all_gather(norm_gain2, ("ctx", "fsdp"), axis=0, tiled=True),
        lax.all_gather(w_gate, ("ctx", "fsdp"), axis=0, tiled=True),
        lax.all_gather(w_up, ("ctx", "fsdp"), axis=0, tiled=True),
        lax.all_gather(w_down, ("ctx", "fsdp"), axis=0, tiled=True),
    )
    gain_one = gathered[0].astype(jnp.float32)
    gain_two = gathered[5].astype(jnp.float32)
    normed1 = rms_norm(inputs, gain_one).astype(jnp.bfloat16)
    query_pre = matmul(normed1, gathered[1]).reshape(rows, heads, head_dim)
    key_pre = matmul(normed1, gathered[2]).reshape(rows, key_value_heads, head_dim)
    value = matmul(normed1, gathered[3]).astype(jnp.bfloat16)
    query_rows = (
        apply_rotary(query_pre, token_position)
        .astype(jnp.bfloat16)
        .reshape(rows, key_value_heads, groups, head_dim)
    )
    key_rows = (
        apply_rotary(key_pre, token_position)
        .reshape(rows, key_value_heads * head_dim)
        .astype(jnp.bfloat16)
    )
    start_state = (
        jnp.full((key_value_heads, groups, rows), masked_value, jnp.float32),
        jnp.zeros((key_value_heads, groups, rows), jnp.float32),
        jnp.zeros((key_value_heads, groups, rows, head_dim), jnp.float32),
    )
    top, total, summed = fold_keys(
        start_state,
        lax.all_gather(key_rows, "ctx", axis=0, tiled=True),
        lax.all_gather(value, "ctx", axis=0, tiled=True),
        query_rows,
        query_pos,
    )
    mixed_heads = jnp.transpose(summed / total[..., None], (2, 0, 1, 3))
    log_total = top + jnp.log(total)
    mixed_low = mixed_heads.reshape(rows, heads * head_dim).astype(jnp.bfloat16)
    middle = inputs + matmul(mixed_low, gathered[4])
    normed2 = rms_norm(middle, gain_two).astype(jnp.bfloat16)
    gate = matmul(normed2, gathered[6])
    upper = matmul(normed2, gathered[7])
    hidden = (jax.nn.silu(gate) * upper).astype(jnp.bfloat16)
    result = middle + matmul(hidden, gathered[8])
    gathered = (
        lax.all_gather(norm_gain1, ("ctx", "fsdp"), axis=0, tiled=True),
        lax.all_gather(w_query, ("ctx", "fsdp"), axis=0, tiled=True),
        lax.all_gather(key_weight, ("ctx", "fsdp"), axis=0, tiled=True),
        lax.all_gather(value_weight, ("ctx", "fsdp"), axis=0, tiled=True),
        lax.all_gather(w_out, ("ctx", "fsdp"), axis=0, tiled=True),
        lax.all_gather(norm_gain2, ("ctx", "fsdp"), axis=0, tiled=True),
        lax.all_gather(w_gate, ("ctx", "fsdp"), axis=0, tiled=True),
        lax.all_gather(w_up, ("ctx", "fsdp"), axis=0, tiled=True),
        lax.all_gather(w_down, ("ctx", "fsdp"), axis=0, tiled=True),
    )
    incoming = cotangent[0].astype(jnp.float32)
    incoming_low = incoming.astype(jnp.bfloat16)
    grad_down = matmul(hidden.T, incoming_low)
    d_hidden = matmul(incoming_low, gathered[8].T)
    _, swiglu_back = jax.vjp(lambda gate_in, upper_in: jax.nn.silu(gate_in) * upper_in, gate, upper)
    d_gate, d_upper = swiglu_back(d_hidden)
    d_gate = d_gate.astype(jnp.bfloat16)
    d_upper = d_upper.astype(jnp.bfloat16)
    grad_gate = matmul(normed2.T, d_gate)
    grad_up = matmul(normed2.T, d_upper)
    d_normed2 = matmul(d_gate, gathered[6].T) + matmul(d_upper, gathered[7].T)
    _, norm_back2 = jax.vjp(rms_norm, middle, gain_two)
    d_middle, grad_gain2 = norm_back2(d_normed2)
    d_middle = d_middle + incoming
    owned_gain2, owned_gate, owned_up, owned_down = (
        lax.psum_scatter(grad_gain2, ("ctx", "fsdp"), scatter_dimension=0, tiled=True),
        lax.psum_scatter(grad_gate, ("ctx", "fsdp"), scatter_dimension=0, tiled=True),
        lax.psum_scatter(grad_up, ("ctx", "fsdp"), scatter_dimension=0, tiled=True),
        lax.psum_scatter(grad_down, ("ctx", "fsdp"), scatter_dimension=0, tiled=True),
    )
    d_middle_low = d_middle.astype(jnp.bfloat16)
    grad_out = matmul(mixed_low.T, d_middle_low)
    d_mixed = matmul(d_middle_low, gathered[4].T).astype(jnp.bfloat16)
    d_heads = d_mixed.reshape(rows, key_value_heads, groups, head_dim)
    delta = jnp.transpose(jnp.sum(d_heads.astype(jnp.float32) * mixed_heads, axis=-1), (1, 2, 0))
    back_keys_all, back_values_all = (
        lax.all_gather(key_rows, "ctx", axis=0, tiled=True),
        lax.all_gather(value, "ctx", axis=0, tiled=True),
    )
    d_query_rot, d_keys_all, d_values_all = back_keys(
        back_keys_all, back_values_all, query_rows, query_pos, d_heads, log_total, delta
    )
    d_keys_rot, d_value = (
        lax.psum_scatter(d_keys_all, "ctx", scatter_dimension=0, tiled=True),
        lax.psum_scatter(d_values_all, "ctx", scatter_dimension=0, tiled=True),
    )
    _, rotate_back_query = jax.vjp(
        lambda values_in: apply_rotary(values_in, token_position), query_pre
    )
    _, rotate_back_key = jax.vjp(lambda values_in: apply_rotary(values_in, token_position), key_pre)
    d_query = (
        rotate_back_query(d_query_rot.reshape(rows, heads, head_dim))[0]
        .reshape(rows, heads * head_dim)
        .astype(jnp.bfloat16)
    )
    d_key = (
        rotate_back_key(d_keys_rot.reshape(rows, key_value_heads, head_dim))[0]
        .reshape(rows, key_value_heads * head_dim)
        .astype(jnp.bfloat16)
    )
    d_value = d_value.astype(jnp.bfloat16)
    grad_query = matmul(normed1.T, d_query)
    grad_key = matmul(normed1.T, d_key)
    grad_value = matmul(normed1.T, d_value)
    d_normed1 = (
        matmul(d_query, gathered[1].T)
        + matmul(d_key, gathered[2].T)
        + matmul(d_value, gathered[3].T)
    )
    _, norm_back1 = jax.vjp(rms_norm, inputs, gain_one)
    d_inputs, grad_gain1 = norm_back1(d_normed1)
    input_grad = d_inputs + d_middle
    owned_gain1, owned_query, owned_key, owned_value, owned_out = (
        lax.psum_scatter(grad_gain1, ("ctx", "fsdp"), scatter_dimension=0, tiled=True),
        lax.psum_scatter(grad_query, ("ctx", "fsdp"), scatter_dimension=0, tiled=True),
        lax.psum_scatter(grad_key, ("ctx", "fsdp"), scatter_dimension=0, tiled=True),
        lax.psum_scatter(grad_value, ("ctx", "fsdp"), scatter_dimension=0, tiled=True),
        lax.psum_scatter(grad_out, ("ctx", "fsdp"), scatter_dimension=0, tiled=True),
    )
    return (
        result.astype(jnp.bfloat16)[None],
        input_grad[None],
        owned_gain1,
        owned_query,
        owned_key,
        owned_value,
        owned_out,
        owned_gain2,
        owned_gate,
        owned_up,
        owned_down,
    )


bf16 = jnp.bfloat16
f32 = jnp.float32
score_scale = HEAD_SIZE ** (-0.5)
log2_e = 1.4426950408889634
ln_2 = 0.6931471805599453


def dot_at(left, right, left_dim, right_dim):
    return lax.dot_general(
        left, right, (((left_dim,), (right_dim,)), ((), ())), preferred_element_type=jnp.float32
    )


def rotate(values, cosine, sine):
    half = values.shape[0] // 2
    first, second = values[:half], values[half:]
    return jnp.concatenate([first * cosine - second * sine, second * cosine + first * sine], axis=0)


def rotate_back(values, cosine, sine):
    half = values.shape[0] // 2
    first, second = values[:half], values[half:]
    return jnp.concatenate([first * cosine + second * sine, second * cosine - first * sine], axis=0)


def heads_forward_kernel(
    count, at_ref, kept_ref, other_ref, cos_ref, sin_ref,
    send_ref, mixed_ref, prob_ref, q_ref, k_ref, v_ref,
):
    size = q_ref.shape[0]
    half = size // 2
    rows = kept_ref[...] + other_ref[...].astype(f32)
    q = rotate(rows[:size], cos_ref[...], sin_ref[...])
    q_ref[...] = (q * (score_scale * log2_e)).astype(bf16)
    k_ref[...] = rotate(rows[size : 2 * size], cos_ref[...], sin_ref[...]).astype(bf16)
    v_ref[...] = rows[2 * size :].astype(bf16)
    step = send_ref.shape[2]
    offset = 0
    for block in range(count):
        begin = block * step
        end = begin + step
        scores = dot_at(k_ref[:, 0:end], q_ref[:, begin:end], 0, 0)
        key = lax.broadcasted_iota(jnp.int32, (step, step), 0)
        query = lax.broadcasted_iota(jnp.int32, (step, step), 1)
        last = jnp.where(key <= query, scores[begin:end], masked_value)
        top = jnp.max(last, axis=0, keepdims=True)
        if begin:
            top = jnp.maximum(top, jnp.max(scores[:begin], axis=0, keepdims=True))
        last = jnp.exp2(last - top)
        total = jnp.sum(last, axis=0, keepdims=True)
        if begin:
            first = jnp.exp2(scores[:begin] - top)
            total = total + jnp.sum(first, axis=0, keepdims=True)
        inverse = 1.0 / total
        prob_ref[offset + begin : offset + end, :] = (last * inverse).astype(bf16)
        if begin:
            prob_ref[offset : offset + begin, :] = (first * inverse).astype(bf16)
        mixed = dot_at(v_ref[:, 0:end], prob_ref[offset : offset + end, :], 1, 0)
        mixed_ref[:, begin:end] = mixed
        send_ref[2 * block] = mixed[:half].astype(bf16)
        send_ref[2 * block + 1] = mixed[half:].astype(bf16)
        offset += end


def heads_forward(at, kept, other, cosine, sine, count):
    tokens = kept.shape[1]
    size = kept.shape[0] // 3
    step = tokens // count
    pairs = step * count * (count + 1) // 2
    return on_chip(
        functools.partial(heads_forward_kernel, count),
        [
            like(bf16, 2 * count, size // 2, step),
            like(f32, size, tokens),
            like(bf16, pairs, step),
            like(bf16, size, tokens),
            like(bf16, size, tokens),
            like(bf16, size, tokens),
        ],
        [at, kept, other, cosine, sine],
        4 * size * pairs * step,
        name="heads_forward",
        room=32,
    )


def heads_backward_kernel(
    count, at_ref, q_ref, k_ref, v_ref, prob_ref, mixed_ref, back_ref, cos_ref, sin_ref,
    kept_ref, away_ref,
):
    half, step = back_ref.shape[1:]
    size = 2 * half
    d_k_ref = kept_ref.at[size : 2 * size]
    d_v_ref = kept_ref.at[2 * size :]
    offset = 0
    for block in range(count):
        begin = block * step
        end = begin + step
        d_mixed = jnp.concatenate([back_ref[2 * block], back_ref[2 * block + 1]], axis=0)
        delta = jnp.sum(d_mixed.astype(f32) * mixed_ref[:, begin:end], axis=0, keepdims=True)
        prob = prob_ref[offset : offset + end, :]
        d_prob = dot_at(v_ref[:, 0:end], d_mixed, 0, 0)
        d_scores = (prob.astype(f32) * (d_prob - delta)).astype(bf16)
        d_q = dot_at(k_ref[:, 0:end], d_scores, 1, 0) * score_scale
        kept_ref[:size, begin:end] = rotate_back(d_q, cos_ref[:, begin:end], sin_ref[:, begin:end])
        d_v = dot_at(d_mixed, prob, 1, 1)
        d_k = dot_at(q_ref[:, begin:end], d_scores, 1, 1) * ln_2
        if begin:
            d_v_ref[:, 0:begin] += d_v[:, 0:begin]
            d_k_ref[:, 0:begin] += d_k[:, 0:begin]
        d_v_ref[:, begin:end] = d_v[:, begin:end]
        d_k_ref[:, begin:end] = d_k[:, begin:end]
        offset += end
    d_k_ref[...] = rotate_back(d_k_ref[...], cos_ref[...], sin_ref[...])
    away_ref[...] = kept_ref[...].astype(bf16)


def heads_backward(at, q, k, v, prob, mixed, d_mixed, cosine, sine, count):
    size, tokens = q.shape
    return on_chip(
        functools.partial(heads_backward_kernel, count),
        [like(f32, 3 * size, tokens), like(bf16, 3 * size, tokens)],
        [at, q, k, v, prob, mixed, d_mixed, cosine, sine],
        8 * size * prob.size,
        name="heads_backward",
        room=32,
    )


def heads_join_kernel(count, at_ref, kept_ref, other_ref, joined_ref):
    core = at_ref[2 * count]
    size = kept_ref.shape[0] // 3
    joined_ref[pl.ds(pl.multiple_of(core * size, size), size), :] = kept_ref[:size, :].astype(bf16)
    joined_ref[pl.ds(pl.multiple_of((1 - core) * size, size), size), :] = other_ref[:size, :]
    d_kv = kept_ref[size:, :] + other_ref[size:, :].astype(f32)
    joined_ref[2 * size :, :] = d_kv.astype(bf16)


def heads_join(at, kept, other, count):
    size, tokens = kept.shape
    (out,) = on_chip(
        functools.partial(heads_join_kernel, count),
        [like(bf16, size // 3 * 4, tokens)],
        [at, kept, other],
        4 * kept.size,
        name="heads_join",
    )
    return out


def on_chip(kernel, out_shape, args, flops, blocks=(), scratch=(), name=None, room=24):
    moved = sum(a.size * a.dtype.itemsize for a in list(args) + list(blocks))
    moved += sum(o.size * o.dtype.itemsize for o in out_shape)
    near = pl.BlockSpec(memory_space=pltpu.VMEM)
    return pl.pallas_call(
        kernel,
        out_shape=tuple(out_shape),
        in_specs=[pl.BlockSpec(memory_space=pltpu.SMEM)]
        + [near] * (len(args) - 1)
        + [pl.BlockSpec(memory_space=pltpu.HBM)] * len(blocks),
        out_specs=(near,) * len(out_shape),
        scratch_shapes=scratch,
        compiler_params=pltpu.CompilerParams(vmem_limit_bytes=room * 2**20),
        cost_estimate=pl.CostEstimate(flops=flops, bytes_accessed=moved, transcendentals=0),
        name=name,
    )(*args, *blocks)


def like(dtype, *shape):
    return jax.ShapeDtypeStruct(shape, dtype)


def block_copies(at_ref, block_refs, whole_ref, sem_ref, first=0):
    size = whole_ref.shape[0] // len(block_refs)
    copies = []
    for k, block_ref in enumerate(block_refs):
        start = pl.multiple_of(at_ref[k] * size, size)
        copies.append(
            pltpu.make_async_copy(
                block_ref.at[pl.ds(first, size), :], whole_ref.at[pl.ds(start, size), :], sem_ref.at[k]
            )
        )
    return copies


def core_rows(at_ref, count, rows, seq, other):
    core = at_ref[2 * count]
    start = seq * 2 * rows + (1 - core if other else core) * rows
    return pl.ds(pl.multiple_of(start, rows), rows)


def join_rows(at_ref, count, own_ref, other_ref, whole_ref):
    rows = own_ref.shape[1]
    for seq in range(2):
        whole_ref[core_rows(at_ref, count, rows, seq, False), :] = own_ref[seq]
        whole_ref[core_rows(at_ref, count, rows, seq, True), :] = other_ref[seq]


def part_rows(at_ref, count, whole_ref, kept_ref, away_ref):
    rows = kept_ref.shape[1]
    for seq in range(2):
        kept_ref[seq] = whole_ref[core_rows(at_ref, count, rows, seq, False), :]
        away_ref[seq] = whole_ref[core_rows(at_ref, count, rows, seq, True), :].astype(bf16)


def pair_columns_kernel(size, at_ref, gain_ref, gate_ref, up_ref, out_ref):
    gain = gain_ref[...]
    half = out_ref.shape[2] // 2
    for t in range(4):
        for position in range(half // size):
            columns = pl.ds((4 * position + t) * size, size)
            for side, ref in enumerate((gate_ref, up_ref)):
                out_ref[t, :, pl.ds(side * half + position * size, size)] = (
                    ref[:, columns].astype(f32) * gain
                ).astype(bf16)


def pair_columns(at, gain, gate, up, size):
    own, ff = gate.shape
    (out,) = on_chip(
        functools.partial(pair_columns_kernel, size),
        [like(bf16, 4, own, ff // 2)],
        [at, gain, gate, up],
        own * ff,
        name="pair_columns",
    )
    return out


def head_columns_kernel(at_ref, gain_ref, query_ref, key_ref, value_ref, out_ref):
    gain = gain_ref[...]
    query = query_ref[...].astype(f32) * gain
    key = key_ref[...].astype(f32) * gain
    value = value_ref[...].astype(f32) * gain
    for group in range(out_ref.shape[0]):
        shared = slice(group * HEAD_SIZE, (group + 1) * HEAD_SIZE)
        out_ref[group] = jnp.concatenate(
            [
                query[:, 2 * group * HEAD_SIZE : 2 * (group + 1) * HEAD_SIZE],
                key[:, shared],
                value[:, shared],
            ],
            axis=1,
        ).astype(bf16)


def head_columns(at, gain, query, key, value):
    own, width = query.shape
    (out,) = on_chip(
        head_columns_kernel,
        [like(bf16, width // HEAD_SIZE // 2, own, 4 * HEAD_SIZE)],
        [at, gain, query, key, value],
        own * width,
        name="head_columns",
    )
    return out


def normed_halves_kernel(count, at_ref, rows_ref, kept_ref, away_ref):
    core = at_ref[2 * count]
    rows = rows_ref[...].astype(f32)
    mean = jnp.mean(rows * rows, axis=-1, keepdims=True)
    normed = rows * lax.rsqrt(mean + norm_eps)
    size = rows.shape[1] // (2 * count)
    halves = [
        jnp.concatenate(
            [normed[:, (2 * i + c) * size : (2 * i + c + 1) * size] for i in range(count)], axis=1
        )
        for c in range(2)
    ]
    kept_ref[...] = jnp.where(core == 0, halves[0], halves[1]).astype(bf16)
    away_ref[...] = jnp.where(core == 0, halves[1], halves[0]).astype(bf16)


def normed_halves(at, rows, count):
    tokens, width = rows.shape
    return on_chip(
        functools.partial(normed_halves_kernel, count),
        [like(bf16, tokens, width // 2), like(bf16, tokens, width // 2)],
        [at, rows],
        8 * rows.size,
        name="normed_halves",
    )


def sequence_copies(at_ref, block_refs, whole_ref, sem_ref):
    count = len(block_refs)
    core = at_ref[2 * count]
    rows = whole_ref.shape[0] // (2 * count)
    copies = []
    for i, block_ref in enumerate(block_refs):
        for k, side in enumerate((core, 1 - core)):
            start = pl.multiple_of((2 * at_ref[i] + side) * rows, rows)
            copies.append(
                pltpu.make_async_copy(
                    block_ref.at[pl.ds(k * rows, rows), :],
                    whole_ref.at[pl.ds(start, rows), :],
                    sem_ref.at[2 * i + k],
                )
            )
    return copies


def project_heads_kernel(at_ref, own_ref, other_ref, *refs):
    blocks, (kept_ref, away_ref, weight_ref, n_ref, out_ref, sem_ref) = refs[:-6], refs[-6:]
    copies = sequence_copies(at_ref, blocks, n_ref, sem_ref)
    for copy in copies:
        copy.start()
    core = at_ref[2 * len(blocks)]
    seq = at_ref[2 * len(blocks) + 1]
    own = own_ref.shape[1]
    for position in range(len(blocks)):
        for ref, side in ((own_ref, seq), (other_ref, 1 - seq)):
            start = pl.multiple_of((2 * position + side) * own, own)
            weight_ref[pl.ds(start, own), :] = ref[position]
    for copy in copies:
        copy.wait()
    size = kept_ref.shape[0] // 3
    out_ref[...] = dot_at(weight_ref[...], n_ref[...], 0, 1)
    kept_ref[:size, :] = out_ref[pl.ds(pl.multiple_of(core * size, size), size), :]
    kept_ref[size:, :] = out_ref[2 * size :, :]
    there = pl.ds(pl.multiple_of((1 - core) * size, size), size)
    away_ref[:size, :] = out_ref[there, :].astype(bf16)
    away_ref[size:, :] = out_ref[2 * size :, :].astype(bf16)


def project_heads(at, weight_own, weight_other, blocks, rows):
    count = len(blocks)
    _, own, columns = weight_own.shape
    width = 2 * count * own
    tokens = 2 * count * rows
    size = columns // 4
    return on_chip(
        project_heads_kernel,
        [
            like(f32, 3 * size, tokens),
            like(bf16, 3 * size, tokens),
            like(bf16, width, columns),
        ],
        [at, weight_own, weight_other],
        2 * columns * tokens * width,
        blocks=blocks,
        scratch=[
            pltpu.VMEM((tokens, width), bf16),
            pltpu.VMEM((columns, tokens), f32),
            pltpu.SemaphoreType.DMA((2 * count,)),
        ],
        name="project_heads",
    )


def join_heads(heads_ref, joined_ref):
    size, rows = heads_ref.shape[1:]
    for seq in range(2):
        for head in range(heads_ref.shape[0] // 2):
            joined_ref[head * size : (head + 1) * size, seq * rows : (seq + 1) * rows] = heads_ref[
                2 * head + seq
            ]


def project_out_kernel(first, at_ref, heads_ref, *refs):
    blocks, (weight_ref, joined_ref, kept_ref, away_ref, out_ref, sem_ref) = refs[:-6], refs[-6:]
    count = len(blocks)
    own = weight_ref.shape[0] // count
    width = weight_ref.shape[1] // 2
    copies = []
    for i, block_ref in enumerate(blocks):
        start = pl.multiple_of(at_ref[i] * own, own)
        for k in range(2):
            copies.append(
                pltpu.make_async_copy(
                    block_ref.at[pl.ds(first + k * own, own), :],
                    weight_ref.at[pl.ds(start, own), pl.ds(k * width, width)],
                    sem_ref.at[2 * i + k],
                )
            )
    for copy in copies:
        copy.start()
    join_heads(heads_ref, joined_ref)
    for copy in copies:
        copy.wait()
    out_ref[...] = dot_at(joined_ref[...], weight_ref[...], 0, 0)
    part_rows(at_ref, count, out_ref, kept_ref, away_ref)


def project_out(at, heads, blocks, first, own):
    count = len(blocks)
    width = 2 * blocks[0].shape[1]
    rows = heads.shape[2] // 2
    return on_chip(
        functools.partial(project_out_kernel, first),
        [
            like(bf16, count * own, width),
            like(bf16, count * own, 4 * rows),
            like(f32, 2, rows, width),
            like(bf16, 2, rows, width),
        ],
        [at, heads],
        8 * rows * width * count * own,
        blocks=blocks,
        scratch=[pltpu.VMEM((4 * rows, width), f32), pltpu.SemaphoreType.DMA((2 * count,))],
        name="project_out",
    )


def down_pieces(rows, width, wide):
    left = wide // 2
    right = width - left
    pieces = [(i * rows // 2, 0, rows // 2, left, 0, i * left) for i in range(2)]
    parts = wide // right
    size = rows // parts
    pieces += [(i * size, left, size, right, rows // 2, i * right) for i in range(parts)]
    return pieces


def pack_down_kernel(at_ref, down_ref, pair_ref, out_ref):
    first = pair_ref.shape[0]
    out_ref[:first, :] = pair_ref[...]
    for row, column, rows, columns, to, place in down_pieces(*down_ref.shape, out_ref.shape[1]):
        out_ref[first + to : first + to + rows, place : place + columns] = down_ref[
            row : row + rows, column : column + columns
        ]


def pack_down(at, down, pair):
    first, wide = pair.shape
    (out,) = on_chip(
        pack_down_kernel,
        [like(bf16, first + down.size // wide, wide)],
        [at, down, pair],
        0,
        name="pack_down",
    )
    return out


def down_copies(at_ref, block_refs, first, down_ref, sem_ref):
    own = down_ref.shape[0] // len(block_refs)
    pieces = down_pieces(own, down_ref.shape[1], block_refs[0].shape[1])
    copies = []
    for i, block_ref in enumerate(block_refs):
        for k, (row, column, rows, columns, to, place) in enumerate(pieces):
            start = pl.multiple_of(at_ref[i] * own + row, rows)
            copies.append(
                pltpu.make_async_copy(
                    block_ref.at[pl.ds(first + to, rows), pl.ds(place, columns)],
                    down_ref.at[pl.ds(start, rows), pl.ds(column, columns)],
                    sem_ref.at[i * len(pieces) + k],
                )
            )
    return copies


def feed_forward_kernel(step, at_ref, own_ref, other_ref, d_own_ref, d_other_ref, *refs):
    blocks = refs[:-12]
    n_ref, d_out_ref, hidden_ref, d_both_ref, kept_ref, away_ref = refs[-12:-6]
    d_n_ref, d_hidden_ref, whole_ref, down_ref, sem_ref, down_sem_ref = refs[-6:]
    ff = hidden_ref.shape[1]
    first = whole_ref.shape[0] // len(blocks)
    down = down_copies(at_ref, blocks, first, down_ref, down_sem_ref)
    whole = block_copies(at_ref, blocks, whole_ref, sem_ref)
    for copy in down + whole:
        copy.start()
    join_rows(at_ref, len(blocks), own_ref, other_ref, n_ref)
    join_rows(at_ref, len(blocks), d_own_ref, d_other_ref, d_out_ref)
    for copy in down:
        copy.wait()
    d_hidden_ref[...] = dot_at(d_out_ref[...], down_ref[...], 1, 1).astype(bf16)
    for copy in whole:
        copy.wait()
    for begin in range(0, n_ref.shape[0], step):
        rows = slice(begin, begin + step)
        d_hidden = d_hidden_ref[rows, :].astype(f32)
        both = dot_at(n_ref[rows, :], whole_ref[...], 1, 0)
        gate = both[:, :ff]
        upper = both[:, ff:]
        sigma = 1.0 / (1.0 + jnp.exp(-gate))
        silu = gate * sigma
        hidden_ref[rows, :] = (silu * upper).astype(bf16)
        d_both_ref[rows, :ff] = (d_hidden * upper * (sigma + silu * (1.0 - sigma))).astype(bf16)
        d_both_ref[rows, ff:] = (d_hidden * silu).astype(bf16)
        d_n_ref[rows, :] = dot_at(d_both_ref[rows, :], whole_ref[...], 1, 1)
    part_rows(at_ref, len(blocks), d_n_ref, kept_ref, away_ref)


def feed_forward(at, own, other, d_own, d_other, blocks, ff):
    _, rows, width = own.shape
    count = len(blocks)
    pieces = len(down_pieces(ff // count, width, 2 * ff))
    return on_chip(
        functools.partial(feed_forward_kernel, 4 * rows),
        [
            like(bf16, 4 * rows, width),
            like(bf16, 4 * rows, width),
            like(bf16, 4 * rows, ff),
            like(bf16, 4 * rows, 2 * ff),
            like(f32, 2, rows, width),
            like(bf16, 2, rows, width),
        ],
        [at, own, other, d_own, d_other],
        40 * rows * width * ff,
        blocks=blocks,
        scratch=[
            pltpu.VMEM((4 * rows, width), f32),
            pltpu.VMEM((4 * rows, ff), bf16),
            pltpu.VMEM((width, 2 * ff), bf16),
            pltpu.VMEM((ff, width), bf16),
            pltpu.SemaphoreType.DMA((count,)),
            pltpu.SemaphoreType.DMA((count * pieces,)),
        ],
        name="feed_forward",
        room=40,
    )


def packed_grads(n_ref, d_both_ref, hidden_ref, d_out_ref, position, block, own, wide):
    columns = slice(position * block, (position + 1) * block)
    yield 0, block, 0, wide, dot_at(n_ref[:, columns], d_both_ref[...], 0, 0).astype(bf16)
    columns = slice(position * own, (position + 1) * own)
    down = dot_at(hidden_ref[:, columns], d_out_ref[...], 0, 0).astype(bf16)
    for row, column, rows, width, to, start in down_pieces(own, n_ref.shape[1], wide):
        yield block + to, rows, start, width, down[row : row + rows, column : column + width]


def far_grads_kernel(count, at_ref, n_ref, d_both_ref, hidden_ref, d_out_ref, grad_ref):
    wide = grad_ref.shape[1]
    block = n_ref.shape[1] // count
    own = hidden_ref.shape[1] // count
    for position in range(count):

        @pl.when(at_ref[count // 2] == position)
        def _(position=position):
            refs = (n_ref, d_both_ref, hidden_ref, d_out_ref)
            for to, rows, start, width, part in packed_grads(*refs, position, block, own, wide):
                grad_ref[to : to + rows, start : start + width] = part


def far_grads(at, n, d_both, hidden, d_out, count):
    rows, width = n.shape
    ff = hidden.shape[1]
    (out,) = on_chip(
        functools.partial(far_grads_kernel, count),
        [like(bf16, width // count + ff // count * width // (2 * ff), 2 * ff)],
        [at, n, d_both, hidden, d_out],
        6 * rows * width * ff // count,
        name="far_grads",
    )
    return out


def feed_forward_grads_kernel(at_ref, n_ref, d_both_ref, hidden_ref, d_out_ref, grad_ref):
    count, _, wide = grad_ref.shape
    block = n_ref.shape[1] // count
    own = hidden_ref.shape[1] // count
    for position in range(count):
        place = at_ref[count + position]
        refs = (n_ref, d_both_ref, hidden_ref, d_out_ref)
        for to, rows, start, width, part in packed_grads(*refs, position, block, own, wide):
            grad_ref[place, to : to + rows, start : start + width] = part


def feed_forward_grads(at, n, d_both, hidden, d_out, count):
    rows, width = n.shape
    ff = hidden.shape[1]
    (out,) = on_chip(
        feed_forward_grads_kernel,
        [like(bf16, count, width // count + ff // count * width // (2 * ff), 2 * ff)],
        [at, n, d_both, hidden, d_out],
        6 * rows * width * ff,
        name="feed_forward_grads",
        room=32,
    )
    return out


def joined_grads_kernel(at_ref, left_ref, right_ref, grad_ref):
    count, block, _ = grad_ref.shape
    for position in range(count):
        rows = slice(position * block, (position + 1) * block)
        grad_ref[at_ref[count + position]] = dot_at(
            left_ref[rows, :], right_ref[...], 1, 0
        ).astype(bf16)


def joined_grads(at, left, right, count):
    width, rows = left.shape
    (out,) = on_chip(
        joined_grads_kernel,
        [like(bf16, count, width // count, right.shape[1])],
        [at, left, right],
        2 * rows * width * right.shape[1],
        name="joined_grads",
    )
    return out


def split_heads_kernel(at_ref, own_ref, other_ref, weight_ref, d_mid_ref, heads_ref):
    join_rows(at_ref, heads_ref.shape[0] // 2, own_ref, other_ref, d_mid_ref)
    size, rows = heads_ref.shape[1:]
    for seq in range(2):
        part = dot_at(weight_ref[...], d_mid_ref[seq * rows : (seq + 1) * rows, :], 1, 1)
        part = part.astype(bf16)
        for head in range(heads_ref.shape[0] // 2):
            heads_ref[2 * head + seq] = part[head * size : (head + 1) * size, :]


def split_heads(at, own, other, weight, heads):
    _, rows, width = own.shape
    return on_chip(
        split_heads_kernel,
        [
            like(bf16, 4 * rows, width),
            like(bf16, 2 * heads, weight.shape[0] // heads, 2 * rows),
        ],
        [at, own, other, weight],
        8 * rows * width * weight.shape[0],
        name="split_heads",
    )


def heads_grad_kernel(at_ref, joined_ref, *refs):
    blocks, (grad_ref, n_ref, sem_ref) = refs[:-3], refs[-3:]
    copies = sequence_copies(at_ref, blocks, n_ref, sem_ref)
    for copy in copies:
        copy.start()
    for copy in copies:
        copy.wait()
    grad_ref[...] = dot_at(n_ref[...], joined_ref[...], 0, 1).astype(bf16)


def heads_grad(at, joined, blocks):
    columns, tokens = joined.shape
    width = blocks[0].shape[1]
    (out,) = on_chip(
        heads_grad_kernel,
        [like(bf16, width, columns)],
        [at, joined],
        2 * tokens * width * columns,
        blocks=blocks,
        scratch=[pltpu.VMEM((tokens, width), bf16), pltpu.SemaphoreType.DMA((2 * len(blocks),))],
        name="heads_grad",
    )
    return out


def heads_input_kernel(at_ref, joined_ref, weight_ref, out_ref):
    count, rows, _ = out_ref.shape
    for position in range(count):
        columns = slice(position * rows, (position + 1) * rows)
        out_ref[at_ref[count + position]] = dot_at(
            joined_ref[:, columns], weight_ref[...], 0, 1
        ).astype(bf16)


def heads_input(at, joined, weight, count):
    width, columns = weight.shape
    tokens = joined.shape[1]
    (out,) = on_chip(
        heads_input_kernel,
        [like(bf16, count, tokens // count, width)],
        [at, joined, weight],
        2 * tokens * width * columns,
        name="heads_input",
    )
    return out


def input_rows_kernel(count, at_ref, kept_ref, other_ref, rows_ref, d_middle_ref, out_ref):
    core = at_ref[2 * count]
    kept = kept_ref[core]
    other = other_ref[...].astype(f32)
    first = jnp.where(core == 0, kept, other)
    second = jnp.where(core == 0, other, kept)
    size = kept.shape[1] // count
    pieces = []
    for i in range(count):
        pieces.append(first[:, i * size : (i + 1) * size])
        pieces.append(second[:, i * size : (i + 1) * size])
    d_normed = jnp.concatenate(pieces, axis=1)
    rows = rows_ref[...].astype(f32)
    inverse = lax.rsqrt(jnp.mean(rows * rows, axis=-1, keepdims=True) + norm_eps)
    normed = rows * inverse
    mean = jnp.mean(d_normed * normed, axis=-1, keepdims=True)
    d_middle = d_middle_ref[at_ref[2 * count + 1]]
    out_ref[...] = d_middle + inverse * (d_normed - normed * mean)


def input_rows(at, kept, other, rows, d_middle, count):
    (out,) = on_chip(
        functools.partial(input_rows_kernel, count),
        [like(f32, *rows.shape)],
        [at, kept, other, rows, d_middle],
        8 * rows.size,
        name="input_rows",
    )
    return out


def layer_output_kernel(first, at_ref, hidden_ref, *refs):
    blocks, (kept_ref, away_ref, out_ref, down_ref, sem_ref) = refs[:-5], refs[-5:]
    copies = down_copies(at_ref, blocks, first, down_ref, sem_ref)
    for copy in copies:
        copy.start()
    for copy in copies:
        copy.wait()
    out_ref[...] = dot_at(hidden_ref[...], down_ref[...], 1, 0)
    part_rows(at_ref, len(blocks), out_ref, kept_ref, away_ref)


def layer_output(at, hidden, blocks, first, width):
    ff = hidden.shape[1]
    rows = hidden.shape[0] // 4
    count = len(blocks)
    pieces = len(down_pieces(ff // count, width, 2 * ff))
    return on_chip(
        functools.partial(layer_output_kernel, first),
        [like(f32, 2, rows, width), like(bf16, 2, rows, width)],
        [at, hidden],
        0,
        blocks=blocks,
        scratch=[
            pltpu.VMEM((4 * rows, width), f32),
            pltpu.VMEM((ff, width), bf16),
            pltpu.SemaphoreType.DMA((count * pieces,)),
        ],
        name="layer_output",
    )


def query_rows_kernel(
    at_ref, terms_ref, gain_ref, query_ref, key_ref, value_ref, d_query, d_key, d_value, d_gain
):
    pieces = ([], [], [])
    for group in range(terms_ref.shape[0] // 2):
        part = terms_ref[2 * group].astype(f32) + terms_ref[2 * group + 1].astype(f32)
        pieces[0].append(part[:, : 2 * HEAD_SIZE])
        pieces[1].append(part[:, 2 * HEAD_SIZE : 3 * HEAD_SIZE])
        pieces[2].append(part[:, 3 * HEAD_SIZE :])
    gain = gain_ref[...]
    rows_sum = None
    outs = (d_query, d_key, d_value)
    for pieces_of, weight_ref, out_ref in zip(pieces, (query_ref, key_ref, value_ref), outs):
        grad = jnp.concatenate(pieces_of, axis=1)
        out_ref[...] = gain * grad
        part = jnp.sum(grad * weight_ref[...].astype(f32), axis=1, keepdims=True)
        rows_sum = part if rows_sum is None else rows_sum + part
    d_gain[...] = rows_sum


def query_rows_grads(at, terms, gain, query, key, value):
    own = query.shape[0]
    return on_chip(
        query_rows_kernel,
        [
            like(f32, *query.shape),
            like(f32, *key.shape),
            like(f32, *value.shape),
            like(f32, own, 1),
        ],
        [at, terms, gain, query, key, value],
        terms.size,
        name="query_rows_grads",
    )


def pair_rows_kernel(
    size, count, at_ref, terms_ref, down_terms, gain_ref, gate_ref, up_ref,
    d_gate, d_up, d_gain, d_down,
):
    gain = gain_ref[...]
    core = at_ref[2 * count]
    seq = at_ref[2 * count + 1]
    half = terms_ref.shape[2] // 2
    rows_sum = jnp.zeros_like(gain)
    for side, (weight_ref, out_ref) in enumerate(((gate_ref, d_gate), (up_ref, d_up))):
        for position in range(half // size):
            for t in range(4):
                columns = slice((4 * position + t) * size, (4 * position + t + 1) * size)
                start = side * half + position * size
                block = (core + t // 2) % 2 * 2 + (seq + t % 2) % 2
                grad = terms_ref[block, :, start : start + size].astype(f32)
                out_ref[:, columns] = gain * grad
                rows_sum = rows_sum + jnp.sum(
                    grad * weight_ref[:, columns].astype(f32), axis=1, keepdims=True
                )
    d_gain[...] = rows_sum
    for row, column, rows, columns, to, place in down_pieces(*d_down.shape, down_terms.shape[1]):
        d_down[row : row + rows, column : column + columns] = down_terms[
            to : to + rows, place : place + columns
        ]


def pair_rows_grads(at, terms, down_terms, gain, gate, up, size, count):
    own = gate.shape[0]
    return on_chip(
        functools.partial(pair_rows_kernel, size, count),
        [
            like(f32, *gate.shape),
            like(f32, *up.shape),
            like(f32, own, 1),
            like(f32, size, down_terms.size // size),
        ],
        [at, terms, down_terms, gain, gate, up],
        terms.size,
        name="pair_rows_grads",
    )


ring_axes = ("z", "x")
owner_axes = ("z", "x", "core", "y")
head_axes = ("z", "x", "y")


def ring_of(count):
    order = list(range(0, count, 2)) + list(range(count - 1, 0, -2))
    forward = [(order[i], order[(i + 1) % count]) for i in range(count)]
    backward = [(there, here) for here, there in forward]
    return forward, backward


def place_of(position, count):
    return jnp.where(position % 2 == 0, position // 2, count - (position + 1) // 2)


def position_at(place, count):
    place = lax.rem(place, count)
    return jnp.where(place < count // 2, 2 * place, 2 * (count - place) - 1)


def tie(*values):
    return lax.optimization_barrier(values)


def after(value, *others):
    return lax.optimization_barrier((value,) + others)[0]


class GatherRing:
    def __init__(self, shard, count):
        self.count = count
        self.forward, self.backward = ring_of(count)
        self.parts = [shard] + [None] * (count - 1)
        self.ahead = self.behind = shard
        self.hops = 0

    def start(self, *others):
        self.hops += 1
        ahead, behind = self.ahead, self.behind
        if self.hops == self.count // 2:
            half = ahead.shape[0] // 2
            ahead, behind = ahead[:half], behind[half:]
        if others:
            ahead, behind = lax.optimization_barrier((ahead, behind) + others)[:2]
        self.pending = [
            lax.ppermute(ahead, ring_axes, self.forward),
            lax.ppermute(behind, ring_axes, self.backward),
        ]

    def land(self, arrived):
        self.ahead, self.behind = arrived
        if self.hops == self.count // 2:
            self.parts[self.hops] = jnp.concatenate(arrived, axis=0)
        else:
            self.parts[self.count - self.hops] = self.ahead
            self.parts[self.hops] = self.behind


class ScatterRing:
    def __init__(self, far, count, pieces=1):
        self.count = count
        self.pieces = pieces
        self.forward, self.backward = ring_of(count)
        self.rows = far.shape[0] // 2
        self.ahead, self.behind = far[: self.rows], far[self.rows :]
        self.hops = 0

    def start(self):
        self.hops += 1
        self.pending = [
            lax.ppermute(self.ahead, ring_axes, self.forward),
            lax.ppermute(self.behind, ring_axes, self.backward),
        ]

    def land(self, arrived):
        ahead, behind = arrived
        left = self.count // 2 - self.hops
        if self.hops == 1:
            rest = ((0, 0, 0),) * (ahead.ndim - 1)
            ahead = lax.pad(ahead, bf16(0), ((0, self.rows, 0),) + rest)
            behind = lax.pad(behind, bf16(0), ((self.rows, 0, 0),) + rest)
        sides = ((self.term[left], ahead), (self.term[self.count - left], behind))
        if left > 1:
            self.ahead, self.behind = (t + v for t, v in sides)
            return
        rows = self.term.shape[1]
        self.lasts = []
        for piece in range(self.pieces):
            cut = slice(piece * rows // self.pieces, (piece + 1) * rows // self.pieces)
            ends = [t[cut] + v[cut] for t, v in sides]
            self.lasts.append(LastHop(self, self.term[0, cut], ends))


class LastHop:
    def __init__(self, ring, own, ends):
        self.ring, self.own, self.ends = ring, own, ends

    def start(self):
        ahead, behind = self.ends
        self.pending = [
            lax.ppermute(ahead, ring_axes, self.ring.forward),
            lax.ppermute(behind, ring_axes, self.ring.backward),
        ]

    def land(self, arrived):
        self.arrived = arrived

    def total(self, *others):
        ahead, behind = lax.optimization_barrier(tuple(self.arrived) + others)[:2]
        return self.own.astype(f32) + ahead.astype(f32) + behind.astype(f32)


def settle(moves, *others):
    moving = tuple(tuple(move.pending) for move in moves)
    out = lax.optimization_barrier((moving, others))
    for move, arrived in zip(moves, out[0]):
        move.land(list(arrived))
    return out[1][0] if len(others) == 1 else out[1]


def swap(values, axis):
    return lax.ppermute(values, axis, [(0, 1), (1, 0)])


def rows_of_group(own):
    pair = lax.all_gather(own, "y", axis=0)
    return lax.all_gather(pair, "core", axis=1)


def core_sum(kept, away):
    return kept + swap(away, "core").astype(f32)


def both_rows_sum(pair):
    return pair + swap(pair.astype(bf16), "y").astype(f32)


def own_rows_sum(pair):
    seq = lax.axis_index("y")
    away = lax.dynamic_index_in_dim(pair, 1 - seq, 0, False).astype(bf16)
    return lax.dynamic_index_in_dim(pair, seq, 0, False) + swap(away, "y").astype(f32)


def own_columns(blocks):
    core = lax.axis_index("core")
    seq = lax.axis_index("y")
    away = lax.dynamic_index_in_dim(blocks, 1 - seq, 1, False)
    kept = lax.dynamic_index_in_dim(blocks, seq, 1, False)
    pair = jnp.stack([kept, swap(away, "y")])
    away = lax.dynamic_index_in_dim(pair, 1 - core, 1, False)
    kept = lax.dynamic_index_in_dim(pair, core, 1, False)
    return jnp.concatenate([kept, swap(away, "core")])


def both_rows(own, *others):
    other = after(swap(own, "y"), *others)
    first = lax.axis_index("y") == 0
    return jnp.stack([jnp.where(first, own, other), jnp.where(first, other, own)])


def all_to_all(values, axes):
    return lax.all_to_all(values, axes, 0, 0, tiled=True)


def inverse_rms(values):
    return lax.rsqrt(jnp.mean(values * values, axis=-1, keepdims=True) + norm_eps)


def head_layer(
    count,
    tokens,
    cotangent,
    norm_gain1,
    w_query,
    key_weight,
    value_weight,
    w_out,
    norm_gain2,
    w_gate,
    w_up,
    w_down,
):
    rows, width = tokens.shape[1:]
    own = w_query.shape[0]
    ff_own = w_down.shape[0]
    half = HEAD_SIZE // 2
    quarter = HEAD_SIZE // 4
    group = 4 * own
    seq_rows = 2 * rows
    length = count * seq_rows
    step = seq_rows

    gain1 = norm_gain1.astype(f32)[:, None]
    gain2 = norm_gain2.astype(f32)[:, None]

    place = place_of(lax.axis_index(ring_axes), count)
    steps = jnp.arange(count, dtype=jnp.int32)
    core = lax.axis_index("core")
    seq = lax.axis_index("y")
    at = jnp.concatenate(
        [
            position_at(place + steps, count),
            lax.rem(place_of(steps, count) - place + count, count),
            jnp.stack([core, seq]).astype(jnp.int32),
        ]
    )

    position = jnp.arange(length, dtype=f32)
    exponent = jnp.arange(half, dtype=f32) * (2.0 / HEAD_SIZE)
    angle = (rope_base ** (-exponent))[:, None] * position[None, :]
    cosine = jnp.cos(angle)
    sine = jnp.sin(angle)

    own_rows = tokens[0].astype(f32)
    n1_kept, n1_away = normed_halves(at, tokens[0], count)
    n1_other = swap(n1_away, "core")
    half_width = width // 2
    n1_ring = GatherRing(
        jnp.concatenate([n1_kept, n1_other, w_out[:, :half_width], w_out[:, half_width:]], axis=0),
        count,
    )
    n1_ring.start()
    head_cols = head_columns(at, gain1, w_query, key_weight, value_weight)
    weight_own = all_to_all(head_cols, ring_axes)
    pair_cols = pair_columns(at, gain2, w_gate, w_up, ff_own)
    head_cols, pair_cols = settle([n1_ring], head_cols, pair_cols)
    n1_ring.start()
    tokens_pair = both_rows(tokens[0], head_cols)
    weight_own, tokens_pair = settle([n1_ring], weight_own, tokens_pair)
    n1_ring.start()
    weight_other = swap(weight_own, "y")
    pair_rows = all_to_all(pair_cols, ("core", "y")).reshape(group, 2 * count * ff_own)
    pair_rows = settle([n1_ring], pair_rows)
    n1_ring.start()
    ff_rows = pack_down(at, w_down, pair_rows)
    ff_rows = settle([n1_ring], ff_rows)

    gather = GatherRing(ff_rows, count)
    gather.start()
    kept, away, head_weight = project_heads(at, weight_own, weight_other, n1_ring.parts, rows)
    cotangent_pair = both_rows(after(cotangent[0], ff_rows), kept)
    mixed_send, mixed, prob, q, k, v = heads_forward(
        at, kept, swap(away, "core"), cosine, sine, count
    )
    mixed_send, cotangent_pair = settle([gather], mixed_send, cotangent_pair)
    gather.start()
    mixed_low = all_to_all(mixed_send, head_axes)
    mixed_low = settle([gather], mixed_low)
    gather.start()
    out_weight, mixed_low, kept, away = project_out(at, mixed_low, n1_ring.parts, 2 * rows, own)
    branch = both_rows_sum(core_sum(kept, away))
    cotangent_other = swap(after(cotangent_pair, mixed_low), "core")
    branch, cotangent_other = settle([gather], branch, cotangent_other)
    gather.start()
    inputs = tokens_pair.astype(f32)
    middle = inputs + branch

    r2 = inverse_rms(middle)
    n2_pair = middle * r2
    n2_own = n2_pair.astype(bf16)
    n2_other = swap(n2_own, "core")
    n2_own, n2_other = settle([gather], n2_own, n2_other)
    n2, d_out, hidden, d_both, kept, away = feed_forward(
        at, n2_own, n2_other, cotangent_pair, cotangent_other, gather.parts, count * ff_own
    )
    d_n2 = core_sum(kept, away)
    hidden = after(hidden, d_n2)
    d_normed2 = both_rows_sum(d_n2)
    far = far_grads(at, n2, d_both, hidden, d_out, count)
    scatter = ScatterRing(far, count, pieces=2)
    scatter.start()
    scatter.term = feed_forward_grads(at, n2, d_both, after(hidden, far), d_out, count)
    scatter.term = settle([scatter], scatter.term)
    scatter.start()
    d_middle = cotangent_pair.astype(f32) + r2 * (
        d_normed2 - n2_pair * jnp.mean(d_normed2 * n2_pair, axis=-1, keepdims=True)
    )

    d_mid_own = d_middle.astype(bf16)
    d_mid_other = swap(d_mid_own, "core")
    d_mid, d_mixed = split_heads(at, d_mid_own, d_mid_other, out_weight, count)
    d_mixed = all_to_all(d_mixed, head_axes)
    out_grads = joined_grads(at, mixed_low, d_mid, count)
    kept_out, away_out = layer_output(
        at, after(hidden, d_mid), gather.parts, group, width
    )
    d_mixed, out_grads, kept_out, away_out = settle(
        [scatter], d_mixed, out_grads, kept_out, away_out
    )
    out_scatter = ScatterRing(out_grads[count // 2], count)
    out_scatter.term = out_grads
    scatter.start()
    out_scatter.start()
    kept, away = heads_backward(at, q, k, v, prob, mixed, d_mixed, cosine, sine, count)
    kept, away = settle([scatter, out_scatter], kept, away)
    early, late = scatter.lasts
    early.start()
    out_scatter.start()
    away = after(away, *early.ends)
    joined = heads_join(at, kept, swap(away, "core"), count)
    grad_heads = heads_grad(at, joined, n1_ring.parts)
    d_n1 = heads_input(at, after(joined, grad_heads), head_weight, count)
    d_n1_ring = ScatterRing(d_n1[count // 2], count)
    d_n1_ring.term = d_n1
    d_n1_ring.start()
    away_out = after(away_out, joined)
    out_rows = core_sum(kept_out, away_out)
    grad_heads, out_rows = settle([early, out_scatter, d_n1_ring], grad_heads, out_rows)
    late.start()
    d_n1_ring.start()
    out_scatter.start()
    out_rows = own_rows_sum(out_rows)
    grad_heads, out_rows = settle([late, d_n1_ring, out_scatter], grad_heads, out_rows)
    d_n1_ring.start()
    (out_last,) = out_scatter.lasts
    out_last.start()
    grad_heads = all_to_all(grad_heads.reshape(2 * count, own, 4 * HEAD_SIZE), head_axes)
    sent = (d_n1_ring.ahead, d_n1_ring.behind)
    owned = jnp.concatenate([early.total(*sent), late.total(*sent)], axis=0)
    own_both = own_columns(owned[:group].astype(bf16).reshape(2, 2, own, -1))
    own_both = settle([d_n1_ring], own_both)
    (d_n1_last,) = d_n1_ring.lasts
    d_n1_last.start()
    grad_gate, grad_up, grad_gain2, owned_down = pair_rows_grads(
        at, own_both, owned[group:], gain2, w_gate, w_up, ff_own, count
    )
    grad_gate, grad_heads = settle([d_n1_last, out_last], grad_gate, grad_heads)
    grad_query, grad_key, grad_value, grad_gain1 = query_rows_grads(
        at, grad_heads, gain1, w_query, key_weight, value_weight
    )
    by_core = d_n1_last.total().reshape(2, rows, half_width)
    other = swap(lax.dynamic_index_in_dim(by_core, 1 - core, 0, False).astype(bf16), "core")
    input_grad = input_rows(at, by_core, other, tokens[0], d_middle, count)
    result = lax.dynamic_index_in_dim(middle, seq, 0, False) + out_rows
    owned_out = out_last.total()
    return (
        result.astype(bf16)[None],
        input_grad[None],
        grad_gain1[:, 0],
        grad_query,
        grad_key,
        grad_value,
        owned_out,
        grad_gain2[:, 0],
        grad_gate,
        grad_up,
        owned_down,
    )


def by_heads(mesh):
    count = mesh.shape["ctx"] // 2
    parts = Mesh(mesh.devices.reshape(count // 2, 2, 2, 2), owner_axes)
    row_spec = P("y", ("z", "x", "core"), None)
    in_specs = (row_spec, row_spec) + (P(owner_axes),) * 9
    out_specs = (row_spec, row_spec) + (P(owner_axes),) * 9
    return jax.shard_map(
        functools.partial(head_layer, count),
        mesh=parts,
        in_specs=in_specs,
        out_specs=out_specs,
        check_vma=False,
    )


def solution(mesh):
    in_specs = (
        P("fsdp", "ctx", None),
        P("fsdp", "ctx", None),
        P(("ctx", "fsdp")),
        P(("ctx", "fsdp"), None),
        P(("ctx", "fsdp"), None),
        P(("ctx", "fsdp"), None),
        P(("ctx", "fsdp"), None),
        P(("ctx", "fsdp")),
        P(("ctx", "fsdp"), None),
        P(("ctx", "fsdp"), None),
        P(("ctx", "fsdp"), None),
    )
    out_specs = (
        P("fsdp", "ctx", None),
        P("fsdp", "ctx", None),
        P(("ctx", "fsdp")),
        P(("ctx", "fsdp"), None),
        P(("ctx", "fsdp"), None),
        P(("ctx", "fsdp"), None),
        P(("ctx", "fsdp"), None),
        P(("ctx", "fsdp")),
        P(("ctx", "fsdp"), None),
        P(("ctx", "fsdp"), None),
        P(("ctx", "fsdp"), None),
    )
    if mesh.shape["ctx"] == QUERY_HEADS and mesh.shape["fsdp"] == 2:
        return by_heads(mesh)
    return jax.shard_map(local, mesh=mesh, in_specs=in_specs, out_specs=out_specs, check_vma=False)
```
